32 devices in a mesh: fsdp: 32 (over z, y, x, core).
Axes of the slice: x: 2, y: 2, z: 4, core: 2. Of those that a mesh axis runs over, the one named last changes fastest.
Arguments:
- input_one: bfloat16 [32768, 1024], P('fsdp'), may hold values from -6 to 6
- input_two: bfloat16 [32768, 1024], P('fsdp'), may hold values from -6 to 6
- upstream_one: bfloat16 [32768, 1024], P('fsdp'), may hold values from -6 to 6
- upstream_two: bfloat16 [32768, 1024], P('fsdp'), may hold values from -6 to 6
- lengths: int32 [32], replicated, may hold values from 512 to 1024, as said below
- destination: int32 [32], replicated, may hold values from 0 to 31, each once
- buckets: int32 [32, 32, 1024], P('fsdp'), may hold values from 0 to 31
- w_shared: bfloat16 [1024, 1024], P('fsdp'), may hold values from -3 to 3
- w_value: bfloat16 [1024, 1024], P('fsdp'), may hold values from -0.1875 to 0.1875
- w_output: bfloat16 [1024, 1024], P('fsdp'), may hold values from -1.5 to 1.5
- w_expand: bfloat16 [1024, 4096], P('fsdp'), may hold values from -0.1875 to 0.1875
- w_reduce: bfloat16 [4096, 1024], P('fsdp'), may hold values from -0.125 to 0.125
- gain_attend: float32 [1024], P('fsdp'), may hold values from 0.25 to 1.75
- shift_attend: float32 [1024], P('fsdp'), may hold values from -2.5 to 2.5
- gain_mixing: float32 [1024], P('fsdp'), may hold values from 0.25 to 1.75
- shift_mixing: float32 [1024], P('fsdp'), may hold values from -2.5 to 2.5
- bias_output: float32 [1024], P('fsdp'), may hold values from -2.5 to 2.5
- bias_expand: float32 [4096], P('fsdp'), may hold values from -2.5 to 2.5
- bias_reduce: float32 [1024], P('fsdp'), may hold values from -2.5 to 2.5
Outputs:
- result_one: bfloat16 [32768, 1024], P('fsdp')
- result_two: bfloat16 [32768, 1024], P('fsdp')
- grad_one: bfloat16 [32768, 1024], P('fsdp')
- grad_two: bfloat16 [32768, 1024], P('fsdp')
- grad_shared: float32 [1024, 1024], P('fsdp')
- grad_value: float32 [1024, 1024], P('fsdp')
- grad_output: float32 [1024, 1024], P('fsdp')
- grad_expand: float32 [1024, 4096], P('fsdp')
- grad_reduce: float32 [4096, 1024], P('fsdp')
- grad_gain_attend: float32 [1024], P('fsdp')
- grad_shift_attend: float32 [1024], P('fsdp')
- grad_gain_mixing: float32 [1024], P('fsdp')
- grad_shift_mixing: float32 [1024], P('fsdp')
- grad_bias_output: float32 [1024], P('fsdp')
- grad_bias_expand: float32 [4096], P('fsdp')
- grad_bias_reduce: float32 [1024], P('fsdp')
The draws below stay inside these ranges and needn't reach their ends.
Inputs may be any that keep to these rules, and one draw needn't show every extreme that they name: `lengths`: the longest sequence has exactly 1024 tokens. `destination`: each device index receives exactly one sequence.
All inputs are finite; a program needn't handle non-finite values.
Results may differ from the reference program's by a relative error of at most 0.035.
Values may be sent and summed in bfloat16 or wider, within the bound.
A program may use at most 384 MiB of HBM per device.

```python
import math
import jax
import jax.numpy as jnp
from jax import lax

D = 1024
HEADS = 8
DH = 128
FF = 4096
GROUP = 64
ROUNDS = 4
BUCKETS = 32
SEQ_CAP = 1024
MIN_LEN = 512
NSEQ = 32
TOKENS = 32768


def draw_lengths(key, part):
    first_key, second_key = jax.random.split(key)
    picked = jax.random.randint(first_key, (NSEQ,), MIN_LEN, SEQ_CAP + 1, dtype=jnp.int32)
    longest = jax.random.randint(second_key, (), 0, NSEQ, dtype=jnp.int32)
    return jnp.where(jnp.arange(NSEQ, dtype=jnp.int32) == longest, SEQ_CAP, picked).astype(jnp.int32)


def touch_ends(result, rng, smallest, top_value):
    place = [jax.random.randint(jax.random.fold_in(rng, axis), (), 0, length) for axis, length in enumerate(result.shape)]
    widest = result.shape.index(max(result.shape))
    neighbour = place[:widest] + [(place[widest] + 1) % result.shape[widest]] + place[widest + 1:]
    return result.at[tuple(place)].set(smallest).at[tuple(neighbour)].set(top_value)


def level_of(rng, shape, shards, smallest, largest):
    def one(dim, shards_of):
        steps = jax.random.uniform(jax.random.fold_in(jax.random.fold_in(rng, 6), dim), (shards_of,), jnp.float32, smallest / len(shards), largest / len(shards))
        return jnp.repeat(jnp.exp(steps), shape[dim] // shards_of).reshape((-1,) + (1,) * (len(shape) - dim - 1))

    loudness = one(*shards[0])
    for cut in shards[1:]:
        loudness = loudness * one(*cut)
    return loudness


def centred(rng, dims, scale, reach, cuts=(), kind=jnp.bfloat16):
    values = jax.random.normal(rng, dims, jnp.float32) * scale
    if len(cuts) > 0:
        values = level_of(rng, dims, cuts, -0.22, 0.18) * values
    return jnp.clip(values, min=-reach, max=reach).astype(kind)


def setup_inputs(seed: int = 0) -> dict:
    splits = jax.random.split(jax.random.key(seed), 20)
    input_one = centred(splits[0], (TOKENS, D), 1.0, 6.0, ((0, 32),))
    input_two = centred(splits[1], (TOKENS, D), 1.0, 6.0, ((0, 32),))
    upstream_one = centred(splits[2], (TOKENS, D), 1.0, 6.0, ((0, 32),))
    upstream_two = centred(splits[3], (TOKENS, D), 1.0, 6.0, ((0, 32),))
    lengths = draw_lengths(jax.random.fold_in(splits[19], 71), 0)
    destination = jax.random.permutation(splits[5], NSEQ).astype(jnp.int32)
    buckets = touch_ends(jax.random.randint(splits[6], (NSEQ, ROUNDS * HEADS, SEQ_CAP), 0, BUCKETS), jax.random.fold_in(splits[6], 1), 0, BUCKETS - 1).astype(jnp.int32)
    w_shared = centred(splits[7], (D, D), (max(D // 256, 1)) ** -0.5, 3.0, ((0, 32),))
    w_value = centred(splits[8], (D, D), D ** -0.5, 0.1875, ((0, 32),))
    w_output = centred(splits[9], (D, D), (max(D // 64, 1)) ** -0.5, 1.5, ((0, 32),))
    w_expand = centred(splits[10], (D, FF), D ** -0.5, 0.1875, ((0, 32),))
    w_reduce = centred(splits[11], (FF, D), (FF // 2) ** -0.5, 0.125, ((0, 32),))
    gain_attend = jnp.clip(1.0 + 0.15 * jax.random.normal(splits[12], (D,), jnp.float32), 0.25, 1.75)
    shift_attend = centred(splits[13], (D,), 0.3, 2.5, ((0, 32),), jnp.float32)
    gain_mixing = jnp.clip(1.0 + 0.15 * jax.random.normal(splits[14], (D,), jnp.float32), 0.25, 1.75)
    shift_mixing = centred(splits[15], (D,), 0.3, 2.5, ((0, 32),), jnp.float32)
    bias_output = centred(splits[16], (D,), 0.3, 2.5, ((0, 32),), jnp.float32)
    bias_expand = centred(splits[17], (FF,), 0.3, 2.5, ((0, 32),), jnp.float32)
    bias_reduce = centred(splits[18], (D,), 0.3, 2.5, ((0, 32),), jnp.float32)
    return {"input_one": input_one, "input_two": input_two, "upstream_one": upstream_one, "upstream_two": upstream_two, "lengths": lengths, "destination": destination, "buckets": buckets, "w_shared": w_shared, "w_value": w_value, "w_output": w_output, "w_expand": w_expand, "w_reduce": w_reduce, "gain_attend": gain_attend, "shift_attend": shift_attend, "gain_mixing": gain_mixing, "shift_mixing": shift_mixing, "bias_output": bias_output, "bias_expand": bias_expand, "bias_reduce": bias_reduce}


@jax.custom_vjp
def low(v):
    return lax.optimization_barrier(v.astype(jnp.bfloat16)).astype(jnp.float32)

@jax.custom_vjp
def low_back(v):
    return v

def low_keep(v):
    return (low(v), None)

def low_pass(kept, grad):
    return (grad,)

def back_keep(v):
    return (v, None)

def back_low(kept, grad):
    return (low(grad),)
low.defvjp(low_keep, low_pass)
low_back.defvjp(back_keep, back_low)
HIGHEST = lax.Precision.HIGHEST
EPS_NORM = 1e-05
EPS_UNIT = 1e-06
SELF_SCORE = -100000.0
MASKED_SCORE = -1000000000.0

def layer_norm(values, gain, shift):
    center = values - lax.optimization_barrier(jnp.mean(values, axis=-1, keepdims=True))
    spread = lax.optimization_barrier(jnp.mean(center * center, axis=-1, keepdims=True))
    return center * lax.rsqrt(spread + EPS_NORM) * gain + shift

def unit_keys(shared):
    return shared * lax.rsqrt(lax.optimization_barrier(jnp.sum(shared * shared, axis=-1, keepdims=True)) + EPS_UNIT)

def attend_head(query, keys, values, ordering, length):
    blocks = SEQ_CAP // GROUP
    place_sorted = ordering.reshape(blocks, GROUP)
    query_blocks = query[ordering].reshape(blocks, GROUP, DH)
    key_blocks = keys[ordering].reshape(blocks, GROUP, DH)
    value_blocks = values[ordering].reshape(blocks, GROUP, DH)
    key_pairs = jnp.concatenate([jnp.concatenate([jnp.zeros_like(key_blocks[:1]), key_blocks[:-1]], axis=0), key_blocks], axis=1)
    value_pairs = jnp.concatenate([jnp.concatenate([jnp.zeros_like(value_blocks[:1]), value_blocks[:-1]], axis=0), value_blocks], axis=1)
    prior_place = jnp.concatenate([jnp.full((1, GROUP), 2 * SEQ_CAP, jnp.int32), place_sorted[:-1]], axis=0)
    key_place = jnp.concatenate([prior_place, place_sorted], axis=1)
    raw_scores = jnp.einsum('cqd,ckd->cqk', query_blocks, key_pairs, precision=HIGHEST) / math.sqrt(DH)
    raw_scores = low_back(raw_scores)
    key_at = key_place[:, None, :]
    query_at = place_sorted[:, :, None]
    allowed = (key_at <= query_at) & (key_at < length)
    scores = jnp.where(allowed, jnp.where(key_at == query_at, SELF_SCORE, raw_scores), MASKED_SCORE)
    log_total = jax.scipy.special.logsumexp(scores, axis=-1)
    weights = low(jnp.exp(scores - log_total[..., None]))
    partial_value = jnp.einsum('cqk,ckd->cqd', weights, value_pairs, precision=HIGHEST).reshape(SEQ_CAP, DH)
    inverse = jnp.argsort(ordering).astype(jnp.int32)
    return (partial_value[inverse], log_total.reshape(SEQ_CAP)[inverse])

def sequence_forward(part_one, part_two, length, bucket_rows, params):
    w_shared, w_value, w_output, w_expand, w_reduce, gain_attend, shift_attend, gain_mixing, shift_mixing, bias_output, bias_expand, bias_reduce = params
    positions = jnp.arange(SEQ_CAP, dtype=jnp.int32)
    live_rows = (positions < length).astype(jnp.float32)[:, None]
    normed_one = low(layer_norm(part_two, gain_attend, shift_attend))
    shared = low_back(low(jnp.dot(normed_one, w_shared, precision=HIGHEST)))
    values = low_back(low(jnp.dot(normed_one, w_value, precision=HIGHEST)))
    shared_heads = shared.reshape(SEQ_CAP, HEADS, DH).transpose(1, 0, 2)
    value_heads = values.reshape(SEQ_CAP, HEADS, DH).transpose(1, 0, 2)
    unit_heads = low(unit_keys(shared_heads))
    bucket_of = bucket_rows.reshape(ROUNDS, HEADS, SEQ_CAP)
    sort_key = jnp.where(positions < length, bucket_of * SEQ_CAP + positions, BUCKETS * SEQ_CAP + positions)
    ordering = jnp.argsort(sort_key, axis=-1).astype(jnp.int32)
    over_heads = jax.vmap(attend_head, in_axes=(0, 0, 0, 0, None))
    over_rounds = jax.vmap(over_heads, in_axes=(None, None, None, 0, None))
    partials, log_totals = over_rounds(shared_heads, unit_heads, value_heads, ordering, length)
    partials = low_back(partials)
    mixing = jax.nn.softmax(log_totals, axis=0)
    combined = lax.optimization_barrier(jnp.sum(mixing[..., None] * partials, axis=0)).transpose(1, 0, 2).reshape(SEQ_CAP, D)
    combined = low(combined)
    attend = low_back(jnp.dot(combined, w_output, precision=HIGHEST) + bias_output)
    out_one = part_one + live_rows * attend
    second = low(layer_norm(out_one, gain_mixing, shift_mixing))
    pre_act = low_back(jnp.dot(second, w_expand, precision=HIGHEST) + bias_expand)
    expand = low(jax.nn.gelu(pre_act, approximate=True))
    reduce_out = low_back(jnp.dot(expand, w_reduce, precision=HIGHEST) + bias_reduce)
    out_two = part_two + live_rows * reduce_out
    return (out_one, out_two)

def forward(stream_one, stream_two, params, lengths, destination, buckets):
    ends = jnp.cumsum(lengths).astype(jnp.int32)
    starts = (ends - lengths).astype(jnp.int32)
    positions = jnp.arange(SEQ_CAP, dtype=jnp.int32)
    step_layer = jax.checkpoint(sequence_forward)

    def visit(carry, sequence):
        length = lengths[sequence]
        row_index = jnp.clip(starts[sequence] + positions, 0, TOKENS - 1).astype(jnp.int32)
        inside = (positions < length).astype(jnp.float32)[:, None]
        part_one = stream_one[row_index] * inside
        part_two = stream_two[row_index] * inside
        outcome = step_layer(part_one, part_two, length, buckets[destination[sequence]], params)
        return (carry, outcome)
    unused, slot_values = lax.scan(visit, jnp.int32(0), jnp.arange(NSEQ, dtype=jnp.int32))
    stream_rows = jnp.arange(TOKENS, dtype=jnp.int32)
    owner = jnp.minimum(jnp.searchsorted(ends, stream_rows, side='right'), NSEQ - 1).astype(jnp.int32)
    offset = jnp.clip(stream_rows - starts[owner], 0, SEQ_CAP - 1).astype(jnp.int32)
    valid = (stream_rows < ends[-1]).astype(jnp.float32)[:, None]
    return (slot_values[0][owner, offset] * valid, slot_values[1][owner, offset] * valid)

def reference(input_one, input_two, upstream_one, upstream_two, lengths, destination, buckets, w_shared, w_value, w_output, w_expand, w_reduce, gain_attend, shift_attend, gain_mixing, shift_mixing, bias_output, bias_expand, bias_reduce):
    params = tuple((member.astype(jnp.float32) for member in (w_shared, w_value, w_output, w_expand, w_reduce, gain_attend, shift_attend, gain_mixing, shift_mixing, bias_output, bias_expand, bias_reduce)))

    def apply_layer(stream_one, stream_two, weights_all):
        return forward(stream_one, stream_two, weights_all, lengths, destination, buckets)
    outcome, pullback = jax.vjp(apply_layer, input_one.astype(jnp.float32), input_two.astype(jnp.float32), params)
    back_one, back_two, grads = pullback((upstream_one.astype(jnp.float32), upstream_two.astype(jnp.float32)))
    return (outcome[0].astype(jnp.bfloat16), outcome[1].astype(jnp.bfloat16), back_one.astype(jnp.bfloat16), back_two.astype(jnp.bfloat16), grads[0], grads[1], grads[2], grads[3], grads[4], grads[5], grads[6], grads[7], grads[8], grads[9], grads[10], grads[11])
```

```python
import functools
import math

import jax
import jax.numpy as jnp
from jax import lax
from jax.experimental import pallas as pl
from jax.experimental.pallas import tpu as pltpu
from jax.sharding import PartitionSpec as P

HEADS = 8
DH = 128
GROUP = 64
ROUNDS = 4
BUCKETS = 32
EPS_NORM = 1e-05
EPS_UNIT = 1e-06
LOG2E = math.log2(math.e)
SELF2 = -100000.0 * LOG2E
NEG = -1e30
SCALE = 1.0 / math.sqrt(DH)
TILE = 256
FREE = 99.0

NT = (((1,), (1,)), ((), ()))
NN = (((1,), (0,)), ((), ()))
TN = (((0,), (0,)), ((), ()))
F32 = jnp.float32
BF16 = jnp.bfloat16


def dot(a, b, dims=NN):
    return lax.dot_general(a, b, dims, preferred_element_type=F32)


def layer_norm(values, gain, shift):
    center = values - jnp.mean(values, axis=-1, keepdims=True)
    spread = jnp.mean(center * center, axis=-1, keepdims=True)
    return center * lax.rsqrt(spread + EPS_NORM) * gain + shift


def norm_back(values, gain, shift, upstream):
    outcome, pullback = jax.vjp(layer_norm, values, gain, shift)
    return pullback(upstream)


def prepare(q_ref, code_ref, spread_ref, unit_s, ask_s, key_s):
    rows = q_ref.shape[0]
    lane = lax.broadcasted_iota(jnp.int32, (TILE, DH), 1)
    target = ((lane // 64) * 32 + lane % 16).astype(F32)
    for i in range(rows // TILE):
        at = pl.ds(i * TILE, TILE)
        q = q_ref[at, :].astype(F32)
        norm = lax.rsqrt(jnp.sum(q * q, axis=1, keepdims=True) + EPS_UNIT)
        unit_s[at, :] = (q * (norm * (SCALE * LOG2E))).astype(BF16)
        code = dot(code_ref[at, :], spread_ref[...])
        here = code == target
        ask_s[at, :] = jnp.where(here, 1.0, 0.0).astype(BF16)
        key_s[at, :] = jnp.where(here | (code + 1.0 == target), 1.0, 0.0).astype(BF16)


def attend_kernel(low_ref, q_ref, v_ref, code_ref, spread_ref, comb_ref, lse_ref, lone_ref, unit_s, ask_s, key_s, vt_s, acc_s):
    rows = q_ref.shape[0]
    prepare(q_ref, code_ref, spread_ref, unit_s, ask_s, key_s)
    for i in range(rows // TILE):
        at = pl.ds(i * TILE, TILE)
        vt_s[:, at] = v_ref[at, :].astype(F32).T.astype(BF16)
    key_at = lax.broadcasted_iota(jnp.int32, (TILE, TILE), 0)
    ask_at = lax.broadcasted_iota(jnp.int32, (TILE, TILE), 1)
    for i in range(rows // TILE):
        at = pl.ds(i * TILE, TILE)
        low = low_ref[i]

        @pl.when(low <= i)
        def _():
            q = q_ref[at, :]
            ask = ask_s[at, :]
            score = dot(unit_s[at, :], q, NT)
            count = dot(key_s[at, :], ask, NT)
            score = jnp.where(key_at == ask_at, SELF2, score)
            score = jnp.where((key_at <= ask_at) & (count > 0.5), score, NEG)
            top = jnp.max(score, axis=0, keepdims=True)
            prob = count * jnp.exp2(score - top)
            total = jnp.sum(prob, axis=0, keepdims=True)
            acc_s[...] = dot(vt_s[:, at], prob.astype(BF16))

            def step(j, carry):
                top, total = carry
                key_rows = pl.ds(pl.multiple_of(j * TILE, TILE), TILE)
                score = dot(unit_s[key_rows, :], q, NT)
                count = dot(key_s[key_rows, :], ask, NT)
                score = jnp.where(count > 0.5, score, NEG)
                newer = jnp.maximum(top, jnp.max(score, axis=0, keepdims=True))
                fade = jnp.exp2(top - newer)
                prob = count * jnp.exp2(score - newer)
                acc_s[...] = acc_s[...] * fade + dot(vt_s[:, key_rows], prob.astype(BF16))
                return newer, total * fade + jnp.sum(prob, axis=0, keepdims=True)

            top, total = lax.fori_loop(low, i, step, (top, total))
            some = total > 0.0
            safe = jnp.where(some, total, 1.0)
            inverse = jnp.where(some, 1.0 / safe, 0.0)
            comb_ref[at, :] = (acc_s[...] * inverse).T.astype(BF16)
            lse_ref[0, :, at] = top + jnp.log2(safe)
            lone_ref[0, :, at] = ROUNDS * jnp.exp2(SELF2 - jnp.maximum(top, SELF2)) * inverse

        @pl.when(low > i)
        def _():
            comb_ref[at, :] = jnp.zeros((TILE, DH), BF16)
            lse_ref[0, :, at] = jnp.zeros((1, TILE), F32)
            lone_ref[0, :, at] = jnp.zeros((1, TILE), F32)


def back_kernel(
    low_ref, q_ref, v_ref, code_ref, spread_ref, comb_ref, above_ref, lse_ref, lone_ref,
    dq_ref, dv_ref, unit_s, ask_s, key_s, dunit_s, dvalue_s, dask_s,
):
    rows = q_ref.shape[0]
    prepare(q_ref, code_ref, spread_ref, unit_s, ask_s, key_s)
    key_at = lax.broadcasted_iota(jnp.int32, (TILE, TILE), 0)
    ask_at = lax.broadcasted_iota(jnp.int32, (TILE, TILE), 1)
    dunit_s[...] = jnp.zeros(dunit_s.shape, F32)
    dvalue_s[...] = jnp.zeros(dvalue_s.shape, F32)
    dask_s[...] = jnp.zeros(dask_s.shape, F32)
    for i in range(rows // TILE):
        at = pl.ds(i * TILE, TILE)
        low = low_ref[i]

        @pl.when(low <= i)
        def _():
            q = q_ref[at, :]
            ask = ask_s[at, :]
            above = above_ref[at, :]
            lse = lse_ref[0, :, at]
            mixed = above.astype(F32) * comb_ref[at, :].astype(F32)
            delta = jnp.sum(mixed.T, axis=0, keepdims=True)
            score = dot(unit_s[at, :], q, NT)
            count = dot(key_s[at, :], ask, NT)
            d_prob = dot(v_ref[at, :], above, NT)
            earlier = key_at < ask_at
            prob = count * jnp.exp2(jnp.minimum(score - lse, 0.0))
            prob = jnp.where(earlier, prob, 0.0)
            d_score = (prob * (d_prob - delta)).astype(BF16)
            prob = jnp.where(key_at == ask_at, lone_ref[0, :, at], prob).astype(BF16)
            dvalue_s[at, :] += dot(prob, above)
            dunit_s[at, :] += dot(d_score, q)
            dask_s[at, :] += dot(d_score, unit_s[at, :], TN)

            def step(j, carry):
                key_rows = pl.ds(pl.multiple_of(j * TILE, TILE), TILE)
                unit = unit_s[key_rows, :]
                score = dot(unit, q, NT)
                count = dot(key_s[key_rows, :], ask, NT)
                d_prob = dot(v_ref[key_rows, :], above, NT)
                prob = count * jnp.exp2(jnp.minimum(score - lse, 0.0))
                d_score = (prob * (d_prob - delta)).astype(BF16)
                dvalue_s[key_rows, :] += dot(prob.astype(BF16), above)
                dunit_s[key_rows, :] += dot(d_score, q)
                dask_s[at, :] += dot(d_score, unit, TN)
                return carry

            lax.fori_loop(low, i, step, 0)

    for i in range(rows // TILE):
        at = pl.ds(i * TILE, TILE)
        q = q_ref[at, :].astype(F32)
        norm = lax.rsqrt(jnp.sum(q * q, axis=1, keepdims=True) + EPS_UNIT)
        d_unit = dunit_s[at, :] * SCALE
        along = jnp.sum(q * d_unit, axis=1, keepdims=True)
        d_q = dask_s[at, :] * (1.0 / LOG2E) + d_unit * norm - q * (norm * norm * norm * along)
        dq_ref[at, :] = d_q.astype(BF16)
        dv_ref[at, :] = dvalue_s[at, :].astype(BF16)


def head_specs(rows):
    by_head = pl.BlockSpec((rows, DH), lambda h, low: (0, h))
    code = pl.BlockSpec((rows, ROUNDS * HEADS), lambda h, low: (0, 0))
    spread = pl.BlockSpec((ROUNDS * HEADS, DH), lambda h, low: (0, h))
    stat = pl.BlockSpec((1, 1, rows), lambda h, low: (h, 0, 0))
    return by_head, code, spread, stat


def attend(low, shared, values, code, spread):
    rows = shared.shape[0]
    by_head, code_spec, spread_spec, stat = head_specs(rows)
    wide = jax.ShapeDtypeStruct((rows, HEADS * DH), BF16)
    thin = jax.ShapeDtypeStruct((HEADS, 1, rows), F32)
    return pl.pallas_call(
        attend_kernel,
        grid_spec=pltpu.PrefetchScalarGridSpec(
            num_scalar_prefetch=1,
            grid=(HEADS,),
            in_specs=[by_head, by_head, code_spec, spread_spec],
            out_specs=[by_head, stat, stat],
            scratch_shapes=[pltpu.VMEM((rows, DH), BF16)] * 3
            + [pltpu.VMEM((DH, rows), BF16), pltpu.VMEM((DH, TILE), F32)],
        ),
        out_shape=(wide, thin, thin),
        name="attend",
        cost_estimate=pl.CostEstimate(
            flops=HEADS * 20 * 3 * 2 * TILE * TILE * DH, bytes_accessed=rows * HEADS * DH * 6, transcendentals=HEADS * 20 * TILE * TILE
        ),
    )(low, shared, values, code, spread)


def attend_back(low, shared, values, code, spread, combined, above, lse, lone):
    rows = shared.shape[0]
    by_head, code_spec, spread_spec, stat = head_specs(rows)
    wide = jax.ShapeDtypeStruct((rows, HEADS * DH), BF16)
    return pl.pallas_call(
        back_kernel,
        grid_spec=pltpu.PrefetchScalarGridSpec(
            num_scalar_prefetch=1,
            grid=(HEADS,),
            in_specs=[by_head, by_head, code_spec, spread_spec, by_head, by_head, stat, stat],
            out_specs=[by_head, by_head],
            scratch_shapes=[pltpu.VMEM((rows, DH), BF16)] * 3 + [pltpu.VMEM((rows, DH), F32)] * 3,
        ),
        out_shape=(wide, wide),
        name="attend_back",
        cost_estimate=pl.CostEstimate(
            flops=HEADS * 20 * 6 * 2 * TILE * TILE * DH, bytes_accessed=rows * HEADS * DH * 12, transcendentals=HEADS * 20 * TILE * TILE
        ),
    )(low, shared, values, code, spread, combined, above, lse, lone)


def block_of_rank(buckets, length):
    slots = buckets.shape[-1]
    place = lax.broadcasted_iota(jnp.int32, (1, 1, slots), 2)
    bucket = lax.broadcasted_iota(jnp.int32, (1, BUCKETS, 1), 1)
    one_hot = (buckets[:, None, :] == bucket) & (place < length)
    first = lax.broadcasted_iota(jnp.int32, (slots, slots), 0)
    second = lax.broadcasted_iota(jnp.int32, (slots, slots), 1)
    before = dot(one_hot.astype(BF16).reshape(-1, slots), (first < second).astype(BF16)).reshape(one_hot.shape)
    size = jnp.sum(one_hot.astype(F32), axis=2, keepdims=True)
    offset = jnp.cumsum(size, axis=1) - size
    rank = jnp.sum(jnp.where(one_hot, before + offset, 0.0), axis=1)
    return jnp.where(place[0] < length, jnp.floor(rank * (1.0 / GROUP)), FREE)


def body(
    input_one, input_two, upstream_one, upstream_two, lengths, destination, buckets,
    w_shared, w_value, w_output, w_expand, w_reduce,
    gain_attend, shift_attend, gain_mixing, shift_mixing, bias_output, bias_expand, bias_reduce,
):
    devices = lax.axis_size("fsdp")
    me = lax.axis_index("fsdp")
    slots, width = input_one.shape
    half = slots // 2
    window = 2 * slots
    part = w_shared.shape[0]
    hidden = w_expand.shape[1]
    sides = hidden // width
    down = [(i, i - 1) for i in range(1, devices)]
    up = [(i, i + 1) for i in range(devices - 1)]

    def widen(own):
        head = lax.ppermute(own[half:], "fsdp", up)
        tail = lax.ppermute(own[:half], "fsdp", down)
        return jnp.concatenate([head, own, tail], axis=0)

    def narrow(wide):
        tail = lax.ppermute(wide[:half], "fsdp", down)
        head = lax.ppermute(wide[half + slots :], "fsdp", up)
        return wide[half : half + slots], jnp.concatenate([head, tail], axis=0)

    ends = jnp.cumsum(lengths)
    starts = ends - lengths
    middle = starts + lengths // 2
    base = me * slots
    owner = jnp.zeros((devices,), jnp.int32).at[destination].set(jnp.arange(devices, dtype=jnp.int32))
    mine = lengths[owner[me]]
    block = block_of_rank(buckets[0], mine)

    vectors = jnp.concatenate(
        [gain_attend, shift_attend, gain_mixing, shift_mixing, bias_output, bias_reduce, bias_expand]
    )
    high = lax.reduce_precision(vectors, 8, 7)
    count = vectors.shape[0]
    packed = jnp.zeros((8, width), BF16).at[0, :count].set(high.astype(BF16)).at[1, :count].set((vectors - high).astype(BF16))
    first = lax.all_gather(
        jnp.concatenate([w_shared, w_value, block.astype(BF16), packed], axis=0), "fsdp", axis=0, tiled=False
    )
    lists = ROUNDS * HEADS
    full_shared = first[:, :part].reshape(width, width)
    full_value = first[:, part : 2 * part].reshape(width, width)
    blocks_all = first[:, 2 * part : 2 * part + lists]
    full_vectors = first[:, 2 * part + lists, :count].astype(F32) + first[:, 2 * part + lists + 1, :count].astype(F32)
    gain_a, shift_a, gain_m, shift_m, bias_o, bias_r = (
        full_vectors[:, k * part : (k + 1) * part].reshape(width) for k in range(6)
    )
    bias_e = full_vectors[:, 6 * part :].reshape(hidden)
    second_gather = lax.all_gather(
        jnp.concatenate(
            [w_output] + [w_expand[:, k * width : (k + 1) * width] for k in range(sides)] + [w_reduce], axis=0
        ),
        "fsdp", axis=0, tiled=False,
    )
    full_output = second_gather[:, :part].reshape(width, width)
    full_expand = jnp.concatenate(
        [second_gather[:, (k + 1) * part : (k + 2) * part].reshape(width, width) for k in range(sides)], axis=1
    )
    full_reduce = second_gather[:, (sides + 1) * part :].reshape(hidden, width)

    inside = (middle >= base) & (middle < base + slots)
    chosen = jnp.sum(inside.astype(jnp.int32))
    lowest = jnp.minimum(jnp.argmax(inside).astype(jnp.int32), devices - 1)
    code = jnp.full((window + slots, lists), FREE, F32)
    begin = jnp.full((window + slots,), window, jnp.int32)
    spot = jnp.arange(slots, dtype=jnp.int32)
    for k in range(2):
        s = jnp.minimum(lowest + k, devices - 1)
        valid = chosen > k
        offset = jnp.where(valid, starts[s] - (base - half), window)
        rows = lax.dynamic_index_in_dim(blocks_all, destination[s], 0, keepdims=False).astype(F32).T
        rows = jnp.where(rows < 50.0, rows + 32.0 * k, FREE)
        code = lax.dynamic_update_slice(code, rows, (offset, 0))
        begin = lax.dynamic_update_slice(begin, jnp.where(spot < lengths[s], offset, window), (offset,))
    code = code[:window].astype(BF16)
    lowest_row = jnp.min(begin[:window].reshape(-1, TILE), axis=1)
    low = (lowest_row // TILE).astype(jnp.int32)
    lane = jnp.arange(HEADS * DH, dtype=jnp.int32)
    row = jnp.arange(lists, dtype=jnp.int32)[:, None]
    spread = (row == ((lane % 64) // 16) * HEADS + lane // DH).astype(BF16)

    live = ((base + jnp.arange(slots, dtype=jnp.int32)) < ends[-1]).astype(F32)[:, None]
    slot_one = input_one.astype(F32)
    slot_two = input_two.astype(F32)
    above_one = live * upstream_one.astype(F32)
    above_two = live * upstream_two.astype(F32)

    two_window = widen(input_two).astype(F32)
    normed = layer_norm(two_window, gain_a, shift_a).astype(BF16)
    shared = dot(normed, full_shared).astype(BF16)
    values = dot(normed, full_value).astype(BF16)
    combined_window, lse, lone = attend(low, shared, values, code, spread)
    own, other = narrow(combined_window)
    combined = own + other
    attended = dot(combined, full_output) + bias_o
    out_one = slot_one + live * attended
    second = layer_norm(out_one, gain_m, shift_m).astype(BF16)
    pre_act = dot(second, full_expand) + bias_e
    expand = jax.nn.gelu(pre_act, approximate=True).astype(BF16)
    out_two = slot_two + live * (dot(expand, full_reduce) + bias_r)

    d_reduce = above_two.astype(BF16)
    grad_reduce = dot(expand, d_reduce, TN)
    grad_bias_reduce = jnp.sum(d_reduce, axis=0, dtype=F32)
    d_expand = dot(d_reduce, full_reduce, NT)
    gelu_out, gelu_pull = jax.vjp(lambda inner: jax.nn.gelu(inner, approximate=True), pre_act)
    d_pre = gelu_pull(d_expand)[0].astype(BF16)
    grad_expand = dot(second, d_pre, TN)
    grad_bias_expand = jnp.sum(d_pre, axis=0, dtype=F32)
    d_second = dot(d_pre, full_expand, NT)
    d_one_mix, grad_gain_m, grad_shift_m = norm_back(out_one, gain_m, shift_m, d_second)
    total_one = above_one + d_one_mix
    d_attend = (live * total_one).astype(BF16)
    grad_output = dot(combined, d_attend, TN)
    grad_bias_output = jnp.sum(d_attend, axis=0, dtype=F32)
    d_combined = dot(d_attend, full_output, NT).astype(BF16)
    d_shared, d_values = attend_back(
        low, shared, values, code, spread, combined_window, widen(d_combined), lse, lone
    )
    grad_shared = dot(normed, d_shared, TN)
    grad_value = dot(normed, d_values, TN)
    d_normed = dot(d_shared, full_shared, NT) + dot(d_values, full_value, NT)
    d_two_window, grad_gain_a, grad_shift_a = norm_back(two_window, gain_a, shift_a, d_normed)
    own, other = narrow(d_two_window.astype(BF16))
    back_two = above_two + own.astype(F32) + other.astype(F32)

    def scatter(whole):
        return lax.psum_scatter(whole, "fsdp", scatter_dimension=0, tiled=True)

    def split(whole):
        return whole.astype(BF16).reshape(devices, -1, width)

    early = jnp.concatenate(
        [split(grad_output)] + [split(grad_expand[:, k * width : (k + 1) * width]) for k in range(sides)] + [split(grad_reduce)],
        axis=1,
    )
    late = jnp.concatenate([split(grad_shared), split(grad_value)], axis=1)
    early = scatter(early.reshape(-1, width)).astype(F32)
    late = scatter(late.reshape(-1, width)).astype(F32)
    small = [
        scatter(member.reshape(devices, -1)).reshape(-1)
        for member in (
            jnp.concatenate(
                [
                    member.reshape(devices, -1)
                    for member in (
                        grad_gain_a, grad_shift_a, grad_gain_m, grad_shift_m, grad_bias_output, grad_bias_reduce, grad_bias_expand
                    )
                ],
                axis=1,
            ),
        )
    ][0]
    return (
        (live * out_one).astype(BF16),
        (live * out_two).astype(BF16),
        (live * total_one).astype(BF16),
        (live * back_two).astype(BF16),
        late[:part],
        late[part:],
        early[:part],
        jnp.concatenate([early[(k + 1) * part : (k + 2) * part] for k in range(sides)], axis=1),
        early[(sides + 1) * part :],
        small[:part],
        small[part : 2 * part],
        small[2 * part : 3 * part],
        small[3 * part : 4 * part],
        small[4 * part : 5 * part],
        small[6 * part :],
        small[5 * part : 6 * part],
    )


def solution(mesh):
    rows, flat, whole = P("fsdp", None), P("fsdp"), P()
    return jax.shard_map(
        body,
        mesh=mesh,
        in_specs=(rows,) * 4 + (whole, whole, P("fsdp", None, None)) + (rows,) * 5 + (flat,) * 7,
        out_specs=(rows,) * 9 + (flat,) * 7,
        check_vma=False,
    )
```

```python
import functools
import math

import jax
import jax.numpy as jnp
from jax import lax
from jax.experimental import pallas as pl
from jax.experimental.pallas import tpu as pltpu
from jax.sharding import PartitionSpec as P

HEADS = 8
DH = 128
GROUP = 64
ROUNDS = 4
BUCKETS = 32
EPS_NORM = 1e-05
EPS_UNIT = 1e-06
LOG2E = math.log2(math.e)
SELF2 = -100000.0 * LOG2E
NEG = -1e30
SCALE = 1.0 / math.sqrt(DH)
TILE = 256
FREE = 99.0
STRIP = 512
ROWS = 1024
LAG = 1
CURVE = math.sqrt(2.0 / math.pi)
MESH = pl.DeviceIdType.MESH

NT = (((1,), (1,)), ((), ()))
NN = (((1,), (0,)), ((), ()))
TN = (((0,), (0,)), ((), ()))
F32 = jnp.float32
BF16 = jnp.bfloat16


def dot(a, b, dims=NN):
    return lax.dot_general(a, b, dims, preferred_element_type=F32)


def layer_norm(values, gain, shift):
    center = values - jnp.mean(values, axis=-1, keepdims=True)
    spread = jnp.mean(center * center, axis=-1, keepdims=True)
    return center * lax.rsqrt(spread + EPS_NORM) * gain + shift


def norm_back(values, gain, shift, upstream):
    outcome, pullback = jax.vjp(layer_norm, values, gain, shift)
    return pullback(upstream)


def prepare(q_ref, code_ref, spread_ref, unit_s, ask_s, key_s):
    rows = q_ref.shape[0]
    lane = lax.broadcasted_iota(jnp.int32, (TILE, DH), 1)
    target = ((lane // 64) * 32 + lane % 16).astype(F32)
    for i in range(rows // TILE):
        at = pl.ds(i * TILE, TILE)
        q = q_ref[at, :].astype(F32)
        norm = lax.rsqrt(jnp.sum(q * q, axis=1, keepdims=True) + EPS_UNIT)
        unit_s[at, :] = (q * (norm * (SCALE * LOG2E))).astype(BF16)
        code = dot(code_ref[at, :], spread_ref[...])
        here = code == target
        ask_s[at, :] = jnp.where(here, 1.0, 0.0).astype(BF16)
        key_s[at, :] = jnp.where(here | (code + 1.0 == target), 1.0, 0.0).astype(BF16)


def attend_kernel(low_ref, q_ref, v_ref, code_ref, spread_ref, comb_ref, lse_ref, lone_ref, unit_s, ask_s, key_s, vt_s, acc_s):
    rows = q_ref.shape[0]
    prepare(q_ref, code_ref, spread_ref, unit_s, ask_s, key_s)
    for i in range(rows // TILE):
        at = pl.ds(i * TILE, TILE)
        vt_s[:, at] = v_ref[at, :].astype(F32).T.astype(BF16)
    key_at = lax.broadcasted_iota(jnp.int32, (TILE, TILE), 0)
    ask_at = lax.broadcasted_iota(jnp.int32, (TILE, TILE), 1)
    for i in range(rows // TILE):
        at = pl.ds(i * TILE, TILE)
        low = low_ref[i]

        @pl.when(low <= i)
        def _():
            q = q_ref[at, :]
            ask = ask_s[at, :]
            score = dot(unit_s[at, :], q, NT)
            count = dot(key_s[at, :], ask, NT)
            score = jnp.where(key_at == ask_at, SELF2, score)
            score = jnp.where((key_at <= ask_at) & (count > 0.5), score, NEG)
            top = jnp.max(score, axis=0, keepdims=True)
            prob = count * jnp.exp2(score - top)
            total = jnp.sum(prob, axis=0, keepdims=True)
            acc_s[...] = dot(vt_s[:, at], prob.astype(BF16))

            def step(j, carry):
                top, total = carry
                key_rows = pl.ds(pl.multiple_of(j * TILE, TILE), TILE)
                score = dot(unit_s[key_rows, :], q, NT)
                count = dot(key_s[key_rows, :], ask, NT)
                score = jnp.where(count > 0.5, score, NEG)
                newer = jnp.maximum(top, jnp.max(score, axis=0, keepdims=True))
                fade = jnp.exp2(top - newer)
                prob = count * jnp.exp2(score - newer)
                acc_s[...] = acc_s[...] * fade + dot(vt_s[:, key_rows], prob.astype(BF16))
                return newer, total * fade + jnp.sum(prob, axis=0, keepdims=True)

            top, total = lax.fori_loop(low, i, step, (top, total))
            some = total > 0.0
            safe = jnp.where(some, total, 1.0)
            inverse = jnp.where(some, 1.0 / safe, 0.0)
            comb_ref[at, :] = (acc_s[...] * inverse).T.astype(BF16)
            lse_ref[0, :, at] = top + jnp.log2(safe)
            lone_ref[0, :, at] = ROUNDS * jnp.exp2(SELF2 - jnp.maximum(top, SELF2)) * inverse

        @pl.when(low > i)
        def _():
            comb_ref[at, :] = jnp.zeros((TILE, DH), BF16)
            lse_ref[0, :, at] = jnp.zeros((1, TILE), F32)
            lone_ref[0, :, at] = jnp.zeros((1, TILE), F32)


def back_kernel(
    low_ref, q_ref, v_ref, code_ref, spread_ref, comb_ref, above_ref, lse_ref, lone_ref,
    dq_ref, dv_ref, unit_s, ask_s, key_s, dunit_s, dvalue_s, dask_s,
):
    rows = q_ref.shape[0]
    prepare(q_ref, code_ref, spread_ref, unit_s, ask_s, key_s)
    key_at = lax.broadcasted_iota(jnp.int32, (TILE, TILE), 0)
    ask_at = lax.broadcasted_iota(jnp.int32, (TILE, TILE), 1)
    dunit_s[...] = jnp.zeros(dunit_s.shape, F32)
    dvalue_s[...] = jnp.zeros(dvalue_s.shape, F32)
    dask_s[...] = jnp.zeros(dask_s.shape, F32)
    for i in range(rows // TILE):
        at = pl.ds(i * TILE, TILE)
        low = low_ref[i]

        @pl.when(low <= i)
        def _():
            q = q_ref[at, :]
            ask = ask_s[at, :]
            above = above_ref[at, :]
            lse = lse_ref[0, :, at]
            mixed = above.astype(F32) * comb_ref[at, :].astype(F32)
            delta = jnp.sum(mixed.T, axis=0, keepdims=True)
            score = dot(unit_s[at, :], q, NT)
            count = dot(key_s[at, :], ask, NT)
            d_prob = dot(v_ref[at, :], above, NT)
            earlier = key_at < ask_at
            prob = count * jnp.exp2(jnp.minimum(score - lse, 0.0))
            prob = jnp.where(earlier, prob, 0.0)
            d_score = (prob * (d_prob - delta)).astype(BF16)
            prob = jnp.where(key_at == ask_at, lone_ref[0, :, at], prob).astype(BF16)
            dvalue_s[at, :] += dot(prob, above)
            dunit_s[at, :] += dot(d_score, q)
            dask_s[at, :] += dot(d_score, unit_s[at, :], TN)

            def step(j, carry):
                key_rows = pl.ds(pl.multiple_of(j * TILE, TILE), TILE)
                unit = unit_s[key_rows, :]
                score = dot(unit, q, NT)
                count = dot(key_s[key_rows, :], ask, NT)
                d_prob = dot(v_ref[key_rows, :], above, NT)
                prob = count * jnp.exp2(jnp.minimum(score - lse, 0.0))
                d_score = (prob * (d_prob - delta)).astype(BF16)
                dvalue_s[key_rows, :] += dot(prob.astype(BF16), above)
                dunit_s[key_rows, :] += dot(d_score, q)
                dask_s[at, :] += dot(d_score, unit, TN)
                return carry

            lax.fori_loop(low, i, step, 0)

    for i in range(rows // TILE):
        at = pl.ds(i * TILE, TILE)
        q = q_ref[at, :].astype(F32)
        norm = lax.rsqrt(jnp.sum(q * q, axis=1, keepdims=True) + EPS_UNIT)
        d_unit = dunit_s[at, :] * SCALE
        along = jnp.sum(q * d_unit, axis=1, keepdims=True)
        d_q = dask_s[at, :] * (1.0 / LOG2E) + d_unit * norm - q * (norm * norm * norm * along)
        dq_ref[at, :] = d_q.astype(BF16)
        dv_ref[at, :] = dvalue_s[at, :].astype(BF16)


def head_specs(rows):
    by_head = pl.BlockSpec((rows, DH), lambda h, low: (0, h))
    code = pl.BlockSpec((rows, ROUNDS * HEADS), lambda h, low: (0, 0))
    spread = pl.BlockSpec((ROUNDS * HEADS, DH), lambda h, low: (0, h))
    stat = pl.BlockSpec((1, 1, rows), lambda h, low: (h, 0, 0))
    return by_head, code, spread, stat


def attend(low, shared, values, code, spread):
    rows = shared.shape[0]
    by_head, code_spec, spread_spec, stat = head_specs(rows)
    wide = jax.ShapeDtypeStruct((rows, HEADS * DH), BF16)
    thin = jax.ShapeDtypeStruct((HEADS, 1, rows), F32)
    return pl.pallas_call(
        attend_kernel,
        grid_spec=pltpu.PrefetchScalarGridSpec(
            num_scalar_prefetch=1,
            grid=(HEADS,),
            in_specs=[by_head, by_head, code_spec, spread_spec],
            out_specs=[by_head, stat, stat],
            scratch_shapes=[pltpu.VMEM((rows, DH), BF16)] * 3
            + [pltpu.VMEM((DH, rows), BF16), pltpu.VMEM((DH, TILE), F32)],
        ),
        out_shape=(wide, thin, thin),
        name="attend",
        cost_estimate=pl.CostEstimate(
            flops=HEADS * 20 * 3 * 2 * TILE * TILE * DH, bytes_accessed=rows * HEADS * DH * 6, transcendentals=HEADS * 20 * TILE * TILE
        ),
    )(low, shared, values, code, spread)


def attend_back(low, shared, values, code, spread, combined, above, lse, lone):
    rows = shared.shape[0]
    by_head, code_spec, spread_spec, stat = head_specs(rows)
    wide = jax.ShapeDtypeStruct((rows, HEADS * DH), BF16)
    return pl.pallas_call(
        back_kernel,
        grid_spec=pltpu.PrefetchScalarGridSpec(
            num_scalar_prefetch=1,
            grid=(HEADS,),
            in_specs=[by_head, by_head, code_spec, spread_spec, by_head, by_head, stat, stat],
            out_specs=[by_head, by_head],
            scratch_shapes=[pltpu.VMEM((rows, DH), BF16)] * 3 + [pltpu.VMEM((rows, DH), F32)] * 3,
        ),
        out_shape=(wide, wide),
        name="attend_back",
        cost_estimate=pl.CostEstimate(
            flops=HEADS * 20 * 6 * 2 * TILE * TILE * DH, bytes_accessed=rows * HEADS * DH * 12, transcendentals=HEADS * 20 * TILE * TILE
        ),
    )(low, shared, values, code, spread, combined, above, lse, lone)


def mixing_kernel(second_ref, above_ref, expand_ref, reduce_ref, bias_e_ref, bias_r_ref,
                  out_ref, back_ref, grad_r_ref, grad_e_ref, grad_b_ref, act_s, pre_s):
    step = pl.program_id(0)
    rows, width = second_ref.shape
    w_e = expand_ref[...].reshape(width, STRIP)
    w_r = reduce_ref[...].reshape(STRIP, width)
    bias = bias_e_ref[...]

    @pl.when(step == 0)
    def _():
        out_ref[...] = jnp.broadcast_to(bias_r_ref[...], out_ref.shape)
        back_ref[...] = jnp.zeros(back_ref.shape, F32)

    def strip(i, total):
        at = pl.ds(pl.multiple_of(i * ROWS, ROWS), ROWS)
        pre = dot(second_ref[at, :], w_e) + bias
        square = pre * pre
        curve = jnp.tanh(CURVE * pre * (1.0 + 0.044715 * square))
        hinge = 0.5 * (1.0 + curve)
        act = (pre * hinge).astype(BF16)
        slope = hinge + 0.5 * pre * (1.0 - curve * curve) * (CURVE * (1.0 + 3 * 0.044715 * square))
        d_pre_wide = dot(above_ref[at, :], w_r, NT) * slope
        d_pre = d_pre_wide.astype(BF16)
        act_s[at, :] = act
        pre_s[at, :] = d_pre
        out_ref[at, :] += dot(act, w_r)
        back_ref[at, :] += dot(d_pre, w_e, NT)
        return total + jnp.sum(d_pre.astype(F32), axis=0, keepdims=True)

    grad_b_ref[...] = lax.fori_loop(0, rows // ROWS, strip, jnp.zeros((1, STRIP), F32))
    grad_r_ref[...] = dot(act_s[...], above_ref[...], TN).astype(BF16).reshape(grad_r_ref.shape)
    grad_e_ref[...] = dot(second_ref[...], pre_s[...], TN).astype(BF16).reshape(grad_e_ref.shape)


def mixing(second, above, gathered, bias_e, bias_r, part):
    rows, width = second.shape
    devices = gathered.shape[0]
    hidden = bias_e.shape[1]
    many = hidden // devices
    per = width // STRIP
    fixed = pl.BlockSpec((rows, width), lambda i: (0, 0), pipeline_mode=pl.Buffered(1))
    return pl.pallas_call(
        mixing_kernel,
        grid=(hidden // STRIP,),
        in_specs=[
            fixed, fixed,
            pl.BlockSpec((devices, part, STRIP), lambda i: (0, many // part + 1 + i // per, i % per)),
            pl.BlockSpec((STRIP // many, many, width), lambda i: (i, 0, 0)),
            pl.BlockSpec((1, STRIP), lambda i: (0, i)),
            pl.BlockSpec((1, width), lambda i: (0, 0)),
        ],
        out_specs=[
            pl.BlockSpec((rows, width), lambda i: (0, 0)),
            pl.BlockSpec((rows, width), lambda i: (0, 0)),
            pl.BlockSpec((STRIP // many, many, width), lambda i: (i, 0, 0)),
            pl.BlockSpec((devices, part, STRIP), lambda i: (0, i // per, i % per)),
            pl.BlockSpec((1, STRIP), lambda i: (0, i)),
        ],
        out_shape=[
            jax.ShapeDtypeStruct((rows, width), F32),
            jax.ShapeDtypeStruct((rows, width), F32),
            jax.ShapeDtypeStruct((devices, many, width), BF16),
            jax.ShapeDtypeStruct((devices, hidden // width * part, width), BF16),
            jax.ShapeDtypeStruct((1, hidden), F32),
        ],
        scratch_shapes=[pltpu.VMEM((rows, STRIP), BF16)] * 2,
        compiler_params=pltpu.CompilerParams(vmem_limit_bytes=56 << 20),
        name="mixing",
    )(second, above, gathered, gathered, bias_e, bias_r)


def digits(devices):
    side = 2
    while 8 * side * side < devices:
        side += 1
    assert 8 * side * side == devices, devices
    return 4, side, 2


def neighbours(devices):
    outer, side, core = digits(devices)
    me = lax.axis_index("fsdp")
    c = lax.rem(me, core)
    q = lax.rem(lax.div(me, core), side)
    p = lax.rem(lax.div(me, core * side), side)
    o = lax.div(me, core * side * side)

    def at(o_, p_, q_, c_):
        return ((o_ * side + p_) * side + q_) * core + c_

    core_peer = at(o, p, q, 1 - c)
    q_peers = [lax.rem(q + d, side) for d in range(1, side)]
    p_peers = [lax.rem(p + d, side) for d in range(1, side)]
    o_peers = [lax.rem(o + d, outer) for d in range(1, outer)]
    return (o, p, q, c), core_peer, [(k, at(o, p, k, c)) for k in q_peers], [(k, at(o, k, q, c)) for k in p_peers], [(k, at(k, p, q, c)) for k in o_peers]


def greet(peers):
    barrier = pltpu.get_barrier_semaphore()
    for peer in peers:
        pl.semaphore_signal(barrier, inc=1, device_id=(peer,), device_id_type=MESH)
    pl.semaphore_wait(barrier, len(peers))


def reduce_kernel(devices, plan, arrays, *refs):
    outer, side, core = digits(devices)
    sources, outs = refs[:arrays], refs[arrays : 2 * arrays]
    rest = refs[2 * arrays :]
    count = len(plan)
    own = rest[:count]
    landed_c = rest[count : 2 * count]
    landed_a = rest[2 * count : 4 * count]
    landed_b = rest[4 * count : 5 * count]
    landed_o = rest[5 * count : 6 * count]
    load_sem, sem_c, sem_a, sem_b, sem_o = rest[6 * count :]
    (o, p, q, c), core_peer, q_peers, p_peers, o_peers = neighbours(devices)
    greet([core_peer] + [d for _, d in q_peers] + [d for _, d in p_peers] + [d for _, d in o_peers])
    width = own[0].shape[-1]
    half = width // 2
    columns = (pl.ds(0, half), pl.ds(half, half))

    def remote(src, dst, sems, slot, device):
        return pltpu.make_async_remote_copy(
            src_ref=src, dst_ref=dst, send_sem=sems.at[(0,) + slot], recv_sem=sems.at[(1,) + slot],
            device_id=(device,), device_id_type=MESH,
        )

    loads, to_core, first, second, third = {}, {}, {}, {}, {}
    for s, (k, row, rows) in enumerate(plan):
        at = pl.ds(row, rows)
        to_core[s] = remote(sources[k].at[:, :, :, 1 - c, at, :], landed_c[s], sem_c, (s,), core_peer)
        to_core[s].start()
        loads[s] = pltpu.make_async_copy(sources[k].at[:, :, :, c, at, :], own[s], load_sem.at[s])
        loads[s].start()

    def stage_core(s):
        loads[s].wait()
        to_core[s].wait_recv()
        mine, other = own[s], landed_c[s]

        def add(i, carry):
            a, b, d = i // (side * side), (i // side) % side, i % side
            mine[a, b, d] = mine[a, b, d] + other[a, b, d]
            return carry

        lax.fori_loop(0, outer * side * side, add, 0)
        for h in range(2):
            for d in range(side - 1):
                if h == 0:
                    k, device = q_peers[d]
                    src = mine.at[:, :, k, :, columns[h]]
                else:
                    k, device = p_peers[d]
                    src = mine.at[:, k, :, :, columns[h]]
                first[s, h, d] = remote(src, landed_a[2 * s + h].at[d], sem_a, (s, h, d), device)
                first[s, h, d].start()

    def stage_first(s):
        mine = own[s]
        for h in range(2):
            box = landed_a[2 * s + h]
            for d in range(side - 1):
                first[s, h, d].wait_recv()

            def add(i, carry):
                a, b = i // side, i % side
                total = mine[a, b, q, :, columns[h]] if h == 0 else mine[a, p, b, :, columns[h]]
                for d in range(side - 1):
                    total = total + box[d, a, b]
                box[0, a, b] = total
                return carry

            lax.fori_loop(0, outer * side, add, 0)
            for d in range(side - 1):
                k, device = (p_peers if h == 0 else q_peers)[d]
                second[s, h, d] = remote(
                    box.at[0, :, k], landed_b[s].at[d, :, :, columns[h]], sem_b, (s, h, d), device
                )
                second[s, h, d].start()

    def stage_second(s):
        box = landed_b[s]
        for h in range(2):
            part = landed_a[2 * s + h]
            k = p if h == 0 else q
            for d in range(side - 1):
                second[s, h, d].wait_recv()

            def add(a, carry):
                total = part[0, a, k]
                for d in range(side - 1):
                    total = total + box[d, a, :, columns[h]]
                box[0, a, :, columns[h]] = total
                return carry

            lax.fori_loop(0, outer, add, 0)
        for d in range(outer - 1):
            k, device = o_peers[d]
            third[s, d] = remote(box.at[0, k], landed_o[s].at[d], sem_o, (s, d), device)
            third[s, d].start()

    def stage_third(s):
        k, row, rows = plan[s]
        total = landed_b[s][0, o].astype(F32)
        for d in range(outer - 1):
            third[s, d].wait_recv()
            total = total + landed_o[s][d].astype(F32)
        outs[k][pl.ds(row, rows), :] = total

    for t in range(count + 3 * LAG):
        if t < count:
            stage_core(t)
        if 0 <= t - LAG < count:
            stage_first(t - LAG)
        if 0 <= t - 2 * LAG < count:
            stage_second(t - 2 * LAG)
        if 0 <= t - 3 * LAG < count:
            stage_third(t - 3 * LAG)
    for copies in (to_core, first, second, third):
        for copy in copies.values():
            copy.wait_send()


def reduce_scatter(devices, arrays, cuts):
    outer, side, core = digits(devices)
    plan = []
    for k, array in enumerate(arrays):
        rows = array.shape[1] // cuts[k]
        plan += [(k, i * rows, rows) for i in range(cuts[k])]
    width = arrays[0].shape[2]
    half = width // 2
    count = len(plan)
    vmem = pltpu.VMEM
    scratch = [vmem((outer, side, side, r, width), BF16) for _, _, r in plan]
    scratch += [vmem((outer, side, side, r, width), BF16) for _, _, r in plan]
    for _, _, r in plan:
        scratch += [vmem((side - 1, outer, side, r, half), BF16)] * 2
    scratch += [vmem((side - 1, outer, r, width), BF16) for _, _, r in plan]
    scratch += [vmem((outer - 1, r, width), BF16) for _, _, r in plan]
    dma = pltpu.SemaphoreType.DMA
    scratch += [dma((count,)), dma((2, count)), dma((2, count, 2, side - 1)), dma((2, count, 2, side - 1)), dma((2, count, outer - 1))]
    return pl.pallas_call(
        functools.partial(reduce_kernel, devices, plan, len(arrays)),
        out_shape=tuple(jax.ShapeDtypeStruct(array.shape[1:], F32) for array in arrays),
        in_specs=[pl.BlockSpec(memory_space=pl.ANY)] * len(arrays),
        out_specs=tuple(pl.BlockSpec(memory_space=pltpu.VMEM) for _ in arrays),
        scratch_shapes=scratch,
        compiler_params=pltpu.CompilerParams(collective_id=1, has_side_effects=True, vmem_limit_bytes=56 << 20),
        name="reduce_scatter",
    )(*[array.reshape(outer, side, side, core, *array.shape[1:]) for array in arrays])


def block_of_rank(buckets, length):
    slots = buckets.shape[-1]
    place = lax.broadcasted_iota(jnp.int32, (1, 1, slots), 2)
    bucket = lax.broadcasted_iota(jnp.int32, (1, BUCKETS, 1), 1)
    one_hot = (buckets[:, None, :] == bucket) & (place < length)
    first = lax.broadcasted_iota(jnp.int32, (slots, slots), 0)
    second = lax.broadcasted_iota(jnp.int32, (slots, slots), 1)
    before = dot(one_hot.astype(BF16).reshape(-1, slots), (first < second).astype(BF16)).reshape(one_hot.shape)
    size = jnp.sum(one_hot.astype(F32), axis=2, keepdims=True)
    offset = jnp.cumsum(size, axis=1) - size
    rank = jnp.sum(jnp.where(one_hot, before + offset, 0.0), axis=1)
    return jnp.where(place[0] < length, jnp.floor(rank * (1.0 / GROUP)), FREE)


def body(
    input_one, input_two, upstream_one, upstream_two, lengths, destination, buckets,
    w_shared, w_value, w_output, w_expand, w_reduce,
    gain_attend, shift_attend, gain_mixing, shift_mixing, bias_output, bias_expand, bias_reduce,
):
    devices = lax.axis_size("fsdp")
    me = lax.axis_index("fsdp")
    slots, width = input_one.shape
    half = slots // 2
    window = 2 * slots
    part = w_shared.shape[0]
    hidden = w_expand.shape[1]
    sides = hidden // width
    down = [(i, i - 1) for i in range(1, devices)]
    up = [(i, i + 1) for i in range(devices - 1)]

    def widen(own):
        head = lax.ppermute(own[half:], "fsdp", up)
        tail = lax.ppermute(own[:half], "fsdp", down)
        return jnp.concatenate([head, own, tail], axis=0)

    def narrow(wide):
        tail = lax.ppermute(wide[:half], "fsdp", down)
        head = lax.ppermute(wide[half + slots :], "fsdp", up)
        return wide[half : half + slots], jnp.concatenate([head, tail], axis=0)

    ends = jnp.cumsum(lengths)
    starts = ends - lengths
    middle = starts + lengths // 2
    base = me * slots
    owner = jnp.zeros((devices,), jnp.int32).at[destination].set(jnp.arange(devices, dtype=jnp.int32))
    mine = lengths[owner[me]]
    block = block_of_rank(buckets[0], mine)

    vectors = jnp.concatenate(
        [gain_attend, shift_attend, gain_mixing, shift_mixing, bias_output, bias_reduce, bias_expand]
    )
    high = lax.reduce_precision(vectors, 8, 7)
    count = vectors.shape[0]
    packed = jnp.zeros((8, width), BF16).at[0, :count].set(high.astype(BF16)).at[1, :count].set((vectors - high).astype(BF16))
    first = lax.all_gather(
        jnp.concatenate([w_shared, w_value, block.astype(BF16), packed], axis=0), "fsdp", axis=0, tiled=False
    )
    lists = ROUNDS * HEADS
    full_shared = first[:, :part].reshape(width, width)
    full_value = first[:, part : 2 * part].reshape(width, width)
    blocks_all = first[:, 2 * part : 2 * part + lists]
    full_vectors = first[:, 2 * part + lists, :count].astype(F32) + first[:, 2 * part + lists + 1, :count].astype(F32)
    gain_a, shift_a, gain_m, shift_m, bias_o, bias_r = (
        full_vectors[:, k * part : (k + 1) * part].reshape(width) for k in range(6)
    )
    bias_e = full_vectors[:, 6 * part :].reshape(hidden)
    second_gather = lax.all_gather(
        jnp.concatenate(
            [w_reduce, w_output] + [w_expand[:, k * width : (k + 1) * width] for k in range(sides)], axis=0
        ),
        "fsdp", axis=0, tiled=False,
    )
    full_output = second_gather[:, sides * part : (sides + 1) * part].reshape(width, width)

    inside = (middle >= base) & (middle < base + slots)
    chosen = jnp.sum(inside.astype(jnp.int32))
    lowest = jnp.minimum(jnp.argmax(inside).astype(jnp.int32), devices - 1)
    code = jnp.full((window + slots, lists), FREE, F32)
    begin = jnp.full((window + slots,), window, jnp.int32)
    spot = jnp.arange(slots, dtype=jnp.int32)
    for k in range(2):
        s = jnp.minimum(lowest + k, devices - 1)
        valid = chosen > k
        offset = jnp.where(valid, starts[s] - (base - half), window)
        rows = lax.dynamic_index_in_dim(blocks_all, destination[s], 0, keepdims=False).astype(F32).T
        rows = jnp.where(rows < 50.0, rows + 32.0 * k, FREE)
        code = lax.dynamic_update_slice(code, rows, (offset, 0))
        begin = lax.dynamic_update_slice(begin, jnp.where(spot < lengths[s], offset, window), (offset,))
    code = code[:window].astype(BF16)
    lowest_row = jnp.min(begin[:window].reshape(-1, TILE), axis=1)
    low = (lowest_row // TILE).astype(jnp.int32)
    lane = jnp.arange(HEADS * DH, dtype=jnp.int32)
    row = jnp.arange(lists, dtype=jnp.int32)[:, None]
    spread = (row == ((lane % 64) // 16) * HEADS + lane // DH).astype(BF16)

    live = ((base + jnp.arange(slots, dtype=jnp.int32)) < ends[-1]).astype(F32)[:, None]
    slot_one = input_one.astype(F32)
    slot_two = input_two.astype(F32)
    above_one = live * upstream_one.astype(F32)
    above_two = live * upstream_two.astype(F32)

    two_window = widen(input_two).astype(F32)
    normed = layer_norm(two_window, gain_a, shift_a).astype(BF16)
    shared = dot(normed, full_shared).astype(BF16)
    values = dot(normed, full_value).astype(BF16)
    combined_window, lse, lone = attend(low, shared, values, code, spread)
    own, other = narrow(combined_window)
    combined = own + other
    attended = dot(combined, full_output) + bias_o
    out_one = slot_one + live * attended
    second = layer_norm(out_one, gain_m, shift_m).astype(BF16)
    d_reduce = above_two.astype(BF16)
    grad_bias_reduce = jnp.sum(d_reduce, axis=0, dtype=F32)
    mixed, d_second, grad_reduce, grad_expand, grad_bias_expand = mixing(
        second, d_reduce, second_gather, bias_e[None], bias_r[None], part
    )
    out_two = slot_two + live * mixed
    d_one_mix, grad_gain_m, grad_shift_m = norm_back(out_one, gain_m, shift_m, d_second)
    total_one = above_one + d_one_mix
    d_attend = (live * total_one).astype(BF16)
    grad_output = dot(combined, d_attend, TN)
    grad_bias_output = jnp.sum(d_attend, axis=0, dtype=F32)
    d_combined = dot(d_attend, full_output, NT).astype(BF16)
    d_shared, d_values = attend_back(
        low, shared, values, code, spread, combined_window, widen(d_combined), lse, lone
    )
    grad_shared = dot(normed, d_shared, TN)
    grad_value = dot(normed, d_values, TN)
    d_normed = dot(d_shared, full_shared, NT) + dot(d_values, full_value, NT)
    d_two_window, grad_gain_a, grad_shift_a = norm_back(two_window, gain_a, shift_a, d_normed)
    own, other = narrow(d_two_window.astype(BF16))
    back_two = above_two + own.astype(F32) + other.astype(F32)

    def split(whole):
        return whole.astype(BF16).reshape(devices, -1, width)

    small = jnp.concatenate(
        [
            member.reshape(devices, -1)
            for member in (
                grad_gain_a, grad_shift_a, grad_gain_m, grad_shift_m, grad_bias_output, grad_bias_reduce, grad_bias_expand
            )
        ],
        axis=1,
    )
    small = jnp.zeros((devices, 8, width), BF16).at[:, 0, : small.shape[1]].set(small.astype(BF16))
    grad_reduce, grad_expand, grad_output, grad_shared, grad_value, small = reduce_scatter(
        devices,
        (grad_reduce, grad_expand, split(grad_output), split(grad_shared), split(grad_value), small),
        (2, 2, 1, 1, 1, 1),
    )
    small = small[0]
    return (
        (live * out_one).astype(BF16),
        (live * out_two).astype(BF16),
        (live * total_one).astype(BF16),
        (live * back_two).astype(BF16),
        grad_shared,
        grad_value,
        grad_output,
        jnp.concatenate([grad_expand[k * part : (k + 1) * part] for k in range(sides)], axis=1),
        grad_reduce,
        small[:part],
        small[part : 2 * part],
        small[2 * part : 3 * part],
        small[3 * part : 4 * part],
        small[4 * part : 5 * part],
        small[6 * part : 6 * part + hidden // devices],
        small[5 * part : 6 * part],
    )


def solution(mesh):
    rows, flat, whole = P("fsdp", None), P("fsdp"), P()
    return jax.shard_map(
        body,
        mesh=mesh,
        in_specs=(rows,) * 4 + (whole, whole, P("fsdp", None, None)) + (rows,) * 5 + (flat,) * 7,
        out_specs=(rows,) * 9 + (flat,) * 7,
        check_vma=False,
    )
```

```python
import functools
import math

import jax
import jax.numpy as jnp
from jax import lax
from jax.experimental import pallas as pl
from jax.experimental.pallas import tpu as pltpu
from jax.sharding import PartitionSpec as P

HEADS = 8
DH = 128
GROUP = 64
ROUNDS = 4
BUCKETS = 32
EPS_NORM = 1e-05
EPS_UNIT = 1e-06
LOG2E = math.log2(math.e)
SELF2 = -100000.0 * LOG2E
NEG = -1e30
SCALE = 1.0 / math.sqrt(DH)
TILE = 512
HALF = TILE // 2
STEP = 128.0
SHIFT = 1.5 * 2.0**30
TAME = 3000.0
PAIR = 2
FREE = 99.0
STRIP = 512
ROWS = 1024
LAG = 1
CURVE = math.sqrt(2.0 / math.pi)
MESH = pl.DeviceIdType.MESH

NT = (((1,), (1,)), ((), ()))
NN = (((1,), (0,)), ((), ()))
TN = (((0,), (0,)), ((), ()))
F32 = jnp.float32
BF16 = jnp.bfloat16


def dot(a, b, dims=NN):
    return lax.dot_general(a, b, dims, preferred_element_type=F32)


def layer_norm(values, gain, shift):
    center = values - jnp.mean(values, axis=-1, keepdims=True)
    spread = jnp.mean(center * center, axis=-1, keepdims=True)
    return center * lax.rsqrt(spread + EPS_NORM) * gain + shift


def norm_back(values, gain, shift, upstream):
    outcome, pullback = jax.vjp(layer_norm, values, gain, shift)
    return pullback(upstream)


def prepare(q, code_ref, spread, ask_s, key_s, h, at):
    lane = lax.broadcasted_iota(jnp.int32, (TILE, DH), 1)
    target = ((lane // 64) * 32 + lane % 16).astype(F32)
    wide = q.astype(F32)
    square = jnp.sum(wide * wide, axis=1, keepdims=True)
    code = dot(code_ref[:, at], spread, TN)
    here = code == target
    ask_s[h, at, :DH] = q
    ask_s[h, at, DH:] = jnp.where(here, STEP, 0.0).astype(BF16)
    key_s[h, at, :DH] = (wide * (lax.rsqrt(square + EPS_UNIT) * (SCALE * LOG2E))).astype(BF16)
    key_s[h, at, DH:] = jnp.where(here | (code + 1.0 == target), 1.0, 0.0).astype(BF16)
    return jnp.max(square)


def lowest(info_ref, i):
    start, stop = i * TILE, (i + 1) * TILE
    one = (info_ref[0] < stop) & (info_ref[1] > start)
    two = (info_ref[2] < stop) & (info_ref[3] > start)
    begin = jnp.where(one, info_ref[0], jnp.where(two, info_ref[2], stop))
    return lax.div(begin, TILE)


def tile_rows(i):
    return pl.ds(pl.multiple_of(i * TILE, TILE), TILE)


def halves(i):
    start = i * TILE
    return [((0, pl.multiple_of(start, HALF), pl.multiple_of(start, HALF)), HALF),
            ((HALF, pl.multiple_of(start + HALF, HALF), pl.multiple_of(start, HALF)), TILE)]


def part_of(both):
    count = (both + SHIFT) - SHIFT
    return count, both - count


def apart(left, right):
    return dot(left[:, DH:], right[:, DH:], NT), dot(left[:, :DH], right[:, :DH], NT)


def attend_kernel(low_ref, q_ref, v_ref, code_ref, spread_ref, comb_ref, lse_ref, lone_ref, ask_s, key_s, more_s, acc_s, top_s):
    rows = q_ref.shape[0]
    tiles = rows // TILE
    heads = [slice(h * DH, (h + 1) * DH) for h in range(PAIR)]

    def ready(i, largest):
        def fill():
            most = jnp.float32(0.0)
            at = tile_rows(i)
            for h, cols in enumerate(heads):
                most = jnp.maximum(most, prepare(q_ref[at, cols], code_ref, spread_ref[:, cols], ask_s, key_s, h, at))
                more_s[h, at, :DH] = v_ref[at, cols]
                more_s[h, at, DH:] = jnp.ones((TILE, DH), BF16)
            return most

        return jnp.maximum(largest, lax.cond(lowest(low_ref, i) <= i, fill, lambda: jnp.float32(0.0)))

    largest = lax.fori_loop(0, tiles, ready, jnp.float32(0.0))
    tame = largest * (SCALE * LOG2E) ** 2 < TAME
    ask_at = lax.broadcasted_iota(jnp.int32, (TILE, TILE), 0)
    key_at = lax.broadcasted_iota(jnp.int32, (TILE, TILE), 1)

    def finish(h, cols, at, top):
        total = acc_s[h, :, DH:]
        some = total > 0.0
        safe = jnp.where(some, total, 1.0)
        inverse = jnp.where(some, 1.0 / safe, 0.0)
        comb_ref[at, cols] = (acc_s[h, :, :DH] * inverse).astype(BF16)
        lse_ref[h, :, at] = (jnp.log2(safe) + top).T[:1]

    def rows_of(i, carry):
        at = tile_rows(i)
        low = lowest(low_ref, i)

        @pl.when((low <= i) & tame)
        def _():
            for h in range(PAIR):
                acc_s[h] = jnp.zeros((TILE, 2 * DH), F32)

            def step(j, carry):
                keys = tile_rows(j)
                for h in range(PAIR):
                    count, score = part_of(dot(ask_s[h, at, :], key_s[h, keys, :], NT))
                    acc_s[h] += dot((count * jnp.exp2(score)).astype(BF16), more_s[h, keys, :])
                return carry

            lax.fori_loop(low, i, step, 0)
            for h, cols in enumerate(heads):
                for asks, span in halves(i):
                    here = pl.ds(asks[0], HALF)
                    there = pl.ds(asks[1], HALF)
                    keys = pl.ds(asks[2], span)
                    key_at = lax.broadcasted_iota(jnp.int32, (HALF, span), 1)
                    ask_at = lax.broadcasted_iota(jnp.int32, (HALF, span), 0) + (span - HALF)
                    count, score = part_of(dot(ask_s[h, there, :], key_s[h, keys, :], NT))
                    prob = jnp.where(key_at < ask_at, count * jnp.exp2(score), 0.0).astype(BF16)
                    acc_s[h, here, :] += dot(prob, more_s[h, keys, :])
                    active = jnp.max(jnp.where(key_at == ask_at, count, 0.0), axis=1, keepdims=True) > 0.0
                    lone = jnp.where(active & (acc_s[h, here, DH:] == 0.0), 1.0, 0.0)
                    acc_s[h, here, :DH] += lone * v_ref[there, cols].astype(F32)
                    acc_s[h, here, DH:] += lone
                    lone_ref[h, :, there] = lone.T[:1]
                finish(h, cols, at, 0.0)

        @pl.when((low <= i) & jnp.logical_not(tame))
        def _():
            for h, cols in enumerate(heads):
                count, score = apart(ask_s[h, at, :], key_s[h, at, :])
                score = jnp.where(key_at == ask_at, SELF2, score)
                score = jnp.where((key_at <= ask_at) & (count > 0.5), score, NEG)
                top = jnp.max(score, axis=1, keepdims=True)
                prob = count * jnp.exp2(score - top)
                acc_s[h] = dot(prob.astype(BF16), more_s[h, at, :])
                top_s[h] = jnp.broadcast_to(top, (TILE, DH))

                def step(j, carry):
                    keys = tile_rows(j)
                    count, score = apart(ask_s[h, at, :], key_s[h, keys, :])
                    score = jnp.where(count > 0.5, score, NEG)
                    top = top_s[h]
                    newer = jnp.maximum(top, jnp.max(score, axis=1, keepdims=True))
                    fade = jnp.exp2(top - newer)
                    prob = count * jnp.exp2(score - newer[:, :1])
                    acc_s[h] = acc_s[h] * jnp.concatenate([fade, fade], axis=1) + dot(prob.astype(BF16), more_s[h, keys, :])
                    top_s[h] = newer
                    return carry

                lax.fori_loop(low, i, step, 0)
                total = acc_s[h, :, DH:]
                own = STEP * ROUNDS * jnp.exp2(SELF2 - jnp.maximum(top_s[h], SELF2))
                lone_ref[h, :, at] = jnp.where(total > 0.0, own / jnp.where(total > 0.0, total, 1.0), 0.0).T[:1]
                finish(h, cols, at, top_s[h])

        @pl.when(low > i)
        def _():
            comb_ref[at, :] = jnp.zeros((TILE, PAIR * DH), BF16)
            for h in range(PAIR):
                lse_ref[h, :, at] = jnp.zeros((1, TILE), F32)
                lone_ref[h, :, at] = jnp.zeros((1, TILE), F32)

        return carry

    lax.fori_loop(0, tiles, rows_of, 0)


def back_kernel(
    low_ref, q_ref, v_ref, code_ref, spread_ref, comb_ref, above_ref, lse_ref, lone_ref,
    dq_ref, dv_ref, ask_s, key_s, dunit_s, dvalue_s, dask_s,
):
    rows = q_ref.shape[0]
    tiles = rows // TILE
    heads = [slice(h * DH, (h + 1) * DH) for h in range(PAIR)]

    def ready(i, largest):
        def fill():
            most = jnp.float32(0.0)
            at = tile_rows(i)
            for h, cols in enumerate(heads):
                most = jnp.maximum(most, prepare(q_ref[at, cols], code_ref, spread_ref[:, cols], ask_s, key_s, h, at))
                for total in (dunit_s, dvalue_s, dask_s):
                    total[h, at, :] = jnp.zeros((TILE, DH), F32)
            return most

        return jnp.maximum(largest, lax.cond(lowest(low_ref, i) <= i, fill, lambda: jnp.float32(0.0)))

    largest = lax.fori_loop(0, tiles, ready, jnp.float32(0.0))
    tame = largest * (SCALE * LOG2E) ** 2 < TAME

    def pass_over(i, low, split):
        at = tile_rows(i)
        deltas = []
        for h, cols in enumerate(heads):
            mixed = above_ref[at, cols].astype(F32) * comb_ref[at, cols].astype(F32)
            deltas.append(jnp.sum(mixed.T, axis=0, keepdims=True))

        def step(j, carry):
            keys = tile_rows(j)
            for h, cols in enumerate(heads):
                q, above, unit = q_ref[at, cols], above_ref[at, cols], key_s[h, keys, :DH]
                count, score = split(key_s[h, keys, :], ask_s[h, at, :])
                d_prob = dot(v_ref[keys, cols], above, NT)
                prob = count * jnp.exp2(score - lse_ref[h, :, at])
                d_score = (prob * (d_prob - carry[h])).astype(BF16)
                dvalue_s[h, keys, :] += dot(prob.astype(BF16), above)
                dunit_s[h, keys, :] += dot(d_score, q)
                dask_s[h, at, :] += dot(d_score, unit, TN)
            return carry

        deltas = lax.fori_loop(low, i, step, tuple(deltas))
        for h, cols in enumerate(heads):
            for asks, span in halves(i):
                there = pl.ds(asks[1], HALF)
                keys = pl.ds(asks[2], span)
                key_at = lax.broadcasted_iota(jnp.int32, (span, HALF), 0)
                ask_at = lax.broadcasted_iota(jnp.int32, (span, HALF), 1) + (span - HALF)
                q, above, unit = q_ref[there, cols], above_ref[there, cols], key_s[h, keys, :DH]
                count, score = split(key_s[h, keys, :], ask_s[h, there, :])
                d_prob = dot(v_ref[keys, cols], above, NT)
                prob = count * jnp.exp2(score - lse_ref[h, :, there])
                prob = jnp.where(key_at < ask_at, prob, 0.0)
                d_score = (prob * (d_prob - deltas[h][:, asks[0] : asks[0] + HALF])).astype(BF16)
                prob = jnp.where(key_at == ask_at, lone_ref[h, :, there], prob).astype(BF16)
                dvalue_s[h, keys, :] += dot(prob, above)
                dunit_s[h, keys, :] += dot(d_score, q)
                dask_s[h, there, :] += dot(d_score, unit, TN)

    def together(left, right):
        return part_of(dot(left, right, NT))

    def guarded(left, right):
        count, score = apart(left, right)
        return count, jnp.where(count > 0.5, score, NEG)

    def rows_of(i, carry):
        low = lowest(low_ref, i)

        @pl.when((low <= i) & tame)
        def _():
            pass_over(i, low, together)

        @pl.when((low <= i) & jnp.logical_not(tame))
        def _():
            pass_over(i, low, guarded)

        return carry

    lax.fori_loop(0, tiles, rows_of, 0)

    def close(i, carry):
        at = tile_rows(i)

        @pl.when(lowest(low_ref, i) <= i)
        def _():
            for h, cols in enumerate(heads):
                q = q_ref[at, cols].astype(F32)
                norm = lax.rsqrt(jnp.sum(q * q, axis=1, keepdims=True) + EPS_UNIT)
                d_unit = dunit_s[h, at, :] * SCALE
                along = jnp.sum(q * d_unit, axis=1, keepdims=True)
                d_q = dask_s[h, at, :] * (1.0 / LOG2E) + d_unit * norm - q * (norm * norm * norm * along)
                dq_ref[at, cols] = d_q.astype(BF16)
                dv_ref[at, cols] = dvalue_s[h, at, :].astype(BF16)

        @pl.when(lowest(low_ref, i) > i)
        def _():
            dq_ref[at, :] = jnp.zeros((TILE, PAIR * DH), BF16)
            dv_ref[at, :] = jnp.zeros((TILE, PAIR * DH), BF16)

        return carry

    lax.fori_loop(0, tiles, close, 0)


def head_specs(rows):
    by_head = pl.BlockSpec((rows, PAIR * DH), lambda h, low: (0, h))
    code = pl.BlockSpec((ROUNDS * HEADS, rows), lambda h, low: (0, 0))
    spread = pl.BlockSpec((ROUNDS * HEADS, PAIR * DH), lambda h, low: (0, h))
    stat = pl.BlockSpec((PAIR, 1, rows), lambda h, low: (h, 0, 0))
    return by_head, code, spread, stat


def attend(low, shared, values, code, spread):
    rows = shared.shape[0]
    by_head, code_spec, spread_spec, stat = head_specs(rows)
    wide = jax.ShapeDtypeStruct((rows, HEADS * DH), BF16)
    thin = jax.ShapeDtypeStruct((HEADS, 1, rows), F32)
    return pl.pallas_call(
        attend_kernel,
        grid_spec=pltpu.PrefetchScalarGridSpec(
            num_scalar_prefetch=1,
            grid=(HEADS // PAIR,),
            in_specs=[by_head, by_head, code_spec, spread_spec],
            out_specs=[by_head, stat, stat],
            scratch_shapes=[pltpu.VMEM((PAIR, rows, 2 * DH), BF16)] * 3
            + [pltpu.VMEM((PAIR, TILE, 2 * DH), F32), pltpu.VMEM((PAIR, TILE, DH), F32)],
        ),
        out_shape=(wide, thin, thin),
        compiler_params=pltpu.CompilerParams(vmem_limit_bytes=48 << 20),
        name="attend",
        cost_estimate=pl.CostEstimate(
            flops=HEADS * 20 * 3 * 2 * TILE * TILE * DH, bytes_accessed=rows * HEADS * DH * 6, transcendentals=HEADS * 20 * TILE * TILE
        ),
    )(low, shared, values, code, spread)


def attend_back(low, shared, values, code, spread, combined, above, lse, lone):
    rows = shared.shape[0]
    by_head, code_spec, spread_spec, stat = head_specs(rows)
    wide = jax.ShapeDtypeStruct((rows, HEADS * DH), BF16)
    return pl.pallas_call(
        back_kernel,
        grid_spec=pltpu.PrefetchScalarGridSpec(
            num_scalar_prefetch=1,
            grid=(HEADS // PAIR,),
            in_specs=[by_head, by_head, code_spec, spread_spec, by_head, by_head, stat, stat],
            out_specs=[by_head, by_head],
            scratch_shapes=[pltpu.VMEM((PAIR, rows, 2 * DH), BF16)] * 2 + [pltpu.VMEM((PAIR, rows, DH), F32)] * 3,
        ),
        out_shape=(wide, wide),
        compiler_params=pltpu.CompilerParams(vmem_limit_bytes=48 << 20),
        name="attend_back",
        cost_estimate=pl.CostEstimate(
            flops=HEADS * 20 * 6 * 2 * TILE * TILE * DH, bytes_accessed=rows * HEADS * DH * 12, transcendentals=HEADS * 20 * TILE * TILE
        ),
    )(low, shared, values, code, spread, combined, above, lse, lone)


def mixing_kernel(second_ref, above_ref, expand_ref, reduce_ref, bias_e_ref, bias_r_ref,
                  out_ref, back_ref, grad_r_ref, grad_e_ref, grad_b_ref, act_s, pre_s):
    step = pl.program_id(0)
    rows, width = second_ref.shape
    w_e = expand_ref[...].reshape(width, STRIP)
    w_r = reduce_ref[...].reshape(STRIP, width)
    bias = bias_e_ref[...]

    @pl.when(step == 0)
    def _():
        out_ref[...] = jnp.broadcast_to(bias_r_ref[...], out_ref.shape)
        back_ref[...] = jnp.zeros(back_ref.shape, F32)

    def strip(i, total):
        at = pl.ds(pl.multiple_of(i * ROWS, ROWS), ROWS)
        pre = dot(second_ref[at, :], w_e) + bias
        square = pre * pre
        curve = jnp.tanh(CURVE * pre * (1.0 + 0.044715 * square))
        hinge = 0.5 * (1.0 + curve)
        act = (pre * hinge).astype(BF16)
        slope = hinge + 0.5 * pre * (1.0 - curve * curve) * (CURVE * (1.0 + 3 * 0.044715 * square))
        d_pre_wide = dot(above_ref[at, :], w_r, NT) * slope
        d_pre = d_pre_wide.astype(BF16)
        act_s[at, :] = act
        pre_s[at, :] = d_pre
        out_ref[at, :] += dot(act, w_r)
        back_ref[at, :] += dot(d_pre, w_e, NT)
        return total + jnp.sum(d_pre.astype(F32), axis=0, keepdims=True)

    grad_b_ref[...] = lax.fori_loop(0, rows // ROWS, strip, jnp.zeros((1, STRIP), F32))
    grad_r_ref[...] = dot(act_s[...], above_ref[...], TN).astype(BF16).reshape(grad_r_ref.shape)
    grad_e_ref[...] = dot(second_ref[...], pre_s[...], TN).astype(BF16).reshape(grad_e_ref.shape)


def mixing(second, above, gathered, bias_e, bias_r, part):
    rows, width = second.shape
    devices = gathered.shape[0]
    hidden = bias_e.shape[1]
    many = hidden // devices
    per = width // STRIP
    fixed = pl.BlockSpec((rows, width), lambda i: (0, 0), pipeline_mode=pl.Buffered(1))
    return pl.pallas_call(
        mixing_kernel,
        grid=(hidden // STRIP,),
        in_specs=[
            fixed, fixed,
            pl.BlockSpec((devices, part, STRIP), lambda i: (0, many // part + 1 + i // per, i % per)),
            pl.BlockSpec((STRIP // many, many, width), lambda i: (i, 0, 0)),
            pl.BlockSpec((1, STRIP), lambda i: (0, i)),
            pl.BlockSpec((1, width), lambda i: (0, 0)),
        ],
        out_specs=[
            pl.BlockSpec((rows, width), lambda i: (0, 0)),
            pl.BlockSpec((rows, width), lambda i: (0, 0)),
            pl.BlockSpec((STRIP // many, many, width), lambda i: (i, 0, 0)),
            pl.BlockSpec((devices, part, STRIP), lambda i: (0, i // per, i % per)),
            pl.BlockSpec((1, STRIP), lambda i: (0, i)),
        ],
        out_shape=[
            jax.ShapeDtypeStruct((rows, width), F32),
            jax.ShapeDtypeStruct((rows, width), F32),
            jax.ShapeDtypeStruct((devices, many, width), BF16),
            jax.ShapeDtypeStruct((devices, hidden // width * part, width), BF16),
            jax.ShapeDtypeStruct((1, hidden), F32),
        ],
        scratch_shapes=[pltpu.VMEM((rows, STRIP), BF16)] * 2,
        compiler_params=pltpu.CompilerParams(vmem_limit_bytes=56 << 20),
        name="mixing",
    )(second, above, gathered, gathered, bias_e, bias_r)


def digits(devices):
    side = 2
    while 8 * side * side < devices:
        side += 1
    assert 8 * side * side == devices, devices
    return 4, side, 2


def neighbours(devices):
    outer, side, core = digits(devices)
    me = lax.axis_index("fsdp")
    c = lax.rem(me, core)
    q = lax.rem(lax.div(me, core), side)
    p = lax.rem(lax.div(me, core * side), side)
    o = lax.div(me, core * side * side)

    def at(o_, p_, q_, c_):
        return ((o_ * side + p_) * side + q_) * core + c_

    core_peer = at(o, p, q, 1 - c)
    q_peers = [lax.rem(q + d, side) for d in range(1, side)]
    p_peers = [lax.rem(p + d, side) for d in range(1, side)]
    o_peers = [lax.rem(o + d, outer) for d in range(1, outer)]
    return (o, p, q, c), core_peer, [(k, at(o, p, k, c)) for k in q_peers], [(k, at(o, k, q, c)) for k in p_peers], [(k, at(k, p, q, c)) for k in o_peers]


def greet(peers):
    barrier = pltpu.get_barrier_semaphore()
    for peer in peers:
        pl.semaphore_signal(barrier, inc=1, device_id=(peer,), device_id_type=MESH)
    pl.semaphore_wait(barrier, len(peers))


def reduce_kernel(devices, plan, arrays, *refs):
    outer, side, core = digits(devices)
    sources, outs = refs[:arrays], refs[arrays : 2 * arrays]
    rest = refs[2 * arrays :]
    count = len(plan)
    own = rest[:count]
    landed_c = rest[count : 2 * count]
    landed_a = rest[2 * count : 4 * count]
    landed_b = rest[4 * count : 5 * count]
    landed_o = rest[5 * count : 6 * count]
    load_sem, sem_c, sem_a, sem_b, sem_o = rest[6 * count :]
    (o, p, q, c), core_peer, q_peers, p_peers, o_peers = neighbours(devices)
    greet([core_peer] + [d for _, d in q_peers] + [d for _, d in p_peers] + [d for _, d in o_peers])
    width = own[0].shape[-1]
    half = width // 2
    columns = (pl.ds(0, half), pl.ds(half, half))

    def remote(src, dst, sems, slot, device):
        return pltpu.make_async_remote_copy(
            src_ref=src, dst_ref=dst, send_sem=sems.at[(0,) + slot], recv_sem=sems.at[(1,) + slot],
            device_id=(device,), device_id_type=MESH,
        )

    loads, to_core, first, second, third = {}, {}, {}, {}, {}
    for s, (k, row, rows) in enumerate(plan):
        at = pl.ds(row, rows)
        to_core[s] = remote(sources[k].at[:, :, :, 1 - c, at, :], landed_c[s], sem_c, (s,), core_peer)
        to_core[s].start()
        loads[s] = pltpu.make_async_copy(sources[k].at[:, :, :, c, at, :], own[s], load_sem.at[s])
        loads[s].start()

    def stage_core(s):
        loads[s].wait()
        to_core[s].wait_recv()
        mine, other = own[s], landed_c[s]

        def add(i, carry):
            a, b, d = i // (side * side), (i // side) % side, i % side
            mine[a, b, d] = mine[a, b, d] + other[a, b, d]
            return carry

        lax.fori_loop(0, outer * side * side, add, 0)
        for h in range(2):
            for d in range(side - 1):
                if h == 0:
                    k, device = q_peers[d]
                    src = mine.at[:, :, k, :, columns[h]]
                else:
                    k, device = p_peers[d]
                    src = mine.at[:, k, :, :, columns[h]]
                first[s, h, d] = remote(src, landed_a[2 * s + h].at[d], sem_a, (s, h, d), device)
                first[s, h, d].start()

    def stage_first(s):
        mine = own[s]
        for h in range(2):
            box = landed_a[2 * s + h]
            for d in range(side - 1):
                first[s, h, d].wait_recv()

            def add(i, carry):
                a, b = i // side, i % side
                total = mine[a, b, q, :, columns[h]] if h == 0 else mine[a, p, b, :, columns[h]]
                for d in range(side - 1):
                    total = total + box[d, a, b]
                box[0, a, b] = total
                return carry

            lax.fori_loop(0, outer * side, add, 0)
            for d in range(side - 1):
                k, device = (p_peers if h == 0 else q_peers)[d]
                second[s, h, d] = remote(
                    box.at[0, :, k], landed_b[s].at[d, :, :, columns[h]], sem_b, (s, h, d), device
                )
                second[s, h, d].start()

    def stage_second(s):
        box = landed_b[s]
        for h in range(2):
            part = landed_a[2 * s + h]
            k = p if h == 0 else q
            for d in range(side - 1):
                second[s, h, d].wait_recv()

            def add(a, carry):
                total = part[0, a, k]
                for d in range(side - 1):
                    total = total + box[d, a, :, columns[h]]
                box[0, a, :, columns[h]] = total
                return carry

            lax.fori_loop(0, outer, add, 0)
        for d in range(outer - 1):
            k, device = o_peers[d]
            third[s, d] = remote(box.at[0, k], landed_o[s].at[d], sem_o, (s, d), device)
            third[s, d].start()

    def stage_third(s):
        k, row, rows = plan[s]
        total = landed_b[s][0, o].astype(F32)
        for d in range(outer - 1):
            third[s, d].wait_recv()
            total = total + landed_o[s][d].astype(F32)
        outs[k][pl.ds(row, rows), :] = total

    for t in range(count + 3 * LAG):
        if t < count:
            stage_core(t)
        if 0 <= t - LAG < count:
            stage_first(t - LAG)
        if 0 <= t - 2 * LAG < count:
            stage_second(t - 2 * LAG)
        if 0 <= t - 3 * LAG < count:
            stage_third(t - 3 * LAG)
    for copies in (to_core, first, second, third):
        for copy in copies.values():
            copy.wait_send()


def reduce_scatter(devices, arrays, cuts):
    outer, side, core = digits(devices)
    plan = []
    for k, array in enumerate(arrays):
        rows = array.shape[1] // cuts[k]
        plan += [(k, i * rows, rows) for i in range(cuts[k])]
    width = arrays[0].shape[2]
    half = width // 2
    count = len(plan)
    vmem = pltpu.VMEM
    scratch = [vmem((outer, side, side, r, width), BF16) for _, _, r in plan]
    scratch += [vmem((outer, side, side, r, width), BF16) for _, _, r in plan]
    for _, _, r in plan:
        scratch += [vmem((side - 1, outer, side, r, half), BF16)] * 2
    scratch += [vmem((side - 1, outer, r, width), BF16) for _, _, r in plan]
    scratch += [vmem((outer - 1, r, width), BF16) for _, _, r in plan]
    dma = pltpu.SemaphoreType.DMA
    scratch += [dma((count,)), dma((2, count)), dma((2, count, 2, side - 1)), dma((2, count, 2, side - 1)), dma((2, count, outer - 1))]
    return pl.pallas_call(
        functools.partial(reduce_kernel, devices, plan, len(arrays)),
        out_shape=tuple(jax.ShapeDtypeStruct(array.shape[1:], F32) for array in arrays),
        in_specs=[pl.BlockSpec(memory_space=pl.ANY)] * len(arrays),
        out_specs=tuple(pl.BlockSpec(memory_space=pltpu.VMEM) for _ in arrays),
        scratch_shapes=scratch,
        compiler_params=pltpu.CompilerParams(collective_id=1, has_side_effects=True, vmem_limit_bytes=56 << 20),
        name="reduce_scatter",
    )(*[array.reshape(outer, side, side, core, *array.shape[1:]) for array in arrays])


def rank_kernel(length_ref, target_ref, bucket_ref, block_ref, info_ref, before_s):
    devices = length_ref.shape[0]
    lists, slots = bucket_ref.shape
    me = lax.axis_index("fsdp")
    base = me * slots
    window = 2 * slots

    def look(s, carry):
        start, mine, found, one, two = carry
        size = length_ref[s]
        target = target_ref[s]
        middle = start + lax.shift_right_logical(size, 1)
        inside = (middle >= base) & (middle < base + slots)
        offset = start - base + slots // 2
        entry = (offset, offset + size, target)
        first, second = inside & (found == 0), inside & (found == 1)
        one = tuple(jnp.where(first, new, old) for new, old in zip(entry, one))
        two = tuple(jnp.where(second, new, old) for new, old in zip(entry, two))
        return start + size, jnp.where(target == me, size, mine), found + inside.astype(jnp.int32), one, two

    zero = jnp.int32(0)
    nothing = (jnp.int32(window), jnp.int32(window), zero)
    total, mine, found, one, two = lax.fori_loop(0, devices, look, (zero, zero, zero, nothing, nothing))
    for k, value in enumerate((one[0], one[1], two[0], two[1], one[2], two[2], total, found)):
        info_ref[k] = value

    def fill(i, carry):
        at = pl.ds(pl.multiple_of(i * DH, DH), DH)
        first = lax.broadcasted_iota(jnp.int32, (DH, slots), 0) + i * DH
        second = lax.broadcasted_iota(jnp.int32, (DH, slots), 1)
        before_s[at, :] = jnp.where(first < second, 1.0, 0.0).astype(BF16)
        return carry

    lax.fori_loop(0, slots // DH, fill, 0)
    left = lax.broadcasted_iota(jnp.int32, (DH, DH), 0)
    right = lax.broadcasted_iota(jnp.int32, (DH, DH), 1)
    smaller = jnp.where((left // BUCKETS == right // BUCKETS) & (right < left), 1.0, 0.0).astype(BF16)
    many = DH // BUCKETS
    bucket = lax.broadcasted_iota(jnp.int32, (many, BUCKETS, slots), 1)
    live = lax.broadcasted_iota(jnp.int32, (many, BUCKETS, slots), 2) < mine
    ranks = []
    for g in range(lists // many):
        here = (jnp.broadcast_to(bucket_ref[g * many : (g + 1) * many, :][:, None, :], bucket.shape) == bucket) & live
        one_hot = jnp.where(here, 1.0, 0.0)
        flat = one_hot.reshape(DH, slots).astype(BF16)
        offset = jnp.sum(dot(smaller, flat), axis=1, keepdims=True)
        place = (dot(flat, before_s[...]) + offset).reshape(many, BUCKETS, slots)
        ranks.append(jnp.sum(one_hot * place, axis=1))
    rank = jnp.concatenate(ranks, axis=0)
    live = lax.broadcasted_iota(jnp.int32, (lists, slots), 1) < mine
    block_ref[...] = jnp.where(live, jnp.floor(rank * (1.0 / GROUP)), FREE).astype(BF16)


def rank_blocks(lengths, destination, buckets):
    lists, slots = buckets.shape
    smem = pl.BlockSpec(memory_space=pltpu.SMEM)
    vmem = pl.BlockSpec(memory_space=pltpu.VMEM)
    return pl.pallas_call(
        rank_kernel,
        in_specs=[smem, smem, vmem],
        out_specs=[vmem, smem],
        out_shape=[jax.ShapeDtypeStruct((lists, slots), BF16), jax.ShapeDtypeStruct((8,), jnp.int32)],
        scratch_shapes=[pltpu.VMEM((slots, slots), BF16)],
        compiler_params=pltpu.CompilerParams(vmem_limit_bytes=32 << 20),
        name="rank_blocks",
    )(lengths, destination, buckets)


def project_kernel(
    info_ref, head_ref, own_ref, tail_ref, gain_ref, shift_ref, w_s_ref, w_v_ref, one_ref, two_ref,
    normed_ref, shared_ref, value_ref, code_ref,
):
    i = pl.program_id(0)
    tile = own_ref.shape[0]
    steps = pl.num_programs(0)

    def go(ref):
        normed = layer_norm(ref[...].astype(F32), gain_ref[...], shift_ref[...]).astype(BF16)
        normed_ref[...] = normed
        shared_ref[...] = dot(normed, w_s_ref[...]).astype(BF16)
        value_ref[...] = dot(normed, w_v_ref[...]).astype(BF16)

    @pl.when(i < steps // 4)
    def _():
        go(head_ref)

    @pl.when((i >= steps // 4) & (i < steps - steps // 4))
    def _():
        go(own_ref)

    @pl.when(i >= steps - steps // 4)
    def _():
        go(tail_ref)

    @pl.when(i == 0)
    def _():
        lists, window = code_ref.shape
        lane = lax.broadcasted_iota(jnp.int32, (lists, window), 1)
        code = jnp.full((lists, window), FREE, F32)
        for k, ref in enumerate((one_ref, two_ref)):
            begin, end = info_ref[2 * k], info_ref[2 * k + 1]
            rows = ref[0].astype(F32)
            moved = pltpu.roll(jnp.concatenate([rows, rows], axis=1), lax.rem(begin, window), 1)
            code = jnp.where((lane >= begin) & (lane < end), moved + 32.0 * k, code)
        code_ref[...] = code.astype(BF16)


def project(info, head, own, tail, gain, shift, w_s, w_v, blocks):
    slots, width = own.shape
    window = 2 * slots
    lists = ROUNDS * HEADS
    tile = 256
    steps = window // tile
    quarter = steps // 4
    rows = pl.BlockSpec((tile, width), lambda i, info: (i, 0))
    vector = pl.BlockSpec((1, width), lambda i, info: (0, 0))
    matrix = pl.BlockSpec((width, width), lambda i, info: (0, 0), pipeline_mode=pl.Buffered(1))
    wide = jax.ShapeDtypeStruct((window, width), BF16)
    return pl.pallas_call(
        project_kernel,
        grid_spec=pltpu.PrefetchScalarGridSpec(
            num_scalar_prefetch=1,
            grid=(steps,),
            in_specs=[
                pl.BlockSpec((tile, width), lambda i, info: (jnp.minimum(i, quarter - 1), 0)),
                pl.BlockSpec((tile, width), lambda i, info: (jnp.clip(i - quarter, 0, 2 * quarter - 1), 0)),
                pl.BlockSpec((tile, width), lambda i, info: (jnp.clip(i - 3 * quarter, 0, quarter - 1), 0)),
                vector, vector, matrix, matrix,
                pl.BlockSpec((1, lists, slots), lambda i, info: (info[4], 0, 0)),
                pl.BlockSpec((1, lists, slots), lambda i, info: (info[5], 0, 0)),
            ],
            out_specs=[rows, rows, rows, pl.BlockSpec((lists, window), lambda i, info: (0, 0))],
        ),
        out_shape=[wide, wide, wide, jax.ShapeDtypeStruct((lists, window), BF16)],
        compiler_params=pltpu.CompilerParams(vmem_limit_bytes=40 << 20),
        name="project",
    )(info, head, own, tail, gain, shift, w_s, w_v, blocks, blocks)


def gather_kernel(devices, arrays, *refs):
    sources, outs = refs[:arrays], refs[arrays : 2 * arrays]
    own_sem, sem_o, sem_a, sem_b, sem_c = refs[2 * arrays :]
    outer, side, core = digits(devices)
    (o, p, q, c), core_peer, q_peers, p_peers, o_peers = neighbours(devices)
    greet([core_peer] + [d for _, d in q_peers] + [d for _, d in p_peers] + [d for _, d in o_peers])
    half = sources[0].shape[-1] // 2
    columns = (pl.ds(0, half), pl.ds(half, half))

    def remote(src, dst, sems, slot, device):
        return pltpu.make_async_remote_copy(
            src_ref=src, dst_ref=dst, send_sem=sems.at[(0,) + slot], recv_sem=sems.at[(1,) + slot],
            device_id=(device,), device_id_type=MESH,
        )

    copies, locals_, begun, first, second, last = [], [], {}, {}, {}, {}
    for s in range(arrays):
        locals_.append(pltpu.make_async_copy(sources[s], outs[s].at[o, p, q, c], own_sem.at[s]))
        locals_[s].start()
        for d, (k, device) in enumerate(o_peers):
            begun[s, d] = remote(sources[s], outs[s].at[o, p, q, c], sem_o, (s, d), device)
            begun[s, d].start()

    def stage_a(s):
        locals_[s].wait()
        for d in range(outer - 1):
            begun[s, d].wait_recv()
        for h, peers in enumerate((q_peers, p_peers)):
            piece = outs[s].at[:, p, q, c, :, columns[h]]
            for d, (k, device) in enumerate(peers):
                first[s, h, d] = remote(piece, piece, sem_a, (s, h, d), device)
                first[s, h, d].start()

    def stage_b(s):
        for h, peers in enumerate((p_peers, q_peers)):
            for d in range(side - 1):
                first[s, h, d].wait_recv()
            piece = outs[s].at[:, p, :, c, :, columns[h]] if h == 0 else outs[s].at[:, :, q, c, :, columns[h]]
            for d, (k, device) in enumerate(peers):
                second[s, h, d] = remote(piece, piece, sem_b, (s, h, d), device)
                second[s, h, d].start()

    def stage_c(s):
        for h in range(2):
            for d in range(side - 1):
                second[s, h, d].wait_recv()
        piece = outs[s].at[:, :, :, c]
        last[s] = remote(piece, piece, sem_c, (s,), core_peer)
        last[s].start()

    for t in range(arrays + 2):
        if t < arrays:
            stage_a(t)
        if 0 <= t - 1 < arrays:
            stage_b(t - 1)
        if 0 <= t - 2 < arrays:
            stage_c(t - 2)
    for s in range(arrays):
        last[s].wait_recv()
    for group in (begun, first, second, last):
        for copy in group.values():
            copy.wait_send()


def gather(devices, arrays):
    outer, side, core = digits(devices)
    count = len(arrays)
    dma = pltpu.SemaphoreType.DMA
    anywhere = pl.BlockSpec(memory_space=pl.ANY)
    outs = pl.pallas_call(
        functools.partial(gather_kernel, devices, count),
        out_shape=tuple(jax.ShapeDtypeStruct((outer, side, side, core) + array.shape, array.dtype) for array in arrays),
        in_specs=[anywhere] * count,
        out_specs=(anywhere,) * count,
        scratch_shapes=[
            dma((count,)), dma((2, count, outer - 1)), dma((2, count, 2, side - 1)), dma((2, count, 2, side - 1)), dma((2, count))
        ],
        compiler_params=pltpu.CompilerParams(collective_id=2, has_side_effects=True),
        name="gather",
    )(*arrays)
    return [out.reshape((devices,) + array.shape) for out, array in zip(outs, arrays)]


def body(
    input_one, input_two, upstream_one, upstream_two, lengths, destination, buckets,
    w_shared, w_value, w_output, w_expand, w_reduce,
    gain_attend, shift_attend, gain_mixing, shift_mixing, bias_output, bias_expand, bias_reduce,
):
    devices = lax.axis_size("fsdp")
    me = lax.axis_index("fsdp")
    slots, width = input_one.shape
    half = slots // 2
    window = 2 * slots
    part = w_shared.shape[0]
    hidden = w_expand.shape[1]
    sides = hidden // width
    down = [(i, i - 1) for i in range(1, devices)]
    up = [(i, i + 1) for i in range(devices - 1)]

    def to_sides(head, tail):
        return lax.ppermute(tail, "fsdp", up), lax.ppermute(head, "fsdp", down)

    def widen(own):
        head, tail = to_sides(own[:half], own[half:])
        return jnp.concatenate([head, own, tail], axis=0)

    def narrow(wide):
        head, tail = to_sides(wide[:half], wide[half + slots :])
        return wide[half : half + slots], jnp.concatenate([head, tail], axis=0)

    base = me * slots
    lists = ROUNDS * HEADS
    block, info = rank_blocks(lengths, destination, buckets[0])
    spot = jnp.arange(width, dtype=jnp.int32)
    short = jnp.stack([gain_attend, shift_attend, gain_mixing, shift_mixing, bias_output, bias_reduce])
    short = jnp.where(spot // part == me, jnp.tile(short, (1, devices)), 0.0)
    many = hidden // devices
    long = jnp.tile(bias_expand, width // many)[None]
    long = jnp.where(spot[None] // many + (width // many) * jnp.arange(sides, dtype=jnp.int32)[:, None] == me, long, 0.0)
    vectors = jnp.concatenate([short, long], axis=0)
    high = lax.reduce_precision(vectors, 8, 7)
    count = vectors.shape[0]
    packed = jnp.concatenate(
        [block, high.astype(BF16), (vectors - high).astype(BF16), jnp.zeros((24 - 2 * count, width), BF16)], axis=0
    )
    second_gather = lax.all_gather(
        jnp.concatenate(
            [w_reduce, w_output] + [w_expand[:, k * width : (k + 1) * width] for k in range(sides)], axis=0
        ),
        "fsdp", axis=0, tiled=False,
    )
    full_shared, full_value, packed = gather(devices, [w_shared, w_value, packed])
    full_shared, full_value = full_shared.reshape(width, width), full_value.reshape(width, width)
    vectors = jnp.sum(packed[:, lists : lists + 2 * count].astype(F32), axis=0)
    vectors = vectors[:count] + vectors[count:]
    gain_a, shift_a, gain_m, shift_m, bias_o, bias_r = (vectors[k : k + 1] for k in range(6))
    bias_e = vectors[6:].reshape(1, hidden)
    full_output = second_gather[:, sides * part : (sides + 1) * part].reshape(width, width)
    lane = jnp.arange(HEADS * DH, dtype=jnp.int32)
    row = jnp.arange(lists, dtype=jnp.int32)[:, None]
    spread = (row == ((lane % 64) // 16) * HEADS + lane // DH).astype(BF16)

    live = ((base + jnp.arange(slots, dtype=jnp.int32)) < info[6]).astype(F32)[:, None]
    slot_one = input_one.astype(F32)
    slot_two = input_two.astype(F32)
    above_one = live * upstream_one.astype(F32)
    above_two = live * upstream_two.astype(F32)

    two_head, two_tail = to_sides(input_two[:half], input_two[half:])
    two_window = jnp.concatenate([two_head, input_two, two_tail], axis=0).astype(F32)
    normed, shared, values, code = project(
        info, two_head, input_two, two_tail, gain_a, shift_a, full_shared, full_value, packed
    )
    combined_window, lse, lone = attend(info, shared, values, code, spread)
    own, other = narrow(combined_window)
    combined = own + other
    attended = dot(combined, full_output) + bias_o
    out_one = slot_one + live * attended
    second = layer_norm(out_one, gain_m, shift_m).astype(BF16)
    d_reduce = above_two.astype(BF16)
    grad_bias_reduce = jnp.sum(d_reduce, axis=0, dtype=F32)
    mixed, d_second, grad_reduce, grad_expand, grad_bias_expand = mixing(
        second, d_reduce, second_gather, bias_e, bias_r, part
    )
    out_two = slot_two + live * mixed
    d_one_mix, grad_gain_m, grad_shift_m = norm_back(out_one, gain_m, shift_m, d_second)
    total_one = above_one + d_one_mix
    d_attend = (live * total_one).astype(BF16)
    grad_output = dot(combined, d_attend, TN)
    grad_bias_output = jnp.sum(d_attend, axis=0, dtype=F32)
    d_combined = dot(d_attend, full_output, NT).astype(BF16)
    d_shared, d_values = attend_back(
        info, shared, values, code, spread, combined_window, widen(d_combined), lse, lone
    )
    grad_shared = dot(normed, d_shared, TN)
    grad_value = dot(normed, d_values, TN)
    d_normed = dot(d_shared, full_shared, NT) + dot(d_values, full_value, NT)
    d_two_window, grad_gain_a, grad_shift_a = norm_back(two_window, gain_a, shift_a, d_normed)
    own, other = narrow(d_two_window.astype(BF16))
    back_two = above_two + own.astype(F32) + other.astype(F32)

    def split(whole):
        return whole.astype(BF16).reshape(devices, -1, width)

    small = jnp.concatenate(
        [
            member.reshape(devices, -1)
            for member in (
                grad_gain_a, grad_shift_a, grad_gain_m, grad_shift_m, grad_bias_output, grad_bias_reduce, grad_bias_expand
            )
        ],
        axis=1,
    )
    small = jnp.zeros((devices, 8, width), BF16).at[:, 0, : small.shape[1]].set(small.astype(BF16))
    grad_reduce, grad_expand, grad_output, grad_shared, grad_value, small = reduce_scatter(
        devices,
        (grad_reduce, grad_expand, split(grad_output), split(grad_shared), split(grad_value), small),
        (2, 2, 1, 1, 1, 1),
    )
    small = small[0]
    return (
        (live * out_one).astype(BF16),
        (live * out_two).astype(BF16),
        (live * total_one).astype(BF16),
        (live * back_two).astype(BF16),
        grad_shared,
        grad_value,
        grad_output,
        jnp.concatenate([grad_expand[k * part : (k + 1) * part] for k in range(sides)], axis=1),
        grad_reduce,
        small[:part],
        small[part : 2 * part],
        small[2 * part : 3 * part],
        small[3 * part : 4 * part],
        small[4 * part : 5 * part],
        small[6 * part : 6 * part + hidden // devices],
        small[5 * part : 6 * part],
    )


def solution(mesh):
    rows, flat, whole = P("fsdp", None), P("fsdp"), P()
    return jax.shard_map(
        body,
        mesh=mesh,
        in_specs=(rows,) * 4 + (whole, whole, P("fsdp", None, None)) + (rows,) * 5 + (flat,) * 7,
        out_specs=(rows,) * 9 + (flat,) * 7,
        check_vma=False,
    )
```

```python
import functools
import math

import jax
import jax.numpy as jnp
from jax import lax
from jax.experimental import pallas as pl
from jax.experimental.pallas import tpu as pltpu
from jax.sharding import PartitionSpec as P

HEADS = 8
DH = 128
GROUP = 64
ROUNDS = 4
BUCKETS = 32
EPS_NORM = 1e-05
EPS_UNIT = 1e-06
LOG2E = math.log2(math.e)
SELF2 = -100000.0 * LOG2E
NEG = -1e30
SCALE = 1.0 / math.sqrt(DH)
TILE = 512
HALF = TILE // 2
STEP = 128.0
SHIFT = 1.5 * 2.0**30
TAME = 3000.0
PAIR = 2
FREE = 99.0
STRIP = 512
CURVE = math.sqrt(2.0 / math.pi)
MESH = pl.DeviceIdType.MESH

NT = (((1,), (1,)), ((), ()))
NN = (((1,), (0,)), ((), ()))
TN = (((0,), (0,)), ((), ()))
F32 = jnp.float32
BF16 = jnp.bfloat16


def dot(a, b, dims=NN):
    return lax.dot_general(a, b, dims, preferred_element_type=F32)


def layer_norm(values, gain, shift):
    center = values - jnp.mean(values, axis=-1, keepdims=True)
    spread = jnp.mean(center * center, axis=-1, keepdims=True)
    return center * lax.rsqrt(spread + EPS_NORM) * gain + shift


def norm_back(values, gain, shift, upstream):
    outcome, pullback = jax.vjp(layer_norm, values, gain, shift)
    return pullback(upstream)


def prepare(q, code_ref, spread, ask_s, key_s, h, at):
    lane = lax.broadcasted_iota(jnp.int32, (TILE, DH), 1)
    target = ((lane // 64) * 32 + lane % 16).astype(F32)
    wide = q.astype(F32)
    square = jnp.sum(wide * wide, axis=1, keepdims=True)
    code = dot(code_ref[:, at], spread, TN)
    here = code == target
    ask_s[h, at, :DH] = q
    ask_s[h, at, DH:] = jnp.where(here, STEP, 0.0).astype(BF16)
    key_s[h, at, :DH] = (wide * (lax.rsqrt(square + EPS_UNIT) * (SCALE * LOG2E))).astype(BF16)
    key_s[h, at, DH:] = jnp.where(here | (code + 1.0 == target), 1.0, 0.0).astype(BF16)
    return jnp.max(square)


def lowest(info_ref, i):
    start, stop = i * TILE, (i + 1) * TILE
    one = (info_ref[0] < stop) & (info_ref[1] > start)
    two = (info_ref[2] < stop) & (info_ref[3] > start)
    begin = jnp.where(one, info_ref[0], jnp.where(two, info_ref[2], stop))
    return lax.div(begin, TILE)


def tile_rows(i):
    return pl.ds(pl.multiple_of(i * TILE, TILE), TILE)


def halves(i):
    start = i * TILE
    return [((0, pl.multiple_of(start, HALF), pl.multiple_of(start, HALF)), HALF),
            ((HALF, pl.multiple_of(start + HALF, HALF), pl.multiple_of(start, HALF)), TILE)]


def part_of(both):
    count = (both + SHIFT) - SHIFT
    return count, both - count


def apart(left, right):
    return dot(left[:, DH:], right[:, DH:], NT), dot(left[:, :DH], right[:, :DH], NT)


def attend_kernel(low_ref, q_ref, v_ref, code_ref, spread_ref, comb_ref, lse_ref, lone_ref, ask_s, key_s, more_s, acc_s, top_s):
    rows = q_ref.shape[0]
    tiles = rows // TILE
    heads = [slice(h * DH, (h + 1) * DH) for h in range(PAIR)]

    def ready(i, largest):
        def fill():
            most = jnp.float32(0.0)
            at = tile_rows(i)
            for h, cols in enumerate(heads):
                most = jnp.maximum(most, prepare(q_ref[at, cols], code_ref, spread_ref[:, cols], ask_s, key_s, h, at))
                more_s[h, at, :DH] = v_ref[at, cols]
                more_s[h, at, DH:] = jnp.ones((TILE, DH), BF16)
            return most

        return jnp.maximum(largest, lax.cond(lowest(low_ref, i) <= i, fill, lambda: jnp.float32(0.0)))

    largest = lax.fori_loop(0, tiles, ready, jnp.float32(0.0))
    tame = largest * (SCALE * LOG2E) ** 2 < TAME
    ask_at = lax.broadcasted_iota(jnp.int32, (TILE, TILE), 0)
    key_at = lax.broadcasted_iota(jnp.int32, (TILE, TILE), 1)

    def finish(h, cols, at, top):
        total = acc_s[h, :, DH:]
        some = total > 0.0
        safe = jnp.where(some, total, 1.0)
        inverse = jnp.where(some, 1.0 / safe, 0.0)
        comb_ref[at, cols] = (acc_s[h, :, :DH] * inverse).astype(BF16)
        lse_ref[h, :, at] = (jnp.log2(safe) + top).T[:1]

    def rows_of(i, carry):
        at = tile_rows(i)
        low = lowest(low_ref, i)

        @pl.when((low <= i) & tame)
        def _():
            for h in range(PAIR):
                acc_s[h] = jnp.zeros((TILE, 2 * DH), F32)

            def step(j, carry):
                keys = tile_rows(j)
                for h in range(PAIR):
                    count, score = part_of(dot(ask_s[h, at, :], key_s[h, keys, :], NT))
                    acc_s[h] += dot((count * jnp.exp2(score)).astype(BF16), more_s[h, keys, :])
                return carry

            lax.fori_loop(low, i, step, 0)
            for h, cols in enumerate(heads):
                for asks, span in halves(i):
                    here = pl.ds(asks[0], HALF)
                    there = pl.ds(asks[1], HALF)
                    keys = pl.ds(asks[2], span)
                    key_at = lax.broadcasted_iota(jnp.int32, (HALF, span), 1)
                    ask_at = lax.broadcasted_iota(jnp.int32, (HALF, span), 0) + (span - HALF)
                    count, score = part_of(dot(ask_s[h, there, :], key_s[h, keys, :], NT))
                    prob = jnp.where(key_at < ask_at, count * jnp.exp2(score), 0.0).astype(BF16)
                    acc_s[h, here, :] += dot(prob, more_s[h, keys, :])
                    active = jnp.max(jnp.where(key_at == ask_at, count, 0.0), axis=1, keepdims=True) > 0.0
                    lone = jnp.where(active & (acc_s[h, here, DH:] == 0.0), 1.0, 0.0)
                    acc_s[h, here, :DH] += lone * v_ref[there, cols].astype(F32)
                    acc_s[h, here, DH:] += lone
                    lone_ref[h, :, there] = lone.T[:1]
                finish(h, cols, at, 0.0)

        @pl.when((low <= i) & jnp.logical_not(tame))
        def _():
            for h, cols in enumerate(heads):
                count, score = apart(ask_s[h, at, :], key_s[h, at, :])
                score = jnp.where(key_at == ask_at, SELF2, score)
                score = jnp.where((key_at <= ask_at) & (count > 0.5), score, NEG)
                top = jnp.max(score, axis=1, keepdims=True)
                prob = count * jnp.exp2(score - top)
                acc_s[h] = dot(prob.astype(BF16), more_s[h, at, :])
                top_s[h] = jnp.broadcast_to(top, (TILE, DH))

                def step(j, carry):
                    keys = tile_rows(j)
                    count, score = apart(ask_s[h, at, :], key_s[h, keys, :])
                    score = jnp.where(count > 0.5, score, NEG)
                    top = top_s[h]
                    newer = jnp.maximum(top, jnp.max(score, axis=1, keepdims=True))
                    fade = jnp.exp2(top - newer)
                    prob = count * jnp.exp2(score - newer[:, :1])
                    acc_s[h] = acc_s[h] * jnp.concatenate([fade, fade], axis=1) + dot(prob.astype(BF16), more_s[h, keys, :])
                    top_s[h] = newer
                    return carry

                lax.fori_loop(low, i, step, 0)
                total = acc_s[h, :, DH:]
                own = STEP * ROUNDS * jnp.exp2(SELF2 - jnp.maximum(top_s[h], SELF2))
                lone_ref[h, :, at] = jnp.where(total > 0.0, own / jnp.where(total > 0.0, total, 1.0), 0.0).T[:1]
                finish(h, cols, at, top_s[h])

        @pl.when(low > i)
        def _():
            comb_ref[at, :] = jnp.zeros((TILE, PAIR * DH), BF16)
            for h in range(PAIR):
                lse_ref[h, :, at] = jnp.zeros((1, TILE), F32)
                lone_ref[h, :, at] = jnp.zeros((1, TILE), F32)

        return carry

    lax.fori_loop(0, tiles, rows_of, 0)


def back_kernel(
    low_ref, q_ref, v_ref, code_ref, spread_ref, comb_ref, above_ref, lse_ref, lone_ref,
    dq_ref, dv_ref, ask_s, key_s, dunit_s, dvalue_s, dask_s,
):
    rows = q_ref.shape[0]
    tiles = rows // TILE
    heads = [slice(h * DH, (h + 1) * DH) for h in range(PAIR)]

    def ready(i, largest):
        def fill():
            most = jnp.float32(0.0)
            at = tile_rows(i)
            for h, cols in enumerate(heads):
                most = jnp.maximum(most, prepare(q_ref[at, cols], code_ref, spread_ref[:, cols], ask_s, key_s, h, at))
                for total in (dunit_s, dvalue_s, dask_s):
                    total[h, at, :] = jnp.zeros((TILE, DH), F32)
            return most

        return jnp.maximum(largest, lax.cond(lowest(low_ref, i) <= i, fill, lambda: jnp.float32(0.0)))

    largest = lax.fori_loop(0, tiles, ready, jnp.float32(0.0))
    tame = largest * (SCALE * LOG2E) ** 2 < TAME

    def pass_over(i, low, split):
        at = tile_rows(i)
        deltas = []
        for h, cols in enumerate(heads):
            mixed = above_ref[at, cols].astype(F32) * comb_ref[at, cols].astype(F32)
            deltas.append(jnp.sum(mixed.T, axis=0, keepdims=True))

        def step(j, carry):
            keys = tile_rows(j)
            for h, cols in enumerate(heads):
                q, above, unit = q_ref[at, cols], above_ref[at, cols], key_s[h, keys, :DH]
                count, score = split(key_s[h, keys, :], ask_s[h, at, :])
                d_prob = dot(v_ref[keys, cols], above, NT)
                prob = count * jnp.exp2(score - lse_ref[h, :, at])
                d_score = (prob * (d_prob - carry[h])).astype(BF16)
                dvalue_s[h, keys, :] += dot(prob.astype(BF16), above)
                dunit_s[h, keys, :] += dot(d_score, q)
                dask_s[h, at, :] += dot(d_score, unit, TN)
            return carry

        deltas = lax.fori_loop(low, i, step, tuple(deltas))
        for h, cols in enumerate(heads):
            for asks, span in halves(i):
                there = pl.ds(asks[1], HALF)
                keys = pl.ds(asks[2], span)
                key_at = lax.broadcasted_iota(jnp.int32, (span, HALF), 0)
                ask_at = lax.broadcasted_iota(jnp.int32, (span, HALF), 1) + (span - HALF)
                q, above, unit = q_ref[there, cols], above_ref[there, cols], key_s[h, keys, :DH]
                count, score = split(key_s[h, keys, :], ask_s[h, there, :])
                d_prob = dot(v_ref[keys, cols], above, NT)
                prob = count * jnp.exp2(score - lse_ref[h, :, there])
                prob = jnp.where(key_at < ask_at, prob, 0.0)
                d_score = (prob * (d_prob - deltas[h][:, asks[0] : asks[0] + HALF])).astype(BF16)
                prob = jnp.where(key_at == ask_at, lone_ref[h, :, there], prob).astype(BF16)
                dvalue_s[h, keys, :] += dot(prob, above)
                dunit_s[h, keys, :] += dot(d_score, q)
                dask_s[h, there, :] += dot(d_score, unit, TN)

    def together(left, right):
        return part_of(dot(left, right, NT))

    def guarded(left, right):
        count, score = apart(left, right)
        return count, jnp.where(count > 0.5, score, NEG)

    def rows_of(i, carry):
        low = lowest(low_ref, i)

        @pl.when((low <= i) & tame)
        def _():
            pass_over(i, low, together)

        @pl.when((low <= i) & jnp.logical_not(tame))
        def _():
            pass_over(i, low, guarded)

        return carry

    lax.fori_loop(0, tiles, rows_of, 0)

    def close(i, carry):
        at = tile_rows(i)

        @pl.when(lowest(low_ref, i) <= i)
        def _():
            for h, cols in enumerate(heads):
                q = q_ref[at, cols].astype(F32)
                norm = lax.rsqrt(jnp.sum(q * q, axis=1, keepdims=True) + EPS_UNIT)
                d_unit = dunit_s[h, at, :] * SCALE
                along = jnp.sum(q * d_unit, axis=1, keepdims=True)
                d_q = dask_s[h, at, :] * (1.0 / LOG2E) + d_unit * norm - q * (norm * norm * norm * along)
                dq_ref[at, cols] = d_q.astype(BF16)
                dv_ref[at, cols] = dvalue_s[h, at, :].astype(BF16)

        @pl.when(lowest(low_ref, i) > i)
        def _():
            dq_ref[at, :] = jnp.zeros((TILE, PAIR * DH), BF16)
            dv_ref[at, :] = jnp.zeros((TILE, PAIR * DH), BF16)

        return carry

    lax.fori_loop(0, tiles, close, 0)


def head_specs(rows):
    by_head = pl.BlockSpec((rows, PAIR * DH), lambda h, low: (0, h))
    code = pl.BlockSpec((ROUNDS * HEADS, rows), lambda h, low: (0, 0))
    spread = pl.BlockSpec((ROUNDS * HEADS, PAIR * DH), lambda h, low: (0, h))
    stat = pl.BlockSpec((PAIR, 1, rows), lambda h, low: (h, 0, 0))
    return by_head, code, spread, stat


def attend(low, shared, values, code, spread):
    rows = shared.shape[0]
    by_head, code_spec, spread_spec, stat = head_specs(rows)
    wide = jax.ShapeDtypeStruct((rows, HEADS * DH), BF16)
    thin = jax.ShapeDtypeStruct((HEADS, 1, rows), F32)
    return pl.pallas_call(
        attend_kernel,
        grid_spec=pltpu.PrefetchScalarGridSpec(
            num_scalar_prefetch=1,
            grid=(HEADS // PAIR,),
            in_specs=[by_head, by_head, code_spec, spread_spec],
            out_specs=[by_head, stat, stat],
            scratch_shapes=[pltpu.VMEM((PAIR, rows, 2 * DH), BF16)] * 3
            + [pltpu.VMEM((PAIR, TILE, 2 * DH), F32), pltpu.VMEM((PAIR, TILE, DH), F32)],
        ),
        out_shape=(wide, thin, thin),
        compiler_params=pltpu.CompilerParams(vmem_limit_bytes=48 << 20),
        name="attend",
        cost_estimate=pl.CostEstimate(
            flops=HEADS * 20 * 3 * 2 * TILE * TILE * DH, bytes_accessed=rows * HEADS * DH * 6, transcendentals=HEADS * 20 * TILE * TILE
        ),
    )(low, shared, values, code, spread)


def attend_back(low, shared, values, code, spread, combined, above, lse, lone):
    rows = shared.shape[0]
    by_head, code_spec, spread_spec, stat = head_specs(rows)
    wide = jax.ShapeDtypeStruct((rows, HEADS * DH), BF16)
    return pl.pallas_call(
        back_kernel,
        grid_spec=pltpu.PrefetchScalarGridSpec(
            num_scalar_prefetch=1,
            grid=(HEADS // PAIR,),
            in_specs=[by_head, by_head, code_spec, spread_spec, by_head, by_head, stat, stat],
            out_specs=[by_head, by_head],
            scratch_shapes=[pltpu.VMEM((PAIR, rows, 2 * DH), BF16)] * 2 + [pltpu.VMEM((PAIR, rows, DH), F32)] * 3,
        ),
        out_shape=(wide, wide),
        compiler_params=pltpu.CompilerParams(vmem_limit_bytes=48 << 20),
        name="attend_back",
        cost_estimate=pl.CostEstimate(
            flops=HEADS * 20 * 6 * 2 * TILE * TILE * DH, bytes_accessed=rows * HEADS * DH * 12, transcendentals=HEADS * 20 * TILE * TILE
        ),
    )(low, shared, values, code, spread, combined, above, lse, lone)


def digits(devices):
    side = 2
    while 8 * side * side < devices:
        side += 1
    assert 8 * side * side == devices, devices
    return 4, side, 2


def neighbours(devices):
    outer, side, core = digits(devices)
    me = lax.axis_index("fsdp")
    c = lax.rem(me, core)
    q = lax.rem(lax.div(me, core), side)
    p = lax.rem(lax.div(me, core * side), side)
    o = lax.div(me, core * side * side)

    def at(o_, p_, q_, c_):
        return ((o_ * side + p_) * side + q_) * core + c_

    core_peer = at(o, p, q, 1 - c)
    q_peers = [(k, at(o, p, k, c)) for k in (lax.rem(q + d, side) for d in range(1, side))]
    p_peers = [(k, at(o, k, q, c)) for k in (lax.rem(p + d, side) for d in range(1, side))]
    o_peers = [(k, at(k, p, q, c)) for k in (lax.rem(o + d, outer) for d in range(1, outer))]
    return (o, p, q, c), core_peer, q_peers, p_peers, o_peers


def peers_of(where):
    return [where[1]] + [device for group in where[2:] for _, device in group]


def greet(peers):
    barrier = pltpu.get_barrier_semaphore()
    for peer in peers:
        pl.semaphore_signal(barrier, inc=1, device_id=(peer,), device_id_type=MESH)
    pl.semaphore_wait(barrier, len(peers))


def remote(src, dst, sems, slot, device):
    return pltpu.make_async_remote_copy(
        src_ref=src, dst_ref=dst, send_sem=sems.at[(0,) + slot], recv_sem=sems.at[(1,) + slot],
        device_id=(device,), device_id_type=MESH,
    )


class Scatter:
    def __init__(self, devices, where, slot, boxes, sems, other, mine, load=None):
        self.outer, self.side, _ = digits(devices)
        (self.o, self.p, self.q, self.c), self.core_peer, self.q_peers, self.p_peers, self.o_peers = where
        self.slot = slot
        self.box_c, box_a0, box_a1, self.box_b, self.box_o = boxes
        self.box_a = (box_a0, box_a1)
        self.sem_c, self.sem_a, self.sem_b, self.sem_o = sems
        self.other, self.mine, self.load = other, mine, load
        half = self.box_o.shape[-1] // 2
        self.columns = (pl.ds(0, half), pl.ds(half, half))

    def core(self):
        return remote(self.other(), self.box_c, self.sem_c, (self.slot,), self.core_peer)

    def first(self, h, d):
        k, device = (self.q_peers, self.p_peers)[h][d]
        spot = (slice(None), slice(None), k) if h == 0 else (slice(None), k, slice(None))
        return remote(self.mine(spot, self.columns[h]), self.box_a[h].at[d], self.sem_a, (self.slot, h, d), device)

    def second(self, h, d):
        k, device = (self.p_peers, self.q_peers)[h][d]
        return remote(
            self.box_a[h].at[0, :, k], self.box_b.at[d, :, :, self.columns[h]], self.sem_b, (self.slot, h, d), device
        )

    def third(self, d):
        k, device = self.o_peers[d]
        return remote(self.box_b.at[0, k], self.box_o.at[d], self.sem_o, (self.slot, d), device)

    def begin(self):
        self.core().start()
        if self.load is not None:
            self.load().start()

    def stage_core(self):
        if self.load is not None:
            self.load().wait()
        self.core().wait_recv()
        side = self.side

        def add(i, carry):
            spot = (lax.div(i, side * side), lax.rem(lax.div(i, side), side), lax.rem(i, side))
            ref = self.mine(spot, slice(None))
            ref[...] = ref[...] + self.box_c[spot]
            return carry

        lax.fori_loop(0, self.outer * side * side, add, 0)
        for h in range(2):
            for d in range(side - 1):
                self.first(h, d).start()

    def stage_first(self):
        side = self.side
        for h in range(2):
            box = self.box_a[h]
            for d in range(side - 1):
                self.first(h, d).wait_recv()

            def add(i, carry):
                a, b = lax.div(i, side), lax.rem(i, side)
                total = self.mine((a, b, self.q) if h == 0 else (a, self.p, b), self.columns[h])[...]
                for d in range(side - 1):
                    total = total + box[d, a, b]
                box[0, a, b] = total
                return carry

            lax.fori_loop(0, self.outer * side, add, 0)
            for d in range(side - 1):
                self.second(h, d).start()

    def stage_second(self):
        box = self.box_b
        for h in range(2):
            k = self.p if h == 0 else self.q
            for d in range(self.side - 1):
                self.second(h, d).wait_recv()

            def add(a, carry):
                total = self.box_a[h][0, a, k]
                for d in range(self.side - 1):
                    total = total + box[d, a, :, self.columns[h]]
                box[0, a, :, self.columns[h]] = total
                return carry

            lax.fori_loop(0, self.outer, add, 0)
        for d in range(self.outer - 1):
            self.third(d).start()

    def stage_third(self):
        total = self.box_b[0, self.o].astype(F32)
        for d in range(self.outer - 1):
            self.third(d).wait_recv()
            total = total + self.box_o[d].astype(F32)
        return total

    def sent_first(self):
        self.core().wait_send()
        for h in range(2):
            for d in range(self.side - 1):
                self.first(h, d).wait_send()

    def sent_last(self):
        for h in range(2):
            for d in range(self.side - 1):
                self.second(h, d).wait_send()
        for d in range(self.outer - 1):
            self.third(d).wait_send()


def boxes_for(devices, rows, width):
    outer, side, _ = digits(devices)
    half = width // 2
    return [
        pltpu.VMEM((outer, side, side, rows, width), BF16),
        pltpu.VMEM((side - 1, outer, side, rows, half), BF16),
        pltpu.VMEM((side - 1, outer, side, rows, half), BF16),
        pltpu.VMEM((side - 1, outer, rows, width), BF16),
        pltpu.VMEM((outer - 1, rows, width), BF16),
    ]


def sems_for(devices, count):
    outer, side, _ = digits(devices)
    dma = pltpu.SemaphoreType.DMA
    return [dma((2, count)), dma((2, count, 2, side - 1)), dma((2, count, 2, side - 1)), dma((2, count, outer - 1))]


def mixing_kernel(
    devices, hidden_steps, second_ref, above_ref, expand_ref, reduce_ref, bias_e_ref, bias_r_ref,
    out_ref, back_ref, grad_r_ref, grad_b_ref, grad_e_ref, rest_e_ref, above_b_ref, act_s, pre_s, grad_s, *rest,
):
    step = pl.program_id(0)
    rows, width = second_ref.shape
    strip = act_s.shape[1]
    per = width // strip
    slices = (len(rest) - 4) // 5
    sems = rest[5 * slices :]
    where = neighbours(devices)
    (o, p, q, c), core_peer, q_peers, p_peers, o_peers = where
    part = grad_s.shape[-2]

    def mover(k):
        def other():
            return grad_s.at[k % 2, :, :, :, 1 - c]

        def mine(spot, cols):
            return grad_s.at[(k % 2,) + tuple(spot) + (c, slice(None), cols)]

        return Scatter(devices, where, k, rest[5 * k : 5 * k + 5], sems, other, mine)

    movers = [mover(k) for k in range(slices)]
    w_e = expand_ref[...].reshape(width, strip)
    w_r = reduce_ref[...].reshape(strip, width)

    @pl.when(step == 0)
    def _():
        greet(peers_of(where))
        out_ref[...] = jnp.broadcast_to(bias_r_ref[...], out_ref.shape)
        back_ref[...] = jnp.zeros(back_ref.shape, F32)
        above_b_ref[...] = jnp.sum(above_ref[...].astype(F32), axis=0, keepdims=True)

    pre = dot(second_ref[...], w_e) + bias_e_ref[...]
    square = pre * pre
    curve = jnp.tanh(CURVE * pre * (1.0 + 0.044715 * square))
    hinge = 0.5 * (1.0 + curve)
    act_s[...] = (pre * hinge).astype(BF16)
    slope = hinge + 0.5 * pre * (1.0 - curve * curve) * (CURVE * (1.0 + 3 * 0.044715 * square))
    d_pre = (dot(above_ref[...], w_r, NT) * slope).astype(BF16)
    pre_s[...] = d_pre
    grad_b_ref[...] = jnp.sum(d_pre.astype(F32), axis=0, keepdims=True)
    out_ref[...] += dot(act_s[...], w_r)
    back_ref[...] += dot(d_pre, w_e, NT)
    grad_r_ref[...] = dot(act_s[...], above_ref[...], TN).astype(BF16).reshape(grad_r_ref.shape)
    grad_e = dot(second_ref[...], pre_s[...], TN).astype(BF16)
    for k in range(slices):
        for j in range(per):
            @pl.when(step == k * per + j)
            def _():
                if j == 0 and k >= 2:
                    movers[k - 2].sent_first()
                grad_s[k % 2, :, :, :, :, :, j * strip : (j + 1) * strip] = grad_e.reshape(grad_s.shape[1:-1] + (strip,))
                if j == per - 1:
                    movers[k].begin()

    @pl.when(step >= slices * per)
    def _():
        rest_e_ref[...] = grad_e.reshape(rest_e_ref.shape)

    def close(k):
        grad_e_ref[k * part : (k + 1) * part, :] = movers[k].stage_third()

    final = hidden_steps - 1
    late = []
    for k in range(slices):
        for number, action in enumerate((movers[k].stage_core, movers[k].stage_first, movers[k].stage_second, functools.partial(close, k))):
            when = (k + 1) * per + number
            if when > final:
                late.append((when, -k, action))
            else:
                pl.when(step == when)(action)

    @pl.when(step == final)
    def _():
        for _, _, action in sorted(late, key=lambda entry: entry[:2]):
            action()
        for k in range(max(0, slices - 2), slices):
            movers[k].sent_first()
        for k in range(slices):
            movers[k].sent_last()


def mixing(devices, second, above, gathered, bias_e, bias_r, part):
    rows, width = second.shape
    hidden = bias_e.shape[1]
    many = hidden // devices
    sides = hidden // width
    strip = STRIP
    per = width // strip
    outer, side, core = digits(devices)
    fixed = pl.BlockSpec((rows, width), lambda i: (0, 0), pipeline_mode=pl.Buffered(1))
    whole = pl.BlockSpec(memory_space=pltpu.VMEM)
    scratch = [pltpu.VMEM((rows, strip), BF16)] * 2 + [pltpu.VMEM((2, outer, side, side, core, part, width), BF16)]
    slices = sides - 1
    for k in range(slices):
        scratch += boxes_for(devices, part, width)
    return pl.pallas_call(
        functools.partial(mixing_kernel, devices, hidden // strip),
        grid=(hidden // strip,),
        in_specs=[
            fixed, fixed,
            pl.BlockSpec((devices, part, strip), lambda i: (0, many // part + 1 + i // per, i % per)),
            pl.BlockSpec((strip // many, many, width), lambda i: (i, 0, 0)),
            pl.BlockSpec((1, strip), lambda i: (0, i)),
            pl.BlockSpec((1, width), lambda i: (0, 0)),
        ],
        out_specs=[
            fixed,
            fixed,
            pl.BlockSpec((strip // many, many, width), lambda i: (i, 0, 0)),
            pl.BlockSpec((1, strip), lambda i: (0, i)),
            pl.BlockSpec((slices * part, width), lambda i: (0, 0)),
            pl.BlockSpec((devices, part, strip), lambda i: (0, 0, jnp.maximum(i - slices * per, 0))),
            pl.BlockSpec((1, width), lambda i: (0, 0)),
        ],
        out_shape=[
            jax.ShapeDtypeStruct((rows, width), F32),
            jax.ShapeDtypeStruct((rows, width), F32),
            jax.ShapeDtypeStruct((devices, many, width), BF16),
            jax.ShapeDtypeStruct((1, hidden), F32),
            jax.ShapeDtypeStruct((slices * part, width), F32),
            jax.ShapeDtypeStruct((devices, part, width), BF16),
            jax.ShapeDtypeStruct((1, width), F32),
        ],
        scratch_shapes=scratch + sems_for(devices, slices),
        compiler_params=pltpu.CompilerParams(collective_id=3, has_side_effects=True, vmem_limit_bytes=57 << 20),
        name="mixing",
    )(second, above, gathered, gathered, bias_e, bias_r)


def turn_kernel(
    devices, grad_r_ref, grad_e_ref, out_one_ref, d_second_ref, mixed_ref, two_ref, above_ref, combined_ref, live_ref, gain_ref, w_o_ref,
    bias_r_ref, bias_e_ref,
    wide_ref, grad_one_ref, one_ref, res_two_ref, grad_o_ref, small_ref, part_e_ref, part_r_ref,
    attend_s, load_sem, halo_sem, *rest,
):
    slots, width = two_ref.shape
    half = slots // 2
    tile = 256
    part = part_e_ref.shape[0]
    where = neighbours(devices)
    (o, p, q, c), *_ = where
    me = lax.axis_index("fsdp")
    owns, rest = rest[:2], rest[2:]
    sems = rest[-4:]

    def distant(source, row, rows, k):
        at = pl.ds(row, rows)

        def other():
            return source.at[:, :, :, 1 - c, at, :]

        def mine(spot, cols):
            return owns[k].at[tuple(spot) + (slice(None), cols)]

        def load():
            return pltpu.make_async_copy(source.at[:, :, :, c, at, :], owns[k], load_sem.at[k])

        return Scatter(devices, where, k, rest[5 * k : 5 * k + 5], sems, other, mine, load)

    movers = [distant(grad_e_ref, 0, part, 0), distant(grad_r_ref, 0, part_r_ref.shape[0], 1)]
    last = devices - 1
    left, right = lax.rem(me + last, devices), lax.rem(me + 1, devices)
    greet(peers_of(where) + [left, right])
    for mover in movers:
        mover.begin()

    def to_left():
        return remote(wide_ref.at[half : 2 * half], wide_ref.at[half + slots :], halo_sem, (0,), left)

    def to_right():
        return remote(wide_ref.at[2 * half : 3 * half], wide_ref.at[:half], halo_sem, (1,), right)

    small_ref[...] = jnp.zeros(small_ref.shape, F32)
    gain = gain_ref[...]

    def norm_tile(i, carry):
        at = pl.ds(pl.multiple_of(i * tile, tile), tile)
        live = live_ref[at, :]
        values = out_one_ref[at, :]
        above = d_second_ref[at, :]
        center = values - jnp.mean(values, axis=1, keepdims=True)
        scale = lax.rsqrt(jnp.mean(center * center, axis=1, keepdims=True) + EPS_NORM)
        center = center * scale
        small_ref[2:3, :] += jnp.sum(above * center, axis=0, keepdims=True)
        small_ref[3:4, :] += jnp.sum(above, axis=0, keepdims=True)
        above = above * gain
        mean = jnp.mean(above, axis=1, keepdims=True)
        along = jnp.mean(above * center, axis=1, keepdims=True)
        total = live * (above_ref[at, :].astype(F32) + scale * (above - mean - center * along))
        low = total.astype(BF16)
        grad_one_ref[at, :] = low
        attend_s[at, :] = low
        small_ref[4:5, :] += jnp.sum(low.astype(F32), axis=0, keepdims=True)
        wide_ref[pl.ds(pl.multiple_of(half + i * tile, tile), tile), :] = dot(low, w_o_ref[...], NT).astype(BF16)
        return carry

    lax.fori_loop(0, half // tile, norm_tile, 0)

    @pl.when(me > 0)
    def _():
        to_left().start()

    movers[0].stage_core()
    lax.fori_loop(half // tile, slots // tile, norm_tile, 0)

    @pl.when(me < last)
    def _():
        to_right().start()

    movers[1].stage_core()

    def finish_tile(i, carry):
        at = pl.ds(pl.multiple_of(i * tile, tile), tile)
        live = live_ref[at, :]
        one_ref[at, :] = (live * out_one_ref[at, :]).astype(BF16)
        res_two_ref[at, :] = (live * (two_ref[at, :].astype(F32) + mixed_ref[at, :])).astype(BF16)
        return carry

    lax.fori_loop(0, slots // tile, finish_tile, 0)
    movers[0].stage_first()

    def weights(i, carry):
        cols = pl.ds(pl.multiple_of(i * tile, tile), tile)
        many = tile // part
        grad_o_ref[pl.ds(pl.multiple_of(i * many, many), many)] = (
            dot(combined_ref[:, cols], attend_s[...], TN).astype(BF16).reshape(many, part, width)
        )
        return carry

    lax.fori_loop(0, width // tile, weights, 0)
    movers[1].stage_first()
    movers[0].stage_second()
    small_ref[5:6, :] = bias_r_ref[...]
    for k in range(bias_e_ref.shape[1] // width):
        small_ref[6 + k : 7 + k, :] = bias_e_ref[:, k * width : (k + 1) * width]
    movers[1].stage_second()
    part_e_ref[...] = movers[0].stage_third()
    part_r_ref[...] = movers[1].stage_third()

    @pl.when(me > 0)
    def _():
        to_right().wait_recv()
        to_left().wait_send()

    @pl.when(me == 0)
    def _():
        wide_ref[:half] = jnp.zeros((half, width), BF16)

    @pl.when(me < last)
    def _():
        to_left().wait_recv()
        to_right().wait_send()

    @pl.when(me == last)
    def _():
        wide_ref[half + slots :] = jnp.zeros((half, width), BF16)

    for mover in movers:
        mover.sent_first()
        mover.sent_last()


def turn(devices, grad_r, grad_e, out_one, d_second, mixed, two, above, combined, live, gain, w_o, bias_r, bias_e):
    slots, width = two.shape
    outer, side, core = digits(devices)
    part, many = grad_e.shape[1], grad_r.shape[1]
    vmem = pl.BlockSpec(memory_space=pltpu.VMEM)
    anywhere = pl.BlockSpec(memory_space=pl.ANY)
    dma = pltpu.SemaphoreType.DMA
    sizes = [part, many // 2]
    scratch = [pltpu.VMEM((slots, width), BF16), dma((2,)), dma((2, 2))]
    scratch += [pltpu.VMEM((outer, side, side, rows, width), BF16) for rows in sizes]
    for rows in sizes:
        scratch += boxes_for(devices, rows, width)
    shape = (outer, side, side, core)
    rows_low = jax.ShapeDtypeStruct((slots, width), BF16)
    return pl.pallas_call(
        functools.partial(turn_kernel, devices),
        in_specs=[anywhere, anywhere] + [vmem] * 11,
        out_specs=(vmem,) * 8,
        out_shape=(
            jax.ShapeDtypeStruct((2 * slots, width), BF16), rows_low, rows_low, rows_low,
            jax.ShapeDtypeStruct((devices, part, width), BF16),
            jax.ShapeDtypeStruct((16, width), F32),
            jax.ShapeDtypeStruct((part, width), F32),
            jax.ShapeDtypeStruct((many // 2, width), F32),
        ),
        scratch_shapes=scratch + sems_for(devices, len(sizes)),
        compiler_params=pltpu.CompilerParams(collective_id=5, has_side_effects=True, vmem_limit_bytes=57 << 20),
        name="turn",
    )(
        grad_r.reshape(shape + grad_r.shape[1:]), grad_e.reshape(shape + grad_e.shape[1:]),
        out_one, d_second, mixed, two, above, combined, live, gain, w_o, bias_r, bias_e,
    )


def tail_kernel(
    devices, grad_r_ref, grad_o_ref, d_shared_ref, d_value_ref, normed_ref, head_ref, own_ref, end_ref, above_ref, live_ref,
    gain_ref, w_s_ref, w_v_ref, small_ref,
    back_ref, out_s_ref, out_v_ref, out_o_ref, out_r_ref, thin_ref, long_ref,
    side_s, side_in, vector_s, vector_in, grad_s, load_sem, halo_sem, vector_sem, *rest,
):
    window, width = normed_ref.shape
    slots = own_ref.shape[0]
    half = slots // 2
    part = out_s_ref.shape[0]
    many = 2 * out_r_ref.shape[0]
    tile = 256
    where = neighbours(devices)
    (o, p, q, c), core_peer, q_peers, p_peers, o_peers = where
    me = lax.axis_index("fsdp")
    outer, side, core = digits(devices)
    owns, rest = rest[:2], rest[2:]
    sems = rest[-4:]

    def distant(source, row, rows, k):
        at = pl.ds(row, rows)

        def other():
            return source.at[:, :, :, 1 - c, at, :]

        def mine(spot, cols):
            return owns[k].at[tuple(spot) + (slice(None), cols)]

        def load():
            return pltpu.make_async_copy(source.at[:, :, :, c, at, :], owns[k], load_sem.at[k])

        return Scatter(devices, where, k, rest[5 * k : 5 * k + 5], sems, other, mine, load)

    def near(j, k):
        def other():
            return grad_s.at[j, :, :, :, 1 - c]

        def mine(spot, cols):
            return grad_s.at[(j,) + tuple(spot) + (c, slice(None), cols)]

        return Scatter(devices, where, k, rest[5 * k : 5 * k + 5], sems, other, mine)

    movers = [
        distant(grad_r_ref, many // 2, many // 2, 0), distant(grad_o_ref, 0, part, 1), near(0, 2), near(1, 3),
    ]
    last = devices - 1
    left, right = lax.rem(me + last, devices), lax.rem(me + 1, devices)
    greet(peers_of(where) + [left, right])
    for k in range(2):
        movers[k].begin()

    def to_left():
        return remote(side_s.at[0], side_in.at[1], halo_sem, (0,), left)

    def to_right():
        return remote(side_s.at[1], side_in.at[0], halo_sem, (1,), right)

    vector_s[...] = small_ref[...]
    gain = gain_ref[...]

    def norm_tile(ref, row, at):
        values = ref[pl.ds(row, tile), :].astype(F32)
        above = dot(d_shared_ref[at, :], w_s_ref[...], NT) + dot(d_value_ref[at, :], w_v_ref[...], NT)
        center = values - jnp.mean(values, axis=1, keepdims=True)
        scale = lax.rsqrt(jnp.mean(center * center, axis=1, keepdims=True) + EPS_NORM)
        center = center * scale
        vector_s[0:1, :] += jnp.sum(above * center, axis=0, keepdims=True)
        vector_s[1:2, :] += jnp.sum(above, axis=0, keepdims=True)
        above = above * gain
        mean = jnp.mean(above, axis=1, keepdims=True)
        along = jnp.mean(above * center, axis=1, keepdims=True)
        return scale * (above - mean - center * along)

    def side_tiles(i, carry):
        row = pl.multiple_of(i * tile, tile)
        side_s[0, pl.ds(row, tile), :] = norm_tile(head_ref, row, pl.ds(row, tile)).astype(BF16)
        at = pl.ds(pl.multiple_of(half + slots + i * tile, tile), tile)
        side_s[1, pl.ds(row, tile), :] = norm_tile(end_ref, row, at).astype(BF16)
        return carry

    lax.fori_loop(0, half // tile, side_tiles, 0)

    @pl.when(me > 0)
    def _():
        to_left().start()

    @pl.when(me < last)
    def _():
        to_right().start()

    movers[0].stage_core()

    def weights(j, ref):
        wide = tile // part

        def strip(i, carry):
            cols = pl.ds(pl.multiple_of(i * tile, tile), tile)
            block = dot(normed_ref[:, cols], ref[...], TN).astype(BF16).reshape(wide // core, core, part, width)
            for k in range(wide // core):
                index = i * (wide // core) + k
                spot = (lax.div(index, side * side), lax.rem(lax.div(index, side), side), lax.rem(index, side))
                grad_s[(j,) + spot] = block[k]
            return carry

        lax.fori_loop(0, width // tile, strip, 0)

    weights(0, d_shared_ref)
    movers[2].begin()
    movers[1].stage_core()
    movers[0].stage_first()
    weights(1, d_value_ref)
    movers[3].begin()
    movers[1].stage_first()
    movers[0].stage_second()
    movers[2].stage_core()

    def own_tiles(i, carry):
        row = pl.multiple_of(i * tile, tile)
        at = pl.ds(pl.multiple_of(half + i * tile, tile), tile)
        here = pl.ds(row, tile)
        total = above_ref[here, :].astype(F32) + norm_tile(own_ref, row, at)
        back_ref[here, :] = (live_ref[here, :] * total).astype(BF16)
        return carry

    lax.fori_loop(0, slots // tile, own_tiles, 0)

    def vector_copies(stage):
        group = ([(0, core_peer)], q_peers, p_peers, o_peers)[stage]
        base = (0, 1, side, 2 * side - 1)[stage]
        return [
            remote(vector_s if stage == 0 else vector_in.at[base - 1], vector_in.at[base + d], vector_sem, (base + d,), device)
            for d, (_, device) in enumerate(group)
        ]

    def vector_stage(stage):
        base = (0, 1, side, 2 * side - 1)[stage]
        copies = vector_copies(stage)
        total = vector_s[...] if stage == 0 else vector_in[base - 1]
        for d, copy in enumerate(copies):
            copy.wait_recv()
            total = total + vector_in[base + d]
        vector_in[base + len(copies) - 1] = total

    for copy in vector_copies(0):
        copy.start()
    movers[3].stage_core()
    movers[1].stage_second()
    out_r_ref[...] = movers[0].stage_third()
    movers[2].stage_first()
    vector_stage(0)
    for copy in vector_copies(1):
        copy.start()
    movers[3].stage_first()
    out_o_ref[...] = movers[1].stage_third()
    movers[2].stage_second()
    vector_stage(1)
    for copy in vector_copies(2):
        copy.start()
    movers[3].stage_second()
    vector_stage(2)
    for copy in vector_copies(3):
        copy.start()

    @pl.when(me > 0)
    def _():
        to_right().wait_recv()

    @pl.when(me == 0)
    def _():
        side_in[0] = jnp.zeros((half, width), BF16)

    @pl.when(me < last)
    def _():
        to_left().wait_recv()

    @pl.when(me == last)
    def _():
        side_in[1] = jnp.zeros((half, width), BF16)

    for k in range(2):
        at = slice(k * half, (k + 1) * half)
        back_ref[at, :] = (back_ref[at, :].astype(F32) + side_in[k].astype(F32)).astype(BF16)
    out_s_ref[...] = movers[2].stage_third()
    vector_stage(3)
    out_v_ref[...] = movers[3].stage_third()
    vectors = 2 * side + outer - 3
    total = vector_in[vectors]
    thin_ref[...] = pltpu.roll(total, lax.rem(width - me * part, width), 1)[:, :DH]
    each = long_ref.shape[1]
    long_rows = [total[6 + k : 7 + k, :] for k in range(devices * each // width)]
    mine = lax.div(me * each, width)
    chosen = long_rows[0]
    for k in range(1, len(long_rows)):
        chosen = jnp.where(mine == k, long_rows[k], chosen)
    long_ref[...] = pltpu.roll(chosen, lax.rem(width - lax.rem(me * each, width), width), 1)[:, :each]
    for stage in range(4):
        for copy in vector_copies(stage):
            copy.wait_send()

    @pl.when(me > 0)
    def _():
        to_left().wait_send()

    @pl.when(me < last)
    def _():
        to_right().wait_send()

    for mover in movers:
        mover.sent_first()
        mover.sent_last()


def tail(devices, grad_r, grad_o, d_shared, d_values, normed, head, own, end, above, live, gain, w_s, w_v, small):
    window, width = normed.shape
    slots = own.shape[0]
    outer, side, core = digits(devices)
    part, many = grad_o.shape[1], grad_r.shape[1]
    each = many
    vmem = pl.BlockSpec(memory_space=pltpu.VMEM)
    anywhere = pl.BlockSpec(memory_space=pl.ANY)
    dma = pltpu.SemaphoreType.DMA
    sizes = [many // 2, part, part, part]
    scratch = [
        pltpu.VMEM((2, slots // 2, width), BF16), pltpu.VMEM((2, slots // 2, width), BF16),
        pltpu.VMEM((16, width), F32), pltpu.VMEM((2 * side + outer - 2, 16, width), F32),
        pltpu.VMEM((2, outer, side, side, core, part, width), BF16),
        dma((2,)), dma((2, 2)), dma((2, 2 * side + outer - 2)),
    ]
    scratch += [pltpu.VMEM((outer, side, side, rows, width), BF16) for rows in sizes[:2]]
    for rows in sizes:
        scratch += boxes_for(devices, rows, width)
    shape = (outer, side, side, core)
    return pl.pallas_call(
        functools.partial(tail_kernel, devices),
        in_specs=[anywhere, anywhere] + [vmem] * 12,
        out_specs=(vmem,) * 7,
        out_shape=(
            jax.ShapeDtypeStruct((slots, width), BF16),
            jax.ShapeDtypeStruct((part, width), F32),
            jax.ShapeDtypeStruct((part, width), F32),
            jax.ShapeDtypeStruct((part, width), F32),
            jax.ShapeDtypeStruct((many // 2, width), F32),
            jax.ShapeDtypeStruct((16, DH), F32),
            jax.ShapeDtypeStruct((1, each), F32),
        ),
        scratch_shapes=scratch + sems_for(devices, len(sizes)),
        compiler_params=pltpu.CompilerParams(collective_id=4, has_side_effects=True, vmem_limit_bytes=57 << 20),
        name="tail",
    )(
        grad_r.reshape(shape + grad_r.shape[1:]), grad_o.reshape(shape + grad_o.shape[1:]),
        d_shared, d_values, normed, head, own, end, above, live, gain, w_s, w_v, small,
    )


def rank_kernel(length_ref, target_ref, bucket_ref, block_ref, info_ref, before_s):
    devices = length_ref.shape[0]
    lists, slots = bucket_ref.shape
    me = lax.axis_index("fsdp")
    base = me * slots
    window = 2 * slots

    def look(s, carry):
        start, mine, found, one, two = carry
        size = length_ref[s]
        target = target_ref[s]
        middle = start + lax.shift_right_logical(size, 1)
        inside = (middle >= base) & (middle < base + slots)
        offset = start - base + slots // 2
        entry = (offset, offset + size, target)
        first, second = inside & (found == 0), inside & (found == 1)
        one = tuple(jnp.where(first, new, old) for new, old in zip(entry, one))
        two = tuple(jnp.where(second, new, old) for new, old in zip(entry, two))
        return start + size, jnp.where(target == me, size, mine), found + inside.astype(jnp.int32), one, two

    zero = jnp.int32(0)
    nothing = (jnp.int32(window), jnp.int32(window), zero)
    total, mine, found, one, two = lax.fori_loop(0, devices, look, (zero, zero, zero, nothing, nothing))
    for k, value in enumerate((one[0], one[1], two[0], two[1], one[2], two[2], total, found)):
        info_ref[k] = value

    def fill(i, carry):
        at = pl.ds(pl.multiple_of(i * DH, DH), DH)
        first = lax.broadcasted_iota(jnp.int32, (DH, slots), 0) + i * DH
        second = lax.broadcasted_iota(jnp.int32, (DH, slots), 1)
        before_s[at, :] = jnp.where(first < second, 1.0, 0.0).astype(BF16)
        return carry

    lax.fori_loop(0, slots // DH, fill, 0)
    left = lax.broadcasted_iota(jnp.int32, (DH, DH), 0)
    right = lax.broadcasted_iota(jnp.int32, (DH, DH), 1)
    smaller = jnp.where((left // BUCKETS == right // BUCKETS) & (right < left), 1.0, 0.0).astype(BF16)
    many = DH // BUCKETS
    bucket = lax.broadcasted_iota(jnp.int32, (many, BUCKETS, slots), 1)
    live = lax.broadcasted_iota(jnp.int32, (many, BUCKETS, slots), 2) < mine
    ranks = []
    for g in range(lists // many):
        here = (jnp.broadcast_to(bucket_ref[g * many : (g + 1) * many, :][:, None, :], bucket.shape) == bucket) & live
        one_hot = jnp.where(here, 1.0, 0.0)
        flat = one_hot.reshape(DH, slots).astype(BF16)
        offset = jnp.sum(dot(smaller, flat), axis=1, keepdims=True)
        place = (dot(flat, before_s[...]) + offset).reshape(many, BUCKETS, slots)
        ranks.append(jnp.sum(one_hot * place, axis=1))
    rank = jnp.concatenate(ranks, axis=0)
    live = lax.broadcasted_iota(jnp.int32, (lists, slots), 1) < mine
    block_ref[...] = jnp.where(live, jnp.floor(rank * (1.0 / GROUP)), FREE).astype(BF16)


def rank_blocks(lengths, destination, buckets):
    lists, slots = buckets.shape
    smem = pl.BlockSpec(memory_space=pltpu.SMEM)
    vmem = pl.BlockSpec(memory_space=pltpu.VMEM)
    return pl.pallas_call(
        rank_kernel,
        in_specs=[smem, smem, vmem],
        out_specs=[vmem, smem],
        out_shape=[jax.ShapeDtypeStruct((lists, slots), BF16), jax.ShapeDtypeStruct((8,), jnp.int32)],
        scratch_shapes=[pltpu.VMEM((slots, slots), BF16)],
        compiler_params=pltpu.CompilerParams(vmem_limit_bytes=32 << 20),
        name="rank_blocks",
    )(lengths, destination, buckets)


def project_kernel(
    info_ref, head_ref, own_ref, tail_ref, gain_ref, shift_ref, w_s_ref, w_v_ref, one_ref, two_ref,
    normed_ref, shared_ref, value_ref, code_ref,
):
    i = pl.program_id(0)
    tile = own_ref.shape[0]
    steps = pl.num_programs(0)

    def go(ref):
        normed = layer_norm(ref[...].astype(F32), gain_ref[...], shift_ref[...]).astype(BF16)
        normed_ref[...] = normed
        shared_ref[...] = dot(normed, w_s_ref[...]).astype(BF16)
        value_ref[...] = dot(normed, w_v_ref[...]).astype(BF16)

    @pl.when(i < steps // 4)
    def _():
        go(head_ref)

    @pl.when((i >= steps // 4) & (i < steps - steps // 4))
    def _():
        go(own_ref)

    @pl.when(i >= steps - steps // 4)
    def _():
        go(tail_ref)

    @pl.when(i == 0)
    def _():
        lists, window = code_ref.shape
        lane = lax.broadcasted_iota(jnp.int32, (lists, window), 1)
        code = jnp.full((lists, window), FREE, F32)
        for k, ref in enumerate((one_ref, two_ref)):
            begin, end = info_ref[2 * k], info_ref[2 * k + 1]
            rows = ref[0].astype(F32)
            moved = pltpu.roll(jnp.concatenate([rows, rows], axis=1), lax.rem(begin, window), 1)
            code = jnp.where((lane >= begin) & (lane < end), moved + 32.0 * k, code)
        code_ref[...] = code.astype(BF16)


def project(info, head, own, tail, gain, shift, w_s, w_v, blocks):
    slots, width = own.shape
    window = 2 * slots
    lists = ROUNDS * HEADS
    tile = 256
    steps = window // tile
    quarter = steps // 4
    rows = pl.BlockSpec((tile, width), lambda i, info: (i, 0))
    vector = pl.BlockSpec((1, width), lambda i, info: (0, 0))
    matrix = pl.BlockSpec((width, width), lambda i, info: (0, 0), pipeline_mode=pl.Buffered(1))
    wide = jax.ShapeDtypeStruct((window, width), BF16)
    return pl.pallas_call(
        project_kernel,
        grid_spec=pltpu.PrefetchScalarGridSpec(
            num_scalar_prefetch=1,
            grid=(steps,),
            in_specs=[
                pl.BlockSpec((tile, width), lambda i, info: (jnp.minimum(i, quarter - 1), 0)),
                pl.BlockSpec((tile, width), lambda i, info: (jnp.clip(i - quarter, 0, 2 * quarter - 1), 0)),
                pl.BlockSpec((tile, width), lambda i, info: (jnp.clip(i - 3 * quarter, 0, quarter - 1), 0)),
                vector, vector, matrix, matrix,
                pl.BlockSpec((1, lists, slots), lambda i, info: (info[4], 0, 0)),
                pl.BlockSpec((1, lists, slots), lambda i, info: (info[5], 0, 0)),
            ],
            out_specs=[rows, rows, rows, pl.BlockSpec((lists, window), lambda i, info: (0, 0))],
        ),
        out_shape=[wide, wide, wide, jax.ShapeDtypeStruct((lists, window), BF16)],
        compiler_params=pltpu.CompilerParams(vmem_limit_bytes=40 << 20),
        name="project",
    )(info, head, own, tail, gain, shift, w_s, w_v, blocks, blocks)


def gather_kernel(devices, arrays, *refs):
    sources, outs = refs[:arrays], refs[arrays : 2 * arrays]
    own_sem, sem_o, sem_a, sem_b, sem_c = refs[2 * arrays :]
    outer, side, core = digits(devices)
    (o, p, q, c), core_peer, q_peers, p_peers, o_peers = neighbours(devices)
    greet([core_peer] + [d for _, d in q_peers] + [d for _, d in p_peers] + [d for _, d in o_peers])
    half = sources[0].shape[-1] // 2
    columns = (pl.ds(0, half), pl.ds(half, half))

    def remote(src, dst, sems, slot, device):
        return pltpu.make_async_remote_copy(
            src_ref=src, dst_ref=dst, send_sem=sems.at[(0,) + slot], recv_sem=sems.at[(1,) + slot],
            device_id=(device,), device_id_type=MESH,
        )

    copies, locals_, begun, first, second, last = [], [], {}, {}, {}, {}
    for s in range(arrays):
        locals_.append(pltpu.make_async_copy(sources[s], outs[s].at[o, p, q, c], own_sem.at[s]))
        locals_[s].start()
        for d, (k, device) in enumerate(o_peers):
            begun[s, d] = remote(sources[s], outs[s].at[o, p, q, c], sem_o, (s, d), device)
            begun[s, d].start()

    def stage_a(s):
        locals_[s].wait()
        for d in range(outer - 1):
            begun[s, d].wait_recv()
        for h, peers in enumerate((q_peers, p_peers)):
            piece = outs[s].at[:, p, q, c, :, columns[h]]
            for d, (k, device) in enumerate(peers):
                first[s, h, d] = remote(piece, piece, sem_a, (s, h, d), device)
                first[s, h, d].start()

    def stage_b(s):
        for h, peers in enumerate((p_peers, q_peers)):
            for d in range(side - 1):
                first[s, h, d].wait_recv()
            piece = outs[s].at[:, p, :, c, :, columns[h]] if h == 0 else outs[s].at[:, :, q, c, :, columns[h]]
            for d, (k, device) in enumerate(peers):
                second[s, h, d] = remote(piece, piece, sem_b, (s, h, d), device)
                second[s, h, d].start()

    def stage_c(s):
        for h in range(2):
            for d in range(side - 1):
                second[s, h, d].wait_recv()
        piece = outs[s].at[:, :, :, c]
        last[s] = remote(piece, piece, sem_c, (s,), core_peer)
        last[s].start()

    for t in range(arrays + 2):
        if t < arrays:
            stage_a(t)
        if 0 <= t - 1 < arrays:
            stage_b(t - 1)
        if 0 <= t - 2 < arrays:
            stage_c(t - 2)
    for s in range(arrays):
        last[s].wait_recv()
    for group in (begun, first, second, last):
        for copy in group.values():
            copy.wait_send()


def gather(devices, arrays):
    outer, side, core = digits(devices)
    count = len(arrays)
    dma = pltpu.SemaphoreType.DMA
    anywhere = pl.BlockSpec(memory_space=pl.ANY)
    outs = pl.pallas_call(
        functools.partial(gather_kernel, devices, count),
        out_shape=tuple(jax.ShapeDtypeStruct((outer, side, side, core) + array.shape, array.dtype) for array in arrays),
        in_specs=[anywhere] * count,
        out_specs=(anywhere,) * count,
        scratch_shapes=[
            dma((count,)), dma((2, count, outer - 1)), dma((2, count, 2, side - 1)), dma((2, count, 2, side - 1)), dma((2, count))
        ],
        compiler_params=pltpu.CompilerParams(collective_id=2, has_side_effects=True),
        name="gather",
    )(*arrays)
    return [out.reshape((devices,) + array.shape) for out, array in zip(outs, arrays)]


def body(
    input_one, input_two, upstream_one, upstream_two, lengths, destination, buckets,
    w_shared, w_value, w_output, w_expand, w_reduce,
    gain_attend, shift_attend, gain_mixing, shift_mixing, bias_output, bias_expand, bias_reduce,
):
    devices = lax.axis_size("fsdp")
    me = lax.axis_index("fsdp")
    slots, width = input_one.shape
    half = slots // 2
    window = 2 * slots
    part = w_shared.shape[0]
    hidden = w_expand.shape[1]
    sides = hidden // width
    down = [(i, i - 1) for i in range(1, devices)]
    up = [(i, i + 1) for i in range(devices - 1)]

    def to_sides(head, tail):
        return lax.ppermute(tail, "fsdp", up), lax.ppermute(head, "fsdp", down)

    def narrow(wide):
        head, tail = to_sides(wide[:half], wide[half + slots :])
        return wide[half : half + slots], jnp.concatenate([head, tail], axis=0)

    base = me * slots
    lists = ROUNDS * HEADS
    block, info = rank_blocks(lengths, destination, buckets[0])
    spot = jnp.arange(width, dtype=jnp.int32)
    short = jnp.stack([gain_attend, shift_attend, gain_mixing, shift_mixing, bias_output, bias_reduce])
    short = jnp.where(spot // part == me, jnp.tile(short, (1, devices)), 0.0)
    many = hidden // devices
    long = jnp.tile(bias_expand, width // many)[None]
    long = jnp.where(spot[None] // many + (width // many) * jnp.arange(sides, dtype=jnp.int32)[:, None] == me, long, 0.0)
    vectors = jnp.concatenate([short, long], axis=0)
    high = lax.reduce_precision(vectors, 8, 7)
    count = vectors.shape[0]
    packed = jnp.concatenate(
        [block, high.astype(BF16), (vectors - high).astype(BF16), jnp.zeros((24 - 2 * count, width), BF16)], axis=0
    )
    second_gather = lax.all_gather(
        jnp.concatenate(
            [w_reduce, w_output] + [w_expand[:, k * width : (k + 1) * width] for k in range(sides)], axis=0
        ),
        "fsdp", axis=0, tiled=False,
    )
    full_shared, full_value, packed = gather(devices, [w_shared, w_value, packed])
    full_shared, full_value = full_shared.reshape(width, width), full_value.reshape(width, width)
    vectors = jnp.sum(packed[:, lists : lists + 2 * count].astype(F32), axis=0)
    vectors = vectors[:count] + vectors[count:]
    gain_a, shift_a, gain_m, shift_m, bias_o, bias_r = (vectors[k : k + 1] for k in range(6))
    bias_e = vectors[6:].reshape(1, hidden)
    full_output = second_gather[:, sides * part : (sides + 1) * part].reshape(width, width)
    lane = jnp.arange(HEADS * DH, dtype=jnp.int32)
    row = jnp.arange(lists, dtype=jnp.int32)[:, None]
    spread = (row == ((lane % 64) // 16) * HEADS + lane // DH).astype(BF16)

    live = ((base + jnp.arange(slots, dtype=jnp.int32)) < info[6]).astype(F32)[:, None]
    slot_one = input_one.astype(F32)
    slot_two = input_two.astype(F32)
    two_head, two_tail = to_sides(input_two[:half], input_two[half:])
    normed, shared, values, code = project(
        info, two_head, input_two, two_tail, gain_a, shift_a, full_shared, full_value, packed
    )
    combined_window, lse, lone = attend(info, shared, values, code, spread)
    own, other = narrow(combined_window)
    combined = own + other
    attended = dot(combined, full_output) + bias_o
    out_one = slot_one + live * attended
    second = layer_norm(out_one, gain_m, shift_m).astype(BF16)
    d_reduce = (live * upstream_two.astype(F32)).astype(BF16)
    mixed, d_second, grad_reduce, grad_bias_expand, grad_expand, last_expand, grad_bias_reduce = mixing(
        devices, second, d_reduce, second_gather, bias_e, bias_r, part
    )
    d_combined, grad_one, result_one, result_two, grad_output, small, last_expand, first_reduce = turn(
        devices, grad_reduce, last_expand, out_one, d_second, mixed, input_two, upstream_one, combined, live, gain_m,
        full_output, grad_bias_reduce, grad_bias_expand,
    )
    d_shared, d_values = attend_back(
        info, shared, values, code, spread, combined_window, d_combined, lse, lone
    )
    grad_two, grad_shared, grad_value, grad_output, grad_reduce, thin, long = tail(
        devices, grad_reduce, grad_output, d_shared, d_values, normed,
        two_head, input_two, two_tail, upstream_two, live, gain_a, full_shared, full_value, small,
    )
    return (
        result_one,
        result_two,
        grad_one,
        grad_two,
        grad_shared,
        grad_value,
        grad_output,
        jnp.concatenate([grad_expand[k * part : (k + 1) * part] for k in range(sides - 1)] + [last_expand], axis=1),
        jnp.concatenate([first_reduce, grad_reduce], axis=0),
        thin[0, :part],
        thin[1, :part],
        thin[2, :part],
        thin[3, :part],
        thin[4, :part],
        long.reshape(-1),
        thin[5, :part],
    )


def solution(mesh):
    rows, flat, whole = P("fsdp", None), P("fsdp"), P()
    return jax.shard_map(
        body,
        mesh=mesh,
        in_specs=(rows,) * 4 + (whole, whole, P("fsdp", None, None)) + (rows,) * 5 + (flat,) * 7,
        out_specs=(rows,) * 9 + (flat,) * 7,
        check_vma=False,
    )
```

```python
import functools
import math

import jax
import jax.numpy as jnp
from jax import lax
from jax.experimental import pallas as pl
from jax.experimental.pallas import tpu as pltpu
from jax.sharding import PartitionSpec as P

HEADS = 8
DH = 128
GROUP = 64
ROUNDS = 4
BUCKETS = 32
EPS_NORM = 1e-05
EPS_UNIT = 1e-06
LOG2E = math.log2(math.e)
SELF2 = -100000.0 * LOG2E
NEG = -1e30
SCALE = 1.0 / math.sqrt(DH)
TILE = 512
HALF = TILE // 2
STEP = 128.0
SHIFT = 1.5 * 2.0**30
TAME = 3000.0
PAIR = 2
FREE = 99.0
STRIP = 512
CURVE = math.sqrt(2.0 / math.pi)
MESH = pl.DeviceIdType.MESH

NT = (((1,), (1,)), ((), ()))
NN = (((1,), (0,)), ((), ()))
TN = (((0,), (0,)), ((), ()))
F32 = jnp.float32
BF16 = jnp.bfloat16


def dot(a, b, dims=NN):
    return lax.dot_general(a, b, dims, preferred_element_type=F32)


def layer_norm(values, gain, shift):
    center = values - jnp.mean(values, axis=-1, keepdims=True)
    spread = jnp.mean(center * center, axis=-1, keepdims=True)
    return center * lax.rsqrt(spread + EPS_NORM) * gain + shift


def norm_back(values, gain, shift, upstream):
    outcome, pullback = jax.vjp(layer_norm, values, gain, shift)
    return pullback(upstream)


def prepare(q, code_ref, spread, ask_s, key_s, h, at):
    lane = lax.broadcasted_iota(jnp.int32, (TILE, DH), 1)
    target = ((lane // 64) * 32 + lane % 16).astype(F32)
    wide = q.astype(F32)
    square = jnp.sum(wide * wide, axis=1, keepdims=True)
    code = dot(code_ref[:, at], spread, TN)
    here = code == target
    ask_s[h, at, :DH] = q
    ask_s[h, at, DH:] = jnp.where(here, STEP, 0.0).astype(BF16)
    key_s[h, at, :DH] = (wide * (lax.rsqrt(square + EPS_UNIT) * (SCALE * LOG2E))).astype(BF16)
    key_s[h, at, DH:] = jnp.where(here | (code + 1.0 == target), 1.0, 0.0).astype(BF16)
    return jnp.max(square)


def lowest(info_ref, i):
    start, stop = i * TILE, (i + 1) * TILE
    one = (info_ref[0] < stop) & (info_ref[1] > start)
    two = (info_ref[2] < stop) & (info_ref[3] > start)
    begin = jnp.where(one, info_ref[0], jnp.where(two, info_ref[2], stop))
    return lax.div(begin, TILE)


def tile_rows(i):
    return pl.ds(pl.multiple_of(i * TILE, TILE), TILE)


def halves(i):
    start = i * TILE
    return [((0, pl.multiple_of(start, HALF), pl.multiple_of(start, HALF)), HALF),
            ((HALF, pl.multiple_of(start + HALF, HALF), pl.multiple_of(start, HALF)), TILE)]


def part_of(both):
    count = (both + SHIFT) - SHIFT
    return count, both - count


def apart(left, right):
    return dot(left[:, DH:], right[:, DH:], NT), dot(left[:, :DH], right[:, :DH], NT)


def attend_kernel(low_ref, q_ref, v_ref, code_ref, spread_ref, comb_ref, lse_ref, lone_ref, ask_s, key_s, more_s, acc_s, top_s):
    rows = q_ref.shape[0]
    tiles = rows // TILE
    heads = [slice(h * DH, (h + 1) * DH) for h in range(PAIR)]

    def ready(i, largest):
        def fill():
            most = jnp.float32(0.0)
            at = tile_rows(i)
            for h, cols in enumerate(heads):
                most = jnp.maximum(most, prepare(q_ref[at, cols], code_ref, spread_ref[:, cols], ask_s, key_s, h, at))
                more_s[h, at, :DH] = v_ref[at, cols]
                more_s[h, at, DH:] = jnp.ones((TILE, DH), BF16)
            return most

        return jnp.maximum(largest, lax.cond(lowest(low_ref, i) <= i, fill, lambda: jnp.float32(0.0)))

    largest = lax.fori_loop(0, tiles, ready, jnp.float32(0.0))
    tame = largest * (SCALE * LOG2E) ** 2 < TAME
    ask_at = lax.broadcasted_iota(jnp.int32, (TILE, TILE), 0)
    key_at = lax.broadcasted_iota(jnp.int32, (TILE, TILE), 1)

    def finish(h, cols, at, top):
        total = acc_s[h, :, DH:]
        some = total > 0.0
        safe = jnp.where(some, total, 1.0)
        inverse = jnp.where(some, 1.0 / safe, 0.0)
        comb_ref[at, cols] = (acc_s[h, :, :DH] * inverse).astype(BF16)
        lse_ref[h, :, at] = (jnp.log2(safe) + top).T[:1]

    def rows_of(i, carry):
        at = tile_rows(i)
        low = lowest(low_ref, i)

        @pl.when((low <= i) & tame)
        def _():
            for h in range(PAIR):
                acc_s[h] = jnp.zeros((TILE, 2 * DH), F32)

            def step(j, carry):
                keys = tile_rows(j)
                for h in range(PAIR):
                    count, score = part_of(dot(ask_s[h, at, :], key_s[h, keys, :], NT))
                    acc_s[h] += dot((count * jnp.exp2(score)).astype(BF16), more_s[h, keys, :])
                return carry

            lax.fori_loop(low, i, step, 0)
            for h, cols in enumerate(heads):
                for asks, span in halves(i):
                    here = pl.ds(asks[0], HALF)
                    there = pl.ds(asks[1], HALF)
                    keys = pl.ds(asks[2], span)
                    key_at = lax.broadcasted_iota(jnp.int32, (HALF, span), 1)
                    ask_at = lax.broadcasted_iota(jnp.int32, (HALF, span), 0) + (span - HALF)
                    count, score = part_of(dot(ask_s[h, there, :], key_s[h, keys, :], NT))
                    prob = jnp.where(key_at < ask_at, count * jnp.exp2(score), 0.0).astype(BF16)
                    acc_s[h, here, :] += dot(prob, more_s[h, keys, :])
                    active = jnp.max(jnp.where(key_at == ask_at, count, 0.0), axis=1, keepdims=True) > 0.0
                    lone = jnp.where(active & (acc_s[h, here, DH:] == 0.0), 1.0, 0.0)
                    acc_s[h, here, :DH] += lone * v_ref[there, cols].astype(F32)
                    acc_s[h, here, DH:] += lone
                    lone_ref[h, :, there] = lone.T[:1]
                finish(h, cols, at, 0.0)

        @pl.when((low <= i) & jnp.logical_not(tame))
        def _():
            for h, cols in enumerate(heads):
                count, score = apart(ask_s[h, at, :], key_s[h, at, :])
                score = jnp.where(key_at == ask_at, SELF2, score)
                score = jnp.where((key_at <= ask_at) & (count > 0.5), score, NEG)
                top = jnp.max(score, axis=1, keepdims=True)
                prob = count * jnp.exp2(score - top)
                acc_s[h] = dot(prob.astype(BF16), more_s[h, at, :])
                top_s[h] = jnp.broadcast_to(top, (TILE, DH))

                def step(j, carry):
                    keys = tile_rows(j)
                    count, score = apart(ask_s[h, at, :], key_s[h, keys, :])
                    score = jnp.where(count > 0.5, score, NEG)
                    top = top_s[h]
                    newer = jnp.maximum(top, jnp.max(score, axis=1, keepdims=True))
                    fade = jnp.exp2(top - newer)
                    prob = count * jnp.exp2(score - newer[:, :1])
                    acc_s[h] = acc_s[h] * jnp.concatenate([fade, fade], axis=1) + dot(prob.astype(BF16), more_s[h, keys, :])
                    top_s[h] = newer
                    return carry

                lax.fori_loop(low, i, step, 0)
                total = acc_s[h, :, DH:]
                own = STEP * ROUNDS * jnp.exp2(SELF2 - jnp.maximum(top_s[h], SELF2))
                lone_ref[h, :, at] = jnp.where(total > 0.0, own / jnp.where(total > 0.0, total, 1.0), 0.0).T[:1]
                finish(h, cols, at, top_s[h])

        @pl.when(low > i)
        def _():
            comb_ref[at, :] = jnp.zeros((TILE, PAIR * DH), BF16)
            for h in range(PAIR):
                lse_ref[h, :, at] = jnp.zeros((1, TILE), F32)
                lone_ref[h, :, at] = jnp.zeros((1, TILE), F32)

        return carry

    lax.fori_loop(0, tiles, rows_of, 0)


def back_kernel(
    low_ref, q_ref, v_ref, code_ref, spread_ref, comb_ref, above_ref, lse_ref, lone_ref,
    dq_ref, dv_ref, ask_s, key_s, dunit_s, dvalue_s, dask_s,
):
    rows = q_ref.shape[0]
    tiles = rows // TILE
    heads = [slice(h * DH, (h + 1) * DH) for h in range(PAIR)]

    def ready(i, largest):
        def fill():
            most = jnp.float32(0.0)
            at = tile_rows(i)
            for h, cols in enumerate(heads):
                most = jnp.maximum(most, prepare(q_ref[at, cols], code_ref, spread_ref[:, cols], ask_s, key_s, h, at))
                for total in (dunit_s, dvalue_s, dask_s):
                    total[h, at, :] = jnp.zeros((TILE, DH), F32)
            return most

        return jnp.maximum(largest, lax.cond(lowest(low_ref, i) <= i, fill, lambda: jnp.float32(0.0)))

    largest = lax.fori_loop(0, tiles, ready, jnp.float32(0.0))
    tame = largest * (SCALE * LOG2E) ** 2 < TAME

    def pass_over(i, low, split):
        at = tile_rows(i)
        deltas = []
        for h, cols in enumerate(heads):
            mixed = above_ref[at, cols].astype(F32) * comb_ref[at, cols].astype(F32)
            deltas.append(jnp.sum(mixed.T, axis=0, keepdims=True))

        def step(j, carry):
            keys = tile_rows(j)
            for h, cols in enumerate(heads):
                q, above, unit = q_ref[at, cols], above_ref[at, cols], key_s[h, keys, :DH]
                count, score = split(key_s[h, keys, :], ask_s[h, at, :])
                d_prob = dot(v_ref[keys, cols], above, NT)
                prob = count * jnp.exp2(score - lse_ref[h, :, at])
                d_score = (prob * (d_prob - carry[h])).astype(BF16)
                dvalue_s[h, keys, :] += dot(prob.astype(BF16), above)
                dunit_s[h, keys, :] += dot(d_score, q)
                dask_s[h, at, :] += dot(d_score, unit, TN)
            return carry

        deltas = lax.fori_loop(low, i, step, tuple(deltas))
        for h, cols in enumerate(heads):
            for asks, span in halves(i):
                there = pl.ds(asks[1], HALF)
                keys = pl.ds(asks[2], span)
                key_at = lax.broadcasted_iota(jnp.int32, (span, HALF), 0)
                ask_at = lax.broadcasted_iota(jnp.int32, (span, HALF), 1) + (span - HALF)
                q, above, unit = q_ref[there, cols], above_ref[there, cols], key_s[h, keys, :DH]
                count, score = split(key_s[h, keys, :], ask_s[h, there, :])
                d_prob = dot(v_ref[keys, cols], above, NT)
                prob = count * jnp.exp2(score - lse_ref[h, :, there])
                prob = jnp.where(key_at < ask_at, prob, 0.0)
                d_score = (prob * (d_prob - deltas[h][:, asks[0] : asks[0] + HALF])).astype(BF16)
                prob = jnp.where(key_at == ask_at, lone_ref[h, :, there], prob).astype(BF16)
                dvalue_s[h, keys, :] += dot(prob, above)
                dunit_s[h, keys, :] += dot(d_score, q)
                dask_s[h, there, :] += dot(d_score, unit, TN)

    def together(left, right):
        return part_of(dot(left, right, NT))

    def guarded(left, right):
        count, score = apart(left, right)
        return count, jnp.where(count > 0.5, score, NEG)

    def rows_of(i, carry):
        low = lowest(low_ref, i)

        @pl.when((low <= i) & tame)
        def _():
            pass_over(i, low, together)

        @pl.when((low <= i) & jnp.logical_not(tame))
        def _():
            pass_over(i, low, guarded)

        return carry

    lax.fori_loop(0, tiles, rows_of, 0)

    def close(i, carry):
        at = tile_rows(i)

        @pl.when(lowest(low_ref, i) <= i)
        def _():
            for h, cols in enumerate(heads):
                q = q_ref[at, cols].astype(F32)
                norm = lax.rsqrt(jnp.sum(q * q, axis=1, keepdims=True) + EPS_UNIT)
                d_unit = dunit_s[h, at, :] * SCALE
                along = jnp.sum(q * d_unit, axis=1, keepdims=True)
                d_q = dask_s[h, at, :] * (1.0 / LOG2E) + d_unit * norm - q * (norm * norm * norm * along)
                dq_ref[at, cols] = d_q.astype(BF16)
                dv_ref[at, cols] = dvalue_s[h, at, :].astype(BF16)

        @pl.when(lowest(low_ref, i) > i)
        def _():
            dq_ref[at, :] = jnp.zeros((TILE, PAIR * DH), BF16)
            dv_ref[at, :] = jnp.zeros((TILE, PAIR * DH), BF16)

        return carry

    lax.fori_loop(0, tiles, close, 0)


def head_specs(rows):
    by_head = pl.BlockSpec((rows, PAIR * DH), lambda h, low: (0, h))
    code = pl.BlockSpec((ROUNDS * HEADS, rows), lambda h, low: (0, 0))
    spread = pl.BlockSpec((ROUNDS * HEADS, PAIR * DH), lambda h, low: (0, h))
    stat = pl.BlockSpec((PAIR, 1, rows), lambda h, low: (h, 0, 0))
    return by_head, code, spread, stat


def attend(low, shared, values, code, spread):
    rows = shared.shape[0]
    by_head, code_spec, spread_spec, stat = head_specs(rows)
    wide = jax.ShapeDtypeStruct((rows, HEADS * DH), BF16)
    thin = jax.ShapeDtypeStruct((HEADS, 1, rows), F32)
    return pl.pallas_call(
        attend_kernel,
        grid_spec=pltpu.PrefetchScalarGridSpec(
            num_scalar_prefetch=1,
            grid=(HEADS // PAIR,),
            in_specs=[by_head, by_head, code_spec, spread_spec],
            out_specs=[by_head, stat, stat],
            scratch_shapes=[pltpu.VMEM((PAIR, rows, 2 * DH), BF16)] * 3
            + [pltpu.VMEM((PAIR, TILE, 2 * DH), F32), pltpu.VMEM((PAIR, TILE, DH), F32)],
        ),
        out_shape=(wide, thin, thin),
        compiler_params=pltpu.CompilerParams(vmem_limit_bytes=48 << 20),
        name="attend",
        cost_estimate=pl.CostEstimate(
            flops=HEADS * 20 * 3 * 2 * TILE * TILE * DH, bytes_accessed=rows * HEADS * DH * 6, transcendentals=HEADS * 20 * TILE * TILE
        ),
    )(low, shared, values, code, spread)


def attend_back(low, shared, values, code, spread, combined, above, lse, lone):
    rows = shared.shape[0]
    by_head, code_spec, spread_spec, stat = head_specs(rows)
    wide = jax.ShapeDtypeStruct((rows, HEADS * DH), BF16)
    return pl.pallas_call(
        back_kernel,
        grid_spec=pltpu.PrefetchScalarGridSpec(
            num_scalar_prefetch=1,
            grid=(HEADS // PAIR,),
            in_specs=[by_head, by_head, code_spec, spread_spec, by_head, by_head, stat, stat],
            out_specs=[by_head, by_head],
            scratch_shapes=[pltpu.VMEM((PAIR, rows, 2 * DH), BF16)] * 2 + [pltpu.VMEM((PAIR, rows, DH), F32)] * 3,
        ),
        out_shape=(wide, wide),
        compiler_params=pltpu.CompilerParams(vmem_limit_bytes=48 << 20),
        name="attend_back",
        cost_estimate=pl.CostEstimate(
            flops=HEADS * 20 * 6 * 2 * TILE * TILE * DH, bytes_accessed=rows * HEADS * DH * 12, transcendentals=HEADS * 20 * TILE * TILE
        ),
    )(low, shared, values, code, spread, combined, above, lse, lone)


def digits(devices):
    side = 2
    while 8 * side * side < devices:
        side += 1
    assert 8 * side * side == devices, devices
    return 4, side, 2


def neighbours(devices):
    outer, side, core = digits(devices)
    me = lax.axis_index("fsdp")
    c = lax.rem(me, core)
    q = lax.rem(lax.div(me, core), side)
    p = lax.rem(lax.div(me, core * side), side)
    o = lax.div(me, core * side * side)

    def at(o_, p_, q_, c_):
        return ((o_ * side + p_) * side + q_) * core + c_

    core_peer = at(o, p, q, 1 - c)
    q_peers = [(k, at(o, p, k, c)) for k in (lax.rem(q + d, side) for d in range(1, side))]
    p_peers = [(k, at(o, k, q, c)) for k in (lax.rem(p + d, side) for d in range(1, side))]
    o_peers = [(k, at(k, p, q, c)) for k in (lax.rem(o + d, outer) for d in range(1, outer))]
    return (o, p, q, c), core_peer, q_peers, p_peers, o_peers


def peers_of(where):
    return [where[1]] + [device for group in where[2:] for _, device in group]


def greet(peers):
    barrier = pltpu.get_barrier_semaphore()
    for peer in peers:
        pl.semaphore_signal(barrier, inc=1, device_id=(peer,), device_id_type=MESH)
    pl.semaphore_wait(barrier, len(peers))


def remote(src, dst, sems, slot, device):
    return pltpu.make_async_remote_copy(
        src_ref=src, dst_ref=dst, send_sem=sems.at[(0,) + slot], recv_sem=sems.at[(1,) + slot],
        device_id=(device,), device_id_type=MESH,
    )


class Scatter:
    def __init__(self, devices, where, slot, boxes, sems, other, mine, load=None):
        self.outer, self.side, _ = digits(devices)
        (self.o, self.p, self.q, self.c), self.core_peer, self.q_peers, self.p_peers, self.o_peers = where
        self.slot = slot
        self.box_c, box_a0, box_a1, self.box_b, self.box_o = boxes
        self.box_a = (box_a0, box_a1)
        self.sem_c, self.sem_a, self.sem_b, self.sem_o = sems
        self.other, self.mine, self.load = other, mine, load
        half = self.box_o.shape[-1] // 2
        self.columns = (pl.ds(0, half), pl.ds(half, half))

    def core(self):
        return remote(self.other(), self.box_c, self.sem_c, (self.slot,), self.core_peer)

    def first(self, h, d):
        k, device = (self.q_peers, self.p_peers)[h][d]
        spot = (slice(None), slice(None), k) if h == 0 else (slice(None), k, slice(None))
        return remote(self.mine(spot, self.columns[h]), self.box_a[h].at[d], self.sem_a, (self.slot, h, d), device)

    def second(self, h, d):
        k, device = (self.p_peers, self.q_peers)[h][d]
        return remote(
            self.box_a[h].at[0, :, k], self.box_b.at[d, :, :, self.columns[h]], self.sem_b, (self.slot, h, d), device
        )

    def third(self, d):
        k, device = self.o_peers[d]
        return remote(self.box_b.at[0, k], self.box_o.at[d], self.sem_o, (self.slot, d), device)

    def begin(self):
        self.core().start()
        if self.load is not None:
            self.load().start()

    def stage_core(self):
        if self.load is not None:
            self.load().wait()
        self.core().wait_recv()
        side = self.side

        def add(i, carry):
            spot = (lax.div(i, side * side), lax.rem(lax.div(i, side), side), lax.rem(i, side))
            ref = self.mine(spot, slice(None))
            ref[...] = ref[...] + self.box_c[spot]
            return carry

        lax.fori_loop(0, self.outer * side * side, add, 0)
        for h in range(2):
            for d in range(side - 1):
                self.first(h, d).start()

    def stage_first(self):
        side = self.side
        for h in range(2):
            box = self.box_a[h]
            for d in range(side - 1):
                self.first(h, d).wait_recv()

            def add(i, carry):
                a, b = lax.div(i, side), lax.rem(i, side)
                total = self.mine((a, b, self.q) if h == 0 else (a, self.p, b), self.columns[h])[...]
                for d in range(side - 1):
                    total = total + box[d, a, b]
                box[0, a, b] = total
                return carry

            lax.fori_loop(0, self.outer * side, add, 0)
            for d in range(side - 1):
                self.second(h, d).start()

    def stage_second(self):
        box = self.box_b
        for h in range(2):
            k = self.p if h == 0 else self.q
            for d in range(self.side - 1):
                self.second(h, d).wait_recv()

            def add(a, carry):
                total = self.box_a[h][0, a, k]
                for d in range(self.side - 1):
                    total = total + box[d, a, :, self.columns[h]]
                box[0, a, :, self.columns[h]] = total
                return carry

            lax.fori_loop(0, self.outer, add, 0)
        for d in range(self.outer - 1):
            self.third(d).start()

    def stage_third(self):
        total = self.box_b[0, self.o].astype(F32)
        for d in range(self.outer - 1):
            self.third(d).wait_recv()
            total = total + self.box_o[d].astype(F32)
        return total

    def sent_first(self):
        self.core().wait_send()
        for h in range(2):
            for d in range(self.side - 1):
                self.first(h, d).wait_send()

    def sent_last(self):
        for h in range(2):
            for d in range(self.side - 1):
                self.second(h, d).wait_send()
        for d in range(self.outer - 1):
            self.third(d).wait_send()


class Unit(Scatter):
    def __init__(self, unit, devices, *rest, **named):
        super().__init__(devices, *rest, **named)
        self.planes, self.outer, self.unit = self.outer, 1, unit

    def third(self, d=None):
        if d is not None:
            return remote(self.box_b.at[0, 0], self.box_o.at[d], self.sem_o, (self.slot, d), self.core_peer)
        me = lax.axis_index("fsdp")
        device = me + (self.unit - self.o) * (self.side * self.side * 2)
        d = lax.rem(self.o - self.unit + 2 * self.planes - 1, self.planes)
        return remote(self.box_b.at[0, 0], self.box_o.at[d], self.sem_o, (self.slot, d), device)

    def stage_second(self):
        super().stage_second()

        @pl.when(self.o != self.unit)
        def _():
            self.third().start()

    def close(self, ref):
        @pl.when(self.o == self.unit)
        def _():
            total = self.box_b[0, 0].astype(F32)
            for d in range(self.planes - 1):
                self.third(d).wait_recv()
                total = total + self.box_o[d].astype(F32)
            ref[...] = total

    def sent_last(self):
        super().sent_last()

        @pl.when(self.o != self.unit)
        def _():
            self.third().wait_send()


def boxes_for(devices, rows, width, unit=False):
    planes, side, _ = digits(devices)
    outer = 1 if unit else planes
    half = width // 2
    return [
        pltpu.VMEM((outer, side, side, rows, width), BF16),
        pltpu.VMEM((side - 1, outer, side, rows, half), BF16),
        pltpu.VMEM((side - 1, outer, side, rows, half), BF16),
        pltpu.VMEM((side - 1, outer, rows, width), BF16),
        pltpu.VMEM((planes - 1, rows, width), BF16),
    ]


def sems_for(devices, count):
    outer, side, _ = digits(devices)
    dma = pltpu.SemaphoreType.DMA
    return [dma((2, count)), dma((2, count, 2, side - 1)), dma((2, count, 2, side - 1)), dma((2, count, outer - 1))]


def mixing_kernel(
    devices, hidden_steps, second_ref, above_ref, expand_ref, reduce_ref, bias_e_ref, bias_r_ref,
    out_ref, back_ref, grad_b_ref, grad_e_ref, rest_e_ref, rest_r_ref, grad_r_ref, above_b_ref, act_s, pre_s, grad_s, unit_s, *rest,
):
    step = pl.program_id(0)
    rows, width = second_ref.shape
    strip = act_s.shape[1]
    per = width // strip
    slices = (len(rest) - 4) // 10
    sems = rest[10 * slices :]
    where = neighbours(devices)
    (o, p, q, c), core_peer, q_peers, p_peers, o_peers = where
    part = grad_s.shape[-2]

    def mover(k):
        def other():
            return grad_s.at[k % 2, :, :, :, 1 - c]

        def mine(spot, cols):
            return grad_s.at[(k % 2,) + tuple(spot) + (c, slice(None), cols)]

        return Scatter(devices, where, k, rest[5 * k : 5 * k + 5], sems, other, mine)

    def unit(k):
        def other():
            return unit_s.at[k % 2, :, :, :, 1 - c]

        def mine(spot, cols):
            return unit_s.at[(k % 2,) + tuple(spot) + (c, slice(None), cols)]

        slot = slices + k
        return Unit(k, devices, where, slot, rest[5 * slot : 5 * slot + 5], sems, other, mine)

    movers = [mover(k) for k in range(slices)]
    units = [unit(k) for k in range(slices)]
    w_e = expand_ref[...].reshape(width, strip)
    w_r = reduce_ref[...].reshape(strip, width)

    @pl.when(step == 0)
    def _():
        greet(peers_of(where))
        out_ref[...] = jnp.broadcast_to(bias_r_ref[...], out_ref.shape)
        back_ref[...] = jnp.zeros(back_ref.shape, F32)
        above_b_ref[...] = jnp.sum(above_ref[...].astype(F32), axis=0, keepdims=True)

    pre = dot(second_ref[...], w_e) + bias_e_ref[...]
    square = pre * pre
    curve = jnp.tanh(CURVE * pre * (1.0 + 0.044715 * square))
    hinge = 0.5 * (1.0 + curve)
    act_s[...] = (pre * hinge).astype(BF16)
    slope = hinge + 0.5 * pre * (1.0 - curve * curve) * (CURVE * (1.0 + 3 * 0.044715 * square))
    d_pre = (dot(above_ref[...], w_r, NT) * slope).astype(BF16)
    pre_s[...] = d_pre
    grad_b_ref[...] = jnp.sum(d_pre.astype(F32), axis=0, keepdims=True)
    out_ref[...] += dot(act_s[...], w_r)
    back_ref[...] += dot(d_pre, w_e, NT)
    grad_r = dot(act_s[...], above_ref[...], TN).astype(BF16)
    grad_e = dot(second_ref[...], pre_s[...], TN).astype(BF16)
    for k in range(slices):
        for j in range(per):
            @pl.when(step == k * per + j)
            def _():
                if j == 0 and k >= 2:
                    movers[k - 2].sent_first()
                    units[k - 2].sent_first()
                half = unit_s.shape[2] // per
                unit_s[k % 2, 0, j * half : (j + 1) * half] = grad_r.reshape((half,) + unit_s.shape[3:])
                grad_s[k % 2, :, :, :, :, :, j * strip : (j + 1) * strip] = grad_e.reshape(grad_s.shape[1:-1] + (strip,))
                if j == per - 1:
                    movers[k].begin()
                    units[k].begin()

    @pl.when(step >= slices * per)
    def _():
        rest_e_ref[...] = grad_e.reshape(rest_e_ref.shape)
        rest_r_ref[...] = grad_r.reshape(rest_r_ref.shape)

    def close(k):
        grad_e_ref[k * part : (k + 1) * part, :] = movers[k].stage_third()

    final = hidden_steps - 1
    late = []
    for k in range(slices):
        finish = functools.partial(units[k].close, grad_r_ref)
        for number, actions in enumerate((
            (movers[k].stage_core, units[k].stage_core), (movers[k].stage_first, units[k].stage_first),
            (movers[k].stage_second, units[k].stage_second), (functools.partial(close, k), finish),
        )):
            when = (k + 1) * per + number
            for order, action in enumerate(actions):
                if when > final:
                    late.append((when, -k, order, action))
                else:
                    pl.when(step == when)(action)

    @pl.when(step == final)
    def _():
        for *_, action in sorted(late, key=lambda entry: entry[:3]):
            action()
        for k in range(max(0, slices - 2), slices):
            movers[k].sent_first()
            units[k].sent_first()
        for k in range(slices):
            movers[k].sent_last()
            units[k].sent_last()


def mixing(devices, second, above, gathered, bias_e, bias_r, part):
    rows, width = second.shape
    hidden = bias_e.shape[1]
    many = hidden // devices
    sides = hidden // width
    strip = STRIP
    per = width // strip
    outer, side, core = digits(devices)
    fixed = pl.BlockSpec((rows, width), lambda i: (0, 0), pipeline_mode=pl.Buffered(1))
    whole = pl.BlockSpec(memory_space=pltpu.VMEM)
    scratch = [pltpu.VMEM((rows, strip), BF16)] * 2 + [pltpu.VMEM((2, outer, side, side, core, part, width), BF16)]
    slices = sides - 1
    scratch += [pltpu.VMEM((2, 1, side, side, core, many, width), BF16)]
    for k in range(slices):
        scratch += boxes_for(devices, part, width)
    for k in range(slices):
        scratch += boxes_for(devices, many, width, unit=True)
    return pl.pallas_call(
        functools.partial(mixing_kernel, devices, hidden // strip),
        grid=(hidden // strip,),
        in_specs=[
            fixed, fixed,
            pl.BlockSpec((devices, part, strip), lambda i: (0, many // part + 1 + i // per, i % per)),
            pl.BlockSpec((strip // many, many, width), lambda i: (i, 0, 0)),
            pl.BlockSpec((1, strip), lambda i: (0, i)),
            pl.BlockSpec((1, width), lambda i: (0, 0)),
        ],
        out_specs=[
            fixed,
            fixed,
            pl.BlockSpec((1, strip), lambda i: (0, i)),
            pl.BlockSpec((slices * part, width), lambda i: (0, 0)),
            pl.BlockSpec((devices, part, strip), lambda i: (0, 0, jnp.maximum(i - slices * per, 0))),
            pl.BlockSpec((strip // many, many, width), lambda i: (jnp.maximum(i - slices * per, 0), 0, 0)),
            pl.BlockSpec((many, width), lambda i: (0, 0)),
            pl.BlockSpec((1, width), lambda i: (0, 0)),
        ],
        out_shape=[
            jax.ShapeDtypeStruct((rows, width), F32),
            jax.ShapeDtypeStruct((rows, width), F32),
            jax.ShapeDtypeStruct((1, hidden), F32),
            jax.ShapeDtypeStruct((slices * part, width), F32),
            jax.ShapeDtypeStruct((devices, part, width), BF16),
            jax.ShapeDtypeStruct((devices // outer, many, width), BF16),
            jax.ShapeDtypeStruct((many, width), F32),
            jax.ShapeDtypeStruct((1, width), F32),
        ],
        scratch_shapes=scratch + sems_for(devices, 2 * slices),
        compiler_params=pltpu.CompilerParams(collective_id=3, has_side_effects=True, vmem_limit_bytes=57 << 20),
        name="mixing",
    )(second, above, gathered, gathered, bias_e, bias_r)


def turn_kernel(
    devices, grad_r_ref, grad_e_ref, out_one_ref, d_second_ref, mixed_ref, two_ref, above_ref, combined_ref, live_ref, gain_ref, w_o_ref,
    bias_r_ref, bias_e_ref, first_r_ref,
    wide_ref, grad_one_ref, one_ref, res_two_ref, grad_o_ref, small_ref, part_e_ref, part_r_ref,
    attend_s, load_sem, halo_sem, *rest,
):
    slots, width = two_ref.shape
    half = slots // 2
    tile = 256
    part = part_e_ref.shape[0]
    where = neighbours(devices)
    (o, p, q, c), *_ = where
    me = lax.axis_index("fsdp")
    owns, rest = rest[:2], rest[2:]
    sems = rest[-4:]

    def distant(source, row, rows, k, unit=0):
        at = pl.ds(row, rows)

        def other():
            return source.at[:, :, :, 1 - c, at, :]

        def mine(spot, cols):
            return owns[k].at[tuple(spot) + (slice(None), cols)]

        def load():
            return pltpu.make_async_copy(source.at[:, :, :, c, at, :], owns[k], load_sem.at[k])

        group = (devices, where, k, rest[5 * k : 5 * k + 5], sems, other, mine, load)
        return Unit(unit, *group) if unit else Scatter(*group)

    outer = digits(devices)[0]
    movers = [distant(grad_e_ref, 0, part, 0), distant(grad_r_ref, 0, part_r_ref.shape[0], 1, outer - 1)]
    last = devices - 1
    left, right = lax.rem(me + last, devices), lax.rem(me + 1, devices)
    greet(peers_of(where) + [left, right])
    for mover in movers:
        mover.begin()

    def to_left():
        return remote(wide_ref.at[half : 2 * half], wide_ref.at[half + slots :], halo_sem, (0,), left)

    def to_right():
        return remote(wide_ref.at[2 * half : 3 * half], wide_ref.at[:half], halo_sem, (1,), right)

    small_ref[...] = jnp.zeros(small_ref.shape, F32)
    gain = gain_ref[...]

    def norm_tile(i, carry):
        at = pl.ds(pl.multiple_of(i * tile, tile), tile)
        live = live_ref[at, :]
        values = out_one_ref[at, :]
        above = d_second_ref[at, :]
        center = values - jnp.mean(values, axis=1, keepdims=True)
        scale = lax.rsqrt(jnp.mean(center * center, axis=1, keepdims=True) + EPS_NORM)
        center = center * scale
        small_ref[2:3, :] += jnp.sum(above * center, axis=0, keepdims=True)
        small_ref[3:4, :] += jnp.sum(above, axis=0, keepdims=True)
        above = above * gain
        mean = jnp.mean(above, axis=1, keepdims=True)
        along = jnp.mean(above * center, axis=1, keepdims=True)
        total = live * (above_ref[at, :].astype(F32) + scale * (above - mean - center * along))
        low = total.astype(BF16)
        grad_one_ref[at, :] = low
        attend_s[at, :] = low
        small_ref[4:5, :] += jnp.sum(low.astype(F32), axis=0, keepdims=True)
        wide_ref[pl.ds(pl.multiple_of(half + i * tile, tile), tile), :] = dot(low, w_o_ref[...], NT).astype(BF16)
        return carry

    lax.fori_loop(0, half // tile, norm_tile, 0)

    @pl.when(me > 0)
    def _():
        to_left().start()

    movers[0].stage_core()
    lax.fori_loop(half // tile, slots // tile, norm_tile, 0)

    @pl.when(me < last)
    def _():
        to_right().start()

    movers[1].stage_core()

    def finish_tile(i, carry):
        at = pl.ds(pl.multiple_of(i * tile, tile), tile)
        live = live_ref[at, :]
        one_ref[at, :] = (live * out_one_ref[at, :]).astype(BF16)
        res_two_ref[at, :] = (live * (two_ref[at, :].astype(F32) + mixed_ref[at, :])).astype(BF16)
        return carry

    lax.fori_loop(0, slots // tile, finish_tile, 0)
    movers[0].stage_first()

    def weights(i, carry):
        cols = pl.ds(pl.multiple_of(i * tile, tile), tile)
        many = tile // part
        grad_o_ref[pl.ds(pl.multiple_of(i * many, many), many)] = (
            dot(combined_ref[:, cols], attend_s[...], TN).astype(BF16).reshape(many, part, width)
        )
        return carry

    lax.fori_loop(0, width // tile, weights, 0)
    movers[1].stage_first()
    movers[0].stage_second()
    small_ref[5:6, :] = bias_r_ref[...]
    for k in range(bias_e_ref.shape[1] // width):
        small_ref[6 + k : 7 + k, :] = bias_e_ref[:, k * width : (k + 1) * width]
    movers[1].stage_second()
    part_e_ref[...] = movers[0].stage_third()
    part_r_ref[...] = first_r_ref[...]
    movers[1].close(part_r_ref)

    @pl.when(me > 0)
    def _():
        to_right().wait_recv()
        to_left().wait_send()

    @pl.when(me == 0)
    def _():
        wide_ref[:half] = jnp.zeros((half, width), BF16)

    @pl.when(me < last)
    def _():
        to_left().wait_recv()
        to_right().wait_send()

    @pl.when(me == last)
    def _():
        wide_ref[half + slots :] = jnp.zeros((half, width), BF16)

    for mover in movers:
        mover.sent_first()
        mover.sent_last()


def turn(devices, grad_r, grad_e, out_one, d_second, mixed, two, above, combined, live, gain, w_o, bias_r, bias_e, first_r):
    slots, width = two.shape
    outer, side, core = digits(devices)
    part, many = grad_e.shape[1], grad_r.shape[1]
    vmem = pl.BlockSpec(memory_space=pltpu.VMEM)
    anywhere = pl.BlockSpec(memory_space=pl.ANY)
    dma = pltpu.SemaphoreType.DMA
    scratch = [pltpu.VMEM((slots, width), BF16), dma((2,)), dma((2, 2))]
    scratch += [pltpu.VMEM((outer, side, side, part, width), BF16), pltpu.VMEM((1, side, side, many, width), BF16)]
    scratch += boxes_for(devices, part, width) + boxes_for(devices, many, width, unit=True)
    shape = (outer, side, side, core)
    rows_low = jax.ShapeDtypeStruct((slots, width), BF16)
    return pl.pallas_call(
        functools.partial(turn_kernel, devices),
        in_specs=[anywhere, anywhere] + [vmem] * 12,
        out_specs=(vmem,) * 8,
        out_shape=(
            jax.ShapeDtypeStruct((2 * slots, width), BF16), rows_low, rows_low, rows_low,
            jax.ShapeDtypeStruct((devices, part, width), BF16),
            jax.ShapeDtypeStruct((16, width), F32),
            jax.ShapeDtypeStruct((part, width), F32),
            jax.ShapeDtypeStruct((many, width), F32),
        ),
        scratch_shapes=scratch + sems_for(devices, 2),
        compiler_params=pltpu.CompilerParams(collective_id=5, has_side_effects=True, vmem_limit_bytes=57 << 20),
        name="turn",
    )(
        grad_r.reshape((1,) + shape[1:] + grad_r.shape[1:]), grad_e.reshape(shape + grad_e.shape[1:]),
        out_one, d_second, mixed, two, above, combined, live, gain, w_o, bias_r, bias_e, first_r,
    )


def tail_kernel(
    devices, grad_o_ref, d_shared_ref, d_value_ref, normed_ref, head_ref, own_ref, end_ref, above_ref, live_ref,
    gain_ref, w_s_ref, w_v_ref, small_ref,
    back_ref, out_s_ref, out_v_ref, out_o_ref, thin_ref, long_ref,
    side_s, side_in, vector_s, vector_in, grad_s, load_sem, halo_sem, vector_sem, *rest,
):
    window, width = normed_ref.shape
    slots = own_ref.shape[0]
    half = slots // 2
    part = out_s_ref.shape[0]
    tile = 256
    where = neighbours(devices)
    (o, p, q, c), core_peer, q_peers, p_peers, o_peers = where
    me = lax.axis_index("fsdp")
    outer, side, core = digits(devices)
    owns, rest = rest[:1], rest[1:]
    sems = rest[-4:]

    def distant(source, row, rows, k):
        at = pl.ds(row, rows)

        def other():
            return source.at[:, :, :, 1 - c, at, :]

        def mine(spot, cols):
            return owns[k].at[tuple(spot) + (slice(None), cols)]

        def load():
            return pltpu.make_async_copy(source.at[:, :, :, c, at, :], owns[k], load_sem.at[k])

        return Scatter(devices, where, k, rest[5 * k : 5 * k + 5], sems, other, mine, load)

    def near(j, k):
        def other():
            return grad_s.at[j, :, :, :, 1 - c]

        def mine(spot, cols):
            return grad_s.at[(j,) + tuple(spot) + (c, slice(None), cols)]

        return Scatter(devices, where, k, rest[5 * k : 5 * k + 5], sems, other, mine)

    movers = [
        distant(grad_o_ref, 0, part, 0), near(0, 1), near(1, 2),
    ]
    last = devices - 1
    left, right = lax.rem(me + last, devices), lax.rem(me + 1, devices)
    greet(peers_of(where) + [left, right])
    movers[0].begin()

    def to_left():
        return remote(side_s.at[0], side_in.at[1], halo_sem, (0,), left)

    def to_right():
        return remote(side_s.at[1], side_in.at[0], halo_sem, (1,), right)

    vector_s[...] = small_ref[...]
    gain = gain_ref[...]

    def norm_tile(ref, row, at):
        values = ref[pl.ds(row, tile), :].astype(F32)
        above = dot(d_shared_ref[at, :], w_s_ref[...], NT) + dot(d_value_ref[at, :], w_v_ref[...], NT)
        center = values - jnp.mean(values, axis=1, keepdims=True)
        scale = lax.rsqrt(jnp.mean(center * center, axis=1, keepdims=True) + EPS_NORM)
        center = center * scale
        vector_s[0:1, :] += jnp.sum(above * center, axis=0, keepdims=True)
        vector_s[1:2, :] += jnp.sum(above, axis=0, keepdims=True)
        above = above * gain
        mean = jnp.mean(above, axis=1, keepdims=True)
        along = jnp.mean(above * center, axis=1, keepdims=True)
        return scale * (above - mean - center * along)

    def side_tiles(i, carry):
        row = pl.multiple_of(i * tile, tile)
        side_s[0, pl.ds(row, tile), :] = norm_tile(head_ref, row, pl.ds(row, tile)).astype(BF16)
        at = pl.ds(pl.multiple_of(half + slots + i * tile, tile), tile)
        side_s[1, pl.ds(row, tile), :] = norm_tile(end_ref, row, at).astype(BF16)
        return carry

    lax.fori_loop(0, half // tile, side_tiles, 0)

    @pl.when(me > 0)
    def _():
        to_left().start()

    @pl.when(me < last)
    def _():
        to_right().start()

    movers[0].stage_core()

    def weights(j, ref):
        wide = tile // part

        def strip(i, carry):
            cols = pl.ds(pl.multiple_of(i * tile, tile), tile)
            block = dot(normed_ref[:, cols], ref[...], TN).astype(BF16).reshape(wide // core, core, part, width)
            for k in range(wide // core):
                index = i * (wide // core) + k
                spot = (lax.div(index, side * side), lax.rem(lax.div(index, side), side), lax.rem(index, side))
                grad_s[(j,) + spot] = block[k]
            return carry

        lax.fori_loop(0, width // tile, strip, 0)

    weights(0, d_shared_ref)
    movers[1].begin()
    movers[0].stage_first()
    weights(1, d_value_ref)
    movers[2].begin()
    movers[0].stage_second()
    movers[1].stage_core()

    def own_tiles(i, carry):
        row = pl.multiple_of(i * tile, tile)
        at = pl.ds(pl.multiple_of(half + i * tile, tile), tile)
        here = pl.ds(row, tile)
        total = above_ref[here, :].astype(F32) + norm_tile(own_ref, row, at)
        back_ref[here, :] = (live_ref[here, :] * total).astype(BF16)
        return carry

    lax.fori_loop(0, slots // tile, own_tiles, 0)

    def vector_copies(stage):
        group = ([(0, core_peer)], q_peers, p_peers, o_peers)[stage]
        base = (0, 1, side, 2 * side - 1)[stage]
        return [
            remote(vector_s if stage == 0 else vector_in.at[base - 1], vector_in.at[base + d], vector_sem, (base + d,), device)
            for d, (_, device) in enumerate(group)
        ]

    def vector_stage(stage):
        base = (0, 1, side, 2 * side - 1)[stage]
        copies = vector_copies(stage)
        total = vector_s[...] if stage == 0 else vector_in[base - 1]
        for d, copy in enumerate(copies):
            copy.wait_recv()
            total = total + vector_in[base + d]
        vector_in[base + len(copies) - 1] = total

    for copy in vector_copies(0):
        copy.start()
    movers[2].stage_core()
    movers[1].stage_first()
    out_o_ref[...] = movers[0].stage_third()
    vector_stage(0)
    for copy in vector_copies(1):
        copy.start()
    movers[2].stage_first()
    movers[1].stage_second()
    vector_stage(1)
    for copy in vector_copies(2):
        copy.start()
    movers[2].stage_second()
    vector_stage(2)
    for copy in vector_copies(3):
        copy.start()

    @pl.when(me > 0)
    def _():
        to_right().wait_recv()

    @pl.when(me == 0)
    def _():
        side_in[0] = jnp.zeros((half, width), BF16)

    @pl.when(me < last)
    def _():
        to_left().wait_recv()

    @pl.when(me == last)
    def _():
        side_in[1] = jnp.zeros((half, width), BF16)

    for k in range(2):
        at = slice(k * half, (k + 1) * half)
        back_ref[at, :] = (back_ref[at, :].astype(F32) + side_in[k].astype(F32)).astype(BF16)
    out_s_ref[...] = movers[1].stage_third()
    vector_stage(3)
    out_v_ref[...] = movers[2].stage_third()
    vectors = 2 * side + outer - 3
    total = vector_in[vectors]
    thin_ref[...] = pltpu.roll(total, lax.rem(width - me * part, width), 1)[:, :DH]
    each = long_ref.shape[1]
    long_rows = [total[6 + k : 7 + k, :] for k in range(devices * each // width)]
    mine = lax.div(me * each, width)
    chosen = long_rows[0]
    for k in range(1, len(long_rows)):
        chosen = jnp.where(mine == k, long_rows[k], chosen)
    long_ref[...] = pltpu.roll(chosen, lax.rem(width - lax.rem(me * each, width), width), 1)[:, :each]
    for stage in range(4):
        for copy in vector_copies(stage):
            copy.wait_send()

    @pl.when(me > 0)
    def _():
        to_left().wait_send()

    @pl.when(me < last)
    def _():
        to_right().wait_send()

    for mover in movers:
        mover.sent_first()
        mover.sent_last()


def tail(devices, grad_o, d_shared, d_values, normed, head, own, end, above, live, gain, w_s, w_v, small, hidden):
    window, width = normed.shape
    slots = own.shape[0]
    outer, side, core = digits(devices)
    part = grad_o.shape[1]
    each = hidden // devices
    vmem = pl.BlockSpec(memory_space=pltpu.VMEM)
    anywhere = pl.BlockSpec(memory_space=pl.ANY)
    dma = pltpu.SemaphoreType.DMA
    sizes = [part, part, part]
    scratch = [
        pltpu.VMEM((2, slots // 2, width), BF16), pltpu.VMEM((2, slots // 2, width), BF16),
        pltpu.VMEM((16, width), F32), pltpu.VMEM((2 * side + outer - 2, 16, width), F32),
        pltpu.VMEM((2, outer, side, side, core, part, width), BF16),
        dma((1,)), dma((2, 2)), dma((2, 2 * side + outer - 2)),
    ]
    scratch += [pltpu.VMEM((outer, side, side, rows, width), BF16) for rows in sizes[:1]]
    for rows in sizes:
        scratch += boxes_for(devices, rows, width)
    shape = (outer, side, side, core)
    return pl.pallas_call(
        functools.partial(tail_kernel, devices),
        in_specs=[anywhere] + [vmem] * 12,
        out_specs=(vmem,) * 6,
        out_shape=(
            jax.ShapeDtypeStruct((slots, width), BF16),
            jax.ShapeDtypeStruct((part, width), F32),
            jax.ShapeDtypeStruct((part, width), F32),
            jax.ShapeDtypeStruct((part, width), F32),
            jax.ShapeDtypeStruct((16, DH), F32),
            jax.ShapeDtypeStruct((1, each), F32),
        ),
        scratch_shapes=scratch + sems_for(devices, len(sizes)),
        compiler_params=pltpu.CompilerParams(collective_id=4, has_side_effects=True, vmem_limit_bytes=57 << 20),
        name="tail",
    )(
        grad_o.reshape(shape + grad_o.shape[1:]),
        d_shared, d_values, normed, head, own, end, above, live, gain, w_s, w_v, small,
    )


def find_ranks(length_ref, target_ref, bucket_ref, packed_ref, info_ref, before_s):
    devices = length_ref.shape[0]
    lists, slots = bucket_ref.shape
    me = lax.axis_index("fsdp")
    base = me * slots
    window = 2 * slots

    def look(s, carry):
        start, mine, found, one, two = carry
        size = length_ref[s]
        target = target_ref[s]
        middle = start + lax.shift_right_logical(size, 1)
        inside = (middle >= base) & (middle < base + slots)
        offset = start - base + slots // 2
        entry = (offset, offset + size, target)
        first, second = inside & (found == 0), inside & (found == 1)
        one = tuple(jnp.where(first, new, old) for new, old in zip(entry, one))
        two = tuple(jnp.where(second, new, old) for new, old in zip(entry, two))
        return start + size, jnp.where(target == me, size, mine), found + inside.astype(jnp.int32), one, two

    zero = jnp.int32(0)
    nothing = (jnp.int32(window), jnp.int32(window), zero)
    total, mine, found, one, two = lax.fori_loop(0, devices, look, (zero, zero, zero, nothing, nothing))
    for k, value in enumerate((one[0], one[1], two[0], two[1], one[2], two[2], total, found)):
        info_ref[k] = value

    def fill(i, carry):
        at = pl.ds(pl.multiple_of(i * DH, DH), DH)
        first = lax.broadcasted_iota(jnp.int32, (DH, slots), 0) + i * DH
        second = lax.broadcasted_iota(jnp.int32, (DH, slots), 1)
        before_s[at, :] = jnp.where(first < second, 1.0, 0.0).astype(BF16)
        return carry

    lax.fori_loop(0, slots // DH, fill, 0)
    left = lax.broadcasted_iota(jnp.int32, (DH, DH), 0)
    right = lax.broadcasted_iota(jnp.int32, (DH, DH), 1)
    smaller = jnp.where((left // BUCKETS == right // BUCKETS) & (right < left), 1.0, 0.0).astype(BF16)
    many = DH // BUCKETS
    bucket = lax.broadcasted_iota(jnp.int32, (many, BUCKETS, slots), 1)
    live = lax.broadcasted_iota(jnp.int32, (many, BUCKETS, slots), 2) < mine
    ranks = []
    for g in range(lists // many):
        here = (jnp.broadcast_to(bucket_ref[g * many : (g + 1) * many, :][:, None, :], bucket.shape) == bucket) & live
        one_hot = jnp.where(here, 1.0, 0.0)
        flat = one_hot.reshape(DH, slots).astype(BF16)
        offset = jnp.sum(dot(smaller, flat), axis=1, keepdims=True)
        place = (dot(flat, before_s[...]) + offset).reshape(many, BUCKETS, slots)
        ranks.append(jnp.sum(one_hot * place, axis=1))
    rank = jnp.concatenate(ranks, axis=0)
    live = lax.broadcasted_iota(jnp.int32, (lists, slots), 1) < mine
    packed_ref[:lists, :] = jnp.where(live, jnp.floor(rank * (1.0 / GROUP)), FREE).astype(BF16)


def project_kernel(
    info_ref, head_ref, own_ref, tail_ref, gain_ref, shift_ref, w_s_ref, w_v_ref, one_ref, two_ref,
    normed_ref, shared_ref, value_ref, code_ref,
):
    i = pl.program_id(0)
    tile = own_ref.shape[0]
    steps = pl.num_programs(0)

    def go(ref):
        normed = layer_norm(ref[...].astype(F32), gain_ref[...], shift_ref[...]).astype(BF16)
        normed_ref[...] = normed
        shared_ref[...] = dot(normed, w_s_ref[...]).astype(BF16)
        value_ref[...] = dot(normed, w_v_ref[...]).astype(BF16)

    @pl.when(i < steps // 4)
    def _():
        go(head_ref)

    @pl.when((i >= steps // 4) & (i < steps - steps // 4))
    def _():
        go(own_ref)

    @pl.when(i >= steps - steps // 4)
    def _():
        go(tail_ref)

    @pl.when(i == 0)
    def _():
        lists, window = code_ref.shape
        lane = lax.broadcasted_iota(jnp.int32, (lists, window), 1)
        code = jnp.full((lists, window), FREE, F32)
        for k, ref in enumerate((one_ref, two_ref)):
            begin, end = info_ref[2 * k], info_ref[2 * k + 1]
            rows = ref[0].astype(F32)
            moved = pltpu.roll(jnp.concatenate([rows, rows], axis=1), lax.rem(begin, window), 1)
            code = jnp.where((lane >= begin) & (lane < end), moved + 32.0 * k, code)
        code_ref[...] = code.astype(BF16)


def project(info, head, own, tail, gain, shift, w_s, w_v, blocks):
    slots, width = own.shape
    window = 2 * slots
    lists = ROUNDS * HEADS
    tile = 256
    steps = window // tile
    quarter = steps // 4
    rows = pl.BlockSpec((tile, width), lambda i, info: (i, 0))
    vector = pl.BlockSpec((1, width), lambda i, info: (0, 0))
    matrix = pl.BlockSpec((width, width), lambda i, info: (0, 0), pipeline_mode=pl.Buffered(1))
    wide = jax.ShapeDtypeStruct((window, width), BF16)
    return pl.pallas_call(
        project_kernel,
        grid_spec=pltpu.PrefetchScalarGridSpec(
            num_scalar_prefetch=1,
            grid=(steps,),
            in_specs=[
                pl.BlockSpec((tile, width), lambda i, info: (jnp.minimum(i, quarter - 1), 0)),
                pl.BlockSpec((tile, width), lambda i, info: (jnp.clip(i - quarter, 0, 2 * quarter - 1), 0)),
                pl.BlockSpec((tile, width), lambda i, info: (jnp.clip(i - 3 * quarter, 0, quarter - 1), 0)),
                vector, vector, matrix, matrix,
                pl.BlockSpec((1, lists, slots), lambda i, info: (info[4], 0, 0)),
                pl.BlockSpec((1, lists, slots), lambda i, info: (info[5], 0, 0)),
            ],
            out_specs=[rows, rows, rows, pl.BlockSpec((lists, window), lambda i, info: (0, 0))],
        ),
        out_shape=[wide, wide, wide, jax.ShapeDtypeStruct((lists, window), BF16)],
        compiler_params=pltpu.CompilerParams(vmem_limit_bytes=40 << 20),
        name="project",
    )(info, head, own, tail, gain, shift, w_s, w_v, blocks, blocks)


def gather_kernel(devices, arrays, length_ref, target_ref, bucket_ref, vector_ref, *refs):
    sources, outs, info_ref = refs[: arrays - 1], refs[arrays - 1 : 2 * arrays - 1], refs[2 * arrays - 1]
    packed_s, before_s, own_sem, sem_o, sem_a, sem_b, sem_c = refs[2 * arrays :]
    sources = sources + (packed_s,)
    outer, side, core = digits(devices)
    (o, p, q, c), core_peer, q_peers, p_peers, o_peers = neighbours(devices)
    greet([core_peer] + [d for _, d in q_peers] + [d for _, d in p_peers] + [d for _, d in o_peers])
    half = sources[0].shape[-1] // 2
    columns = (pl.ds(0, half), pl.ds(half, half))

    def remote(src, dst, sems, slot, device):
        return pltpu.make_async_remote_copy(
            src_ref=src, dst_ref=dst, send_sem=sems.at[(0,) + slot], recv_sem=sems.at[(1,) + slot],
            device_id=(device,), device_id_type=MESH,
        )

    copies, locals_, begun, first, second, last = [], [], {}, {}, {}, {}
    for s in range(arrays):
        if s == arrays - 1:
            find_ranks(length_ref, target_ref, bucket_ref, packed_s, info_ref, before_s)
            packed_s[bucket_ref.shape[0] :, :] = vector_ref[...]
        locals_.append(pltpu.make_async_copy(sources[s], outs[s].at[o, p, q, c], own_sem.at[s]))
        locals_[s].start()
        for d, (k, device) in enumerate(o_peers):
            begun[s, d] = remote(sources[s], outs[s].at[o, p, q, c], sem_o, (s, d), device)
            begun[s, d].start()

    def stage_a(s):
        locals_[s].wait()
        for d in range(outer - 1):
            begun[s, d].wait_recv()
        for h, peers in enumerate((q_peers, p_peers)):
            piece = outs[s].at[:, p, q, c, :, columns[h]]
            for d, (k, device) in enumerate(peers):
                first[s, h, d] = remote(piece, piece, sem_a, (s, h, d), device)
                first[s, h, d].start()

    def stage_b(s):
        for h, peers in enumerate((p_peers, q_peers)):
            for d in range(side - 1):
                first[s, h, d].wait_recv()
            piece = outs[s].at[:, p, :, c, :, columns[h]] if h == 0 else outs[s].at[:, :, q, c, :, columns[h]]
            for d, (k, device) in enumerate(peers):
                second[s, h, d] = remote(piece, piece, sem_b, (s, h, d), device)
                second[s, h, d].start()

    def stage_c(s):
        for h in range(2):
            for d in range(side - 1):
                second[s, h, d].wait_recv()
        piece = outs[s].at[:, :, :, c]
        last[s] = remote(piece, piece, sem_c, (s,), core_peer)
        last[s].start()

    for t in range(arrays + 2):
        if t < arrays:
            stage_a(t)
        if 0 <= t - 1 < arrays:
            stage_b(t - 1)
        if 0 <= t - 2 < arrays:
            stage_c(t - 2)
    for s in range(arrays):
        last[s].wait_recv()
    for group in (begun, first, second, last):
        for copy in group.values():
            copy.wait_send()


def gather(devices, lengths, destination, buckets, vectors, arrays):
    outer, side, core = digits(devices)
    lists, slots = buckets.shape
    packed = jax.ShapeDtypeStruct((lists + vectors.shape[0], slots), BF16)
    shapes = [jax.ShapeDtypeStruct(array.shape, array.dtype) for array in arrays] + [packed]
    count = len(shapes)
    dma = pltpu.SemaphoreType.DMA
    anywhere = pl.BlockSpec(memory_space=pl.ANY)
    smem = pl.BlockSpec(memory_space=pltpu.SMEM)
    vmem = pl.BlockSpec(memory_space=pltpu.VMEM)
    outs = pl.pallas_call(
        functools.partial(gather_kernel, devices, count),
        out_shape=tuple(jax.ShapeDtypeStruct((outer, side, side, core) + shape.shape, shape.dtype) for shape in shapes)
        + (jax.ShapeDtypeStruct((8,), jnp.int32),),
        in_specs=[smem, smem, vmem, vmem] + [anywhere] * (count - 1),
        out_specs=(anywhere,) * count + (smem,),
        scratch_shapes=[
            pltpu.VMEM(packed.shape, BF16), pltpu.VMEM((slots, slots), BF16),
            dma((count,)), dma((2, count, outer - 1)), dma((2, count, 2, side - 1)), dma((2, count, 2, side - 1)), dma((2, count)),
        ],
        compiler_params=pltpu.CompilerParams(collective_id=2, has_side_effects=True, vmem_limit_bytes=32 << 20),
        name="gather",
    )(lengths, destination, buckets, vectors, *arrays)
    return [out.reshape((devices,) + shape.shape) for out, shape in zip(outs, shapes)] + [outs[-1]]


def body(
    input_one, input_two, upstream_one, upstream_two, lengths, destination, buckets,
    w_shared, w_value, w_output, w_expand, w_reduce,
    gain_attend, shift_attend, gain_mixing, shift_mixing, bias_output, bias_expand, bias_reduce,
):
    devices = lax.axis_size("fsdp")
    me = lax.axis_index("fsdp")
    slots, width = input_one.shape
    half = slots // 2
    window = 2 * slots
    part = w_shared.shape[0]
    hidden = w_expand.shape[1]
    sides = hidden // width
    down = [(i, i - 1) for i in range(1, devices)]
    up = [(i, i + 1) for i in range(devices - 1)]

    def to_sides(head, tail):
        return lax.ppermute(tail, "fsdp", up), lax.ppermute(head, "fsdp", down)

    def narrow(wide):
        head, tail = to_sides(wide[:half], wide[half + slots :])
        return wide[half : half + slots], jnp.concatenate([head, tail], axis=0)

    base = me * slots
    lists = ROUNDS * HEADS
    spot = jnp.arange(width, dtype=jnp.int32)
    short = jnp.stack([gain_attend, shift_attend, gain_mixing, shift_mixing, bias_output, bias_reduce])
    short = jnp.where(spot // part == me, jnp.tile(short, (1, devices)), 0.0)
    many = hidden // devices
    long = jnp.tile(bias_expand, width // many)[None]
    long = jnp.where(spot[None] // many + (width // many) * jnp.arange(sides, dtype=jnp.int32)[:, None] == me, long, 0.0)
    vectors = jnp.concatenate([short, long], axis=0)
    high = lax.reduce_precision(vectors, 8, 7)
    count = vectors.shape[0]
    packed = jnp.concatenate(
        [high.astype(BF16), (vectors - high).astype(BF16), jnp.zeros((24 - 2 * count, width), BF16)], axis=0
    )
    second_gather = lax.all_gather(
        jnp.concatenate(
            [w_reduce, w_output] + [w_expand[:, k * width : (k + 1) * width] for k in range(sides)], axis=0
        ),
        "fsdp", axis=0, tiled=False,
    )
    full_shared, full_value, packed, info = gather(devices, lengths, destination, buckets[0], packed, [w_shared, w_value])
    full_shared, full_value = full_shared.reshape(width, width), full_value.reshape(width, width)
    vectors = jnp.sum(packed[:, lists : lists + 2 * count].astype(F32), axis=0)
    vectors = vectors[:count] + vectors[count:]
    gain_a, shift_a, gain_m, shift_m, bias_o, bias_r = (vectors[k : k + 1] for k in range(6))
    bias_e = vectors[6:].reshape(1, hidden)
    full_output = second_gather[:, sides * part : (sides + 1) * part].reshape(width, width)
    lane = jnp.arange(HEADS * DH, dtype=jnp.int32)
    row = jnp.arange(lists, dtype=jnp.int32)[:, None]
    spread = (row == ((lane % 64) // 16) * HEADS + lane // DH).astype(BF16)

    live = ((base + jnp.arange(slots, dtype=jnp.int32)) < info[6]).astype(F32)[:, None]
    slot_one = input_one.astype(F32)
    two_head, two_tail = to_sides(input_two[:half], input_two[half:])
    normed, shared, values, code = project(
        info, two_head, input_two, two_tail, gain_a, shift_a, full_shared, full_value, packed
    )
    combined_window, lse, lone = attend(info, shared, values, code, spread)
    own, other = narrow(combined_window)
    combined = own + other
    attended = dot(combined, full_output) + bias_o
    out_one = slot_one + live * attended
    second = layer_norm(out_one, gain_m, shift_m).astype(BF16)
    d_reduce = (live * upstream_two.astype(F32)).astype(BF16)
    mixed, d_second, grad_bias_expand, grad_expand, last_expand, last_reduce, grad_reduce, grad_bias_reduce = mixing(
        devices, second, d_reduce, second_gather, bias_e, bias_r, part
    )
    d_combined, grad_one, result_one, result_two, grad_output, small, last_expand, grad_reduce = turn(
        devices, last_reduce, last_expand, out_one, d_second, mixed, input_two, upstream_one, combined, live, gain_m,
        full_output, grad_bias_reduce, grad_bias_expand, grad_reduce,
    )
    d_shared, d_values = attend_back(
        info, shared, values, code, spread, combined_window, d_combined, lse, lone
    )
    grad_two, grad_shared, grad_value, grad_output, thin, long = tail(
        devices, grad_output, d_shared, d_values, normed,
        two_head, input_two, two_tail, upstream_two, live, gain_a, full_shared, full_value, small, hidden,
    )
    return (
        result_one,
        result_two,
        grad_one,
        grad_two,
        grad_shared,
        grad_value,
        grad_output,
        jnp.concatenate([grad_expand[k * part : (k + 1) * part] for k in range(sides - 1)] + [last_expand], axis=1),
        grad_reduce,
        thin[0, :part],
        thin[1, :part],
        thin[2, :part],
        thin[3, :part],
        thin[4, :part],
        long.reshape(-1),
        thin[5, :part],
    )


def solution(mesh):
    rows, flat, whole = P("fsdp", None), P("fsdp"), P()
    return jax.shard_map(
        body,
        mesh=mesh,
        in_specs=(rows,) * 4 + (whole, whole, P("fsdp", None, None)) + (rows,) * 5 + (flat,) * 7,
        out_specs=(rows,) * 9 + (flat,) * 7,
        check_vma=False,
    )
```

```python
import functools
import math

import jax
import jax.numpy as jnp
from jax import lax
from jax.experimental import pallas as pl
from jax.experimental.pallas import tpu as pltpu
from jax.sharding import PartitionSpec as P

HEADS = 8
DH = 128
GROUP = 64
ROUNDS = 4
BUCKETS = 32
EPS_NORM = 1e-05
EPS_UNIT = 1e-06
LOG2E = math.log2(math.e)
SELF2 = -100000.0 * LOG2E
NEG = -1e30
SCALE = 1.0 / math.sqrt(DH)
TILE = 512
HALF = TILE // 2
STEP = 128.0
SHIFT = 1.5 * 2.0**30
TAME = 3000.0
PAIR = 4
FREE = 99.0
STRIP = 512
AFTER = (1, 4, 6, 8)
CURVE = math.sqrt(2.0 / math.pi)
MESH = pl.DeviceIdType.MESH

NT = (((1,), (1,)), ((), ()))
NN = (((1,), (0,)), ((), ()))
TN = (((0,), (0,)), ((), ()))
F32 = jnp.float32
BF16 = jnp.bfloat16


def dot(a, b, dims=NN):
    return lax.dot_general(a, b, dims, preferred_element_type=F32)


def layer_norm(values, gain, shift):
    center = values - jnp.mean(values, axis=-1, keepdims=True)
    spread = jnp.mean(center * center, axis=-1, keepdims=True)
    return center * lax.rsqrt(spread + EPS_NORM) * gain + shift


def prepare(q, code_ref, spread, ask_s, key_s, h, at):
    lane = lax.broadcasted_iota(jnp.int32, (TILE, DH), 1)
    target = ((lane // 64) * 32 + lane % 16).astype(F32)
    wide = q.astype(F32)
    square = jnp.sum(wide * wide, axis=1, keepdims=True)
    code = dot(code_ref[:, at], spread, TN)
    here = code == target
    ask_s[h, at, :DH] = q
    ask_s[h, at, DH:] = jnp.where(here, STEP, 0.0).astype(BF16)
    key_s[h, at, :DH] = (wide * (lax.rsqrt(square + EPS_UNIT) * (SCALE * LOG2E))).astype(BF16)
    key_s[h, at, DH:] = jnp.where(here | (code + 1.0 == target), 1.0, 0.0).astype(BF16)
    return jnp.max(square)


def lowest(info_ref, i):
    start, stop = i * TILE, (i + 1) * TILE
    one = (info_ref[0] < stop) & (info_ref[1] > start)
    two = (info_ref[2] < stop) & (info_ref[3] > start)
    begin = jnp.where(one, info_ref[0], jnp.where(two, info_ref[2], stop))
    return lax.div(begin, TILE)


def tile_rows(i):
    return pl.ds(pl.multiple_of(i * TILE, TILE), TILE)


def halves(i):
    start = i * TILE
    return [((0, pl.multiple_of(start, HALF), pl.multiple_of(start, HALF)), HALF),
            ((HALF, pl.multiple_of(start + HALF, HALF), pl.multiple_of(start, HALF)), TILE)]


def part_of(both):
    count = (both + SHIFT) - SHIFT
    return count, both - count


def apart(left, right):
    return dot(left[:, DH:], right[:, DH:], NT), dot(left[:, :DH], right[:, :DH], NT)


def attend_kernel(low_ref, q_ref, v_ref, code_ref, spread_ref, comb_ref, lse_ref, lone_ref, ask_s, key_s, more_s, acc_s, top_s):
    rows = q_ref.shape[0]
    tiles = rows // TILE
    heads = [slice(h * DH, (h + 1) * DH) for h in range(PAIR)]

    def ready(i, largest):
        def fill():
            most = jnp.float32(0.0)
            at = tile_rows(i)
            for h, cols in enumerate(heads):
                most = jnp.maximum(most, prepare(q_ref[at, cols], code_ref, spread_ref[:, cols], ask_s, key_s, h, at))
                more_s[h, at, :DH] = v_ref[at, cols]
                more_s[h, at, DH:] = jnp.ones((TILE, DH), BF16)
            return most

        return jnp.maximum(largest, lax.cond(lowest(low_ref, i) <= i, fill, lambda: jnp.float32(0.0)))

    largest = lax.fori_loop(0, tiles, ready, jnp.float32(0.0))
    tame = largest * (SCALE * LOG2E) ** 2 < TAME
    ask_at = lax.broadcasted_iota(jnp.int32, (TILE, TILE), 0)
    key_at = lax.broadcasted_iota(jnp.int32, (TILE, TILE), 1)

    def finish(h, cols, at, top):
        total = acc_s[h, :, DH:]
        some = total > 0.0
        safe = jnp.where(some, total, 1.0)
        inverse = jnp.where(some, 1.0 / safe, 0.0)
        comb_ref[at, cols] = (acc_s[h, :, :DH] * inverse).astype(BF16)
        lse_ref[h, :, at] = (jnp.log2(safe) + top).T[:1]

    def rows_of(i, carry):
        at = tile_rows(i)
        low = lowest(low_ref, i)

        @pl.when((low <= i) & tame)
        def _():
            for h in range(PAIR):
                acc_s[h] = jnp.zeros((TILE, 2 * DH), F32)

            def step(j, carry):
                keys = tile_rows(j)
                for h in range(PAIR):
                    count, score = part_of(dot(ask_s[h, at, :], key_s[h, keys, :], NT))
                    acc_s[h] += dot((count * jnp.exp2(score)).astype(BF16), more_s[h, keys, :])
                return carry

            lax.fori_loop(low, i, step, 0)
            for h, cols in enumerate(heads):
                for asks, span in halves(i):
                    here = pl.ds(asks[0], HALF)
                    there = pl.ds(asks[1], HALF)
                    keys = pl.ds(asks[2], span)
                    key_at = lax.broadcasted_iota(jnp.int32, (HALF, span), 1)
                    ask_at = lax.broadcasted_iota(jnp.int32, (HALF, span), 0) + (span - HALF)
                    count, score = part_of(dot(ask_s[h, there, :], key_s[h, keys, :], NT))
                    prob = jnp.where(key_at < ask_at, count * jnp.exp2(score), 0.0).astype(BF16)
                    acc_s[h, here, :] += dot(prob, more_s[h, keys, :])
                    active = jnp.max(jnp.where(key_at == ask_at, count, 0.0), axis=1, keepdims=True) > 0.0
                    lone = jnp.where(active & (acc_s[h, here, DH:] == 0.0), 1.0, 0.0)
                    acc_s[h, here, :DH] += lone * v_ref[there, cols].astype(F32)
                    acc_s[h, here, DH:] += lone
                    lone_ref[h, :, there] = lone.T[:1]
                finish(h, cols, at, 0.0)

        @pl.when((low <= i) & jnp.logical_not(tame))
        def _():
            for h, cols in enumerate(heads):
                count, score = apart(ask_s[h, at, :], key_s[h, at, :])
                score = jnp.where(key_at == ask_at, SELF2, score)
                score = jnp.where((key_at <= ask_at) & (count > 0.5), score, NEG)
                top = jnp.max(score, axis=1, keepdims=True)
                prob = count * jnp.exp2(score - top)
                acc_s[h] = dot(prob.astype(BF16), more_s[h, at, :])
                top_s[h] = jnp.broadcast_to(top, (TILE, DH))

                def step(j, carry):
                    keys = tile_rows(j)
                    count, score = apart(ask_s[h, at, :], key_s[h, keys, :])
                    score = jnp.where(count > 0.5, score, NEG)
                    top = top_s[h]
                    newer = jnp.maximum(top, jnp.max(score, axis=1, keepdims=True))
                    fade = jnp.exp2(top - newer)
                    prob = count * jnp.exp2(score - newer[:, :1])
                    acc_s[h] = acc_s[h] * jnp.concatenate([fade, fade], axis=1) + dot(prob.astype(BF16), more_s[h, keys, :])
                    top_s[h] = newer
                    return carry

                lax.fori_loop(low, i, step, 0)
                total = acc_s[h, :, DH:]
                own = STEP * ROUNDS * jnp.exp2(SELF2 - jnp.maximum(top_s[h], SELF2))
                lone_ref[h, :, at] = jnp.where(total > 0.0, own / jnp.where(total > 0.0, total, 1.0), 0.0).T[:1]
                finish(h, cols, at, top_s[h])

        @pl.when(low > i)
        def _():
            comb_ref[at, :] = jnp.zeros((TILE, PAIR * DH), BF16)
            for h in range(PAIR):
                lse_ref[h, :, at] = jnp.zeros((1, TILE), F32)
                lone_ref[h, :, at] = jnp.zeros((1, TILE), F32)

        return carry

    lax.fori_loop(0, tiles, rows_of, 0)


def back_kernel(
    low_ref, q_ref, v_ref, code_ref, spread_ref, comb_ref, above_ref, lse_ref, lone_ref,
    dq_ref, dv_ref, ask_s, key_s, dunit_s, dvalue_s, dask_s,
):
    rows = q_ref.shape[0]
    tiles = rows // TILE
    heads = [slice(h * DH, (h + 1) * DH) for h in range(PAIR)]

    def ready(i, largest):
        def fill():
            most = jnp.float32(0.0)
            at = tile_rows(i)
            for h, cols in enumerate(heads):
                most = jnp.maximum(most, prepare(q_ref[at, cols], code_ref, spread_ref[:, cols], ask_s, key_s, h, at))
                for total in (dunit_s, dvalue_s, dask_s):
                    total[h, at, :] = jnp.zeros((TILE, DH), F32)
            return most

        return jnp.maximum(largest, lax.cond(lowest(low_ref, i) <= i, fill, lambda: jnp.float32(0.0)))

    largest = lax.fori_loop(0, tiles, ready, jnp.float32(0.0))
    tame = largest * (SCALE * LOG2E) ** 2 < TAME

    def pass_over(i, low, split):
        at = tile_rows(i)
        deltas = []
        for h, cols in enumerate(heads):
            mixed = above_ref[at, cols].astype(F32) * comb_ref[at, cols].astype(F32)
            deltas.append(jnp.sum(mixed.T, axis=0, keepdims=True))

        def step(j, carry):
            keys = tile_rows(j)
            for h, cols in enumerate(heads):
                q, above, unit = q_ref[at, cols], above_ref[at, cols], key_s[h, keys, :DH]
                count, score = split(key_s[h, keys, :], ask_s[h, at, :])
                d_prob = dot(v_ref[keys, cols], above, NT)
                prob = count * jnp.exp2(score - lse_ref[h, :, at])
                d_score = (prob * (d_prob - carry[h])).astype(BF16)
                dvalue_s[h, keys, :] += dot(prob.astype(BF16), above)
                dunit_s[h, keys, :] += dot(d_score, q)
                dask_s[h, at, :] += dot(d_score, unit, TN)
            return carry

        deltas = lax.fori_loop(low, i, step, tuple(deltas))
        for h, cols in enumerate(heads):
            for asks, span in halves(i):
                there = pl.ds(asks[1], HALF)
                keys = pl.ds(asks[2], span)
                key_at = lax.broadcasted_iota(jnp.int32, (span, HALF), 0)
                ask_at = lax.broadcasted_iota(jnp.int32, (span, HALF), 1) + (span - HALF)
                q, above, unit = q_ref[there, cols], above_ref[there, cols], key_s[h, keys, :DH]
                count, score = split(key_s[h, keys, :], ask_s[h, there, :])
                d_prob = dot(v_ref[keys, cols], above, NT)
                prob = count * jnp.exp2(score - lse_ref[h, :, there])
                prob = jnp.where(key_at < ask_at, prob, 0.0)
                d_score = (prob * (d_prob - deltas[h][:, asks[0] : asks[0] + HALF])).astype(BF16)
                prob = jnp.where(key_at == ask_at, lone_ref[h, :, there], prob).astype(BF16)
                dvalue_s[h, keys, :] += dot(prob, above)
                dunit_s[h, keys, :] += dot(d_score, q)
                dask_s[h, there, :] += dot(d_score, unit, TN)

    def together(left, right):
        return part_of(dot(left, right, NT))

    def guarded(left, right):
        count, score = apart(left, right)
        return count, jnp.where(count > 0.5, score, NEG)

    def rows_of(i, carry):
        low = lowest(low_ref, i)

        @pl.when((low <= i) & tame)
        def _():
            pass_over(i, low, together)

        @pl.when((low <= i) & jnp.logical_not(tame))
        def _():
            pass_over(i, low, guarded)

        return carry

    lax.fori_loop(0, tiles, rows_of, 0)

    def close(i, carry):
        at = tile_rows(i)

        @pl.when(lowest(low_ref, i) <= i)
        def _():
            for h, cols in enumerate(heads):
                q = q_ref[at, cols].astype(F32)
                norm = lax.rsqrt(jnp.sum(q * q, axis=1, keepdims=True) + EPS_UNIT)
                d_unit = dunit_s[h, at, :] * SCALE
                along = jnp.sum(q * d_unit, axis=1, keepdims=True)
                d_q = dask_s[h, at, :] * (1.0 / LOG2E) + d_unit * norm - q * (norm * norm * norm * along)
                dq_ref[at, cols] = d_q.astype(BF16)
                dv_ref[at, cols] = dvalue_s[h, at, :].astype(BF16)

        @pl.when(lowest(low_ref, i) > i)
        def _():
            dq_ref[at, :] = jnp.zeros((TILE, PAIR * DH), BF16)
            dv_ref[at, :] = jnp.zeros((TILE, PAIR * DH), BF16)

        return carry

    lax.fori_loop(0, tiles, close, 0)


def head_specs(rows):
    by_head = pl.BlockSpec((rows, PAIR * DH), lambda h, low: (0, h))
    code = pl.BlockSpec((ROUNDS * HEADS, rows), lambda h, low: (0, 0))
    spread = pl.BlockSpec((ROUNDS * HEADS, PAIR * DH), lambda h, low: (0, h))
    stat = pl.BlockSpec((PAIR, 1, rows), lambda h, low: (h, 0, 0))
    return by_head, code, spread, stat


def attend(low, shared, values, code, spread):
    rows = shared.shape[0]
    by_head, code_spec, spread_spec, stat = head_specs(rows)
    wide = jax.ShapeDtypeStruct((rows, HEADS * DH), BF16)
    thin = jax.ShapeDtypeStruct((HEADS, 1, rows), F32)
    return pl.pallas_call(
        attend_kernel,
        grid_spec=pltpu.PrefetchScalarGridSpec(
            num_scalar_prefetch=1,
            grid=(HEADS // PAIR,),
            in_specs=[by_head, by_head, code_spec, spread_spec],
            out_specs=[by_head, stat, stat],
            scratch_shapes=[pltpu.VMEM((PAIR, rows, 2 * DH), BF16)] * 3
            + [pltpu.VMEM((PAIR, TILE, 2 * DH), F32), pltpu.VMEM((PAIR, TILE, DH), F32)],
        ),
        out_shape=(wide, thin, thin),
        compiler_params=pltpu.CompilerParams(vmem_limit_bytes=57 << 20),
        name="attend",
        cost_estimate=pl.CostEstimate(
            flops=HEADS * 20 * 3 * 2 * TILE * TILE * DH, bytes_accessed=rows * HEADS * DH * 6, transcendentals=HEADS * 20 * TILE * TILE
        ),
    )(low, shared, values, code, spread)


def attend_back(low, shared, values, code, spread, combined, above, lse, lone):
    rows = shared.shape[0]
    by_head, code_spec, spread_spec, stat = head_specs(rows)
    wide = jax.ShapeDtypeStruct((rows, HEADS * DH), BF16)
    return pl.pallas_call(
        back_kernel,
        grid_spec=pltpu.PrefetchScalarGridSpec(
            num_scalar_prefetch=1,
            grid=(HEADS // PAIR,),
            in_specs=[by_head, by_head, code_spec, spread_spec, by_head, by_head, stat, stat],
            out_specs=[by_head, by_head],
            scratch_shapes=[pltpu.VMEM((PAIR, rows, 2 * DH), BF16)] * 2 + [pltpu.VMEM((PAIR, rows, DH), F32)] * 3,
        ),
        out_shape=(wide, wide),
        compiler_params=pltpu.CompilerParams(vmem_limit_bytes=57 << 20),
        name="attend_back",
        cost_estimate=pl.CostEstimate(
            flops=HEADS * 20 * 6 * 2 * TILE * TILE * DH, bytes_accessed=rows * HEADS * DH * 12, transcendentals=HEADS * 20 * TILE * TILE
        ),
    )(low, shared, values, code, spread, combined, above, lse, lone)


def digits(devices):
    side = 2
    while 8 * side * side < devices:
        side += 1
    assert 8 * side * side == devices, devices
    return 4, side, 2


def neighbours(devices):
    outer, side, core = digits(devices)
    me = lax.axis_index("fsdp")
    c = lax.rem(me, core)
    q = lax.rem(lax.div(me, core), side)
    p = lax.rem(lax.div(me, core * side), side)
    o = lax.div(me, core * side * side)

    def at(o_, p_, q_, c_):
        return ((o_ * side + p_) * side + q_) * core + c_

    core_peer = at(o, p, q, 1 - c)
    q_peers = [(k, at(o, p, k, c)) for k in (lax.rem(q + d, side) for d in range(1, side))]
    p_peers = [(k, at(o, k, q, c)) for k in (lax.rem(p + d, side) for d in range(1, side))]
    o_peers = [(k, at(k, p, q, c)) for k in (lax.rem(o + d, outer) for d in range(1, outer))]
    return (o, p, q, c), core_peer, q_peers, p_peers, o_peers


def peers_of(where):
    return [where[1]] + [device for group in where[2:] for _, device in group]


def greet(peers):
    barrier = pltpu.get_barrier_semaphore()
    for peer in peers:
        pl.semaphore_signal(barrier, inc=1, device_id=(peer,), device_id_type=MESH)
    pl.semaphore_wait(barrier, len(peers))


def remote(src, dst, sems, slot, device):
    return pltpu.make_async_remote_copy(
        src_ref=src, dst_ref=dst, send_sem=sems.at[(0,) + slot], recv_sem=sems.at[(1,) + slot],
        device_id=(device,), device_id_type=MESH,
    )


class Scatter:
    def __init__(self, devices, where, slot, boxes, sems, other, mine, load=None):
        self.outer, self.side, _ = digits(devices)
        (self.o, self.p, self.q, self.c), self.core_peer, self.q_peers, self.p_peers, self.o_peers = where
        self.slot = slot
        self.box_c, box_a0, box_a1, self.box_b, self.box_o = boxes
        self.box_a = (box_a0, box_a1)
        self.sem_c, self.sem_a, self.sem_b, self.sem_o = sems
        self.other, self.mine, self.load = other, mine, load
        half = self.box_o.shape[-1] // 2
        self.columns = (pl.ds(0, half), pl.ds(half, half))

    def core(self):
        return remote(self.other(), self.box_c, self.sem_c, (self.slot,), self.core_peer)

    def first(self, h, d):
        k, device = (self.q_peers, self.p_peers)[h][d]
        spot = (slice(None), slice(None), k) if h == 0 else (slice(None), k, slice(None))
        return remote(self.mine(spot, self.columns[h]), self.box_a[h].at[d], self.sem_a, (self.slot, h, d), device)

    def second(self, h, d):
        k, device = (self.p_peers, self.q_peers)[h][d]
        return remote(
            self.box_a[h].at[0, :, k], self.box_b.at[d, :, :, self.columns[h]], self.sem_b, (self.slot, h, d), device
        )

    def third(self, d):
        k, device = self.o_peers[d]
        return remote(self.box_b.at[0, k], self.box_o.at[d], self.sem_o, (self.slot, d), device)

    def begin(self):
        self.core().start()
        if self.load is not None:
            self.load().start()

    def stage_core(self):
        if self.load is not None:
            self.load().wait()
        self.core().wait_recv()
        side = self.side

        def add(i, carry):
            spot = (lax.div(i, side * side), lax.rem(lax.div(i, side), side), lax.rem(i, side))
            ref = self.mine(spot, slice(None))
            ref[...] = ref[...] + self.box_c[spot]
            return carry

        lax.fori_loop(0, self.outer * side * side, add, 0)
        for h in range(2):
            for d in range(side - 1):
                self.first(h, d).start()

    def stage_first(self):
        side = self.side
        for h in range(2):
            box = self.box_a[h]
            for d in range(side - 1):
                self.first(h, d).wait_recv()

            def add(i, carry):
                a, b = lax.div(i, side), lax.rem(i, side)
                total = self.mine((a, b, self.q) if h == 0 else (a, self.p, b), self.columns[h])[...]
                for d in range(side - 1):
                    total = total + box[d, a, b]
                box[0, a, b] = total
                return carry

            lax.fori_loop(0, self.outer * side, add, 0)
            for d in range(side - 1):
                self.second(h, d).start()

    def stage_second(self):
        box = self.box_b
        for h in range(2):
            k = self.p if h == 0 else self.q
            for d in range(self.side - 1):
                self.second(h, d).wait_recv()

            def add(a, carry):
                total = self.box_a[h][0, a, k]
                for d in range(self.side - 1):
                    total = total + box[d, a, :, self.columns[h]]
                box[0, a, :, self.columns[h]] = total
                return carry

            lax.fori_loop(0, self.outer, add, 0)
        for d in range(self.outer - 1):
            self.third(d).start()

    def stage_third(self):
        total = self.box_b[0, self.o].astype(F32)
        for d in range(self.outer - 1):
            self.third(d).wait_recv()
            total = total + self.box_o[d].astype(F32)
        return total

    def sent_first(self):
        self.core().wait_send()
        for h in range(2):
            for d in range(self.side - 1):
                self.first(h, d).wait_send()

    def sent_last(self):
        for h in range(2):
            for d in range(self.side - 1):
                self.second(h, d).wait_send()
        for d in range(self.outer - 1):
            self.third(d).wait_send()


def boxes_for(devices, rows, width):
    outer, side, _ = digits(devices)
    half = width // 2
    return [
        pltpu.VMEM((outer, side, side, rows, width), BF16),
        pltpu.VMEM((side - 1, outer, side, rows, half), BF16),
        pltpu.VMEM((side - 1, outer, side, rows, half), BF16),
        pltpu.VMEM((side - 1, outer, rows, width), BF16),
        pltpu.VMEM((outer - 1, rows, width), BF16),
    ]


def sems_for(devices, count):
    outer, side, _ = digits(devices)
    dma = pltpu.SemaphoreType.DMA
    return [dma((2, count)), dma((2, count, 2, side - 1)), dma((2, count, 2, side - 1)), dma((2, count, outer - 1))]


def mixing_kernel(
    devices, second_ref, above_ref, expand_ref, reduce_ref, bias_e_ref, bias_r_ref,
    out_ref, back_ref, grad_r_ref, grad_b_ref, grad_e_ref, above_b_ref, act_s, pre_s, grad_s, *rest,
):
    step = pl.program_id(0)
    rows, width = second_ref.shape
    strip = act_s.shape[1]
    per = width // strip
    slices = (len(rest) - 4) // 5
    sems = rest[5 * slices :]
    where = neighbours(devices)
    (o, p, q, c), core_peer, q_peers, p_peers, o_peers = where
    part = grad_s.shape[-2]

    def mover(k):
        def other():
            return grad_s.at[k % 2, :, :, :, 1 - c]

        def mine(spot, cols):
            return grad_s.at[(k % 2,) + tuple(spot) + (c, slice(None), cols)]

        return Scatter(devices, where, k, rest[5 * k : 5 * k + 5], sems, other, mine)

    movers = [mover(k) for k in range(slices)]
    w_e = expand_ref[...].reshape(width, strip)
    w_r = reduce_ref[...].reshape(strip, width)

    @pl.when(step == 0)
    def _():
        greet(peers_of(where))
        out_ref[...] = jnp.broadcast_to(bias_r_ref[...], out_ref.shape)
        back_ref[...] = jnp.zeros(back_ref.shape, F32)
        above_b_ref[...] = jnp.sum(above_ref[...].astype(F32), axis=0, keepdims=True)

    def close(k):
        grad_e_ref[k * part : (k + 1) * part, :] = movers[k].stage_third()

    final = slices * per - 1
    timed, late = [], []
    for k in range(slices):
        begun = 2 * ((k + 1) * per - 1) + 1
        for after, action in zip(
            AFTER, (movers[k].stage_core, movers[k].stage_first, movers[k].stage_second, functools.partial(close, k))
        ):
            if begun + after > 2 * final + 1:
                late.append(action)
            else:
                timed.append((begun + after, action))

    def stages(point):
        for when, action in timed:
            if when % 2 == point:
                pl.when(step == when // 2)(action)

    pre = dot(second_ref[...], w_e) + bias_e_ref[...]
    square = pre * pre
    curve = jnp.tanh(CURVE * pre * (1.0 + 0.044715 * square))
    hinge = 0.5 * (1.0 + curve)
    act_s[...] = (pre * hinge).astype(BF16)
    slope = hinge + 0.5 * pre * (1.0 - curve * curve) * (CURVE * (1.0 + 3 * 0.044715 * square))
    d_pre = (dot(above_ref[...], w_r, NT) * slope).astype(BF16)
    pre_s[...] = d_pre
    grad_b_ref[...] = jnp.sum(d_pre.astype(F32), axis=0, keepdims=True)
    stages(0)
    out_ref[...] += dot(act_s[...], w_r)
    back_ref[...] += dot(d_pre, w_e, NT)
    grad_r_ref[...] = dot(act_s[...], above_ref[...], TN).astype(BF16).reshape(grad_r_ref.shape)
    grad_e = dot(second_ref[...], pre_s[...], TN).astype(BF16)
    for k in range(slices):
        for j in range(per):
            @pl.when(step == k * per + j)
            def _():
                if j == 0 and k >= 2:
                    movers[k - 2].sent_first()
                grad_s[k % 2, :, :, :, :, :, j * strip : (j + 1) * strip] = grad_e.reshape(grad_s.shape[1:-1] + (strip,))
                if j == per - 1:
                    movers[k].begin()

    stages(1)

    @pl.when(step == final)
    def _():
        for action in late:
            action()
        for k in range(max(0, slices - 2), slices):
            movers[k].sent_first()
        for k in range(slices):
            movers[k].sent_last()


def mixing(devices, second, above, gathered, bias_e, bias_r, part):
    rows, width = second.shape
    hidden = bias_e.shape[1]
    many = hidden // devices
    sides = hidden // width
    strip = STRIP
    per = width // strip
    outer, side, core = digits(devices)
    fixed = pl.BlockSpec((rows, width), lambda i: (0, 0), pipeline_mode=pl.Buffered(1))
    whole = pl.BlockSpec(memory_space=pltpu.VMEM)
    scratch = [pltpu.VMEM((rows, strip), BF16)] * 2 + [pltpu.VMEM((2, outer, side, side, core, part, width), BF16)]
    for k in range(sides):
        scratch += boxes_for(devices, part, width)
    return pl.pallas_call(
        functools.partial(mixing_kernel, devices),
        grid=(hidden // strip,),
        in_specs=[
            fixed, fixed,
            pl.BlockSpec((devices, part, strip), lambda i: (0, many // part + 1 + i // per, i % per)),
            pl.BlockSpec((strip // many, many, width), lambda i: (i, 0, 0)),
            pl.BlockSpec((1, strip), lambda i: (0, i)),
            pl.BlockSpec((1, width), lambda i: (0, 0)),
        ],
        out_specs=[
            fixed,
            fixed,
            pl.BlockSpec((strip // many, many, width), lambda i: (i, 0, 0)),
            pl.BlockSpec((1, strip), lambda i: (0, i)),
            pl.BlockSpec((sides * part, width), lambda i: (0, 0)),
            pl.BlockSpec((1, width), lambda i: (0, 0)),
        ],
        out_shape=[
            jax.ShapeDtypeStruct((rows, width), F32),
            jax.ShapeDtypeStruct((rows, width), F32),
            jax.ShapeDtypeStruct((devices, many, width), BF16),
            jax.ShapeDtypeStruct((1, hidden), F32),
            jax.ShapeDtypeStruct((sides * part, width), F32),
            jax.ShapeDtypeStruct((1, width), F32),
        ],
        scratch_shapes=scratch + sems_for(devices, sides),
        compiler_params=pltpu.CompilerParams(collective_id=3, has_side_effects=True, vmem_limit_bytes=57 << 20),
        name="mixing",
    )(second, above, gathered, gathered, bias_e, bias_r)


def join_kernel(
    devices, window_ref, first_ref, final_ref, one_ref, above_ref, live_ref, w_ref, bias_ref, gain_ref, shift_ref,
    combined_ref, out_ref, second_ref, reduce_ref, side_in, part_s, halo_sem,
):
    slots, width = one_ref.shape
    half = slots // 2
    tile = 256
    me = lax.axis_index("fsdp")
    last = devices - 1
    left, right = lax.rem(me + last, devices), lax.rem(me + 1, devices)
    greet([left, right])

    def to_left():
        return remote(window_ref.at[:half], side_in.at[1], halo_sem, (0,), left)

    def to_right():
        return remote(window_ref.at[half + slots :], side_in.at[0], halo_sem, (1,), right)

    @pl.when(me > 0)
    def _():
        to_left().start()

    @pl.when(me < last)
    def _():
        to_right().start()

    @pl.when(me == 0)
    def _():
        side_in[0] = jnp.zeros((half, width), BF16)

    @pl.when(me == last)
    def _():
        side_in[1] = jnp.zeros((half, width), BF16)

    w_o = w_ref[...].reshape(width, width)

    owns = (first_ref, final_ref)

    def before(side, i, carry):
        here = pl.ds(pl.multiple_of(i * tile, tile), tile)
        at = pl.ds(pl.multiple_of(side * half + i * tile, tile), tile)
        part_s[at, :] = dot(owns[side][here, :], w_o)
        reduce_ref[at, :] = (live_ref[at, :] * above_ref[at, :].astype(F32)).astype(BF16)
        return carry

    for side in range(2):
        lax.fori_loop(0, half // tile, functools.partial(before, side), 0)

    def after(side, i, carry):
        here = pl.ds(pl.multiple_of(i * tile, tile), tile)
        at = pl.ds(pl.multiple_of(side * half + i * tile, tile), tile)
        other = side_in[side, here, :]
        combined_ref[at, :] = owns[side][here, :] + other
        attended = part_s[at, :] + dot(other, w_o) + bias_ref[...]
        out = one_ref[at, :].astype(F32) + live_ref[at, :] * attended
        out_ref[at, :] = out
        second_ref[at, :] = layer_norm(out, gain_ref[...], shift_ref[...]).astype(BF16)
        return carry

    @pl.when(me > 0)
    def _():
        to_right().wait_recv()

    lax.fori_loop(0, half // tile, functools.partial(after, 0), 0)

    @pl.when(me < last)
    def _():
        to_left().wait_recv()

    lax.fori_loop(0, half // tile, functools.partial(after, 1), 0)

    @pl.when(me > 0)
    def _():
        to_left().wait_send()

    @pl.when(me < last)
    def _():
        to_right().wait_send()


def join(devices, window, one, above, live, gathered, bias, gain, shift, part, sides):
    slots, width = one.shape
    dma = pltpu.SemaphoreType.DMA
    rows = pl.BlockSpec((slots, width), lambda i: (0, 0))
    thin = pl.BlockSpec((1, width), lambda i: (0, 0))
    low = jax.ShapeDtypeStruct((slots, width), BF16)
    return pl.pallas_call(
        functools.partial(join_kernel, devices),
        grid=(1,),
        in_specs=[
            pl.BlockSpec(memory_space=pl.ANY),
            pl.BlockSpec((slots // 2, width), lambda i: (1, 0)), pl.BlockSpec((slots // 2, width), lambda i: (2, 0)), rows, rows, pl.BlockSpec((slots, 1), lambda i: (0, 0)),
            pl.BlockSpec((devices, part, width), lambda i: (0, sides, 0)), thin, thin, thin,
        ],
        out_specs=[rows] * 4,
        out_shape=[low, jax.ShapeDtypeStruct((slots, width), F32), low, low],
        scratch_shapes=[pltpu.VMEM((2, slots // 2, width), BF16), pltpu.VMEM((slots, width), F32), dma((2, 2))],
        compiler_params=pltpu.CompilerParams(collective_id=6, has_side_effects=True, vmem_limit_bytes=57 << 20),
        name="join",
    )(window, window, window, one, above, live, gathered, bias, gain, shift)


def turn_kernel(
    devices, out_one_ref, d_second_ref, mixed_ref, two_ref, above_ref, combined_ref, live_ref, gain_ref, w_o_ref,
    bias_r_ref, bias_e_ref,
    wide_ref, grad_one_ref, one_ref, res_two_ref, grad_o_ref, small_ref, attend_s, halo_sem,
):
    slots, width = two_ref.shape
    half = slots // 2
    tile = 256
    part = grad_o_ref.shape[1]
    me = lax.axis_index("fsdp")
    last = devices - 1
    left, right = lax.rem(me + last, devices), lax.rem(me + 1, devices)
    greet([left, right])

    def to_left():
        return remote(wide_ref.at[half : 2 * half], wide_ref.at[half + slots :], halo_sem, (0,), left)

    def to_right():
        return remote(wide_ref.at[2 * half : 3 * half], wide_ref.at[:half], halo_sem, (1,), right)

    small_ref[...] = jnp.zeros(small_ref.shape, F32)
    gain = gain_ref[...]

    def norm_tile(i, carry):
        at = pl.ds(pl.multiple_of(i * tile, tile), tile)
        live = live_ref[at, :]
        values = out_one_ref[at, :]
        above = d_second_ref[at, :]
        center = values - jnp.mean(values, axis=1, keepdims=True)
        scale = lax.rsqrt(jnp.mean(center * center, axis=1, keepdims=True) + EPS_NORM)
        center = center * scale
        small_ref[2:3, :] += jnp.sum(above * center, axis=0, keepdims=True)
        small_ref[3:4, :] += jnp.sum(above, axis=0, keepdims=True)
        above = above * gain
        mean = jnp.mean(above, axis=1, keepdims=True)
        along = jnp.mean(above * center, axis=1, keepdims=True)
        total = live * (above_ref[at, :].astype(F32) + scale * (above - mean - center * along))
        low = total.astype(BF16)
        grad_one_ref[at, :] = low
        attend_s[at, :] = low
        small_ref[4:5, :] += jnp.sum(low.astype(F32), axis=0, keepdims=True)
        wide_ref[pl.ds(pl.multiple_of(half + i * tile, tile), tile), :] = dot(low, w_o_ref[...], NT).astype(BF16)
        return carry

    lax.fori_loop(0, half // tile, norm_tile, 0)

    @pl.when(me > 0)
    def _():
        to_left().start()

    lax.fori_loop(half // tile, slots // tile, norm_tile, 0)

    @pl.when(me < last)
    def _():
        to_right().start()

    def finish_tile(i, carry):
        at = pl.ds(pl.multiple_of(i * tile, tile), tile)
        live = live_ref[at, :]
        one_ref[at, :] = (live * out_one_ref[at, :]).astype(BF16)
        res_two_ref[at, :] = (live * (two_ref[at, :].astype(F32) + mixed_ref[at, :])).astype(BF16)
        return carry

    lax.fori_loop(0, slots // tile, finish_tile, 0)

    def weights(i, carry):
        cols = pl.ds(pl.multiple_of(i * tile, tile), tile)
        many = tile // part
        grad_o_ref[pl.ds(pl.multiple_of(i * many, many), many)] = (
            dot(combined_ref[:, cols], attend_s[...], TN).astype(BF16).reshape(many, part, width)
        )
        return carry

    lax.fori_loop(0, width // tile, weights, 0)
    small_ref[5:6, :] = bias_r_ref[...]
    for k in range(bias_e_ref.shape[1] // width):
        small_ref[6 + k : 7 + k, :] = bias_e_ref[:, k * width : (k + 1) * width]

    @pl.when(me > 0)
    def _():
        to_right().wait_recv()
        to_left().wait_send()

    @pl.when(me == 0)
    def _():
        wide_ref[:half] = jnp.zeros((half, width), BF16)

    @pl.when(me < last)
    def _():
        to_left().wait_recv()
        to_right().wait_send()

    @pl.when(me == last)
    def _():
        wide_ref[half + slots :] = jnp.zeros((half, width), BF16)


def turn(devices, out_one, d_second, mixed, two, above, combined, live, gain, w_o, bias_r, bias_e):
    slots, width = two.shape
    part = width // devices
    vmem = pl.BlockSpec(memory_space=pltpu.VMEM)
    rows_low = jax.ShapeDtypeStruct((slots, width), BF16)
    return pl.pallas_call(
        functools.partial(turn_kernel, devices),
        in_specs=[vmem] * 11,
        out_specs=(vmem,) * 6,
        out_shape=(
            jax.ShapeDtypeStruct((2 * slots, width), BF16), rows_low, rows_low, rows_low,
            jax.ShapeDtypeStruct((devices, part, width), BF16),
            jax.ShapeDtypeStruct((16, width), F32),
        ),
        scratch_shapes=[pltpu.VMEM((slots, width), BF16), pltpu.SemaphoreType.DMA((2, 2))],
        compiler_params=pltpu.CompilerParams(collective_id=5, has_side_effects=True, vmem_limit_bytes=57 << 20),
        name="turn",
    )(out_one, d_second, mixed, two, above, combined, live, gain, w_o, bias_r, bias_e)


def tail_kernel(
    devices, grad_r_ref, grad_o_ref, d_shared_ref, d_value_ref, normed_ref, head_ref, own_ref, end_ref, above_ref, live_ref,
    gain_ref, w_s_ref, w_v_ref, small_ref,
    back_ref, out_s_ref, out_v_ref, out_o_ref, out_r_ref, thin_ref, long_ref,
    side_s, side_in, vector_s, vector_in, grad_s, load_sem, halo_sem, vector_sem, *rest,
):
    window, width = normed_ref.shape
    slots = own_ref.shape[0]
    half = slots // 2
    part = out_s_ref.shape[0]
    many = out_r_ref.shape[0]
    tile = 256
    where = neighbours(devices)
    (o, p, q, c), core_peer, q_peers, p_peers, o_peers = where
    me = lax.axis_index("fsdp")
    outer, side, core = digits(devices)
    owns, rest = rest[:3], rest[3:]
    sems = rest[-4:]

    def distant(source, row, rows, k):
        at = pl.ds(row, rows)

        def other():
            return source.at[:, :, :, 1 - c, at, :]

        def mine(spot, cols):
            return owns[k].at[tuple(spot) + (slice(None), cols)]

        def load():
            return pltpu.make_async_copy(source.at[:, :, :, c, at, :], owns[k], load_sem.at[k])

        return Scatter(devices, where, k, rest[5 * k : 5 * k + 5], sems, other, mine, load)

    def near(j, k):
        def other():
            return grad_s.at[j, :, :, :, 1 - c]

        def mine(spot, cols):
            return grad_s.at[(j,) + tuple(spot) + (c, slice(None), cols)]

        return Scatter(devices, where, k, rest[5 * k : 5 * k + 5], sems, other, mine)

    movers = [
        distant(grad_r_ref, 0, many // 2, 0), distant(grad_r_ref, many // 2, many // 2, 1), distant(grad_o_ref, 0, part, 2),
        near(0, 3), near(1, 4),
    ]
    last = devices - 1
    left, right = lax.rem(me + last, devices), lax.rem(me + 1, devices)
    greet(peers_of(where) + [left, right])
    for k in range(3):
        movers[k].begin()

    def to_left():
        return remote(side_s.at[0], side_in.at[1], halo_sem, (0,), left)

    def to_right():
        return remote(side_s.at[1], side_in.at[0], halo_sem, (1,), right)

    vector_s[...] = small_ref[...]
    gain = gain_ref[...]

    def norm_tile(ref, row, at):
        values = ref[pl.ds(row, tile), :].astype(F32)
        above = dot(d_shared_ref[at, :], w_s_ref[...], NT) + dot(d_value_ref[at, :], w_v_ref[...], NT)
        center = values - jnp.mean(values, axis=1, keepdims=True)
        scale = lax.rsqrt(jnp.mean(center * center, axis=1, keepdims=True) + EPS_NORM)
        center = center * scale
        vector_s[0:1, :] += jnp.sum(above * center, axis=0, keepdims=True)
        vector_s[1:2, :] += jnp.sum(above, axis=0, keepdims=True)
        above = above * gain
        mean = jnp.mean(above, axis=1, keepdims=True)
        along = jnp.mean(above * center, axis=1, keepdims=True)
        return scale * (above - mean - center * along)

    def side_tiles(i, carry):
        row = pl.multiple_of(i * tile, tile)
        side_s[0, pl.ds(row, tile), :] = norm_tile(head_ref, row, pl.ds(row, tile)).astype(BF16)
        at = pl.ds(pl.multiple_of(half + slots + i * tile, tile), tile)
        side_s[1, pl.ds(row, tile), :] = norm_tile(end_ref, row, at).astype(BF16)
        return carry

    lax.fori_loop(0, half // tile, side_tiles, 0)

    @pl.when(me > 0)
    def _():
        to_left().start()

    @pl.when(me < last)
    def _():
        to_right().start()

    movers[0].stage_core()

    def weights(j, ref):
        wide = tile // part

        def strip(i, carry):
            cols = pl.ds(pl.multiple_of(i * tile, tile), tile)
            block = dot(normed_ref[:, cols], ref[...], TN).astype(BF16).reshape(wide // core, core, part, width)
            for k in range(wide // core):
                index = i * (wide // core) + k
                spot = (lax.div(index, side * side), lax.rem(lax.div(index, side), side), lax.rem(index, side))
                grad_s[(j,) + spot] = block[k]
            return carry

        lax.fori_loop(0, width // tile, strip, 0)

    weights(0, d_shared_ref)
    movers[3].begin()
    movers[1].stage_core()
    movers[0].stage_first()
    weights(1, d_value_ref)
    movers[4].begin()
    movers[2].stage_core()
    movers[1].stage_first()
    movers[0].stage_second()

    def own_tiles(i, carry):
        row = pl.multiple_of(i * tile, tile)
        at = pl.ds(pl.multiple_of(half + i * tile, tile), tile)
        here = pl.ds(row, tile)
        total = above_ref[here, :].astype(F32) + norm_tile(own_ref, row, at)
        back_ref[here, :] = (live_ref[here, :] * total).astype(BF16)
        return carry

    lax.fori_loop(0, slots // tile, own_tiles, 0)

    def vector_copies(stage):
        group = ([(0, core_peer)], q_peers, p_peers, o_peers)[stage]
        base = (0, 1, side, 2 * side - 1)[stage]
        return [
            remote(vector_s if stage == 0 else vector_in.at[base - 1], vector_in.at[base + d], vector_sem, (base + d,), device)
            for d, (_, device) in enumerate(group)
        ]

    def vector_stage(stage):
        base = (0, 1, side, 2 * side - 1)[stage]
        copies = vector_copies(stage)
        total = vector_s[...] if stage == 0 else vector_in[base - 1]
        for d, copy in enumerate(copies):
            copy.wait_recv()
            total = total + vector_in[base + d]
        vector_in[base + len(copies) - 1] = total

    for copy in vector_copies(0):
        copy.start()
    movers[3].stage_core()
    movers[2].stage_first()
    movers[1].stage_second()
    out_r_ref[: many // 2, :] = movers[0].stage_third()
    vector_stage(0)
    for copy in vector_copies(1):
        copy.start()
    movers[4].stage_core()
    movers[3].stage_first()
    movers[2].stage_second()
    out_r_ref[many // 2 :, :] = movers[1].stage_third()
    vector_stage(1)
    for copy in vector_copies(2):
        copy.start()
    movers[4].stage_first()
    movers[3].stage_second()
    out_o_ref[...] = movers[2].stage_third()
    vector_stage(2)
    for copy in vector_copies(3):
        copy.start()

    @pl.when(me > 0)
    def _():
        to_right().wait_recv()

    @pl.when(me == 0)
    def _():
        side_in[0] = jnp.zeros((half, width), BF16)

    @pl.when(me < last)
    def _():
        to_left().wait_recv()

    @pl.when(me == last)
    def _():
        side_in[1] = jnp.zeros((half, width), BF16)

    for k in range(2):
        at = slice(k * half, (k + 1) * half)
        back_ref[at, :] = (back_ref[at, :].astype(F32) + side_in[k].astype(F32)).astype(BF16)
    movers[4].stage_second()
    out_s_ref[...] = movers[3].stage_third()
    vector_stage(3)
    out_v_ref[...] = movers[4].stage_third()
    vectors = 2 * side + outer - 3
    total = vector_in[vectors]
    thin_ref[...] = pltpu.roll(total, lax.rem(width - me * part, width), 1)[:, :DH]
    each = long_ref.shape[1]
    long_rows = [total[6 + k : 7 + k, :] for k in range(devices * each // width)]
    mine = lax.div(me * each, width)
    chosen = long_rows[0]
    for k in range(1, len(long_rows)):
        chosen = jnp.where(mine == k, long_rows[k], chosen)
    long_ref[...] = pltpu.roll(chosen, lax.rem(width - lax.rem(me * each, width), width), 1)[:, :each]
    for stage in range(4):
        for copy in vector_copies(stage):
            copy.wait_send()

    @pl.when(me > 0)
    def _():
        to_left().wait_send()

    @pl.when(me < last)
    def _():
        to_right().wait_send()

    for mover in movers:
        mover.sent_first()
        mover.sent_last()


def tail(devices, grad_r, grad_o, d_shared, d_values, normed, head, own, end, above, live, gain, w_s, w_v, small):
    window, width = normed.shape
    slots = own.shape[0]
    outer, side, core = digits(devices)
    part, many = grad_o.shape[1], grad_r.shape[1]
    each = many
    vmem = pl.BlockSpec(memory_space=pltpu.VMEM)
    anywhere = pl.BlockSpec(memory_space=pl.ANY)
    dma = pltpu.SemaphoreType.DMA
    sizes = [many // 2, many // 2, part, part, part]
    scratch = [
        pltpu.VMEM((2, slots // 2, width), BF16), pltpu.VMEM((2, slots // 2, width), BF16),
        pltpu.VMEM((16, width), F32), pltpu.VMEM((2 * side + outer - 2, 16, width), F32),
        pltpu.VMEM((2, outer, side, side, core, part, width), BF16),
        dma((3,)), dma((2, 2)), dma((2, 2 * side + outer - 2)),
    ]
    scratch += [pltpu.VMEM((outer, side, side, rows, width), BF16) for rows in sizes[:3]]
    for rows in sizes:
        scratch += boxes_for(devices, rows, width)
    shape = (outer, side, side, core)
    return pl.pallas_call(
        functools.partial(tail_kernel, devices),
        in_specs=[anywhere, anywhere] + [vmem] * 12,
        out_specs=(vmem,) * 7,
        out_shape=(
            jax.ShapeDtypeStruct((slots, width), BF16),
            jax.ShapeDtypeStruct((part, width), F32),
            jax.ShapeDtypeStruct((part, width), F32),
            jax.ShapeDtypeStruct((part, width), F32),
            jax.ShapeDtypeStruct((many, width), F32),
            jax.ShapeDtypeStruct((16, DH), F32),
            jax.ShapeDtypeStruct((1, each), F32),
        ),
        scratch_shapes=scratch + sems_for(devices, len(sizes)),
        compiler_params=pltpu.CompilerParams(collective_id=4, has_side_effects=True, vmem_limit_bytes=57 << 20),
        name="tail",
    )(
        grad_r.reshape(shape + grad_r.shape[1:]), grad_o.reshape(shape + grad_o.shape[1:]),
        d_shared, d_values, normed, head, own, end, above, live, gain, w_s, w_v, small,
    )


def find_ranks(length_ref, target_ref, bucket_ref, packed_ref, info_ref, before_s):
    devices = length_ref.shape[0]
    lists, slots = bucket_ref.shape
    me = lax.axis_index("fsdp")
    base = me * slots
    window = 2 * slots

    def look(s, carry):
        start, mine, found, one, two = carry
        size = length_ref[s]
        target = target_ref[s]
        middle = start + lax.shift_right_logical(size, 1)
        inside = (middle >= base) & (middle < base + slots)
        offset = start - base + slots // 2
        entry = (offset, offset + size, target)
        first, second = inside & (found == 0), inside & (found == 1)
        one = tuple(jnp.where(first, new, old) for new, old in zip(entry, one))
        two = tuple(jnp.where(second, new, old) for new, old in zip(entry, two))
        return start + size, jnp.where(target == me, size, mine), found + inside.astype(jnp.int32), one, two

    zero = jnp.int32(0)
    nothing = (jnp.int32(window), jnp.int32(window), zero)
    total, mine, found, one, two = lax.fori_loop(0, devices, look, (zero, zero, zero, nothing, nothing))
    for k, value in enumerate((one[0], one[1], two[0], two[1], one[2], two[2], total, found)):
        info_ref[k] = value

    def fill(i, carry):
        at = pl.ds(pl.multiple_of(i * DH, DH), DH)
        first = lax.broadcasted_iota(jnp.int32, (DH, slots), 0) + i * DH
        second = lax.broadcasted_iota(jnp.int32, (DH, slots), 1)
        before_s[at, :] = jnp.where(first < second, 1.0, 0.0).astype(BF16)
        return carry

    lax.fori_loop(0, slots // DH, fill, 0)
    left = lax.broadcasted_iota(jnp.int32, (DH, DH), 0)
    right = lax.broadcasted_iota(jnp.int32, (DH, DH), 1)
    smaller = jnp.where((left // BUCKETS == right // BUCKETS) & (right < left), 1.0, 0.0).astype(BF16)
    many = DH // BUCKETS
    bucket = lax.broadcasted_iota(jnp.int32, (many, BUCKETS, slots), 1)
    live = lax.broadcasted_iota(jnp.int32, (many, BUCKETS, slots), 2) < mine
    ranks = []
    for g in range(lists // many):
        here = (jnp.broadcast_to(bucket_ref[g * many : (g + 1) * many, :][:, None, :], bucket.shape) == bucket) & live
        one_hot = jnp.where(here, 1.0, 0.0)
        flat = one_hot.reshape(DH, slots).astype(BF16)
        offset = jnp.sum(dot(smaller, flat), axis=1, keepdims=True)
        place = (dot(flat, before_s[...]) + offset).reshape(many, BUCKETS, slots)
        ranks.append(jnp.sum(one_hot * place, axis=1))
    rank = jnp.concatenate(ranks, axis=0)
    live = lax.broadcasted_iota(jnp.int32, (lists, slots), 1) < mine
    packed_ref[:lists, :] = jnp.where(live, jnp.floor(rank * (1.0 / GROUP)), FREE).astype(BF16)


def project_kernel(
    info_ref, head_ref, own_ref, tail_ref, gain_ref, shift_ref, w_s_ref, w_v_ref, one_ref, two_ref,
    normed_ref, shared_ref, value_ref, code_ref,
):
    i = pl.program_id(0)
    tile = own_ref.shape[0]
    steps = pl.num_programs(0)

    def go(ref):
        normed = layer_norm(ref[...].astype(F32), gain_ref[...], shift_ref[...]).astype(BF16)
        normed_ref[...] = normed
        shared_ref[...] = dot(normed, w_s_ref[...]).astype(BF16)
        value_ref[...] = dot(normed, w_v_ref[...]).astype(BF16)

    @pl.when(i < steps // 4)
    def _():
        go(head_ref)

    @pl.when((i >= steps // 4) & (i < steps - steps // 4))
    def _():
        go(own_ref)

    @pl.when(i >= steps - steps // 4)
    def _():
        go(tail_ref)

    @pl.when(i == 0)
    def _():
        lists, window = code_ref.shape
        lane = lax.broadcasted_iota(jnp.int32, (lists, window), 1)
        code = jnp.full((lists, window), FREE, F32)
        for k, ref in enumerate((one_ref, two_ref)):
            begin, end = info_ref[2 * k], info_ref[2 * k + 1]
            rows = ref[0].astype(F32)
            moved = pltpu.roll(jnp.concatenate([rows, rows], axis=1), lax.rem(begin, window), 1)
            code = jnp.where((lane >= begin) & (lane < end), moved + 32.0 * k, code)
        code_ref[...] = code.astype(BF16)


def project(info, head, own, tail, gain, shift, w_s, w_v, blocks):
    slots, width = own.shape
    window = 2 * slots
    lists = ROUNDS * HEADS
    tile = 256
    steps = window // tile
    quarter = steps // 4
    rows = pl.BlockSpec((tile, width), lambda i, info: (i, 0))
    vector = pl.BlockSpec((1, width), lambda i, info: (0, 0))
    matrix = pl.BlockSpec((width, width), lambda i, info: (0, 0), pipeline_mode=pl.Buffered(1))
    wide = jax.ShapeDtypeStruct((window, width), BF16)
    return pl.pallas_call(
        project_kernel,
        grid_spec=pltpu.PrefetchScalarGridSpec(
            num_scalar_prefetch=1,
            grid=(steps,),
            in_specs=[
                pl.BlockSpec((tile, width), lambda i, info: (jnp.minimum(i, quarter - 1), 0)),
                pl.BlockSpec((tile, width), lambda i, info: (jnp.clip(i - quarter, 0, 2 * quarter - 1), 0)),
                pl.BlockSpec((tile, width), lambda i, info: (jnp.clip(i - 3 * quarter, 0, quarter - 1), 0)),
                vector, vector, matrix, matrix,
                pl.BlockSpec((1, lists, slots), lambda i, info: (info[4], 0, 0)),
                pl.BlockSpec((1, lists, slots), lambda i, info: (info[5], 0, 0)),
            ],
            out_specs=[rows, rows, rows, pl.BlockSpec((lists, window), lambda i, info: (0, 0))],
        ),
        out_shape=[wide, wide, wide, jax.ShapeDtypeStruct((lists, window), BF16)],
        compiler_params=pltpu.CompilerParams(vmem_limit_bytes=40 << 20),
        name="project",
    )(info, head, own, tail, gain, shift, w_s, w_v, blocks, blocks)


def gather_kernel(devices, arrays, length_ref, target_ref, bucket_ref, vector_ref, rows_ref, *refs):
    sources, outs, (info_ref, head_ref, end_ref) = refs[: arrays - 1], refs[arrays - 1 : 2 * arrays - 1], refs[2 * arrays - 1 : 2 * arrays + 2]
    packed_s, before_s, own_sem, sem_o, sem_a, sem_b, sem_c, halo_sem, edge_sem = refs[2 * arrays + 2 :]
    sources = sources + (packed_s,)
    outer, side, core = digits(devices)
    (o, p, q, c), core_peer, q_peers, p_peers, o_peers = neighbours(devices)
    me = lax.axis_index("fsdp")
    last_device = devices - 1
    left, right = lax.rem(me + last_device, devices), lax.rem(me + 1, devices)
    greet([core_peer] + [d for _, d in q_peers] + [d for _, d in p_peers] + [d for _, d in o_peers] + [left, right])
    half = sources[0].shape[-1] // 2
    border = head_ref.shape[0]

    def to_left():
        return remote(rows_ref.at[:border], end_ref, halo_sem, (0,), left)

    def to_right():
        return remote(rows_ref.at[border:], head_ref, halo_sem, (1,), right)

    def blank(ref):
        return pltpu.make_async_copy(before_s.at[:border], ref, edge_sem.at[0])

    columns = (pl.ds(0, half), pl.ds(half, half))

    locals_, begun, first, second, last = [], {}, {}, {}, {}
    for s in range(arrays):
        if s == arrays - 1:
            find_ranks(length_ref, target_ref, bucket_ref, packed_s, info_ref, before_s)
            packed_s[bucket_ref.shape[0] :, :] = vector_ref[...]
        locals_.append(pltpu.make_async_copy(sources[s], outs[s].at[o, p, q, c], own_sem.at[s]))
        locals_[s].start()
        for d, (k, device) in enumerate(o_peers):
            begun[s, d] = remote(sources[s], outs[s].at[o, p, q, c], sem_o, (s, d), device)
            begun[s, d].start()

    @pl.when(me > 0)
    def _():
        to_left().start()

    @pl.when(me < last_device)
    def _():
        to_right().start()

    before_s[:border, :] = jnp.zeros((border, before_s.shape[1]), BF16)

    @pl.when(me == 0)
    def _():
        blank(head_ref).start()

    @pl.when(me == last_device)
    def _():
        blank(end_ref).start()

    def stage_a(s):
        locals_[s].wait()
        for d in range(outer - 1):
            begun[s, d].wait_recv()
        for h, peers in enumerate((q_peers, p_peers)):
            piece = outs[s].at[:, p, q, c, :, columns[h]]
            for d, (k, device) in enumerate(peers):
                first[s, h, d] = remote(piece, piece, sem_a, (s, h, d), device)
                first[s, h, d].start()

    def stage_b(s):
        for h, peers in enumerate((p_peers, q_peers)):
            for d in range(side - 1):
                first[s, h, d].wait_recv()
            piece = outs[s].at[:, p, :, c, :, columns[h]] if h == 0 else outs[s].at[:, :, q, c, :, columns[h]]
            for d, (k, device) in enumerate(peers):
                second[s, h, d] = remote(piece, piece, sem_b, (s, h, d), device)
                second[s, h, d].start()

    def stage_c(s):
        for h in range(2):
            for d in range(side - 1):
                second[s, h, d].wait_recv()
        piece = outs[s].at[:, :, :, c]
        last[s] = remote(piece, piece, sem_c, (s,), core_peer)
        last[s].start()

    for t in range(arrays + 2):
        if t < arrays:
            stage_a(t)
        if 0 <= t - 1 < arrays:
            stage_b(t - 1)
        if 0 <= t - 2 < arrays:
            stage_c(t - 2)
    for s in range(arrays):
        last[s].wait_recv()

    @pl.when(me > 0)
    def _():
        to_right().wait_recv()
        to_left().wait_send()

    @pl.when(me == 0)
    def _():
        blank(head_ref).wait()

    @pl.when(me < last_device)
    def _():
        to_left().wait_recv()
        to_right().wait_send()

    @pl.when(me == last_device)
    def _():
        blank(end_ref).wait()

    for group in (begun, first, second, last):
        for copy in group.values():
            copy.wait_send()


def gather(devices, lengths, destination, buckets, vectors, rows, arrays):
    outer, side, core = digits(devices)
    lists, slots = buckets.shape
    packed = jax.ShapeDtypeStruct((lists + vectors.shape[0], slots), BF16)
    shapes = [jax.ShapeDtypeStruct(array.shape, array.dtype) for array in arrays] + [packed]
    count = len(shapes)
    dma = pltpu.SemaphoreType.DMA
    anywhere = pl.BlockSpec(memory_space=pl.ANY)
    smem = pl.BlockSpec(memory_space=pltpu.SMEM)
    vmem = pl.BlockSpec(memory_space=pltpu.VMEM)
    outs = pl.pallas_call(
        functools.partial(gather_kernel, devices, count),
        out_shape=tuple(jax.ShapeDtypeStruct((outer, side, side, core) + shape.shape, shape.dtype) for shape in shapes)
        + (jax.ShapeDtypeStruct((8,), jnp.int32),)
        + (jax.ShapeDtypeStruct((slots // 2, rows.shape[1]), BF16),) * 2,
        in_specs=[smem, smem, vmem, vmem] + [anywhere] * count,
        out_specs=(anywhere,) * count + (smem, anywhere, anywhere),
        scratch_shapes=[
            pltpu.VMEM(packed.shape, BF16), pltpu.VMEM((slots, slots), BF16),
            dma((count,)), dma((2, count, outer - 1)), dma((2, count, 2, side - 1)), dma((2, count, 2, side - 1)), dma((2, count)),
            dma((2, 2)), dma((1,)),
        ],
        compiler_params=pltpu.CompilerParams(collective_id=2, has_side_effects=True, vmem_limit_bytes=32 << 20),
        name="gather",
    )(lengths, destination, buckets, vectors, rows, *arrays)
    return [out.reshape((devices,) + shape.shape) for out, shape in zip(outs, shapes)] + list(outs[count:])


def body(
    input_one, input_two, upstream_one, upstream_two, lengths, destination, buckets,
    w_shared, w_value, w_output, w_expand, w_reduce,
    gain_attend, shift_attend, gain_mixing, shift_mixing, bias_output, bias_expand, bias_reduce,
):
    devices = lax.axis_size("fsdp")
    me = lax.axis_index("fsdp")
    slots, width = input_one.shape
    half = slots // 2
    window = 2 * slots
    part = w_shared.shape[0]
    hidden = w_expand.shape[1]
    sides = hidden // width
    base = me * slots
    lists = ROUNDS * HEADS
    spot = jnp.arange(width, dtype=jnp.int32)
    short = jnp.stack([gain_attend, shift_attend, gain_mixing, shift_mixing, bias_output, bias_reduce])
    short = jnp.where(spot // part == me, jnp.tile(short, (1, devices)), 0.0)
    many = hidden // devices
    long = jnp.tile(bias_expand, width // many)[None]
    long = jnp.where(spot[None] // many + (width // many) * jnp.arange(sides, dtype=jnp.int32)[:, None] == me, long, 0.0)
    vectors = jnp.concatenate([short, long], axis=0)
    high = lax.reduce_precision(vectors, 8, 7)
    count = vectors.shape[0]
    packed = jnp.concatenate(
        [high.astype(BF16), (vectors - high).astype(BF16), jnp.zeros((24 - 2 * count, width), BF16)], axis=0
    )
    second_gather = lax.all_gather(
        jnp.concatenate(
            [w_reduce, w_output] + [w_expand[:, k * width : (k + 1) * width] for k in range(sides)], axis=0
        ),
        "fsdp", axis=0, tiled=False,
    )
    full_shared, full_value, packed, info, two_head, two_tail = gather(
        devices, lengths, destination, buckets[0], packed, input_two, [w_shared, w_value]
    )
    full_shared, full_value = full_shared.reshape(width, width), full_value.reshape(width, width)
    vectors = jnp.sum(packed[:, lists : lists + 2 * count].astype(F32), axis=0)
    vectors = vectors[:count] + vectors[count:]
    gain_a, shift_a, gain_m, shift_m, bias_o, bias_r = (vectors[k : k + 1] for k in range(6))
    bias_e = vectors[6:].reshape(1, hidden)
    full_output = second_gather[:, sides * part : (sides + 1) * part].reshape(width, width)
    lane = jnp.arange(HEADS * DH, dtype=jnp.int32)
    row = jnp.arange(lists, dtype=jnp.int32)[:, None]
    spread = (row == ((lane % 64) // 16) * HEADS + lane // DH).astype(BF16)

    live = ((base + jnp.arange(slots, dtype=jnp.int32)) < info[6]).astype(F32)[:, None]
    normed, shared, values, code = project(
        info, two_head, input_two, two_tail, gain_a, shift_a, full_shared, full_value, packed
    )
    combined_window, lse, lone = attend(info, shared, values, code, spread)
    combined, out_one, second, d_reduce = join(
        devices, combined_window, input_one, upstream_two, live, second_gather, bias_o, gain_m, shift_m, part, sides
    )
    mixed, d_second, grad_reduce, grad_bias_expand, grad_expand, grad_bias_reduce = mixing(
        devices, second, d_reduce, second_gather, bias_e, bias_r, part
    )
    d_combined, grad_one, result_one, result_two, grad_output, small = turn(
        devices, out_one, d_second, mixed, input_two, upstream_one, combined, live, gain_m, full_output, grad_bias_reduce, grad_bias_expand
    )
    d_shared, d_values = attend_back(
        info, shared, values, code, spread, combined_window, d_combined, lse, lone
    )
    grad_two, grad_shared, grad_value, grad_output, grad_reduce, thin, long = tail(
        devices, grad_reduce, grad_output, d_shared, d_values, normed,
        two_head, input_two, two_tail, upstream_two, live, gain_a, full_shared, full_value, small,
    )
    return (
        result_one,
        result_two,
        grad_one,
        grad_two,
        grad_shared,
        grad_value,
        grad_output,
        jnp.concatenate([grad_expand[k * part : (k + 1) * part] for k in range(sides)], axis=1),
        grad_reduce,
        thin[0, :part],
        thin[1, :part],
        thin[2, :part],
        thin[3, :part],
        thin[4, :part],
        long.reshape(-1),
        thin[5, :part],
    )


def solution(mesh):
    rows, flat, whole = P("fsdp", None), P("fsdp"), P()
    return jax.shard_map(
        body,
        mesh=mesh,
        in_specs=(rows,) * 4 + (whole, whole, P("fsdp", None, None)) + (rows,) * 5 + (flat,) * 7,
        out_specs=(rows,) * 9 + (flat,) * 7,
        check_vma=False,
    )
```

```python
import functools
import math

import jax
import jax.numpy as jnp
from jax import lax
from jax.experimental import pallas as pl
from jax.experimental.pallas import tpu as pltpu
from jax.sharding import PartitionSpec as P

HEADS = 8
DH = 128
GROUP = 64
ROUNDS = 4
BUCKETS = 32
EPS_NORM = 1e-05
EPS_UNIT = 1e-06
LOG2E = math.log2(math.e)
SELF2 = -100000.0 * LOG2E
NEG = -1e30
SCALE = 1.0 / math.sqrt(DH)
TILE = 512
HALF = TILE // 2
KEYS = 256
MANY = TILE // KEYS
STEP = 128.0
SHIFT = 1.5 * 2.0**30
TAME = 3000.0
PAIR = 4
FREE = 99.0
STRIP = 512
AFTER = (2, 4, 6, 8)
CURVE = math.sqrt(2.0 / math.pi)
MESH = pl.DeviceIdType.MESH

NT = (((1,), (1,)), ((), ()))
NN = (((1,), (0,)), ((), ()))
TN = (((0,), (0,)), ((), ()))
F32 = jnp.float32
BF16 = jnp.bfloat16


def dot(a, b, dims=NN):
    return lax.dot_general(a, b, dims, preferred_element_type=F32)


def layer_norm(values, gain, shift):
    center = values - jnp.mean(values, axis=-1, keepdims=True)
    spread = jnp.mean(center * center, axis=-1, keepdims=True)
    return center * lax.rsqrt(spread + EPS_NORM) * gain + shift


def prepare(q, code_ref, spread, ask_s, key_s, h, at):
    lane = lax.broadcasted_iota(jnp.int32, (TILE, DH), 1)
    target = ((lane // 64) * 32 + lane % 16).astype(F32)
    wide = q.astype(F32)
    square = jnp.sum(wide * wide, axis=1, keepdims=True)
    code = dot(code_ref[:, at], spread, TN)
    here = code == target
    ask_s[h, at, :DH] = q
    ask_s[h, at, DH:] = jnp.where(here, STEP, 0.0).astype(BF16)
    key_s[h, at, :DH] = (wide * (lax.rsqrt(square + EPS_UNIT) * (SCALE * LOG2E))).astype(BF16)
    key_s[h, at, DH:] = jnp.where(here | (code + 1.0 == target), 1.0, 0.0).astype(BF16)
    return jnp.max(square)


def lowest(info_ref, i):
    start, stop = i * TILE, (i + 1) * TILE
    one = (info_ref[0] < stop) & (info_ref[1] > start)
    two = (info_ref[2] < stop) & (info_ref[3] > start)
    begin = jnp.where(one, info_ref[0], jnp.where(two, info_ref[2], stop))
    return lax.div(begin, KEYS)


def tile_rows(i):
    return pl.ds(pl.multiple_of(i * TILE, TILE), TILE)


def halves(i):
    start = i * TILE
    return [((0, pl.multiple_of(start, HALF), pl.multiple_of(start, HALF)), HALF),
            ((HALF, pl.multiple_of(start + HALF, HALF), pl.multiple_of(start, HALF)), TILE)]


def part_of(both):
    count = (both + SHIFT) - SHIFT
    return count, both - count


def apart(left, right):
    return dot(left[:, DH:], right[:, DH:], NT), dot(left[:, :DH], right[:, :DH], NT)


def attend_kernel(low_ref, q_ref, v_ref, code_ref, spread_ref, comb_ref, lse_ref, lone_ref, ask_s, key_s, more_s, acc_s, top_s):
    rows = q_ref.shape[0]
    tiles = rows // TILE
    heads = [slice(h * DH, (h + 1) * DH) for h in range(PAIR)]

    def ready(i, largest):
        def fill():
            most = jnp.float32(0.0)
            at = tile_rows(i)
            for h, cols in enumerate(heads):
                most = jnp.maximum(most, prepare(q_ref[at, cols], code_ref, spread_ref[:, cols], ask_s, key_s, h, at))
                more_s[h, at, :DH] = v_ref[at, cols]
                more_s[h, at, DH:] = jnp.ones((TILE, DH), BF16)
            return most

        return jnp.maximum(largest, lax.cond(lowest(low_ref, i) <= (i + 1) * MANY - 1, fill, lambda: jnp.float32(0.0)))

    largest = lax.fori_loop(0, tiles, ready, jnp.float32(0.0))
    tame = largest * (SCALE * LOG2E) ** 2 < TAME
    ask_at = lax.broadcasted_iota(jnp.int32, (TILE, TILE), 0)
    key_at = lax.broadcasted_iota(jnp.int32, (TILE, TILE), 1)

    def finish(h, cols, at, top):
        total = acc_s[h, :, DH:]
        some = total > 0.0
        safe = jnp.where(some, total, 1.0)
        inverse = jnp.where(some, 1.0 / safe, 0.0)
        comb_ref[at, cols] = (acc_s[h, :, :DH] * inverse).astype(BF16)
        lse_ref[h, :, at] = (jnp.log2(safe) + top).T[:1]

    def rows_of(i, carry):
        at = tile_rows(i)
        low = lowest(low_ref, i)

        @pl.when((low < (i + 1) * MANY) & tame)
        def _():
            for h in range(PAIR):
                acc_s[h] = jnp.zeros((TILE, 2 * DH), F32)

            def step(j, carry):
                keys = pl.ds(pl.multiple_of(j * KEYS, KEYS), KEYS)
                for h in range(PAIR):
                    count, score = part_of(dot(ask_s[h, at, :], key_s[h, keys, :], NT))
                    acc_s[h] += dot((count * jnp.exp2(score)).astype(BF16), more_s[h, keys, :])
                return carry

            lax.fori_loop(low, i * MANY, step, 0)
            for h, cols in enumerate(heads):
                for asks, span in halves(i):
                    here = pl.ds(asks[0], HALF)
                    there = pl.ds(asks[1], HALF)
                    keys = pl.ds(asks[2], span)
                    key_at = lax.broadcasted_iota(jnp.int32, (HALF, span), 1)
                    ask_at = lax.broadcasted_iota(jnp.int32, (HALF, span), 0) + (span - HALF)
                    count, score = part_of(dot(ask_s[h, there, :], key_s[h, keys, :], NT))
                    prob = jnp.where(key_at < ask_at, count * jnp.exp2(score), 0.0).astype(BF16)
                    acc_s[h, here, :] += dot(prob, more_s[h, keys, :])
                    active = jnp.max(jnp.where(key_at == ask_at, count, 0.0), axis=1, keepdims=True) > 0.0
                    lone = jnp.where(active & (acc_s[h, here, DH:] == 0.0), 1.0, 0.0)
                    acc_s[h, here, :DH] += lone * v_ref[there, cols].astype(F32)
                    acc_s[h, here, DH:] += lone
                    lone_ref[h, :, there] = lone.T[:1]
                finish(h, cols, at, 0.0)

        @pl.when((low < (i + 1) * MANY) & jnp.logical_not(tame))
        def _():
            for h, cols in enumerate(heads):
                count, score = apart(ask_s[h, at, :], key_s[h, at, :])
                score = jnp.where(key_at == ask_at, SELF2, score)
                score = jnp.where((key_at <= ask_at) & (count > 0.5), score, NEG)
                top = jnp.max(score, axis=1, keepdims=True)
                prob = count * jnp.exp2(score - top)
                acc_s[h] = dot(prob.astype(BF16), more_s[h, at, :])
                top_s[h] = jnp.broadcast_to(top, (TILE, DH))

                def step(j, carry):
                    keys = pl.ds(pl.multiple_of(j * KEYS, KEYS), KEYS)
                    count, score = apart(ask_s[h, at, :], key_s[h, keys, :])
                    score = jnp.where(count > 0.5, score, NEG)
                    top = top_s[h]
                    newer = jnp.maximum(top, jnp.max(score, axis=1, keepdims=True))
                    fade = jnp.exp2(top - newer)
                    prob = count * jnp.exp2(score - newer[:, :1])
                    acc_s[h] = acc_s[h] * jnp.concatenate([fade, fade], axis=1) + dot(prob.astype(BF16), more_s[h, keys, :])
                    top_s[h] = newer
                    return carry

                lax.fori_loop(low, i * MANY, step, 0)
                total = acc_s[h, :, DH:]
                own = STEP * ROUNDS * jnp.exp2(SELF2 - jnp.maximum(top_s[h], SELF2))
                lone_ref[h, :, at] = jnp.where(total > 0.0, own / jnp.where(total > 0.0, total, 1.0), 0.0).T[:1]
                finish(h, cols, at, top_s[h])

        @pl.when(low >= (i + 1) * MANY)
        def _():
            comb_ref[at, :] = jnp.zeros((TILE, PAIR * DH), BF16)
            for h in range(PAIR):
                lse_ref[h, :, at] = jnp.zeros((1, TILE), F32)
                lone_ref[h, :, at] = jnp.zeros((1, TILE), F32)

        return carry

    lax.fori_loop(0, tiles, rows_of, 0)


def back_kernel(
    low_ref, q_ref, v_ref, code_ref, spread_ref, comb_ref, above_ref, lse_ref, lone_ref, *rest,
):
    count = (len(rest) - 8) // 2
    sources, (dq_ref, dv_ref, *targets) = rest[:count], rest[count : 2 * count + 2]
    ask_s, key_s, dunit_s, dvalue_s, dask_s, sem = rest[2 * count + 2 :]
    rows = q_ref.shape[0]
    width = q_ref.shape[1] * (HEADS // PAIR)

    def copies():
        started = []
        for source, target in zip(sources, targets):
            for k in range(target.shape[1] // width):
                part = source.shape[0] * width // target.shape[1]
                started.append(
                    pltpu.make_async_copy(
                        source.at[k * part : (k + 1) * part, :], target.at[:, k * width : (k + 1) * width], sem.at[len(started)]
                    )
                )
        return started

    @pl.when(pl.program_id(0) == 0)
    def _():
        for copy in copies():
            copy.start()

    @pl.when(pl.program_id(0) == pl.num_programs(0) - 1)
    def _():
        for copy in copies():
            copy.wait()

    tiles = rows // TILE
    heads = [slice(h * DH, (h + 1) * DH) for h in range(PAIR)]

    def ready(i, largest):
        def fill():
            most = jnp.float32(0.0)
            at = tile_rows(i)
            for h, cols in enumerate(heads):
                most = jnp.maximum(most, prepare(q_ref[at, cols], code_ref, spread_ref[:, cols], ask_s, key_s, h, at))
                for total in (dunit_s, dvalue_s, dask_s):
                    total[h, at, :] = jnp.zeros((TILE, DH), F32)
            return most

        return jnp.maximum(largest, lax.cond(lowest(low_ref, i) <= (i + 1) * MANY - 1, fill, lambda: jnp.float32(0.0)))

    largest = lax.fori_loop(0, tiles, ready, jnp.float32(0.0))
    tame = largest * (SCALE * LOG2E) ** 2 < TAME

    def pass_over(i, low, split):
        at = tile_rows(i)
        deltas = []
        for h, cols in enumerate(heads):
            mixed = above_ref[at, cols].astype(F32) * comb_ref[at, cols].astype(F32)
            deltas.append(jnp.sum(mixed.T, axis=0, keepdims=True))

        def step(j, carry):
            keys = pl.ds(pl.multiple_of(j * KEYS, KEYS), KEYS)
            for h, cols in enumerate(heads):
                q, above, unit = q_ref[at, cols], above_ref[at, cols], key_s[h, keys, :DH]
                count, score = split(key_s[h, keys, :], ask_s[h, at, :])
                d_prob = dot(v_ref[keys, cols], above, NT)
                prob = count * jnp.exp2(score - lse_ref[h, :, at])
                d_score = (prob * (d_prob - carry[h])).astype(BF16)
                dvalue_s[h, keys, :] += dot(prob.astype(BF16), above)
                dunit_s[h, keys, :] += dot(d_score, q)
                dask_s[h, at, :] += dot(d_score, unit, TN)
            return carry

        deltas = lax.fori_loop(low, i * MANY, step, tuple(deltas))
        for h, cols in enumerate(heads):
            for asks, span in halves(i):
                there = pl.ds(asks[1], HALF)
                keys = pl.ds(asks[2], span)
                key_at = lax.broadcasted_iota(jnp.int32, (span, HALF), 0)
                ask_at = lax.broadcasted_iota(jnp.int32, (span, HALF), 1) + (span - HALF)
                q, above, unit = q_ref[there, cols], above_ref[there, cols], key_s[h, keys, :DH]
                count, score = split(key_s[h, keys, :], ask_s[h, there, :])
                d_prob = dot(v_ref[keys, cols], above, NT)
                prob = count * jnp.exp2(score - lse_ref[h, :, there])
                prob = jnp.where(key_at < ask_at, prob, 0.0)
                d_score = (prob * (d_prob - deltas[h][:, asks[0] : asks[0] + HALF])).astype(BF16)
                prob = jnp.where(key_at == ask_at, lone_ref[h, :, there], prob).astype(BF16)
                dvalue_s[h, keys, :] += dot(prob, above)
                dunit_s[h, keys, :] += dot(d_score, q)
                dask_s[h, there, :] += dot(d_score, unit, TN)

    def together(left, right):
        return part_of(dot(left, right, NT))

    def guarded(left, right):
        count, score = apart(left, right)
        return count, jnp.where(count > 0.5, score, NEG)

    def rows_of(i, carry):
        low = lowest(low_ref, i)

        @pl.when((low < (i + 1) * MANY) & tame)
        def _():
            pass_over(i, low, together)

        @pl.when((low < (i + 1) * MANY) & jnp.logical_not(tame))
        def _():
            pass_over(i, low, guarded)

        return carry

    lax.fori_loop(0, tiles, rows_of, 0)

    def close(i, carry):
        at = tile_rows(i)

        @pl.when(lowest(low_ref, i) <= (i + 1) * MANY - 1)
        def _():
            for h, cols in enumerate(heads):
                q = q_ref[at, cols].astype(F32)
                norm = lax.rsqrt(jnp.sum(q * q, axis=1, keepdims=True) + EPS_UNIT)
                d_unit = dunit_s[h, at, :] * SCALE
                along = jnp.sum(q * d_unit, axis=1, keepdims=True)
                d_q = dask_s[h, at, :] * (1.0 / LOG2E) + d_unit * norm - q * (norm * norm * norm * along)
                dq_ref[at, cols] = d_q.astype(BF16)
                dv_ref[at, cols] = dvalue_s[h, at, :].astype(BF16)

        @pl.when(lowest(low_ref, i) > (i + 1) * MANY - 1)
        def _():
            dq_ref[at, :] = jnp.zeros((TILE, PAIR * DH), BF16)
            dv_ref[at, :] = jnp.zeros((TILE, PAIR * DH), BF16)

        return carry

    lax.fori_loop(0, tiles, close, 0)


def head_specs(rows):
    by_head = pl.BlockSpec((rows, PAIR * DH), lambda h, low: (0, h))
    code = pl.BlockSpec((ROUNDS * HEADS, rows), lambda h, low: (0, 0))
    spread = pl.BlockSpec((ROUNDS * HEADS, PAIR * DH), lambda h, low: (0, h))
    stat = pl.BlockSpec((PAIR, 1, rows), lambda h, low: (h, 0, 0))
    return by_head, code, spread, stat


def attend(low, shared, values, code, spread):
    rows = shared.shape[0]
    by_head, code_spec, spread_spec, stat = head_specs(rows)
    wide = jax.ShapeDtypeStruct((rows, HEADS * DH), BF16)
    thin = jax.ShapeDtypeStruct((HEADS, 1, rows), F32)
    return pl.pallas_call(
        attend_kernel,
        grid_spec=pltpu.PrefetchScalarGridSpec(
            num_scalar_prefetch=1,
            grid=(HEADS // PAIR,),
            in_specs=[by_head, by_head, code_spec, spread_spec],
            out_specs=[by_head, stat, stat],
            scratch_shapes=[pltpu.VMEM((PAIR, rows, 2 * DH), BF16)] * 3
            + [pltpu.VMEM((PAIR, TILE, 2 * DH), F32), pltpu.VMEM((PAIR, TILE, DH), F32)],
        ),
        out_shape=(wide, thin, thin),
        compiler_params=pltpu.CompilerParams(vmem_limit_bytes=57 << 20),
        name="attend",
        cost_estimate=pl.CostEstimate(
            flops=HEADS * 20 * 3 * 2 * TILE * TILE * DH, bytes_accessed=rows * HEADS * DH * 6, transcendentals=HEADS * 20 * TILE * TILE
        ),
    )(low, shared, values, code, spread)


def attend_back(low, shared, values, code, spread, combined, above, lse, lone, sources, shapes):
    rows = shared.shape[0]
    by_head, code_spec, spread_spec, stat = head_specs(rows)
    wide = jax.ShapeDtypeStruct((rows, HEADS * DH), BF16)
    return pl.pallas_call(
        back_kernel,
        grid_spec=pltpu.PrefetchScalarGridSpec(
            num_scalar_prefetch=1,
            grid=(HEADS // PAIR,),
            in_specs=[by_head, by_head, code_spec, spread_spec, by_head, by_head, stat, stat]
            + [pl.BlockSpec(memory_space=pl.ANY)] * len(sources),
            out_specs=[by_head, by_head] + [pl.BlockSpec(memory_space=pltpu.HBM)] * len(sources),
            scratch_shapes=[pltpu.VMEM((PAIR, rows, 2 * DH), BF16)] * 2 + [pltpu.VMEM((PAIR, rows, DH), F32)] * 3
            + [pltpu.SemaphoreType.DMA((16,))],
        ),
        out_shape=(wide, wide) + tuple(jax.ShapeDtypeStruct(shape, source.dtype) for shape, source in zip(shapes, sources)),
        compiler_params=pltpu.CompilerParams(vmem_limit_bytes=57 << 20),
        name="attend_back",
        cost_estimate=pl.CostEstimate(
            flops=HEADS * 20 * 6 * 2 * TILE * TILE * DH, bytes_accessed=rows * HEADS * DH * 12, transcendentals=HEADS * 20 * TILE * TILE
        ),
    )(low, shared, values, code, spread, combined, above, lse, lone, *sources)


def digits(devices):
    side = 2
    while 8 * side * side < devices:
        side += 1
    assert 8 * side * side == devices, devices
    return 4, side, 2


def neighbours(devices):
    outer, side, core = digits(devices)
    me = lax.axis_index("fsdp")
    c = lax.rem(me, core)
    q = lax.rem(lax.div(me, core), side)
    p = lax.rem(lax.div(me, core * side), side)
    o = lax.div(me, core * side * side)

    def at(o_, p_, q_, c_):
        return ((o_ * side + p_) * side + q_) * core + c_

    core_peer = at(o, p, q, 1 - c)
    q_peers = [(k, at(o, p, k, c)) for k in (lax.rem(q + d, side) for d in range(1, side))]
    p_peers = [(k, at(o, k, q, c)) for k in (lax.rem(p + d, side) for d in range(1, side))]
    o_peers = [(k, at(k, p, q, c)) for k in (lax.rem(o + d, outer) for d in range(1, outer))]
    return (o, p, q, c), core_peer, q_peers, p_peers, o_peers


def peers_of(where):
    return [where[1]] + [device for group in where[2:] for _, device in group]


def greet(peers):
    barrier = pltpu.get_barrier_semaphore()
    for peer in peers:
        pl.semaphore_signal(barrier, inc=1, device_id=(peer,), device_id_type=MESH)
    pl.semaphore_wait(barrier, len(peers))


def remote(src, dst, sems, slot, device):
    return pltpu.make_async_remote_copy(
        src_ref=src, dst_ref=dst, send_sem=sems.at[(0,) + slot], recv_sem=sems.at[(1,) + slot],
        device_id=(device,), device_id_type=MESH,
    )


class Scatter:
    def __init__(self, devices, where, slot, boxes, sems, other, mine, load=None):
        self.outer, self.side, _ = digits(devices)
        (self.o, self.p, self.q, self.c), self.core_peer, self.q_peers, self.p_peers, self.o_peers = where
        self.slot = slot
        self.box_c, box_a0, box_a1, self.box_b, self.box_o = boxes
        self.box_a = (box_a0, box_a1)
        self.sem_c, self.sem_a, self.sem_b, self.sem_o = sems
        self.other, self.mine, self.load = other, mine, load
        half = self.box_o.shape[-1] // 2
        self.columns = (pl.ds(0, half), pl.ds(half, half))

    def core(self):
        return remote(self.other(), self.box_c, self.sem_c, (self.slot,), self.core_peer)

    def first(self, h, d):
        k, device = (self.q_peers, self.p_peers)[h][d]
        spot = (slice(None), slice(None), k) if h == 0 else (slice(None), k, slice(None))
        return remote(self.mine(spot, self.columns[h]), self.box_a[h].at[d], self.sem_a, (self.slot, h, d), device)

    def second(self, h, d):
        k, device = (self.p_peers, self.q_peers)[h][d]
        return remote(
            self.box_a[h].at[0, :, k], self.box_b.at[d, :, :, self.columns[h]], self.sem_b, (self.slot, h, d), device
        )

    def third(self, d):
        k, device = self.o_peers[d]
        return remote(self.box_b.at[0, k], self.box_o.at[d], self.sem_o, (self.slot, d), device)

    def begin(self):
        self.core().start()
        if self.load is not None:
            self.load().start()

    def stage_core(self):
        if self.load is not None:
            self.load().wait()
        self.core().wait_recv()
        side = self.side

        def add(i, carry):
            spot = (lax.div(i, side * side), lax.rem(lax.div(i, side), side), lax.rem(i, side))
            ref = self.mine(spot, slice(None))
            ref[...] = ref[...] + self.box_c[spot]
            return carry

        lax.fori_loop(0, self.outer * side * side, add, 0)
        for h in range(2):
            for d in range(side - 1):
                self.first(h, d).start()

    def stage_first(self):
        side = self.side
        for h in range(2):
            box = self.box_a[h]
            for d in range(side - 1):
                self.first(h, d).wait_recv()

            def add(i, carry):
                a, b = lax.div(i, side), lax.rem(i, side)
                total = self.mine((a, b, self.q) if h == 0 else (a, self.p, b), self.columns[h])[...]
                for d in range(side - 1):
                    total = total + box[d, a, b]
                box[0, a, b] = total
                return carry

            lax.fori_loop(0, self.outer * side, add, 0)
            for d in range(side - 1):
                self.second(h, d).start()

    def stage_second(self):
        box = self.box_b
        for h in range(2):
            k = self.p if h == 0 else self.q
            for d in range(self.side - 1):
                self.second(h, d).wait_recv()

            def add(a, carry):
                total = self.box_a[h][0, a, k]
                for d in range(self.side - 1):
                    total = total + box[d, a, :, self.columns[h]]
                box[0, a, :, self.columns[h]] = total
                return carry

            lax.fori_loop(0, self.outer, add, 0)
        for d in range(self.outer - 1):
            self.third(d).start()

    def stage_third(self):
        total = self.box_b[0, self.o].astype(F32)
        for d in range(self.outer - 1):
            self.third(d).wait_recv()
            total = total + self.box_o[d].astype(F32)
        return total

    def sent_first(self):
        self.core().wait_send()
        for h in range(2):
            for d in range(self.side - 1):
                self.first(h, d).wait_send()

    def sent_last(self):
        for h in range(2):
            for d in range(self.side - 1):
                self.second(h, d).wait_send()
        for d in range(self.outer - 1):
            self.third(d).wait_send()


def boxes_for(devices, rows, width):
    outer, side, _ = digits(devices)
    half = width // 2
    return [
        pltpu.VMEM((outer, side, side, rows, width), BF16),
        pltpu.VMEM((side - 1, outer, side, rows, half), BF16),
        pltpu.VMEM((side - 1, outer, side, rows, half), BF16),
        pltpu.VMEM((side - 1, outer, rows, width), BF16),
        pltpu.VMEM((outer - 1, rows, width), BF16),
    ]


def sems_for(devices, count):
    outer, side, _ = digits(devices)
    dma = pltpu.SemaphoreType.DMA
    return [dma((2, count)), dma((2, count, 2, side - 1)), dma((2, count, 2, side - 1)), dma((2, count, outer - 1))]


def mixing_kernel(
    devices, second_ref, above_ref, expand_ref, reduce_ref, bias_e_ref, bias_r_ref,
    out_ref, back_ref, grad_r_ref, grad_b_ref, grad_e_ref, above_b_ref, act_s, pre_s, grad_s, *rest,
):
    step = pl.program_id(0)
    rows, width = second_ref.shape
    strip = act_s.shape[1]
    per = width // strip
    slices = (len(rest) - 4) // 5
    sems = rest[5 * slices :]
    where = neighbours(devices)
    (o, p, q, c), core_peer, q_peers, p_peers, o_peers = where
    part = grad_s.shape[-2]

    def mover(k):
        def other():
            return grad_s.at[k % 2, :, :, :, 1 - c]

        def mine(spot, cols):
            return grad_s.at[(k % 2,) + tuple(spot) + (c, slice(None), cols)]

        return Scatter(devices, where, k, rest[5 * k : 5 * k + 5], sems, other, mine)

    movers = [mover(k) for k in range(slices)]
    w_e = expand_ref[...].reshape(width, strip)
    w_r = reduce_ref[...].reshape(strip, width)

    @pl.when(step == 0)
    def _():
        greet(peers_of(where))
        out_ref[...] = jnp.broadcast_to(bias_r_ref[...], out_ref.shape)
        back_ref[...] = jnp.zeros(back_ref.shape, F32)
        above_b_ref[...] = jnp.sum(above_ref[...].astype(F32), axis=0, keepdims=True)

    def close(k):
        grad_e_ref[k * part : (k + 1) * part, :] = movers[k].stage_third()

    final = slices * per - 1
    timed, late = [], []
    for k in range(slices):
        begun = 2 * ((k + 1) * per - 1) + 1
        for after, action in zip(
            AFTER, (movers[k].stage_core, movers[k].stage_first, movers[k].stage_second, functools.partial(close, k))
        ):
            if begun + after > 2 * final + 1:
                late.append((begun + after, -k, action))
            else:
                timed.append((begun + after, action))

    def stages(point):
        for when, action in timed:
            if when % 2 == point:
                pl.when(step == when // 2)(action)

    pre = dot(second_ref[...], w_e) + bias_e_ref[...]
    square = pre * pre
    curve = jnp.tanh(CURVE * pre * (1.0 + 0.044715 * square))
    hinge = 0.5 * (1.0 + curve)
    act_s[...] = (pre * hinge).astype(BF16)
    slope = hinge + 0.5 * pre * (1.0 - curve * curve) * (CURVE * (1.0 + 3 * 0.044715 * square))
    d_pre = (dot(above_ref[...], w_r, NT) * slope).astype(BF16)
    pre_s[...] = d_pre
    grad_b_ref[...] = jnp.sum(d_pre.astype(F32), axis=0, keepdims=True)
    stages(0)
    out_ref[...] += dot(act_s[...], w_r)
    back_ref[...] += dot(d_pre, w_e, NT)
    grad_r_ref[...] = dot(act_s[...], above_ref[...], TN).astype(BF16).reshape(grad_r_ref.shape)
    grad_e = dot(second_ref[...], pre_s[...], TN).astype(BF16)
    for k in range(slices):
        for j in range(per):
            @pl.when(step == k * per + j)
            def _():
                if j == 0 and k >= 2:
                    movers[k - 2].sent_first()
                grad_s[k % 2, :, :, :, :, :, j * strip : (j + 1) * strip] = grad_e.reshape(grad_s.shape[1:-1] + (strip,))
                if j == per - 1:
                    movers[k].begin()

    stages(1)

    @pl.when(step == final)
    def _():
        for *_, action in sorted(late, key=lambda entry: entry[:2]):
            action()
        for k in range(max(0, slices - 2), slices):
            movers[k].sent_first()
        for k in range(slices):
            movers[k].sent_last()


def mixing(devices, second, above, gathered, bias_e, bias_r, part):
    rows, width = second.shape
    hidden = bias_e.shape[1]
    many = hidden // devices
    sides = hidden // width
    strip = STRIP
    per = width // strip
    outer, side, core = digits(devices)
    fixed = pl.BlockSpec((rows, width), lambda i: (0, 0), pipeline_mode=pl.Buffered(1))
    whole = pl.BlockSpec(memory_space=pltpu.VMEM)
    scratch = [pltpu.VMEM((rows, strip), BF16)] * 2 + [pltpu.VMEM((2, outer, side, side, core, part, width), BF16)]
    for k in range(sides):
        scratch += boxes_for(devices, part, width)
    return pl.pallas_call(
        functools.partial(mixing_kernel, devices),
        grid=(hidden // strip,),
        in_specs=[
            fixed, fixed,
            pl.BlockSpec((devices, part, strip), lambda i: (0, many // part + 1 + i // per, i % per)),
            pl.BlockSpec((strip // many, many, width), lambda i: (i, 0, 0)),
            pl.BlockSpec((1, strip), lambda i: (0, i)),
            pl.BlockSpec((1, width), lambda i: (0, 0)),
        ],
        out_specs=[
            fixed,
            fixed,
            pl.BlockSpec((strip // many, many, width), lambda i: (i, 0, 0)),
            pl.BlockSpec((1, strip), lambda i: (0, i)),
            pl.BlockSpec((sides * part, width), lambda i: (0, 0)),
            pl.BlockSpec((1, width), lambda i: (0, 0)),
        ],
        out_shape=[
            jax.ShapeDtypeStruct((rows, width), F32),
            jax.ShapeDtypeStruct((rows, width), F32),
            jax.ShapeDtypeStruct((devices, many, width), BF16),
            jax.ShapeDtypeStruct((1, hidden), F32),
            jax.ShapeDtypeStruct((sides * part, width), F32),
            jax.ShapeDtypeStruct((1, width), F32),
        ],
        scratch_shapes=scratch + sems_for(devices, sides),
        compiler_params=pltpu.CompilerParams(collective_id=3, has_side_effects=True, vmem_limit_bytes=57 << 20),
        name="mixing",
    )(second, above, gathered, gathered, bias_e, bias_r)


def join_kernel(
    devices, window_ref, first_ref, final_ref, one_ref, above_ref, live_ref, w_ref, bias_ref, gain_ref, shift_ref,
    combined_ref, out_ref, second_ref, reduce_ref, side_in, part_s, halo_sem,
):
    slots, width = one_ref.shape
    half = slots // 2
    tile = 256
    me = lax.axis_index("fsdp")
    last = devices - 1
    left, right = lax.rem(me + last, devices), lax.rem(me + 1, devices)
    greet([left, right])

    def to_left():
        return remote(window_ref.at[:half], side_in.at[1], halo_sem, (0,), left)

    def to_right():
        return remote(window_ref.at[half + slots :], side_in.at[0], halo_sem, (1,), right)

    @pl.when(me > 0)
    def _():
        to_left().start()

    @pl.when(me < last)
    def _():
        to_right().start()

    @pl.when(me == 0)
    def _():
        side_in[0] = jnp.zeros((half, width), BF16)

    @pl.when(me == last)
    def _():
        side_in[1] = jnp.zeros((half, width), BF16)

    w_o = w_ref[...].reshape(width, width)

    owns = (first_ref, final_ref)

    def before(side, i, carry):
        here = pl.ds(pl.multiple_of(i * tile, tile), tile)
        at = pl.ds(pl.multiple_of(side * half + i * tile, tile), tile)
        part_s[at, :] = dot(owns[side][here, :], w_o)
        reduce_ref[at, :] = (live_ref[at, :] * above_ref[at, :].astype(F32)).astype(BF16)
        return carry

    for side in range(2):
        lax.fori_loop(0, half // tile, functools.partial(before, side), 0)

    def after(side, i, carry):
        here = pl.ds(pl.multiple_of(i * tile, tile), tile)
        at = pl.ds(pl.multiple_of(side * half + i * tile, tile), tile)
        other = side_in[side, here, :]
        combined_ref[at, :] = owns[side][here, :] + other
        attended = part_s[at, :] + dot(other, w_o) + bias_ref[...]
        out = one_ref[at, :].astype(F32) + live_ref[at, :] * attended
        out_ref[at, :] = out
        second_ref[at, :] = layer_norm(out, gain_ref[...], shift_ref[...]).astype(BF16)
        return carry

    @pl.when(me > 0)
    def _():
        to_right().wait_recv()

    lax.fori_loop(0, half // tile, functools.partial(after, 0), 0)

    @pl.when(me < last)
    def _():
        to_left().wait_recv()

    lax.fori_loop(0, half // tile, functools.partial(after, 1), 0)

    @pl.when(me > 0)
    def _():
        to_left().wait_send()

    @pl.when(me < last)
    def _():
        to_right().wait_send()


def join(devices, window, one, above, live, gathered, bias, gain, shift, part, sides):
    slots, width = one.shape
    dma = pltpu.SemaphoreType.DMA
    rows = pl.BlockSpec((slots, width), lambda i: (0, 0))
    thin = pl.BlockSpec((1, width), lambda i: (0, 0))
    low = jax.ShapeDtypeStruct((slots, width), BF16)
    return pl.pallas_call(
        functools.partial(join_kernel, devices),
        grid=(1,),
        in_specs=[
            pl.BlockSpec(memory_space=pl.ANY),
            pl.BlockSpec((slots // 2, width), lambda i: (1, 0)), pl.BlockSpec((slots // 2, width), lambda i: (2, 0)), rows, rows, pl.BlockSpec((slots, 1), lambda i: (0, 0)),
            pl.BlockSpec((devices, part, width), lambda i: (0, sides, 0)), thin, thin, thin,
        ],
        out_specs=[rows] * 4,
        out_shape=[low, jax.ShapeDtypeStruct((slots, width), F32), low, low],
        scratch_shapes=[pltpu.VMEM((2, slots // 2, width), BF16), pltpu.VMEM((slots, width), F32), dma((2, 2))],
        compiler_params=pltpu.CompilerParams(collective_id=6, has_side_effects=True, vmem_limit_bytes=57 << 20),
        name="join",
    )(window, window, window, one, above, live, gathered, bias, gain, shift)


def turn_kernel(
    devices, out_one_ref, d_second_ref, mixed_ref, two_ref, above_ref, combined_ref, live_ref, gain_ref, w_o_ref,
    bias_r_ref, bias_e_ref,
    wide_ref, grad_one_ref, one_ref, res_two_ref, grad_o_ref, small_ref, attend_s, halo_sem,
):
    slots, width = two_ref.shape
    half = slots // 2
    tile = 256
    part = grad_o_ref.shape[1]
    me = lax.axis_index("fsdp")
    last = devices - 1
    left, right = lax.rem(me + last, devices), lax.rem(me + 1, devices)
    greet([left, right])

    def to_left():
        return remote(wide_ref.at[half : 2 * half], wide_ref.at[half + slots :], halo_sem, (0,), left)

    def to_right():
        return remote(wide_ref.at[2 * half : 3 * half], wide_ref.at[:half], halo_sem, (1,), right)

    small_ref[...] = jnp.zeros(small_ref.shape, F32)
    gain = gain_ref[...]

    def norm_tile(i, carry):
        at = pl.ds(pl.multiple_of(i * tile, tile), tile)
        live = live_ref[at, :]
        values = out_one_ref[at, :]
        above = d_second_ref[at, :]
        center = values - jnp.mean(values, axis=1, keepdims=True)
        scale = lax.rsqrt(jnp.mean(center * center, axis=1, keepdims=True) + EPS_NORM)
        center = center * scale
        small_ref[2:3, :] += jnp.sum(above * center, axis=0, keepdims=True)
        small_ref[3:4, :] += jnp.sum(above, axis=0, keepdims=True)
        above = above * gain
        mean = jnp.mean(above, axis=1, keepdims=True)
        along = jnp.mean(above * center, axis=1, keepdims=True)
        total = live * (above_ref[at, :].astype(F32) + scale * (above - mean - center * along))
        low = total.astype(BF16)
        grad_one_ref[at, :] = low
        attend_s[at, :] = low
        small_ref[4:5, :] += jnp.sum(low.astype(F32), axis=0, keepdims=True)
        wide_ref[pl.ds(pl.multiple_of(half + i * tile, tile), tile), :] = dot(low, w_o_ref[...], NT).astype(BF16)
        return carry

    lax.fori_loop(0, half // tile, norm_tile, 0)

    @pl.when(me > 0)
    def _():
        to_left().start()

    lax.fori_loop(half // tile, slots // tile, norm_tile, 0)

    @pl.when(me < last)
    def _():
        to_right().start()

    def finish_tile(i, carry):
        at = pl.ds(pl.multiple_of(i * tile, tile), tile)
        live = live_ref[at, :]
        one_ref[at, :] = (live * out_one_ref[at, :]).astype(BF16)
        res_two_ref[at, :] = (live * (two_ref[at, :].astype(F32) + mixed_ref[at, :])).astype(BF16)
        return carry

    lax.fori_loop(0, slots // tile, finish_tile, 0)

    def weights(i, carry):
        cols = pl.ds(pl.multiple_of(i * tile, tile), tile)
        many = tile // part
        grad_o_ref[pl.ds(pl.multiple_of(i * many, many), many)] = (
            dot(combined_ref[:, cols], attend_s[...], TN).astype(BF16).reshape(many, part, width)
        )
        return carry

    lax.fori_loop(0, width // tile, weights, 0)
    small_ref[5:6, :] = bias_r_ref[...]
    for k in range(bias_e_ref.shape[1] // width):
        small_ref[6 + k : 7 + k, :] = bias_e_ref[:, k * width : (k + 1) * width]

    @pl.when(me > 0)
    def _():
        to_right().wait_recv()
        to_left().wait_send()

    @pl.when(me == 0)
    def _():
        wide_ref[:half] = jnp.zeros((half, width), BF16)

    @pl.when(me < last)
    def _():
        to_left().wait_recv()
        to_right().wait_send()

    @pl.when(me == last)
    def _():
        wide_ref[half + slots :] = jnp.zeros((half, width), BF16)


def turn(devices, out_one, d_second, mixed, two, above, combined, live, gain, w_o, bias_r, bias_e):
    slots, width = two.shape
    part = width // devices
    vmem = pl.BlockSpec(memory_space=pltpu.VMEM)
    rows_low = jax.ShapeDtypeStruct((slots, width), BF16)
    return pl.pallas_call(
        functools.partial(turn_kernel, devices),
        in_specs=[vmem] * 11,
        out_specs=(vmem,) * 6,
        out_shape=(
            jax.ShapeDtypeStruct((2 * slots, width), BF16), rows_low, rows_low, rows_low,
            jax.ShapeDtypeStruct((devices, part, width), BF16),
            jax.ShapeDtypeStruct((16, width), F32),
        ),
        scratch_shapes=[pltpu.VMEM((slots, width), BF16), pltpu.SemaphoreType.DMA((2, 2))],
        compiler_params=pltpu.CompilerParams(collective_id=5, has_side_effects=True, vmem_limit_bytes=57 << 20),
        name="turn",
    )(out_one, d_second, mixed, two, above, combined, live, gain, w_o, bias_r, bias_e)


def tail_kernel(
    devices, grad_r_ref, grad_o_ref, d_shared_ref, d_value_ref, normed_ref, head_ref, own_ref, end_ref, above_ref, live_ref,
    gain_ref, w_s_ref, w_v_ref, small_ref,
    back_ref, out_s_ref, out_v_ref, out_o_ref, out_r_ref, thin_ref, long_ref,
    side_s, side_in, vector_s, vector_in, grad_s, load_sem, halo_sem, vector_sem, *rest,
):
    window, width = normed_ref.shape
    slots = own_ref.shape[0]
    half = slots // 2
    part = out_s_ref.shape[0]
    many = out_r_ref.shape[0]
    tile = 256
    where = neighbours(devices)
    (o, p, q, c), core_peer, q_peers, p_peers, o_peers = where
    me = lax.axis_index("fsdp")
    outer, side, core = digits(devices)
    owns, rest = rest[:3], rest[3:]
    sems = rest[-4:]

    def distant(source, row, rows, k):
        at = pl.ds(row, rows)

        def other():
            return source.at[:, :, :, 1 - c, at, :]

        def mine(spot, cols):
            return owns[k].at[tuple(spot) + (slice(None), cols)]

        def load():
            return pltpu.make_async_copy(source.at[:, :, :, c, at, :], owns[k], load_sem.at[k])

        return Scatter(devices, where, k, rest[5 * k : 5 * k + 5], sems, other, mine, load)

    def near(j, k):
        def other():
            return grad_s.at[j, :, :, :, 1 - c]

        def mine(spot, cols):
            return grad_s.at[(j,) + tuple(spot) + (c, slice(None), cols)]

        return Scatter(devices, where, k, rest[5 * k : 5 * k + 5], sems, other, mine)

    movers = [
        distant(grad_r_ref, 0, many // 2, 0), distant(grad_r_ref, many // 2, many // 2, 1), distant(grad_o_ref, 0, part, 2),
        near(0, 3), near(1, 4),
    ]
    last = devices - 1
    left, right = lax.rem(me + last, devices), lax.rem(me + 1, devices)
    greet(peers_of(where) + [left, right])
    for k in range(3):
        movers[k].begin()

    def to_left():
        return remote(side_s.at[0], side_in.at[1], halo_sem, (0,), left)

    def to_right():
        return remote(side_s.at[1], side_in.at[0], halo_sem, (1,), right)

    vector_s[...] = small_ref[...]
    gain = gain_ref[...]

    def norm_tile(ref, row, at):
        values = ref[pl.ds(row, tile), :].astype(F32)
        above = dot(d_shared_ref[at, :], w_s_ref[...], NT) + dot(d_value_ref[at, :], w_v_ref[...], NT)
        center = values - jnp.mean(values, axis=1, keepdims=True)
        scale = lax.rsqrt(jnp.mean(center * center, axis=1, keepdims=True) + EPS_NORM)
        center = center * scale
        vector_s[0:1, :] += jnp.sum(above * center, axis=0, keepdims=True)
        vector_s[1:2, :] += jnp.sum(above, axis=0, keepdims=True)
        above = above * gain
        mean = jnp.mean(above, axis=1, keepdims=True)
        along = jnp.mean(above * center, axis=1, keepdims=True)
        return scale * (above - mean - center * along)

    def side_tiles(i, carry):
        row = pl.multiple_of(i * tile, tile)
        side_s[0, pl.ds(row, tile), :] = norm_tile(head_ref, row, pl.ds(row, tile)).astype(BF16)
        at = pl.ds(pl.multiple_of(half + slots + i * tile, tile), tile)
        side_s[1, pl.ds(row, tile), :] = norm_tile(end_ref, row, at).astype(BF16)
        return carry

    lax.fori_loop(0, half // tile, side_tiles, 0)

    @pl.when(me > 0)
    def _():
        to_left().start()

    @pl.when(me < last)
    def _():
        to_right().start()

    movers[0].stage_core()

    def weights(j, ref):
        wide = tile // part

        def strip(i, carry):
            cols = pl.ds(pl.multiple_of(i * tile, tile), tile)
            block = dot(normed_ref[:, cols], ref[...], TN).astype(BF16).reshape(wide // core, core, part, width)
            for k in range(wide // core):
                index = i * (wide // core) + k
                spot = (lax.div(index, side * side), lax.rem(lax.div(index, side), side), lax.rem(index, side))
                grad_s[(j,) + spot] = block[k]
            return carry

        lax.fori_loop(0, width // tile, strip, 0)

    weights(0, d_shared_ref)
    movers[3].begin()
    movers[1].stage_core()
    movers[0].stage_first()
    weights(1, d_value_ref)
    movers[4].begin()
    movers[2].stage_core()
    movers[1].stage_first()
    movers[0].stage_second()

    def own_tiles(i, carry):
        row = pl.multiple_of(i * tile, tile)
        at = pl.ds(pl.multiple_of(half + i * tile, tile), tile)
        here = pl.ds(row, tile)
        total = above_ref[here, :].astype(F32) + norm_tile(own_ref, row, at)
        back_ref[here, :] = (live_ref[here, :] * total).astype(BF16)
        return carry

    lax.fori_loop(0, slots // tile, own_tiles, 0)

    def vector_copies(stage):
        group = ([(0, core_peer)], q_peers, p_peers, o_peers)[stage]
        base = (0, 1, side, 2 * side - 1)[stage]
        return [
            remote(vector_s if stage == 0 else vector_in.at[base - 1], vector_in.at[base + d], vector_sem, (base + d,), device)
            for d, (_, device) in enumerate(group)
        ]

    def vector_stage(stage):
        base = (0, 1, side, 2 * side - 1)[stage]
        copies = vector_copies(stage)
        total = vector_s[...] if stage == 0 else vector_in[base - 1]
        for d, copy in enumerate(copies):
            copy.wait_recv()
            total = total + vector_in[base + d]
        vector_in[base + len(copies) - 1] = total

    for copy in vector_copies(0):
        copy.start()
    movers[3].stage_core()
    movers[2].stage_first()
    movers[1].stage_second()
    out_r_ref[: many // 2, :] = movers[0].stage_third()
    vector_stage(0)
    for copy in vector_copies(1):
        copy.start()
    movers[4].stage_core()
    movers[3].stage_first()
    movers[2].stage_second()
    out_r_ref[many // 2 :, :] = movers[1].stage_third()
    vector_stage(1)
    for copy in vector_copies(2):
        copy.start()
    movers[4].stage_first()
    movers[3].stage_second()
    out_o_ref[...] = movers[2].stage_third()
    vector_stage(2)
    for copy in vector_copies(3):
        copy.start()

    @pl.when(me > 0)
    def _():
        to_right().wait_recv()

    @pl.when(me == 0)
    def _():
        side_in[0] = jnp.zeros((half, width), BF16)

    @pl.when(me < last)
    def _():
        to_left().wait_recv()

    @pl.when(me == last)
    def _():
        side_in[1] = jnp.zeros((half, width), BF16)

    for k in range(2):
        at = slice(k * half, (k + 1) * half)
        back_ref[at, :] = (back_ref[at, :].astype(F32) + side_in[k].astype(F32)).astype(BF16)
    movers[4].stage_second()
    out_s_ref[...] = movers[3].stage_third()
    vector_stage(3)
    out_v_ref[...] = movers[4].stage_third()
    vectors = 2 * side + outer - 3
    total = vector_in[vectors]
    thin_ref[...] = pltpu.roll(total, lax.rem(width - me * part, width), 1)[:, :DH]
    each = long_ref.shape[1]
    long_rows = [total[6 + k : 7 + k, :] for k in range(devices * each // width)]
    mine = lax.div(me * each, width)
    chosen = long_rows[0]
    for k in range(1, len(long_rows)):
        chosen = jnp.where(mine == k, long_rows[k], chosen)
    long_ref[...] = pltpu.roll(chosen, lax.rem(width - lax.rem(me * each, width), width), 1)[:, :each]
    for stage in range(4):
        for copy in vector_copies(stage):
            copy.wait_send()

    @pl.when(me > 0)
    def _():
        to_left().wait_send()

    @pl.when(me < last)
    def _():
        to_right().wait_send()

    for mover in movers:
        mover.sent_first()
        mover.sent_last()


def tail(devices, grad_r, grad_o, d_shared, d_values, normed, head, own, end, above, live, gain, w_s, w_v, small):
    window, width = normed.shape
    slots = own.shape[0]
    outer, side, core = digits(devices)
    part, many = grad_o.shape[1], grad_r.shape[1]
    each = many
    vmem = pl.BlockSpec(memory_space=pltpu.VMEM)
    anywhere = pl.BlockSpec(memory_space=pl.ANY)
    dma = pltpu.SemaphoreType.DMA
    sizes = [many // 2, many // 2, part, part, part]
    scratch = [
        pltpu.VMEM((2, slots // 2, width), BF16), pltpu.VMEM((2, slots // 2, width), BF16),
        pltpu.VMEM((16, width), F32), pltpu.VMEM((2 * side + outer - 2, 16, width), F32),
        pltpu.VMEM((2, outer, side, side, core, part, width), BF16),
        dma((3,)), dma((2, 2)), dma((2, 2 * side + outer - 2)),
    ]
    scratch += [pltpu.VMEM((outer, side, side, rows, width), BF16) for rows in sizes[:3]]
    for rows in sizes:
        scratch += boxes_for(devices, rows, width)
    shape = (outer, side, side, core)
    return pl.pallas_call(
        functools.partial(tail_kernel, devices),
        in_specs=[anywhere, anywhere] + [vmem] * 12,
        out_specs=(vmem,) * 7,
        out_shape=(
            jax.ShapeDtypeStruct((slots, width), BF16),
            jax.ShapeDtypeStruct((part, width), F32),
            jax.ShapeDtypeStruct((part, width), F32),
            jax.ShapeDtypeStruct((part, width), F32),
            jax.ShapeDtypeStruct((many, width), F32),
            jax.ShapeDtypeStruct((16, DH), F32),
            jax.ShapeDtypeStruct((1, each), F32),
        ),
        scratch_shapes=scratch + sems_for(devices, len(sizes)),
        compiler_params=pltpu.CompilerParams(collective_id=4, has_side_effects=True, vmem_limit_bytes=57 << 20),
        name="tail",
    )(
        grad_r.reshape(shape + grad_r.shape[1:]), grad_o.reshape(shape + grad_o.shape[1:]),
        d_shared, d_values, normed, head, own, end, above, live, gain, w_s, w_v, small,
    )


def find_ranks(length_ref, target_ref, bucket_ref, packed_ref, info_ref, before_s):
    devices = length_ref.shape[0]
    lists, slots = bucket_ref.shape
    me = lax.axis_index("fsdp")
    base = me * slots
    window = 2 * slots

    def look(s, carry):
        start, mine, found, one, two = carry
        size = length_ref[s]
        target = target_ref[s]
        middle = start + lax.shift_right_logical(size, 1)
        inside = (middle >= base) & (middle < base + slots)
        offset = start - base + slots // 2
        entry = (offset, offset + size, target)
        first, second = inside & (found == 0), inside & (found == 1)
        one = tuple(jnp.where(first, new, old) for new, old in zip(entry, one))
        two = tuple(jnp.where(second, new, old) for new, old in zip(entry, two))
        return start + size, jnp.where(target == me, size, mine), found + inside.astype(jnp.int32), one, two

    zero = jnp.int32(0)
    nothing = (jnp.int32(window), jnp.int32(window), zero)
    total, mine, found, one, two = lax.fori_loop(0, devices, look, (zero, zero, zero, nothing, nothing))
    for k, value in enumerate((one[0], one[1], two[0], two[1], one[2], two[2], total, found)):
        info_ref[k] = value

    def fill(i, carry):
        at = pl.ds(pl.multiple_of(i * DH, DH), DH)
        first = lax.broadcasted_iota(jnp.int32, (DH, slots), 0) + i * DH
        second = lax.broadcasted_iota(jnp.int32, (DH, slots), 1)
        before_s[at, :] = jnp.where(first < second, 1.0, 0.0).astype(BF16)
        return carry

    lax.fori_loop(0, slots // DH, fill, 0)
    left = lax.broadcasted_iota(jnp.int32, (DH, DH), 0)
    right = lax.broadcasted_iota(jnp.int32, (DH, DH), 1)
    smaller = jnp.where((left // BUCKETS == right // BUCKETS) & (right < left), 1.0, 0.0).astype(BF16)
    many = DH // BUCKETS
    bucket = lax.broadcasted_iota(jnp.int32, (many, BUCKETS, slots), 1)
    live = lax.broadcasted_iota(jnp.int32, (many, BUCKETS, slots), 2) < mine
    ranks = []
    for g in range(lists // many):
        here = (jnp.broadcast_to(bucket_ref[g * many : (g + 1) * many, :][:, None, :], bucket.shape) == bucket) & live
        one_hot = jnp.where(here, 1.0, 0.0)
        flat = one_hot.reshape(DH, slots).astype(BF16)
        offset = jnp.sum(dot(smaller, flat), axis=1, keepdims=True)
        place = (dot(flat, before_s[...]) + offset).reshape(many, BUCKETS, slots)
        ranks.append(jnp.sum(one_hot * place, axis=1))
    rank = jnp.concatenate(ranks, axis=0)
    live = lax.broadcasted_iota(jnp.int32, (lists, slots), 1) < mine
    packed_ref[:lists, :] = jnp.where(live, jnp.floor(rank * (1.0 / GROUP)), FREE).astype(BF16)


def project_kernel(
    info_ref, head_ref, own_ref, tail_ref, gain_ref, shift_ref, w_s_ref, w_v_ref, one_ref, two_ref,
    normed_ref, shared_ref, value_ref, code_ref,
):
    i = pl.program_id(0)
    tile = own_ref.shape[0]
    steps = pl.num_programs(0)

    def go(ref):
        normed = layer_norm(ref[...].astype(F32), gain_ref[...], shift_ref[...]).astype(BF16)
        normed_ref[...] = normed
        shared_ref[...] = dot(normed, w_s_ref[...]).astype(BF16)
        value_ref[...] = dot(normed, w_v_ref[...]).astype(BF16)

    @pl.when(i < steps // 4)
    def _():
        go(head_ref)

    @pl.when((i >= steps // 4) & (i < steps - steps // 4))
    def _():
        go(own_ref)

    @pl.when(i >= steps - steps // 4)
    def _():
        go(tail_ref)

    @pl.when(i == 0)
    def _():
        lists, window = code_ref.shape
        lane = lax.broadcasted_iota(jnp.int32, (lists, window), 1)
        code = jnp.full((lists, window), FREE, F32)
        for k, ref in enumerate((one_ref, two_ref)):
            begin, end = info_ref[2 * k], info_ref[2 * k + 1]
            rows = ref[0].astype(F32)
            moved = pltpu.roll(jnp.concatenate([rows, rows], axis=1), lax.rem(begin, window), 1)
            code = jnp.where((lane >= begin) & (lane < end), moved + 32.0 * k, code)
        code_ref[...] = code.astype(BF16)


def project(info, head, own, tail, gain, shift, w_s, w_v, blocks):
    slots, width = own.shape
    window = 2 * slots
    lists = ROUNDS * HEADS
    tile = 256
    steps = window // tile
    quarter = steps // 4
    rows = pl.BlockSpec((tile, width), lambda i, info: (i, 0))
    vector = pl.BlockSpec((1, width), lambda i, info: (0, 0))
    matrix = pl.BlockSpec((width, width), lambda i, info: (0, 0), pipeline_mode=pl.Buffered(1))
    wide = jax.ShapeDtypeStruct((window, width), BF16)
    return pl.pallas_call(
        project_kernel,
        grid_spec=pltpu.PrefetchScalarGridSpec(
            num_scalar_prefetch=1,
            grid=(steps,),
            in_specs=[
                pl.BlockSpec((tile, width), lambda i, info: (jnp.minimum(i, quarter - 1), 0)),
                pl.BlockSpec((tile, width), lambda i, info: (jnp.clip(i - quarter, 0, 2 * quarter - 1), 0)),
                pl.BlockSpec((tile, width), lambda i, info: (jnp.clip(i - 3 * quarter, 0, quarter - 1), 0)),
                vector, vector, matrix, matrix,
                pl.BlockSpec((1, lists, slots), lambda i, info: (info[4], 0, 0)),
                pl.BlockSpec((1, lists, slots), lambda i, info: (info[5], 0, 0)),
            ],
            out_specs=[rows, rows, rows, pl.BlockSpec((lists, window), lambda i, info: (0, 0))],
        ),
        out_shape=[wide, wide, wide, jax.ShapeDtypeStruct((lists, window), BF16)],
        compiler_params=pltpu.CompilerParams(vmem_limit_bytes=40 << 20),
        name="project",
    )(info, head, own, tail, gain, shift, w_s, w_v, blocks, blocks)


def gather_kernel(devices, arrays, length_ref, target_ref, bucket_ref, vector_ref, rows_ref, *refs):
    sources, outs, (info_ref, head_ref, end_ref) = refs[: arrays - 1], refs[arrays - 1 : 2 * arrays - 1], refs[2 * arrays - 1 : 2 * arrays + 2]
    packed_s, before_s, own_sem, sem_o, sem_a, sem_b, sem_c, halo_sem, edge_sem = refs[2 * arrays + 2 :]
    sources = sources + (packed_s,)
    outer, side, core = digits(devices)
    (o, p, q, c), core_peer, q_peers, p_peers, o_peers = neighbours(devices)
    me = lax.axis_index("fsdp")
    last_device = devices - 1
    left, right = lax.rem(me + last_device, devices), lax.rem(me + 1, devices)
    greet([core_peer] + [d for _, d in q_peers] + [d for _, d in p_peers] + [d for _, d in o_peers] + [left, right])
    half = sources[0].shape[-1] // 2
    border = head_ref.shape[0]

    def to_left():
        return remote(rows_ref.at[:border], end_ref, halo_sem, (0,), left)

    def to_right():
        return remote(rows_ref.at[border:], head_ref, halo_sem, (1,), right)

    def blank(ref):
        return pltpu.make_async_copy(before_s.at[:border], ref, edge_sem.at[0])

    columns = (pl.ds(0, half), pl.ds(half, half))

    locals_, begun, first, second, last = [], {}, {}, {}, {}
    for s in range(arrays):
        if s == arrays - 1:
            find_ranks(length_ref, target_ref, bucket_ref, packed_s, info_ref, before_s)
            packed_s[bucket_ref.shape[0] :, :] = vector_ref[...]
        locals_.append(pltpu.make_async_copy(sources[s], outs[s].at[o, p, q, c], own_sem.at[s]))
        locals_[s].start()
        for d, (k, device) in enumerate(o_peers):
            begun[s, d] = remote(sources[s], outs[s].at[o, p, q, c], sem_o, (s, d), device)
            begun[s, d].start()

    @pl.when(me > 0)
    def _():
        to_left().start()

    @pl.when(me < last_device)
    def _():
        to_right().start()

    before_s[:border, :] = jnp.zeros((border, before_s.shape[1]), BF16)

    @pl.when(me == 0)
    def _():
        blank(head_ref).start()

    @pl.when(me == last_device)
    def _():
        blank(end_ref).start()

    def stage_a(s):
        locals_[s].wait()
        for d in range(outer - 1):
            begun[s, d].wait_recv()
        for h, peers in enumerate((q_peers, p_peers)):
            piece = outs[s].at[:, p, q, c, :, columns[h]]
            for d, (k, device) in enumerate(peers):
                first[s, h, d] = remote(piece, piece, sem_a, (s, h, d), device)
                first[s, h, d].start()

    def stage_b(s):
        for h, peers in enumerate((p_peers, q_peers)):
            for d in range(side - 1):
                first[s, h, d].wait_recv()
            piece = outs[s].at[:, p, :, c, :, columns[h]] if h == 0 else outs[s].at[:, :, q, c, :, columns[h]]
            for d, (k, device) in enumerate(peers):
                second[s, h, d] = remote(piece, piece, sem_b, (s, h, d), device)
                second[s, h, d].start()

    def stage_c(s):
        for h in range(2):
            for d in range(side - 1):
                second[s, h, d].wait_recv()
        piece = outs[s].at[:, :, :, c]
        last[s] = remote(piece, piece, sem_c, (s,), core_peer)
        last[s].start()

    for t in range(arrays + 2):
        if t < arrays:
            stage_a(t)
        if 0 <= t - 1 < arrays:
            stage_b(t - 1)
        if 0 <= t - 2 < arrays:
            stage_c(t - 2)
    for s in range(arrays):
        last[s].wait_recv()

    @pl.when(me > 0)
    def _():
        to_right().wait_recv()
        to_left().wait_send()

    @pl.when(me == 0)
    def _():
        blank(head_ref).wait()

    @pl.when(me < last_device)
    def _():
        to_left().wait_recv()
        to_right().wait_send()

    @pl.when(me == last_device)
    def _():
        blank(end_ref).wait()

    for group in (begun, first, second, last):
        for copy in group.values():
            copy.wait_send()


def gather(devices, lengths, destination, buckets, vectors, rows, arrays):
    outer, side, core = digits(devices)
    lists, slots = buckets.shape
    packed = jax.ShapeDtypeStruct((lists + vectors.shape[0], slots), BF16)
    shapes = [jax.ShapeDtypeStruct(array.shape, array.dtype) for array in arrays] + [packed]
    count = len(shapes)
    dma = pltpu.SemaphoreType.DMA
    anywhere = pl.BlockSpec(memory_space=pl.ANY)
    hbm = pl.BlockSpec(memory_space=pltpu.HBM)
    smem = pl.BlockSpec(memory_space=pltpu.SMEM)
    vmem = pl.BlockSpec(memory_space=pltpu.VMEM)
    outs = pl.pallas_call(
        functools.partial(gather_kernel, devices, count),
        out_shape=tuple(jax.ShapeDtypeStruct((outer, side, side, core) + shape.shape, shape.dtype) for shape in shapes)
        + (jax.ShapeDtypeStruct((8,), jnp.int32),)
        + (jax.ShapeDtypeStruct((slots // 2, rows.shape[1]), BF16),) * 2,
        in_specs=[smem, smem, vmem, vmem] + [anywhere] * count,
        out_specs=(hbm,) * count + (smem, hbm, hbm),
        scratch_shapes=[
            pltpu.VMEM(packed.shape, BF16), pltpu.VMEM((slots, slots), BF16),
            dma((count,)), dma((2, count, outer - 1)), dma((2, count, 2, side - 1)), dma((2, count, 2, side - 1)), dma((2, count)),
            dma((2, 2)), dma((1,)),
        ],
        compiler_params=pltpu.CompilerParams(collective_id=2, has_side_effects=True, vmem_limit_bytes=32 << 20),
        name="gather",
    )(lengths, destination, buckets, vectors, rows, *arrays)
    return [out.reshape((devices,) + shape.shape) for out, shape in zip(outs, shapes)] + list(outs[count:])


def body(
    input_one, input_two, upstream_one, upstream_two, lengths, destination, buckets,
    w_shared, w_value, w_output, w_expand, w_reduce,
    gain_attend, shift_attend, gain_mixing, shift_mixing, bias_output, bias_expand, bias_reduce,
):
    devices = lax.axis_size("fsdp")
    me = lax.axis_index("fsdp")
    slots, width = input_one.shape
    half = slots // 2
    window = 2 * slots
    part = w_shared.shape[0]
    hidden = w_expand.shape[1]
    sides = hidden // width
    base = me * slots
    lists = ROUNDS * HEADS
    spot = jnp.arange(width, dtype=jnp.int32)
    short = jnp.stack([gain_attend, shift_attend, gain_mixing, shift_mixing, bias_output, bias_reduce])
    short = jnp.where(spot // part == me, jnp.tile(short, (1, devices)), 0.0)
    many = hidden // devices
    long = jnp.tile(bias_expand, width // many)[None]
    long = jnp.where(spot[None] // many + (width // many) * jnp.arange(sides, dtype=jnp.int32)[:, None] == me, long, 0.0)
    vectors = jnp.concatenate([short, long], axis=0)
    high = lax.reduce_precision(vectors, 8, 7)
    count = vectors.shape[0]
    packed = jnp.concatenate(
        [high.astype(BF16), (vectors - high).astype(BF16), jnp.zeros((24 - 2 * count, width), BF16)], axis=0
    )
    second_gather = lax.all_gather(
        jnp.concatenate(
            [w_reduce, w_output] + [w_expand[:, k * width : (k + 1) * width] for k in range(sides)], axis=0
        ),
        "fsdp", axis=0, tiled=False,
    )
    full_shared, full_value, packed, info, two_head, two_tail = gather(
        devices, lengths, destination, buckets[0], packed, input_two, [w_shared, w_value]
    )
    full_shared, full_value = full_shared.reshape(width, width), full_value.reshape(width, width)
    vectors = jnp.sum(packed[:, lists : lists + 2 * count].astype(F32), axis=0)
    vectors = vectors[:count] + vectors[count:]
    gain_a, shift_a, gain_m, shift_m, bias_o, bias_r = (vectors[k : k + 1] for k in range(6))
    bias_e = vectors[6:].reshape(1, hidden)
    full_output = second_gather[:, sides * part : (sides + 1) * part].reshape(width, width)
    lane = jnp.arange(HEADS * DH, dtype=jnp.int32)
    row = jnp.arange(lists, dtype=jnp.int32)[:, None]
    spread = (row == ((lane % 64) // 16) * HEADS + lane // DH).astype(BF16)

    live = ((base + jnp.arange(slots, dtype=jnp.int32)) < info[6]).astype(F32)[:, None]
    normed, shared, values, code = project(
        info, two_head, input_two, two_tail, gain_a, shift_a, full_shared, full_value, packed
    )
    combined_window, lse, lone = attend(info, shared, values, code, spread)
    combined, out_one, second, d_reduce = join(
        devices, combined_window, input_one, upstream_two, live, second_gather, bias_o, gain_m, shift_m, part, sides
    )
    mixed, d_second, grad_reduce, grad_bias_expand, grad_expand, grad_bias_reduce = mixing(
        devices, second, d_reduce, second_gather, bias_e, bias_r, part
    )
    d_combined, grad_one, result_one, result_two, grad_output, small = turn(
        devices, out_one, d_second, mixed, input_two, upstream_one, combined, live, gain_m, full_output, grad_bias_reduce, grad_bias_expand
    )
    rows = (slots, width)
    d_shared, d_values, grad_one, result_one, result_two, grad_expand = attend_back(
        info, shared, values, code, spread, combined_window, d_combined, lse, lone,
        (grad_one, result_one, result_two, grad_expand), (rows, rows, rows, (part, hidden)),
    )
    grad_two, grad_shared, grad_value, grad_output, grad_reduce, thin, long = tail(
        devices, grad_reduce, grad_output, d_shared, d_values, normed,
        two_head, input_two, two_tail, upstream_two, live, gain_a, full_shared, full_value, small,
    )
    return (
        result_one,
        result_two,
        grad_one,
        grad_two,
        grad_shared,
        grad_value,
        grad_output,
        grad_expand,
        grad_reduce,
        thin[0, :part],
        thin[1, :part],
        thin[2, :part],
        thin[3, :part],
        thin[4, :part],
        long.reshape(-1),
        thin[5, :part],
    )


def solution(mesh):
    rows, flat, whole = P("fsdp", None), P("fsdp"), P()
    return jax.shard_map(
        body,
        mesh=mesh,
        in_specs=(rows,) * 4 + (whole, whole, P("fsdp", None, None)) + (rows,) * 5 + (flat,) * 7,
        out_specs=(rows,) * 9 + (flat,) * 7,
        check_vma=False,
    )
```

```python
import functools
import math

import jax
import jax.numpy as jnp
from jax import lax
from jax.experimental import pallas as pl
from jax.experimental.pallas import tpu as pltpu
from jax.sharding import PartitionSpec as P

HEADS = 8
DH = 128
GROUP = 64
ROUNDS = 4
BUCKETS = 32
EPS_NORM = 1e-05
EPS_UNIT = 1e-06
LOG2E = math.log2(math.e)
SELF2 = -100000.0 * LOG2E
NEG = -1e30
SCALE = 1.0 / math.sqrt(DH)
TILE = 512
HALF = TILE // 2
KEYS = 256
MANY = TILE // KEYS
STEP = 128.0
SHIFT = 1.5 * 2.0**30
TAME = 3000.0
PAIR = 4
FREE = 99.0
STRIP = 512
AFTER = (2, 4, 6, 8)
CURVE = math.sqrt(2.0 / math.pi)
MESH = pl.DeviceIdType.MESH

NT = (((1,), (1,)), ((), ()))
NN = (((1,), (0,)), ((), ()))
TN = (((0,), (0,)), ((), ()))
F32 = jnp.float32
BF16 = jnp.bfloat16


def dot(a, b, dims=NN):
    return lax.dot_general(a, b, dims, preferred_element_type=F32)


def layer_norm(values, gain, shift):
    center = values - jnp.mean(values, axis=-1, keepdims=True)
    spread = jnp.mean(center * center, axis=-1, keepdims=True)
    return center * lax.rsqrt(spread + EPS_NORM) * gain + shift


def prepare(q, code_ref, spread, ask_s, key_s, h, at):
    lane = lax.broadcasted_iota(jnp.int32, (TILE, DH), 1)
    target = ((lane // 64) * 32 + lane % 16).astype(F32)
    wide = q.astype(F32)
    square = jnp.sum(wide * wide, axis=1, keepdims=True)
    code = dot(code_ref[:, at], spread, TN)
    here = code == target
    ask_s[h, at, :DH] = q
    ask_s[h, at, DH:] = jnp.where(here, STEP, 0.0).astype(BF16)
    key_s[h, at, :DH] = (wide * (lax.rsqrt(square + EPS_UNIT) * (SCALE * LOG2E))).astype(BF16)
    key_s[h, at, DH:] = jnp.where(here | (code + 1.0 == target), 1.0, 0.0).astype(BF16)
    return jnp.max(square)


def lowest(info_ref, i):
    start, stop = i * TILE, (i + 1) * TILE
    one = (info_ref[0] < stop) & (info_ref[1] > start)
    two = (info_ref[2] < stop) & (info_ref[3] > start)
    begin = jnp.where(one, info_ref[0], jnp.where(two, info_ref[2], stop))
    return lax.div(begin, KEYS)


def tile_rows(i):
    return pl.ds(pl.multiple_of(i * TILE, TILE), TILE)


def halves(i):
    start = i * TILE
    return [((0, pl.multiple_of(start, HALF), pl.multiple_of(start, HALF)), HALF),
            ((HALF, pl.multiple_of(start + HALF, HALF), pl.multiple_of(start, HALF)), TILE)]


def part_of(both):
    count = (both + SHIFT) - SHIFT
    return count, both - count


def apart(left, right):
    return dot(left[:, DH:], right[:, DH:], NT), dot(left[:, :DH], right[:, :DH], NT)


def attend_kernel(low_ref, q_ref, v_ref, code_ref, spread_ref, comb_ref, lse_ref, lone_ref, ask_s, key_s, more_s, acc_s, top_s):
    rows = q_ref.shape[0]
    tiles = rows // TILE
    heads = [slice(h * DH, (h + 1) * DH) for h in range(PAIR)]

    def ready(i, largest):
        def fill():
            most = jnp.float32(0.0)
            at = tile_rows(i)
            for h, cols in enumerate(heads):
                most = jnp.maximum(most, prepare(q_ref[at, cols], code_ref, spread_ref[:, cols], ask_s, key_s, h, at))
                more_s[h, at, :DH] = v_ref[at, cols]
                more_s[h, at, DH:] = jnp.ones((TILE, DH), BF16)
            return most

        return jnp.maximum(largest, lax.cond(lowest(low_ref, i) <= (i + 1) * MANY - 1, fill, lambda: jnp.float32(0.0)))

    largest = lax.fori_loop(0, tiles, ready, jnp.float32(0.0))
    tame = largest * (SCALE * LOG2E) ** 2 < TAME
    ask_at = lax.broadcasted_iota(jnp.int32, (TILE, TILE), 0)
    key_at = lax.broadcasted_iota(jnp.int32, (TILE, TILE), 1)

    def finish(h, cols, at, top):
        total = acc_s[h, :, DH:]
        some = total > 0.0
        safe = jnp.where(some, total, 1.0)
        inverse = jnp.where(some, 1.0 / safe, 0.0)
        comb_ref[at, cols] = (acc_s[h, :, :DH] * inverse).astype(BF16)
        lse_ref[h, :, at] = (jnp.log2(safe) + top).T[:1]

    def rows_of(i, carry):
        at = tile_rows(i)
        low = lowest(low_ref, i)

        @pl.when((low < (i + 1) * MANY) & tame)
        def _():
            for h in range(PAIR):
                acc_s[h] = jnp.zeros((TILE, 2 * DH), F32)

            def step(j, carry):
                keys = pl.ds(pl.multiple_of(j * KEYS, KEYS), KEYS)
                for h in range(PAIR):
                    count, score = part_of(dot(ask_s[h, at, :], key_s[h, keys, :], NT))
                    acc_s[h] += dot((count * jnp.exp2(score)).astype(BF16), more_s[h, keys, :])
                return carry

            lax.fori_loop(low, i * MANY, step, 0)
            for h, cols in enumerate(heads):
                for asks, span in halves(i):
                    here = pl.ds(asks[0], HALF)
                    there = pl.ds(asks[1], HALF)
                    keys = pl.ds(asks[2], span)
                    key_at = lax.broadcasted_iota(jnp.int32, (HALF, span), 1)
                    ask_at = lax.broadcasted_iota(jnp.int32, (HALF, span), 0) + (span - HALF)
                    count, score = part_of(dot(ask_s[h, there, :], key_s[h, keys, :], NT))
                    prob = jnp.where(key_at < ask_at, count * jnp.exp2(score), 0.0).astype(BF16)
                    acc_s[h, here, :] += dot(prob, more_s[h, keys, :])
                    active = jnp.max(jnp.where(key_at == ask_at, count, 0.0), axis=1, keepdims=True) > 0.0
                    lone = jnp.where(active & (acc_s[h, here, DH:] == 0.0), 1.0, 0.0)
                    acc_s[h, here, :DH] += lone * v_ref[there, cols].astype(F32)
                    acc_s[h, here, DH:] += lone
                    lone_ref[h, :, there] = lone.T[:1]
                finish(h, cols, at, 0.0)

        @pl.when((low < (i + 1) * MANY) & jnp.logical_not(tame))
        def _():
            for h, cols in enumerate(heads):
                count, score = apart(ask_s[h, at, :], key_s[h, at, :])
                score = jnp.where(key_at == ask_at, SELF2, score)
                score = jnp.where((key_at <= ask_at) & (count > 0.5), score, NEG)
                top = jnp.max(score, axis=1, keepdims=True)
                prob = count * jnp.exp2(score - top)
                acc_s[h] = dot(prob.astype(BF16), more_s[h, at, :])
                top_s[h] = jnp.broadcast_to(top, (TILE, DH))

                def step(j, carry):
                    keys = pl.ds(pl.multiple_of(j * KEYS, KEYS), KEYS)
                    count, score = apart(ask_s[h, at, :], key_s[h, keys, :])
                    score = jnp.where(count > 0.5, score, NEG)
                    top = top_s[h]
                    newer = jnp.maximum(top, jnp.max(score, axis=1, keepdims=True))
                    fade = jnp.exp2(top - newer)
                    prob = count * jnp.exp2(score - newer[:, :1])
                    acc_s[h] = acc_s[h] * jnp.concatenate([fade, fade], axis=1) + dot(prob.astype(BF16), more_s[h, keys, :])
                    top_s[h] = newer
                    return carry

                lax.fori_loop(low, i * MANY, step, 0)
                total = acc_s[h, :, DH:]
                own = STEP * ROUNDS * jnp.exp2(SELF2 - jnp.maximum(top_s[h], SELF2))
                lone_ref[h, :, at] = jnp.where(total > 0.0, own / jnp.where(total > 0.0, total, 1.0), 0.0).T[:1]
                finish(h, cols, at, top_s[h])

        @pl.when(low >= (i + 1) * MANY)
        def _():
            comb_ref[at, :] = jnp.zeros((TILE, PAIR * DH), BF16)
            for h in range(PAIR):
                lse_ref[h, :, at] = jnp.zeros((1, TILE), F32)
                lone_ref[h, :, at] = jnp.zeros((1, TILE), F32)

        return carry

    lax.fori_loop(0, tiles, rows_of, 0)


def back_kernel(
    low_ref, q_ref, v_ref, code_ref, spread_ref, comb_ref, above_ref, lse_ref, lone_ref,
    dq_ref, dv_ref, ask_s, key_s, dunit_s, dvalue_s, dask_s,
):
    rows = q_ref.shape[0]
    tiles = rows // TILE
    heads = [slice(h * DH, (h + 1) * DH) for h in range(PAIR)]

    def ready(i, largest):
        def fill():
            most = jnp.float32(0.0)
            at = tile_rows(i)
            for h, cols in enumerate(heads):
                most = jnp.maximum(most, prepare(q_ref[at, cols], code_ref, spread_ref[:, cols], ask_s, key_s, h, at))
                for total in (dunit_s, dvalue_s, dask_s):
                    total[h, at, :] = jnp.zeros((TILE, DH), F32)
            return most

        return jnp.maximum(largest, lax.cond(lowest(low_ref, i) <= (i + 1) * MANY - 1, fill, lambda: jnp.float32(0.0)))

    largest = lax.fori_loop(0, tiles, ready, jnp.float32(0.0))
    tame = largest * (SCALE * LOG2E) ** 2 < TAME

    def pass_over(i, low, split):
        at = tile_rows(i)
        deltas = []
        for h, cols in enumerate(heads):
            mixed = above_ref[at, cols].astype(F32) * comb_ref[at, cols].astype(F32)
            deltas.append(jnp.sum(mixed.T, axis=0, keepdims=True))

        def step(j, carry):
            keys = pl.ds(pl.multiple_of(j * KEYS, KEYS), KEYS)
            for h, cols in enumerate(heads):
                q, above, unit = q_ref[at, cols], above_ref[at, cols], key_s[h, keys, :DH]
                count, score = split(key_s[h, keys, :], ask_s[h, at, :])
                d_prob = dot(v_ref[keys, cols], above, NT)
                prob = count * jnp.exp2(score - lse_ref[h, :, at])
                d_score = (prob * (d_prob - carry[h])).astype(BF16)
                dvalue_s[h, keys, :] += dot(prob.astype(BF16), above)
                dunit_s[h, keys, :] += dot(d_score, q)
                dask_s[h, at, :] += dot(d_score, unit, TN)
            return carry

        deltas = lax.fori_loop(low, i * MANY, step, tuple(deltas))
        for h, cols in enumerate(heads):
            for asks, span in halves(i):
                there = pl.ds(asks[1], HALF)
                keys = pl.ds(asks[2], span)
                key_at = lax.broadcasted_iota(jnp.int32, (span, HALF), 0)
                ask_at = lax.broadcasted_iota(jnp.int32, (span, HALF), 1) + (span - HALF)
                q, above, unit = q_ref[there, cols], above_ref[there, cols], key_s[h, keys, :DH]
                count, score = split(key_s[h, keys, :], ask_s[h, there, :])
                d_prob = dot(v_ref[keys, cols], above, NT)
                prob = count * jnp.exp2(score - lse_ref[h, :, there])
                prob = jnp.where(key_at < ask_at, prob, 0.0)
                d_score = (prob * (d_prob - deltas[h][:, asks[0] : asks[0] + HALF])).astype(BF16)
                prob = jnp.where(key_at == ask_at, lone_ref[h, :, there], prob).astype(BF16)
                dvalue_s[h, keys, :] += dot(prob, above)
                dunit_s[h, keys, :] += dot(d_score, q)
                dask_s[h, there, :] += dot(d_score, unit, TN)

    def together(left, right):
        return part_of(dot(left, right, NT))

    def guarded(left, right):
        count, score = apart(left, right)
        return count, jnp.where(count > 0.5, score, NEG)

    def rows_of(i, carry):
        low = lowest(low_ref, i)

        @pl.when((low < (i + 1) * MANY) & tame)
        def _():
            pass_over(i, low, together)

        @pl.when((low < (i + 1) * MANY) & jnp.logical_not(tame))
        def _():
            pass_over(i, low, guarded)

        return carry

    lax.fori_loop(0, tiles, rows_of, 0)

    def close(i, carry):
        at = tile_rows(i)

        @pl.when(lowest(low_ref, i) <= (i + 1) * MANY - 1)
        def _():
            for h, cols in enumerate(heads):
                q = q_ref[at, cols].astype(F32)
                norm = lax.rsqrt(jnp.sum(q * q, axis=1, keepdims=True) + EPS_UNIT)
                d_unit = dunit_s[h, at, :] * SCALE
                along = jnp.sum(q * d_unit, axis=1, keepdims=True)
                d_q = dask_s[h, at, :] * (1.0 / LOG2E) + d_unit * norm - q * (norm * norm * norm * along)
                dq_ref[at, cols] = d_q.astype(BF16)
                dv_ref[at, cols] = dvalue_s[h, at, :].astype(BF16)

        @pl.when(lowest(low_ref, i) > (i + 1) * MANY - 1)
        def _():
            dq_ref[at, :] = jnp.zeros((TILE, PAIR * DH), BF16)
            dv_ref[at, :] = jnp.zeros((TILE, PAIR * DH), BF16)

        return carry

    lax.fori_loop(0, tiles, close, 0)


def head_specs(rows):
    by_head = pl.BlockSpec((rows, PAIR * DH), lambda h, low: (0, h))
    code = pl.BlockSpec((ROUNDS * HEADS, rows), lambda h, low: (0, 0))
    spread = pl.BlockSpec((ROUNDS * HEADS, PAIR * DH), lambda h, low: (0, h))
    stat = pl.BlockSpec((PAIR, 1, rows), lambda h, low: (h, 0, 0))
    return by_head, code, spread, stat


def attend(low, shared, values, code, spread):
    rows = shared.shape[0]
    by_head, code_spec, spread_spec, stat = head_specs(rows)
    wide = jax.ShapeDtypeStruct((rows, HEADS * DH), BF16)
    thin = jax.ShapeDtypeStruct((HEADS, 1, rows), F32)
    return pl.pallas_call(
        attend_kernel,
        grid_spec=pltpu.PrefetchScalarGridSpec(
            num_scalar_prefetch=1,
            grid=(HEADS // PAIR,),
            in_specs=[by_head, by_head, code_spec, spread_spec],
            out_specs=[by_head, stat, stat],
            scratch_shapes=[pltpu.VMEM((PAIR, rows, 2 * DH), BF16)] * 3
            + [pltpu.VMEM((PAIR, TILE, 2 * DH), F32), pltpu.VMEM((PAIR, TILE, DH), F32)],
        ),
        out_shape=(wide, thin, thin),
        compiler_params=pltpu.CompilerParams(vmem_limit_bytes=57 << 20),
        name="attend",
        cost_estimate=pl.CostEstimate(
            flops=HEADS * 20 * 3 * 2 * TILE * TILE * DH, bytes_accessed=rows * HEADS * DH * 6, transcendentals=HEADS * 20 * TILE * TILE
        ),
    )(low, shared, values, code, spread)


def attend_back(low, shared, values, code, spread, combined, above, lse, lone):
    rows = shared.shape[0]
    by_head, code_spec, spread_spec, stat = head_specs(rows)
    wide = jax.ShapeDtypeStruct((rows, HEADS * DH), BF16)
    return pl.pallas_call(
        back_kernel,
        grid_spec=pltpu.PrefetchScalarGridSpec(
            num_scalar_prefetch=1,
            grid=(HEADS // PAIR,),
            in_specs=[by_head, by_head, code_spec, spread_spec, by_head, by_head, stat, stat],
            out_specs=[by_head, by_head],
            scratch_shapes=[pltpu.VMEM((PAIR, rows, 2 * DH), BF16)] * 2 + [pltpu.VMEM((PAIR, rows, DH), F32)] * 3,
        ),
        out_shape=(wide, wide),
        compiler_params=pltpu.CompilerParams(vmem_limit_bytes=57 << 20),
        name="attend_back",
        cost_estimate=pl.CostEstimate(
            flops=HEADS * 20 * 6 * 2 * TILE * TILE * DH, bytes_accessed=rows * HEADS * DH * 12, transcendentals=HEADS * 20 * TILE * TILE
        ),
    )(low, shared, values, code, spread, combined, above, lse, lone)


def digits(devices):
    side = 2
    while 8 * side * side < devices:
        side += 1
    assert 8 * side * side == devices, devices
    return 4, side, 2


def neighbours(devices):
    outer, side, core = digits(devices)
    me = lax.axis_index("fsdp")
    c = lax.rem(me, core)
    q = lax.rem(lax.div(me, core), side)
    p = lax.rem(lax.div(me, core * side), side)
    o = lax.div(me, core * side * side)

    def at(o_, p_, q_, c_):
        return ((o_ * side + p_) * side + q_) * core + c_

    core_peer = at(o, p, q, 1 - c)
    q_peers = [(k, at(o, p, k, c)) for k in (lax.rem(q + d, side) for d in range(1, side))]
    p_peers = [(k, at(o, k, q, c)) for k in (lax.rem(p + d, side) for d in range(1, side))]
    o_peers = [(k, at(k, p, q, c)) for k in (lax.rem(o + d, outer) for d in range(1, outer))]
    return (o, p, q, c), core_peer, q_peers, p_peers, o_peers


def peers_of(where):
    return [where[1]] + [device for group in where[2:] for _, device in group]


def greet(peers):
    barrier = pltpu.get_barrier_semaphore()
    for peer in peers:
        pl.semaphore_signal(barrier, inc=1, device_id=(peer,), device_id_type=MESH)
    pl.semaphore_wait(barrier, len(peers))


def remote(src, dst, sems, slot, device):
    return pltpu.make_async_remote_copy(
        src_ref=src, dst_ref=dst, send_sem=sems.at[(0,) + slot], recv_sem=sems.at[(1,) + slot],
        device_id=(device,), device_id_type=MESH,
    )


class Scatter:
    def __init__(self, devices, where, slot, boxes, sems, other, mine, load=None):
        self.outer, self.side, _ = digits(devices)
        (self.o, self.p, self.q, self.c), self.core_peer, self.q_peers, self.p_peers, self.o_peers = where
        self.slot = slot
        self.box_c, box_a0, box_a1, self.box_b, self.box_o = boxes
        self.box_a = (box_a0, box_a1)
        self.sem_c, self.sem_a, self.sem_b, self.sem_o = sems
        self.other, self.mine, self.load = other, mine, load
        half = self.box_o.shape[-1] // 2
        self.columns = (pl.ds(0, half), pl.ds(half, half))

    def core(self):
        return remote(self.other(), self.box_c, self.sem_c, (self.slot,), self.core_peer)

    def first(self, h, d):
        k, device = (self.q_peers, self.p_peers)[h][d]
        spot = (slice(None), slice(None), k) if h == 0 else (slice(None), k, slice(None))
        return remote(self.mine(spot, self.columns[h]), self.box_a[h].at[d], self.sem_a, (self.slot, h, d), device)

    def second(self, h, d):
        k, device = (self.p_peers, self.q_peers)[h][d]
        return remote(
            self.box_a[h].at[0, :, k], self.box_b.at[d, :, :, self.columns[h]], self.sem_b, (self.slot, h, d), device
        )

    def third(self, d):
        k, device = self.o_peers[d]
        return remote(self.box_b.at[0, k], self.box_o.at[d], self.sem_o, (self.slot, d), device)

    def begin(self):
        self.core().start()
        if self.load is not None:
            self.load().start()

    def stage_core(self):
        if self.load is not None:
            self.load().wait()
        self.core().wait_recv()
        side = self.side

        def add(i, carry):
            spot = (lax.div(i, side * side), lax.rem(lax.div(i, side), side), lax.rem(i, side))
            ref = self.mine(spot, slice(None))
            ref[...] = ref[...] + self.box_c[spot]
            return carry

        lax.fori_loop(0, self.outer * side * side, add, 0)
        for h in range(2):
            for d in range(side - 1):
                self.first(h, d).start()

    def stage_first(self):
        side = self.side
        for h in range(2):
            box = self.box_a[h]
            for d in range(side - 1):
                self.first(h, d).wait_recv()

            def add(i, carry):
                a, b = lax.div(i, side), lax.rem(i, side)
                total = self.mine((a, b, self.q) if h == 0 else (a, self.p, b), self.columns[h])[...]
                for d in range(side - 1):
                    total = total + box[d, a, b]
                box[0, a, b] = total
                return carry

            lax.fori_loop(0, self.outer * side, add, 0)
            for d in range(side - 1):
                self.second(h, d).start()

    def stage_second(self):
        box = self.box_b
        for h in range(2):
            k = self.p if h == 0 else self.q
            for d in range(self.side - 1):
                self.second(h, d).wait_recv()

            def add(a, carry):
                total = self.box_a[h][0, a, k]
                for d in range(self.side - 1):
                    total = total + box[d, a, :, self.columns[h]]
                box[0, a, :, self.columns[h]] = total
                return carry

            lax.fori_loop(0, self.outer, add, 0)
        for d in range(self.outer - 1):
            self.third(d).start()

    def stage_third(self):
        total = self.box_b[0, self.o].astype(F32)
        for d in range(self.outer - 1):
            self.third(d).wait_recv()
            total = total + self.box_o[d].astype(F32)
        return total

    def sent_first(self):
        self.core().wait_send()
        for h in range(2):
            for d in range(self.side - 1):
                self.first(h, d).wait_send()

    def sent_last(self):
        for h in range(2):
            for d in range(self.side - 1):
                self.second(h, d).wait_send()
        for d in range(self.outer - 1):
            self.third(d).wait_send()


def boxes_for(devices, rows, width):
    outer, side, _ = digits(devices)
    half = width // 2
    return [
        pltpu.VMEM((outer, side, side, rows, width), BF16),
        pltpu.VMEM((side - 1, outer, side, rows, half), BF16),
        pltpu.VMEM((side - 1, outer, side, rows, half), BF16),
        pltpu.VMEM((side - 1, outer, rows, width), BF16),
        pltpu.VMEM((outer - 1, rows, width), BF16),
    ]


def sems_for(devices, count):
    outer, side, _ = digits(devices)
    dma = pltpu.SemaphoreType.DMA
    return [dma((2, count)), dma((2, count, 2, side - 1)), dma((2, count, 2, side - 1)), dma((2, count, outer - 1))]


def mixing_kernel(
    devices, second_ref, above_ref, expand_ref, reduce_ref, bias_e_ref, bias_r_ref,
    out_ref, back_ref, grad_r_ref, grad_b_ref, grad_e_ref, above_b_ref, act_s, pre_s, grad_s, *rest,
):
    step = pl.program_id(0)
    rows, width = second_ref.shape
    strip = act_s.shape[1]
    per = width // strip
    slices = (len(rest) - 4) // 5
    sems = rest[5 * slices :]
    where = neighbours(devices)
    (o, p, q, c), core_peer, q_peers, p_peers, o_peers = where
    part = grad_s.shape[-2]

    def mover(k):
        def other():
            return grad_s.at[k % 2, :, :, :, 1 - c]

        def mine(spot, cols):
            return grad_s.at[(k % 2,) + tuple(spot) + (c, slice(None), cols)]

        return Scatter(devices, where, k, rest[5 * k : 5 * k + 5], sems, other, mine)

    movers = [mover(k) for k in range(slices)]
    w_e = expand_ref[...].reshape(width, strip)
    w_r = reduce_ref[...].reshape(strip, width)

    @pl.when(step == 0)
    def _():
        greet(peers_of(where))
        out_ref[...] = jnp.broadcast_to(bias_r_ref[...], out_ref.shape)
        back_ref[...] = jnp.zeros(back_ref.shape, F32)
        above_b_ref[...] = jnp.sum(above_ref[...].astype(F32), axis=0, keepdims=True)

    def close(k):
        grad_e_ref[k * part : (k + 1) * part, :] = movers[k].stage_third()

    final = slices * per - 1
    timed, late = [], []
    for k in range(slices):
        begun = 2 * ((k + 1) * per - 1) + 1
        for after, action in zip(
            AFTER, (movers[k].stage_core, movers[k].stage_first, movers[k].stage_second, functools.partial(close, k))
        ):
            if begun + after > 2 * final + 1:
                late.append((begun + after, -k, action))
            else:
                timed.append((begun + after, action))

    def stages(point):
        for when, action in timed:
            if when % 2 == point:
                pl.when(step == when // 2)(action)

    pre = dot(second_ref[...], w_e) + bias_e_ref[...]
    square = pre * pre
    curve = jnp.tanh(CURVE * pre * (1.0 + 0.044715 * square))
    hinge = 0.5 * (1.0 + curve)
    act_s[...] = (pre * hinge).astype(BF16)
    slope = hinge + 0.5 * pre * (1.0 - curve * curve) * (CURVE * (1.0 + 3 * 0.044715 * square))
    d_pre = (dot(above_ref[...], w_r, NT) * slope).astype(BF16)
    pre_s[...] = d_pre
    grad_b_ref[...] = jnp.sum(d_pre.astype(F32), axis=0, keepdims=True)
    stages(0)
    out_ref[...] += dot(act_s[...], w_r)
    back_ref[...] += dot(d_pre, w_e, NT)
    grad_r_ref[...] = dot(act_s[...], above_ref[...], TN).astype(BF16).reshape(grad_r_ref.shape)
    grad_e = dot(second_ref[...], pre_s[...], TN).astype(BF16)
    for k in range(slices):
        for j in range(per):
            @pl.when(step == k * per + j)
            def _():
                if j == 0 and k >= 2:
                    movers[k - 2].sent_first()
                grad_s[k % 2, :, :, :, :, :, j * strip : (j + 1) * strip] = grad_e.reshape(grad_s.shape[1:-1] + (strip,))
                if j == per - 1:
                    movers[k].begin()

    stages(1)

    @pl.when(step == final)
    def _():
        for *_, action in sorted(late, key=lambda entry: entry[:2]):
            action()
        for k in range(max(0, slices - 2), slices):
            movers[k].sent_first()
        for k in range(slices):
            movers[k].sent_last()


def mixing(devices, second, above, gathered, bias_e, bias_r, part):
    rows, width = second.shape
    hidden = bias_e.shape[1]
    many = hidden // devices
    sides = hidden // width
    strip = STRIP
    per = width // strip
    outer, side, core = digits(devices)
    fixed = pl.BlockSpec((rows, width), lambda i: (0, 0), pipeline_mode=pl.Buffered(1))
    whole = pl.BlockSpec(memory_space=pltpu.VMEM)
    scratch = [pltpu.VMEM((rows, strip), BF16)] * 2 + [pltpu.VMEM((2, outer, side, side, core, part, width), BF16)]
    for k in range(sides):
        scratch += boxes_for(devices, part, width)
    return pl.pallas_call(
        functools.partial(mixing_kernel, devices),
        grid=(hidden // strip,),
        in_specs=[
            fixed, fixed,
            pl.BlockSpec((devices, part, strip), lambda i: (0, many // part + 1 + i // per, i % per)),
            pl.BlockSpec((strip // many, many, width), lambda i: (i, 0, 0)),
            pl.BlockSpec((1, strip), lambda i: (0, i)),
            pl.BlockSpec((1, width), lambda i: (0, 0)),
        ],
        out_specs=[
            fixed,
            fixed,
            pl.BlockSpec((strip // many, many, width), lambda i: (i, 0, 0)),
            pl.BlockSpec((1, strip), lambda i: (0, i)),
            pl.BlockSpec((sides * part, width), lambda i: (0, 0)),
            pl.BlockSpec((1, width), lambda i: (0, 0)),
        ],
        out_shape=[
            jax.ShapeDtypeStruct((rows, width), F32),
            jax.ShapeDtypeStruct((rows, width), F32),
            jax.ShapeDtypeStruct((devices, many, width), BF16),
            jax.ShapeDtypeStruct((1, hidden), F32),
            jax.ShapeDtypeStruct((sides * part, width), F32),
            jax.ShapeDtypeStruct((1, width), F32),
        ],
        scratch_shapes=scratch + sems_for(devices, sides),
        compiler_params=pltpu.CompilerParams(collective_id=3, has_side_effects=True, vmem_limit_bytes=57 << 20),
        name="mixing",
    )(second, above, gathered, gathered, bias_e, bias_r)


def join_kernel(
    devices, window_ref, first_ref, final_ref, one_ref, above_ref, live_ref, w_ref, bias_ref, gain_ref, shift_ref,
    combined_ref, out_ref, second_ref, reduce_ref, side_in, part_s, halo_sem,
):
    slots, width = one_ref.shape
    half = slots // 2
    tile = 256
    me = lax.axis_index("fsdp")
    last = devices - 1
    left, right = lax.rem(me + last, devices), lax.rem(me + 1, devices)
    greet([left, right])

    def to_left():
        return remote(window_ref.at[:half], side_in.at[1], halo_sem, (0,), left)

    def to_right():
        return remote(window_ref.at[half + slots :], side_in.at[0], halo_sem, (1,), right)

    @pl.when(me > 0)
    def _():
        to_left().start()

    @pl.when(me < last)
    def _():
        to_right().start()

    @pl.when(me == 0)
    def _():
        side_in[0] = jnp.zeros((half, width), BF16)

    @pl.when(me == last)
    def _():
        side_in[1] = jnp.zeros((half, width), BF16)

    w_o = w_ref[...].reshape(width, width)

    owns = (first_ref, final_ref)

    def before(side, i, carry):
        here = pl.ds(pl.multiple_of(i * tile, tile), tile)
        at = pl.ds(pl.multiple_of(side * half + i * tile, tile), tile)
        part_s[at, :] = dot(owns[side][here, :], w_o)
        reduce_ref[at, :] = (live_ref[at, :] * above_ref[at, :].astype(F32)).astype(BF16)
        return carry

    for side in range(2):
        lax.fori_loop(0, half // tile, functools.partial(before, side), 0)

    def after(side, i, carry):
        here = pl.ds(pl.multiple_of(i * tile, tile), tile)
        at = pl.ds(pl.multiple_of(side * half + i * tile, tile), tile)
        other = side_in[side, here, :]
        combined_ref[at, :] = owns[side][here, :] + other
        attended = part_s[at, :] + dot(other, w_o) + bias_ref[...]
        out = one_ref[at, :].astype(F32) + live_ref[at, :] * attended
        out_ref[at, :] = out
        second_ref[at, :] = layer_norm(out, gain_ref[...], shift_ref[...]).astype(BF16)
        return carry

    @pl.when(me > 0)
    def _():
        to_right().wait_recv()

    lax.fori_loop(0, half // tile, functools.partial(after, 0), 0)

    @pl.when(me < last)
    def _():
        to_left().wait_recv()

    lax.fori_loop(0, half // tile, functools.partial(after, 1), 0)

    @pl.when(me > 0)
    def _():
        to_left().wait_send()

    @pl.when(me < last)
    def _():
        to_right().wait_send()


def join(devices, window, one, above, live, gathered, bias, gain, shift, part, sides):
    slots, width = one.shape
    dma = pltpu.SemaphoreType.DMA
    rows = pl.BlockSpec((slots, width), lambda i: (0, 0))
    thin = pl.BlockSpec((1, width), lambda i: (0, 0))
    low = jax.ShapeDtypeStruct((slots, width), BF16)
    return pl.pallas_call(
        functools.partial(join_kernel, devices),
        grid=(1,),
        in_specs=[
            pl.BlockSpec(memory_space=pl.ANY),
            pl.BlockSpec((slots // 2, width), lambda i: (1, 0)), pl.BlockSpec((slots // 2, width), lambda i: (2, 0)), rows, rows, pl.BlockSpec((slots, 1), lambda i: (0, 0)),
            pl.BlockSpec((devices, part, width), lambda i: (0, sides, 0)), thin, thin, thin,
        ],
        out_specs=[rows] * 4,
        out_shape=[low, jax.ShapeDtypeStruct((slots, width), F32), low, low],
        scratch_shapes=[pltpu.VMEM((2, slots // 2, width), BF16), pltpu.VMEM((slots, width), F32), dma((2, 2))],
        compiler_params=pltpu.CompilerParams(collective_id=6, has_side_effects=True, vmem_limit_bytes=57 << 20),
        name="join",
    )(window, window, window, one, above, live, gathered, bias, gain, shift)


def turn_kernel(
    devices, out_one_ref, d_second_ref, mixed_ref, two_ref, above_ref, combined_ref, live_ref, gain_ref, w_o_ref,
    bias_r_ref, bias_e_ref,
    wide_ref, grad_one_ref, one_ref, res_two_ref, grad_o_ref, small_ref, attend_s, halo_sem,
):
    slots, width = two_ref.shape
    half = slots // 2
    tile = 256
    part = grad_o_ref.shape[1]
    me = lax.axis_index("fsdp")
    last = devices - 1
    left, right = lax.rem(me + last, devices), lax.rem(me + 1, devices)
    greet([left, right])

    def to_left():
        return remote(wide_ref.at[half : 2 * half], wide_ref.at[half + slots :], halo_sem, (0,), left)

    def to_right():
        return remote(wide_ref.at[2 * half : 3 * half], wide_ref.at[:half], halo_sem, (1,), right)

    small_ref[...] = jnp.zeros(small_ref.shape, F32)
    gain = gain_ref[...]

    def norm_tile(i, carry):
        at = pl.ds(pl.multiple_of(i * tile, tile), tile)
        live = live_ref[at, :]
        values = out_one_ref[at, :]
        above = d_second_ref[at, :]
        center = values - jnp.mean(values, axis=1, keepdims=True)
        scale = lax.rsqrt(jnp.mean(center * center, axis=1, keepdims=True) + EPS_NORM)
        center = center * scale
        small_ref[2:3, :] += jnp.sum(above * center, axis=0, keepdims=True)
        small_ref[3:4, :] += jnp.sum(above, axis=0, keepdims=True)
        above = above * gain
        mean = jnp.mean(above, axis=1, keepdims=True)
        along = jnp.mean(above * center, axis=1, keepdims=True)
        total = live * (above_ref[at, :].astype(F32) + scale * (above - mean - center * along))
        low = total.astype(BF16)
        grad_one_ref[at, :] = low
        attend_s[at, :] = low
        small_ref[4:5, :] += jnp.sum(low.astype(F32), axis=0, keepdims=True)
        wide_ref[pl.ds(pl.multiple_of(half + i * tile, tile), tile), :] = dot(low, w_o_ref[...], NT).astype(BF16)
        return carry

    lax.fori_loop(0, half // tile, norm_tile, 0)

    @pl.when(me > 0)
    def _():
        to_left().start()

    lax.fori_loop(half // tile, slots // tile, norm_tile, 0)

    @pl.when(me < last)
    def _():
        to_right().start()

    def finish_tile(i, carry):
        at = pl.ds(pl.multiple_of(i * tile, tile), tile)
        live = live_ref[at, :]
        one_ref[at, :] = (live * out_one_ref[at, :]).astype(BF16)
        res_two_ref[at, :] = (live * (two_ref[at, :].astype(F32) + mixed_ref[at, :])).astype(BF16)
        return carry

    lax.fori_loop(0, slots // tile, finish_tile, 0)

    def weights(i, carry):
        cols = pl.ds(pl.multiple_of(i * tile, tile), tile)
        many = tile // part
        grad_o_ref[pl.ds(pl.multiple_of(i * many, many), many)] = (
            dot(combined_ref[:, cols], attend_s[...], TN).astype(BF16).reshape(many, part, width)
        )
        return carry

    lax.fori_loop(0, width // tile, weights, 0)
    small_ref[5:6, :] = bias_r_ref[...]
    for k in range(bias_e_ref.shape[1] // width):
        small_ref[6 + k : 7 + k, :] = bias_e_ref[:, k * width : (k + 1) * width]

    @pl.when(me > 0)
    def _():
        to_right().wait_recv()
        to_left().wait_send()

    @pl.when(me == 0)
    def _():
        wide_ref[:half] = jnp.zeros((half, width), BF16)

    @pl.when(me < last)
    def _():
        to_left().wait_recv()
        to_right().wait_send()

    @pl.when(me == last)
    def _():
        wide_ref[half + slots :] = jnp.zeros((half, width), BF16)


def turn(devices, out_one, d_second, mixed, two, above, combined, live, gain, w_o, bias_r, bias_e):
    slots, width = two.shape
    part = width // devices
    vmem = pl.BlockSpec(memory_space=pltpu.VMEM)
    rows_low = jax.ShapeDtypeStruct((slots, width), BF16)
    return pl.pallas_call(
        functools.partial(turn_kernel, devices),
        in_specs=[vmem] * 11,
        out_specs=(vmem,) * 6,
        out_shape=(
            jax.ShapeDtypeStruct((2 * slots, width), BF16), rows_low, rows_low, rows_low,
            jax.ShapeDtypeStruct((devices, part, width), BF16),
            jax.ShapeDtypeStruct((16, width), F32),
        ),
        scratch_shapes=[pltpu.VMEM((slots, width), BF16), pltpu.SemaphoreType.DMA((2, 2))],
        compiler_params=pltpu.CompilerParams(collective_id=5, has_side_effects=True, vmem_limit_bytes=57 << 20),
        name="turn",
    )(out_one, d_second, mixed, two, above, combined, live, gain, w_o, bias_r, bias_e)


def tail_kernel(
    devices, grad_r_ref, grad_o_ref, d_shared_ref, d_value_ref, normed_ref, head_ref, own_ref, end_ref, above_ref, live_ref,
    gain_ref, w_s_ref, w_v_ref, small_ref,
    back_ref, out_s_ref, out_v_ref, out_o_ref, out_r_ref, thin_ref, long_ref,
    side_s, side_in, vector_s, vector_in, grad_s, load_sem, halo_sem, vector_sem, *rest,
):
    window, width = normed_ref.shape
    slots = own_ref.shape[0]
    half = slots // 2
    part = out_s_ref.shape[0]
    many = out_r_ref.shape[0]
    tile = 256
    where = neighbours(devices)
    (o, p, q, c), core_peer, q_peers, p_peers, o_peers = where
    me = lax.axis_index("fsdp")
    outer, side, core = digits(devices)
    owns, rest = rest[:3], rest[3:]
    sems = rest[-4:]

    def distant(source, row, rows, k):
        at = pl.ds(row, rows)

        def other():
            return source.at[:, :, :, 1 - c, at, :]

        def mine(spot, cols):
            return owns[k].at[tuple(spot) + (slice(None), cols)]

        def load():
            return pltpu.make_async_copy(source.at[:, :, :, c, at, :], owns[k], load_sem.at[k])

        return Scatter(devices, where, k, rest[5 * k : 5 * k + 5], sems, other, mine, load)

    def near(j, k):
        def other():
            return grad_s.at[j, :, :, :, 1 - c]

        def mine(spot, cols):
            return grad_s.at[(j,) + tuple(spot) + (c, slice(None), cols)]

        return Scatter(devices, where, k, rest[5 * k : 5 * k + 5], sems, other, mine)

    movers = [
        distant(grad_r_ref, 0, many // 2, 0), distant(grad_r_ref, many // 2, many // 2, 1), distant(grad_o_ref, 0, part, 2),
        near(0, 3), near(1, 4),
    ]
    last = devices - 1
    left, right = lax.rem(me + last, devices), lax.rem(me + 1, devices)
    greet(peers_of(where) + [left, right])
    for k in range(3):
        movers[k].begin()

    def to_left():
        return remote(side_s.at[0], side_in.at[1], halo_sem, (0,), left)

    def to_right():
        return remote(side_s.at[1], side_in.at[0], halo_sem, (1,), right)

    vector_s[...] = small_ref[...]
    gain = gain_ref[...]

    def norm_tile(ref, row, at):
        values = ref[pl.ds(row, tile), :].astype(F32)
        above = dot(d_shared_ref[at, :], w_s_ref[...], NT) + dot(d_value_ref[at, :], w_v_ref[...], NT)
        center = values - jnp.mean(values, axis=1, keepdims=True)
        scale = lax.rsqrt(jnp.mean(center * center, axis=1, keepdims=True) + EPS_NORM)
        center = center * scale
        vector_s[0:1, :] += jnp.sum(above * center, axis=0, keepdims=True)
        vector_s[1:2, :] += jnp.sum(above, axis=0, keepdims=True)
        above = above * gain
        mean = jnp.mean(above, axis=1, keepdims=True)
        along = jnp.mean(above * center, axis=1, keepdims=True)
        return scale * (above - mean - center * along)

    def side_tiles(i, carry):
        row = pl.multiple_of(i * tile, tile)
        side_s[0, pl.ds(row, tile), :] = norm_tile(head_ref, row, pl.ds(row, tile)).astype(BF16)
        at = pl.ds(pl.multiple_of(half + slots + i * tile, tile), tile)
        side_s[1, pl.ds(row, tile), :] = norm_tile(end_ref, row, at).astype(BF16)
        return carry

    lax.fori_loop(0, half // tile, side_tiles, 0)

    @pl.when(me > 0)
    def _():
        to_left().start()

    @pl.when(me < last)
    def _():
        to_right().start()

    movers[0].stage_core()

    def weights(j, ref):
        wide = tile // part

        def strip(i, carry):
            cols = pl.ds(pl.multiple_of(i * tile, tile), tile)
            block = dot(normed_ref[:, cols], ref[...], TN).astype(BF16).reshape(wide // core, core, part, width)
            for k in range(wide // core):
                index = i * (wide // core) + k
                spot = (lax.div(index, side * side), lax.rem(lax.div(index, side), side), lax.rem(index, side))
                grad_s[(j,) + spot] = block[k]
            return carry

        lax.fori_loop(0, width // tile, strip, 0)

    weights(0, d_shared_ref)
    movers[3].begin()
    movers[1].stage_core()
    movers[0].stage_first()
    weights(1, d_value_ref)
    movers[4].begin()
    movers[2].stage_core()
    movers[1].stage_first()
    movers[0].stage_second()

    def own_tiles(i, carry):
        row = pl.multiple_of(i * tile, tile)
        at = pl.ds(pl.multiple_of(half + i * tile, tile), tile)
        here = pl.ds(row, tile)
        total = above_ref[here, :].astype(F32) + norm_tile(own_ref, row, at)
        back_ref[here, :] = (live_ref[here, :] * total).astype(BF16)
        return carry

    lax.fori_loop(0, slots // tile, own_tiles, 0)

    def vector_copies(stage):
        group = ([(0, core_peer)], q_peers, p_peers, o_peers)[stage]
        base = (0, 1, side, 2 * side - 1)[stage]
        return [
            remote(vector_s if stage == 0 else vector_in.at[base - 1], vector_in.at[base + d], vector_sem, (base + d,), device)
            for d, (_, device) in enumerate(group)
        ]

    def vector_stage(stage):
        base = (0, 1, side, 2 * side - 1)[stage]
        copies = vector_copies(stage)
        total = vector_s[...] if stage == 0 else vector_in[base - 1]
        for d, copy in enumerate(copies):
            copy.wait_recv()
            total = total + vector_in[base + d]
        vector_in[base + len(copies) - 1] = total

    for copy in vector_copies(0):
        copy.start()
    movers[3].stage_core()
    movers[2].stage_first()
    movers[1].stage_second()
    out_r_ref[: many // 2, :] = movers[0].stage_third()
    vector_stage(0)
    for copy in vector_copies(1):
        copy.start()
    movers[4].stage_core()
    movers[3].stage_first()
    movers[2].stage_second()
    out_r_ref[many // 2 :, :] = movers[1].stage_third()
    vector_stage(1)
    for copy in vector_copies(2):
        copy.start()
    movers[4].stage_first()
    movers[3].stage_second()
    out_o_ref[...] = movers[2].stage_third()
    vector_stage(2)
    for copy in vector_copies(3):
        copy.start()

    @pl.when(me > 0)
    def _():
        to_right().wait_recv()

    @pl.when(me == 0)
    def _():
        side_in[0] = jnp.zeros((half, width), BF16)

    @pl.when(me < last)
    def _():
        to_left().wait_recv()

    @pl.when(me == last)
    def _():
        side_in[1] = jnp.zeros((half, width), BF16)

    for k in range(2):
        at = slice(k * half, (k + 1) * half)
        back_ref[at, :] = (back_ref[at, :].astype(F32) + side_in[k].astype(F32)).astype(BF16)
    movers[4].stage_second()
    out_s_ref[...] = movers[3].stage_third()
    vector_stage(3)
    out_v_ref[...] = movers[4].stage_third()
    vectors = 2 * side + outer - 3
    total = vector_in[vectors]
    thin_ref[...] = pltpu.roll(total, lax.rem(width - me * part, width), 1)[:, :DH]
    each = long_ref.shape[1]
    long_rows = [total[6 + k : 7 + k, :] for k in range(devices * each // width)]
    mine = lax.div(me * each, width)
    chosen = long_rows[0]
    for k in range(1, len(long_rows)):
        chosen = jnp.where(mine == k, long_rows[k], chosen)
    long_ref[...] = pltpu.roll(chosen, lax.rem(width - lax.rem(me * each, width), width), 1)[:, :each]
    for stage in range(4):
        for copy in vector_copies(stage):
            copy.wait_send()

    @pl.when(me > 0)
    def _():
        to_left().wait_send()

    @pl.when(me < last)
    def _():
        to_right().wait_send()

    for mover in movers:
        mover.sent_first()
        mover.sent_last()


def tail(devices, grad_r, grad_o, d_shared, d_values, normed, head, own, end, above, live, gain, w_s, w_v, small):
    window, width = normed.shape
    slots = own.shape[0]
    outer, side, core = digits(devices)
    part, many = grad_o.shape[1], grad_r.shape[1]
    each = many
    vmem = pl.BlockSpec(memory_space=pltpu.VMEM)
    anywhere = pl.BlockSpec(memory_space=pl.ANY)
    dma = pltpu.SemaphoreType.DMA
    sizes = [many // 2, many // 2, part, part, part]
    scratch = [
        pltpu.VMEM((2, slots // 2, width), BF16), pltpu.VMEM((2, slots // 2, width), BF16),
        pltpu.VMEM((16, width), F32), pltpu.VMEM((2 * side + outer - 2, 16, width), F32),
        pltpu.VMEM((2, outer, side, side, core, part, width), BF16),
        dma((3,)), dma((2, 2)), dma((2, 2 * side + outer - 2)),
    ]
    scratch += [pltpu.VMEM((outer, side, side, rows, width), BF16) for rows in sizes[:3]]
    for rows in sizes:
        scratch += boxes_for(devices, rows, width)
    shape = (outer, side, side, core)
    return pl.pallas_call(
        functools.partial(tail_kernel, devices),
        in_specs=[anywhere, anywhere] + [vmem] * 12,
        out_specs=(vmem,) * 7,
        out_shape=(
            jax.ShapeDtypeStruct((slots, width), BF16),
            jax.ShapeDtypeStruct((part, width), F32),
            jax.ShapeDtypeStruct((part, width), F32),
            jax.ShapeDtypeStruct((part, width), F32),
            jax.ShapeDtypeStruct((many, width), F32),
            jax.ShapeDtypeStruct((16, DH), F32),
            jax.ShapeDtypeStruct((1, each), F32),
        ),
        scratch_shapes=scratch + sems_for(devices, len(sizes)),
        compiler_params=pltpu.CompilerParams(collective_id=4, has_side_effects=True, vmem_limit_bytes=57 << 20),
        name="tail",
    )(
        grad_r.reshape(shape + grad_r.shape[1:]), grad_o.reshape(shape + grad_o.shape[1:]),
        d_shared, d_values, normed, head, own, end, above, live, gain, w_s, w_v, small,
    )


def find_ranks(length_ref, target_ref, bucket_ref, packed_ref, info_ref, before_s):
    devices = length_ref.shape[0]
    lists, slots = bucket_ref.shape
    me = lax.axis_index("fsdp")
    base = me * slots
    window = 2 * slots

    def look(s, carry):
        start, mine, found, one, two = carry
        size = length_ref[s]
        target = target_ref[s]
        middle = start + lax.shift_right_logical(size, 1)
        inside = (middle >= base) & (middle < base + slots)
        offset = start - base + slots // 2
        entry = (offset, offset + size, target)
        first, second = inside & (found == 0), inside & (found == 1)
        one = tuple(jnp.where(first, new, old) for new, old in zip(entry, one))
        two = tuple(jnp.where(second, new, old) for new, old in zip(entry, two))
        return start + size, jnp.where(target == me, size, mine), found + inside.astype(jnp.int32), one, two

    zero = jnp.int32(0)
    nothing = (jnp.int32(window), jnp.int32(window), zero)
    total, mine, found, one, two = lax.fori_loop(0, devices, look, (zero, zero, zero, nothing, nothing))
    for k, value in enumerate((one[0], one[1], two[0], two[1], one[2], two[2], total, found)):
        info_ref[k] = value

    def fill(i, carry):
        at = pl.ds(pl.multiple_of(i * DH, DH), DH)
        first = lax.broadcasted_iota(jnp.int32, (DH, slots), 0) + i * DH
        second = lax.broadcasted_iota(jnp.int32, (DH, slots), 1)
        before_s[at, :] = jnp.where(first < second, 1.0, 0.0).astype(BF16)
        return carry

    lax.fori_loop(0, slots // DH, fill, 0)
    left = lax.broadcasted_iota(jnp.int32, (DH, DH), 0)
    right = lax.broadcasted_iota(jnp.int32, (DH, DH), 1)
    smaller = jnp.where((left // BUCKETS == right // BUCKETS) & (right < left), 1.0, 0.0).astype(BF16)
    many = DH // BUCKETS
    bucket = lax.broadcasted_iota(jnp.int32, (many, BUCKETS, slots), 1)
    live = lax.broadcasted_iota(jnp.int32, (many, BUCKETS, slots), 2) < mine
    ranks = []
    for g in range(lists // many):
        here = (jnp.broadcast_to(bucket_ref[g * many : (g + 1) * many, :][:, None, :], bucket.shape) == bucket) & live
        one_hot = jnp.where(here, 1.0, 0.0)
        flat = one_hot.reshape(DH, slots).astype(BF16)
        offset = jnp.sum(dot(smaller, flat), axis=1, keepdims=True)
        place = (dot(flat, before_s[...]) + offset).reshape(many, BUCKETS, slots)
        ranks.append(jnp.sum(one_hot * place, axis=1))
    rank = jnp.concatenate(ranks, axis=0)
    live = lax.broadcasted_iota(jnp.int32, (lists, slots), 1) < mine
    packed_ref[:lists, :] = jnp.where(live, jnp.floor(rank * (1.0 / GROUP)), FREE).astype(BF16)


def project_kernel(
    info_ref, head_ref, own_ref, tail_ref, gain_ref, shift_ref, w_s_ref, w_v_ref, one_ref, two_ref,
    normed_ref, shared_ref, value_ref, code_ref,
):
    i = pl.program_id(0)
    tile = own_ref.shape[0]
    steps = pl.num_programs(0)

    def go(ref):
        normed = layer_norm(ref[...].astype(F32), gain_ref[...], shift_ref[...]).astype(BF16)
        normed_ref[...] = normed
        shared_ref[...] = dot(normed, w_s_ref[...]).astype(BF16)
        value_ref[...] = dot(normed, w_v_ref[...]).astype(BF16)

    @pl.when(i < steps // 4)
    def _():
        go(head_ref)

    @pl.when((i >= steps // 4) & (i < steps - steps // 4))
    def _():
        go(own_ref)

    @pl.when(i >= steps - steps // 4)
    def _():
        go(tail_ref)

    @pl.when(i == 0)
    def _():
        lists, window = code_ref.shape
        lane = lax.broadcasted_iota(jnp.int32, (lists, window), 1)
        code = jnp.full((lists, window), FREE, F32)
        for k, ref in enumerate((one_ref, two_ref)):
            begin, end = info_ref[2 * k], info_ref[2 * k + 1]
            rows = ref[0].astype(F32)
            moved = pltpu.roll(jnp.concatenate([rows, rows], axis=1), lax.rem(begin, window), 1)
            code = jnp.where((lane >= begin) & (lane < end), moved + 32.0 * k, code)
        code_ref[...] = code.astype(BF16)


def project(info, head, own, tail, gain, shift, w_s, w_v, blocks):
    slots, width = own.shape
    window = 2 * slots
    lists = ROUNDS * HEADS
    tile = 256
    steps = window // tile
    quarter = steps // 4
    rows = pl.BlockSpec((tile, width), lambda i, info: (i, 0))
    vector = pl.BlockSpec((1, width), lambda i, info: (0, 0))
    matrix = pl.BlockSpec((width, width), lambda i, info: (0, 0), pipeline_mode=pl.Buffered(1))
    wide = jax.ShapeDtypeStruct((window, width), BF16)
    return pl.pallas_call(
        project_kernel,
        grid_spec=pltpu.PrefetchScalarGridSpec(
            num_scalar_prefetch=1,
            grid=(steps,),
            in_specs=[
                pl.BlockSpec((tile, width), lambda i, info: (jnp.minimum(i, quarter - 1), 0)),
                pl.BlockSpec((tile, width), lambda i, info: (jnp.clip(i - quarter, 0, 2 * quarter - 1), 0)),
                pl.BlockSpec((tile, width), lambda i, info: (jnp.clip(i - 3 * quarter, 0, quarter - 1), 0)),
                vector, vector, matrix, matrix,
                pl.BlockSpec((1, lists, slots), lambda i, info: (info[4], 0, 0)),
                pl.BlockSpec((1, lists, slots), lambda i, info: (info[5], 0, 0)),
            ],
            out_specs=[rows, rows, rows, pl.BlockSpec((lists, window), lambda i, info: (0, 0))],
        ),
        out_shape=[wide, wide, wide, jax.ShapeDtypeStruct((lists, window), BF16)],
        compiler_params=pltpu.CompilerParams(vmem_limit_bytes=40 << 20),
        name="project",
    )(info, head, own, tail, gain, shift, w_s, w_v, blocks, blocks)


def gather_kernel(devices, arrays, length_ref, target_ref, bucket_ref, vector_ref, rows_ref, *refs):
    sources, outs, (info_ref, head_ref, end_ref) = refs[: arrays - 1], refs[arrays - 1 : 2 * arrays - 1], refs[2 * arrays - 1 : 2 * arrays + 2]
    packed_s, before_s, own_sem, sem_o, sem_a, sem_b, sem_c, halo_sem, edge_sem = refs[2 * arrays + 2 :]
    sources = sources + (packed_s,)
    outer, side, core = digits(devices)
    (o, p, q, c), core_peer, q_peers, p_peers, o_peers = neighbours(devices)
    me = lax.axis_index("fsdp")
    last_device = devices - 1
    left, right = lax.rem(me + last_device, devices), lax.rem(me + 1, devices)
    greet([core_peer] + [d for _, d in q_peers] + [d for _, d in p_peers] + [d for _, d in o_peers] + [left, right])
    half = sources[0].shape[-1] // 2
    border = head_ref.shape[0]

    def to_left():
        return remote(rows_ref.at[:border], end_ref, halo_sem, (0,), left)

    def to_right():
        return remote(rows_ref.at[border:], head_ref, halo_sem, (1,), right)

    def blank(ref):
        return pltpu.make_async_copy(before_s.at[:border], ref, edge_sem.at[0])

    columns = (pl.ds(0, half), pl.ds(half, half))

    locals_, begun, first, second, last = [], {}, {}, {}, {}
    for s in range(arrays):
        if s == arrays - 1:
            find_ranks(length_ref, target_ref, bucket_ref, packed_s, info_ref, before_s)
            packed_s[bucket_ref.shape[0] :, :] = vector_ref[...]
        locals_.append(pltpu.make_async_copy(sources[s], outs[s].at[o, p, q, c], own_sem.at[s]))
        locals_[s].start()
        for d, (k, device) in enumerate(o_peers):
            begun[s, d] = remote(sources[s], outs[s].at[o, p, q, c], sem_o, (s, d), device)
            begun[s, d].start()

    @pl.when(me > 0)
    def _():
        to_left().start()

    @pl.when(me < last_device)
    def _():
        to_right().start()

    before_s[:border, :] = jnp.zeros((border, before_s.shape[1]), BF16)

    @pl.when(me == 0)
    def _():
        blank(head_ref).start()

    @pl.when(me == last_device)
    def _():
        blank(end_ref).start()

    def stage_a(s):
        locals_[s].wait()
        for d in range(outer - 1):
            begun[s, d].wait_recv()
        for h, peers in enumerate((q_peers, p_peers)):
            piece = outs[s].at[:, p, q, c, :, columns[h]]
            for d, (k, device) in enumerate(peers):
                first[s, h, d] = remote(piece, piece, sem_a, (s, h, d), device)
                first[s, h, d].start()

    def stage_b(s):
        for h, peers in enumerate((p_peers, q_peers)):
            for d in range(side - 1):
                first[s, h, d].wait_recv()
            piece = outs[s].at[:, p, :, c, :, columns[h]] if h == 0 else outs[s].at[:, :, q, c, :, columns[h]]
            for d, (k, device) in enumerate(peers):
                second[s, h, d] = remote(piece, piece, sem_b, (s, h, d), device)
                second[s, h, d].start()

    def stage_c(s):
        for h in range(2):
            for d in range(side - 1):
                second[s, h, d].wait_recv()
        piece = outs[s].at[:, :, :, c]
        last[s] = remote(piece, piece, sem_c, (s,), core_peer)
        last[s].start()

    for t in range(arrays + 2):
        if t < arrays:
            stage_a(t)
        if 0 <= t - 1 < arrays:
            stage_b(t - 1)
        if 0 <= t - 2 < arrays:
            stage_c(t - 2)
    for s in range(arrays):
        last[s].wait_recv()

    @pl.when(me > 0)
    def _():
        to_right().wait_recv()
        to_left().wait_send()

    @pl.when(me == 0)
    def _():
        blank(head_ref).wait()

    @pl.when(me < last_device)
    def _():
        to_left().wait_recv()
        to_right().wait_send()

    @pl.when(me == last_device)
    def _():
        blank(end_ref).wait()

    for group in (begun, first, second, last):
        for copy in group.values():
            copy.wait_send()


def gather(devices, lengths, destination, buckets, vectors, rows, arrays):
    outer, side, core = digits(devices)
    lists, slots = buckets.shape
    packed = jax.ShapeDtypeStruct((lists + vectors.shape[0], slots), BF16)
    shapes = [jax.ShapeDtypeStruct(array.shape, array.dtype) for array in arrays] + [packed]
    count = len(shapes)
    dma = pltpu.SemaphoreType.DMA
    anywhere = pl.BlockSpec(memory_space=pl.ANY)
    hbm = pl.BlockSpec(memory_space=pltpu.HBM)
    smem = pl.BlockSpec(memory_space=pltpu.SMEM)
    vmem = pl.BlockSpec(memory_space=pltpu.VMEM)
    outs = pl.pallas_call(
        functools.partial(gather_kernel, devices, count),
        out_shape=tuple(jax.ShapeDtypeStruct((outer, side, side, core) + shape.shape, shape.dtype) for shape in shapes)
        + (jax.ShapeDtypeStruct((8,), jnp.int32),)
        + (jax.ShapeDtypeStruct((slots // 2, rows.shape[1]), BF16),) * 2,
        in_specs=[smem, smem, vmem, vmem] + [anywhere] * count,
        out_specs=(hbm,) * count + (smem, hbm, hbm),
        scratch_shapes=[
            pltpu.VMEM(packed.shape, BF16), pltpu.VMEM((slots, slots), BF16),
            dma((count,)), dma((2, count, outer - 1)), dma((2, count, 2, side - 1)), dma((2, count, 2, side - 1)), dma((2, count)),
            dma((2, 2)), dma((1,)),
        ],
        compiler_params=pltpu.CompilerParams(collective_id=2, has_side_effects=True, vmem_limit_bytes=57 << 20),
        name="gather",
    )(lengths, destination, buckets, vectors, rows, *arrays)
    return [out.reshape((devices,) + shape.shape) for out, shape in zip(outs, shapes)] + list(outs[count:])


def body(
    input_one, input_two, upstream_one, upstream_two, lengths, destination, buckets,
    w_shared, w_value, w_output, w_expand, w_reduce,
    gain_attend, shift_attend, gain_mixing, shift_mixing, bias_output, bias_expand, bias_reduce,
):
    devices = lax.axis_size("fsdp")
    me = lax.axis_index("fsdp")
    slots, width = input_one.shape
    half = slots // 2
    window = 2 * slots
    part = w_shared.shape[0]
    hidden = w_expand.shape[1]
    sides = hidden // width
    base = me * slots
    lists = ROUNDS * HEADS
    spot = jnp.arange(width, dtype=jnp.int32)
    short = jnp.stack([gain_attend, shift_attend, gain_mixing, shift_mixing, bias_output, bias_reduce])
    short = jnp.where(spot // part == me, jnp.tile(short, (1, devices)), 0.0)
    many = hidden // devices
    long = jnp.tile(bias_expand, width // many)[None]
    long = jnp.where(spot[None] // many + (width // many) * jnp.arange(sides, dtype=jnp.int32)[:, None] == me, long, 0.0)
    vectors = jnp.concatenate([short, long], axis=0)
    high = lax.reduce_precision(vectors, 8, 7)
    count = vectors.shape[0]
    packed = jnp.concatenate(
        [high.astype(BF16), (vectors - high).astype(BF16), jnp.zeros((24 - 2 * count, width), BF16)], axis=0
    )
    second_gather = lax.all_gather(
        jnp.concatenate(
            [w_reduce, w_output] + [w_expand[:, k * width : (k + 1) * width] for k in range(sides)], axis=0
        ),
        "fsdp", axis=0, tiled=False,
    )
    full_shared, full_value, packed, info, two_head, two_tail = gather(
        devices, lengths, destination, buckets[0], packed, input_two, [w_shared, w_value]
    )
    full_shared, full_value = full_shared.reshape(width, width), full_value.reshape(width, width)
    vectors = jnp.sum(packed[:, lists : lists + 2 * count].astype(F32), axis=0)
    vectors = vectors[:count] + vectors[count:]
    gain_a, shift_a, gain_m, shift_m, bias_o, bias_r = (vectors[k : k + 1] for k in range(6))
    bias_e = vectors[6:].reshape(1, hidden)
    full_output = second_gather[:, sides * part : (sides + 1) * part].reshape(width, width)
    lane = jnp.arange(HEADS * DH, dtype=jnp.int32)
    row = jnp.arange(lists, dtype=jnp.int32)[:, None]
    spread = (row == ((lane % 64) // 16) * HEADS + lane // DH).astype(BF16)

    live = ((base + jnp.arange(slots, dtype=jnp.int32)) < info[6]).astype(F32)[:, None]
    normed, shared, values, code = project(
        info, two_head, input_two, two_tail, gain_a, shift_a, full_shared, full_value, packed
    )
    combined_window, lse, lone = attend(info, shared, values, code, spread)
    combined, out_one, second, d_reduce = join(
        devices, combined_window, input_one, upstream_two, live, second_gather, bias_o, gain_m, shift_m, part, sides
    )
    mixed, d_second, grad_reduce, grad_bias_expand, grad_expand, grad_bias_reduce = mixing(
        devices, second, d_reduce, second_gather, bias_e, bias_r, part
    )
    d_combined, grad_one, result_one, result_two, grad_output, small = turn(
        devices, out_one, d_second, mixed, input_two, upstream_one, combined, live, gain_m, full_output, grad_bias_reduce, grad_bias_expand
    )
    d_shared, d_values = attend_back(
        info, shared, values, code, spread, combined_window, d_combined, lse, lone
    )
    grad_two, grad_shared, grad_value, grad_output, grad_reduce, thin, long = tail(
        devices, grad_reduce, grad_output, d_shared, d_values, normed,
        two_head, input_two, two_tail, upstream_two, live, gain_a, full_shared, full_value, small,
    )
    return (
        result_one,
        result_two,
        grad_one,
        grad_two,
        grad_shared,
        grad_value,
        grad_output,
        jnp.concatenate([grad_expand[k * part : (k + 1) * part] for k in range(sides)], axis=1),
        grad_reduce,
        thin[0, :part],
        thin[1, :part],
        thin[2, :part],
        thin[3, :part],
        thin[4, :part],
        long.reshape(-1),
        thin[5, :part],
    )


def solution(mesh):
    rows, flat, whole = P("fsdp", None), P("fsdp"), P()
    return jax.shard_map(
        body,
        mesh=mesh,
        in_specs=(rows,) * 4 + (whole, whole, P("fsdp", None, None)) + (rows,) * 5 + (flat,) * 7,
        out_specs=(rows,) * 9 + (flat,) * 7,
        check_vma=False,
    )
```

```python
import functools
import math

import jax
import jax.numpy as jnp
from jax import lax
from jax.experimental import pallas as pl
from jax.experimental.pallas import tpu as pltpu
from jax.sharding import PartitionSpec as P

HEADS = 8
DH = 128
GROUP = 64
ROUNDS = 4
BUCKETS = 32
EPS_NORM = 1e-05
EPS_UNIT = 1e-06
LOG2E = math.log2(math.e)
SELF2 = -100000.0 * LOG2E
NEG = -1e30
SCALE = 1.0 / math.sqrt(DH)
TILE = 512
HALF = TILE // 2
KEYS = 256
MANY = TILE // KEYS
STEP = 128.0
SHIFT = 1.5 * 2.0**30
TAME = 3000.0
PAIR = 4
FREE = 99.0
STRIP = 512
AFTER = (2, 4, 6, 8)
CURVE = math.sqrt(2.0 / math.pi)
MESH = pl.DeviceIdType.MESH

NT = (((1,), (1,)), ((), ()))
NN = (((1,), (0,)), ((), ()))
TN = (((0,), (0,)), ((), ()))
F32 = jnp.float32
BF16 = jnp.bfloat16


def dot(a, b, dims=NN):
    return lax.dot_general(a, b, dims, preferred_element_type=F32)


def layer_norm(values, gain, shift):
    center = values - jnp.mean(values, axis=-1, keepdims=True)
    spread = jnp.mean(center * center, axis=-1, keepdims=True)
    return center * lax.rsqrt(spread + EPS_NORM) * gain + shift


def prepare(q, code_ref, spread, ask_s, key_s, h, at):
    lane = lax.broadcasted_iota(jnp.int32, (TILE, DH), 1)
    target = ((lane // 64) * 32 + lane % 16).astype(F32)
    wide = q.astype(F32)
    square = jnp.sum(wide * wide, axis=1, keepdims=True)
    code = dot(code_ref[:, at], spread, TN)
    here = code == target
    ask_s[h, at, :DH] = q
    ask_s[h, at, DH:] = jnp.where(here, STEP, 0.0).astype(BF16)
    key_s[h, at, :DH] = (wide * (lax.rsqrt(square + EPS_UNIT) * (SCALE * LOG2E))).astype(BF16)
    key_s[h, at, DH:] = jnp.where(here | (code + 1.0 == target), 1.0, 0.0).astype(BF16)
    return jnp.max(square)


def lowest(info_ref, i):
    start, stop = i * TILE, (i + 1) * TILE
    one = (info_ref[0] < stop) & (info_ref[1] > start)
    two = (info_ref[2] < stop) & (info_ref[3] > start)
    begin = jnp.where(one, info_ref[0], jnp.where(two, info_ref[2], stop))
    return lax.div(begin, KEYS)


def tile_rows(i):
    return pl.ds(pl.multiple_of(i * TILE, TILE), TILE)


def halves(i):
    start = i * TILE
    return [((0, pl.multiple_of(start, HALF), pl.multiple_of(start, HALF)), HALF),
            ((HALF, pl.multiple_of(start + HALF, HALF), pl.multiple_of(start, HALF)), TILE)]


def part_of(both):
    count = (both + SHIFT) - SHIFT
    return count, both - count


def apart(left, right):
    return dot(left[:, DH:], right[:, DH:], NT), dot(left[:, :DH], right[:, :DH], NT)


def attend_kernel(low_ref, q_ref, v_ref, code_ref, spread_ref, comb_ref, lse_ref, lone_ref, ask_s, key_s, more_s, acc_s, top_s):
    rows = q_ref.shape[0]
    tiles = rows // TILE
    heads = [slice(h * DH, (h + 1) * DH) for h in range(PAIR)]

    def ready(i, largest):
        def fill():
            most = jnp.float32(0.0)
            at = tile_rows(i)
            for h, cols in enumerate(heads):
                most = jnp.maximum(most, prepare(q_ref[at, cols], code_ref, spread_ref[:, cols], ask_s, key_s, h, at))
                more_s[h, at, :DH] = v_ref[at, cols]
                more_s[h, at, DH:] = jnp.ones((TILE, DH), BF16)
            return most

        return jnp.maximum(largest, lax.cond(lowest(low_ref, i) <= (i + 1) * MANY - 1, fill, lambda: jnp.float32(0.0)))

    largest = lax.fori_loop(0, tiles, ready, jnp.float32(0.0))
    tame = largest * (SCALE * LOG2E) ** 2 < TAME
    ask_at = lax.broadcasted_iota(jnp.int32, (TILE, TILE), 0)
    key_at = lax.broadcasted_iota(jnp.int32, (TILE, TILE), 1)

    def finish(h, cols, at, top):
        total = acc_s[h, :, DH:]
        some = total > 0.0
        safe = jnp.where(some, total, 1.0)
        inverse = jnp.where(some, 1.0 / safe, 0.0)
        comb_ref[at, cols] = (acc_s[h, :, :DH] * inverse).astype(BF16)
        lse_ref[h, :, at] = (jnp.log2(safe) + top).T[:1]

    def rows_of(i, carry):
        at = tile_rows(i)
        low = lowest(low_ref, i)

        @pl.when((low < (i + 1) * MANY) & tame)
        def _():
            for h in range(PAIR):
                acc_s[h] = jnp.zeros((TILE, 2 * DH), F32)

            def step(j, carry):
                keys = pl.ds(pl.multiple_of(j * KEYS, KEYS), KEYS)
                for h in range(PAIR):
                    count, score = part_of(dot(ask_s[h, at, :], key_s[h, keys, :], NT))
                    acc_s[h] += dot((count * jnp.exp2(score)).astype(BF16), more_s[h, keys, :])
                return carry

            lax.fori_loop(low, i * MANY, step, 0)
            for h, cols in enumerate(heads):
                for asks, span in halves(i):
                    here = pl.ds(asks[0], HALF)
                    there = pl.ds(asks[1], HALF)
                    keys = pl.ds(asks[2], span)
                    key_at = lax.broadcasted_iota(jnp.int32, (HALF, span), 1)
                    ask_at = lax.broadcasted_iota(jnp.int32, (HALF, span), 0) + (span - HALF)
                    count, score = part_of(dot(ask_s[h, there, :], key_s[h, keys, :], NT))
                    prob = jnp.where(key_at < ask_at, count * jnp.exp2(score), 0.0).astype(BF16)
                    acc_s[h, here, :] += dot(prob, more_s[h, keys, :])
                    active = jnp.max(jnp.where(key_at == ask_at, count, 0.0), axis=1, keepdims=True) > 0.0
                    lone = jnp.where(active & (acc_s[h, here, DH:] == 0.0), 1.0, 0.0)
                    acc_s[h, here, :DH] += lone * v_ref[there, cols].astype(F32)
                    acc_s[h, here, DH:] += lone
                    lone_ref[h, :, there] = lone.T[:1]
                finish(h, cols, at, 0.0)

        @pl.when((low < (i + 1) * MANY) & jnp.logical_not(tame))
        def _():
            for h, cols in enumerate(heads):
                count, score = apart(ask_s[h, at, :], key_s[h, at, :])
                score = jnp.where(key_at == ask_at, SELF2, score)
                score = jnp.where((key_at <= ask_at) & (count > 0.5), score, NEG)
                top = jnp.max(score, axis=1, keepdims=True)
                prob = count * jnp.exp2(score - top)
                acc_s[h] = dot(prob.astype(BF16), more_s[h, at, :])
                top_s[h] = jnp.broadcast_to(top, (TILE, DH))

                def step(j, carry):
                    keys = pl.ds(pl.multiple_of(j * KEYS, KEYS), KEYS)
                    count, score = apart(ask_s[h, at, :], key_s[h, keys, :])
                    score = jnp.where(count > 0.5, score, NEG)
                    top = top_s[h]
                    newer = jnp.maximum(top, jnp.max(score, axis=1, keepdims=True))
                    fade = jnp.exp2(top - newer)
                    prob = count * jnp.exp2(score - newer[:, :1])
                    acc_s[h] = acc_s[h] * jnp.concatenate([fade, fade], axis=1) + dot(prob.astype(BF16), more_s[h, keys, :])
                    top_s[h] = newer
                    return carry

                lax.fori_loop(low, i * MANY, step, 0)
                total = acc_s[h, :, DH:]
                own = STEP * ROUNDS * jnp.exp2(SELF2 - jnp.maximum(top_s[h], SELF2))
                lone_ref[h, :, at] = jnp.where(total > 0.0, own / jnp.where(total > 0.0, total, 1.0), 0.0).T[:1]
                finish(h, cols, at, top_s[h])

        @pl.when(low >= (i + 1) * MANY)
        def _():
            comb_ref[at, :] = jnp.zeros((TILE, PAIR * DH), BF16)
            for h in range(PAIR):
                lse_ref[h, :, at] = jnp.zeros((1, TILE), F32)
                lone_ref[h, :, at] = jnp.zeros((1, TILE), F32)

        return carry

    lax.fori_loop(0, tiles, rows_of, 0)


def back_kernel(
    low_ref, q_ref, v_ref, code_ref, spread_ref, comb_ref, above_ref, lse_ref, lone_ref,
    dq_ref, dv_ref, ask_s, key_s, dunit_s, dvalue_s, dask_s,
):
    rows = q_ref.shape[0]
    tiles = rows // TILE
    heads = [slice(h * DH, (h + 1) * DH) for h in range(PAIR)]

    def ready(i, largest):
        def fill():
            most = jnp.float32(0.0)
            at = tile_rows(i)
            for h, cols in enumerate(heads):
                most = jnp.maximum(most, prepare(q_ref[at, cols], code_ref, spread_ref[:, cols], ask_s, key_s, h, at))
                for total in (dunit_s, dvalue_s, dask_s):
                    total[h, at, :] = jnp.zeros((TILE, DH), F32)
            return most

        return jnp.maximum(largest, lax.cond(lowest(low_ref, i) <= (i + 1) * MANY - 1, fill, lambda: jnp.float32(0.0)))

    largest = lax.fori_loop(0, tiles, ready, jnp.float32(0.0))
    tame = largest * (SCALE * LOG2E) ** 2 < TAME

    def pass_over(i, low, split):
        at = tile_rows(i)
        deltas = []
        for h, cols in enumerate(heads):
            mixed = above_ref[at, cols].astype(F32) * comb_ref[at, cols].astype(F32)
            deltas.append(jnp.sum(mixed.T, axis=0, keepdims=True))

        def step(j, carry):
            keys = pl.ds(pl.multiple_of(j * KEYS, KEYS), KEYS)
            for h, cols in enumerate(heads):
                q, above, unit = q_ref[at, cols], above_ref[at, cols], key_s[h, keys, :DH]
                count, score = split(key_s[h, keys, :], ask_s[h, at, :])
                d_prob = dot(v_ref[keys, cols], above, NT)
                prob = count * jnp.exp2(score - lse_ref[h, :, at])
                d_score = (prob * (d_prob - carry[h])).astype(BF16)
                dvalue_s[h, keys, :] += dot(prob.astype(BF16), above)
                dunit_s[h, keys, :] += dot(d_score, q)
                dask_s[h, at, :] += dot(d_score, unit, TN)
            return carry

        deltas = lax.fori_loop(low, i * MANY, step, tuple(deltas))
        for h, cols in enumerate(heads):
            for asks, span in halves(i):
                there = pl.ds(asks[1], HALF)
                keys = pl.ds(asks[2], span)
                key_at = lax.broadcasted_iota(jnp.int32, (span, HALF), 0)
                ask_at = lax.broadcasted_iota(jnp.int32, (span, HALF), 1) + (span - HALF)
                q, above, unit = q_ref[there, cols], above_ref[there, cols], key_s[h, keys, :DH]
                count, score = split(key_s[h, keys, :], ask_s[h, there, :])
                d_prob = dot(v_ref[keys, cols], above, NT)
                prob = count * jnp.exp2(score - lse_ref[h, :, there])
                prob = jnp.where(key_at < ask_at, prob, 0.0)
                d_score = (prob * (d_prob - deltas[h][:, asks[0] : asks[0] + HALF])).astype(BF16)
                prob = jnp.where(key_at == ask_at, lone_ref[h, :, there], prob).astype(BF16)
                dvalue_s[h, keys, :] += dot(prob, above)
                dunit_s[h, keys, :] += dot(d_score, q)
                dask_s[h, there, :] += dot(d_score, unit, TN)

    def together(left, right):
        return part_of(dot(left, right, NT))

    def guarded(left, right):
        count, score = apart(left, right)
        return count, jnp.where(count > 0.5, score, NEG)

    def rows_of(i, carry):
        low = lowest(low_ref, i)

        @pl.when((low < (i + 1) * MANY) & tame)
        def _():
            pass_over(i, low, together)

        @pl.when((low < (i + 1) * MANY) & jnp.logical_not(tame))
        def _():
            pass_over(i, low, guarded)

        return carry

    lax.fori_loop(0, tiles, rows_of, 0)

    def close(i, carry):
        at = tile_rows(i)

        @pl.when(lowest(low_ref, i) <= (i + 1) * MANY - 1)
        def _():
            for h, cols in enumerate(heads):
                q = q_ref[at, cols].astype(F32)
                norm = lax.rsqrt(jnp.sum(q * q, axis=1, keepdims=True) + EPS_UNIT)
                d_unit = dunit_s[h, at, :] * SCALE
                along = jnp.sum(q * d_unit, axis=1, keepdims=True)
                d_q = dask_s[h, at, :] * (1.0 / LOG2E) + d_unit * norm - q * (norm * norm * norm * along)
                dq_ref[at, cols] = d_q.astype(BF16)
                dv_ref[at, cols] = dvalue_s[h, at, :].astype(BF16)

        @pl.when(lowest(low_ref, i) > (i + 1) * MANY - 1)
        def _():
            dq_ref[at, :] = jnp.zeros((TILE, PAIR * DH), BF16)
            dv_ref[at, :] = jnp.zeros((TILE, PAIR * DH), BF16)

        return carry

    lax.fori_loop(0, tiles, close, 0)


def head_specs(rows):
    by_head = pl.BlockSpec((rows, PAIR * DH), lambda h, low: (0, h))
    code = pl.BlockSpec((ROUNDS * HEADS, rows), lambda h, low: (0, 0))
    spread = pl.BlockSpec((ROUNDS * HEADS, PAIR * DH), lambda h, low: (0, h))
    stat = pl.BlockSpec((PAIR, 1, rows), lambda h, low: (h, 0, 0))
    return by_head, code, spread, stat


def attend(low, shared, values, code, spread):
    rows = shared.shape[0]
    by_head, code_spec, spread_spec, stat = head_specs(rows)
    wide = jax.ShapeDtypeStruct((rows, HEADS * DH), BF16)
    thin = jax.ShapeDtypeStruct((HEADS, 1, rows), F32)
    return pl.pallas_call(
        attend_kernel,
        grid_spec=pltpu.PrefetchScalarGridSpec(
            num_scalar_prefetch=1,
            grid=(HEADS // PAIR,),
            in_specs=[by_head, by_head, code_spec, spread_spec],
            out_specs=[by_head, stat, stat],
            scratch_shapes=[pltpu.VMEM((PAIR, rows, 2 * DH), BF16)] * 3
            + [pltpu.VMEM((PAIR, TILE, 2 * DH), F32), pltpu.VMEM((PAIR, TILE, DH), F32)],
        ),
        out_shape=(wide, thin, thin),
        compiler_params=pltpu.CompilerParams(vmem_limit_bytes=57 << 20),
        name="attend",
        cost_estimate=pl.CostEstimate(
            flops=HEADS * 20 * 3 * 2 * TILE * TILE * DH, bytes_accessed=rows * HEADS * DH * 6, transcendentals=HEADS * 20 * TILE * TILE
        ),
    )(low, shared, values, code, spread)


def attend_back(low, shared, values, code, spread, combined, above, lse, lone):
    rows = shared.shape[0]
    by_head, code_spec, spread_spec, stat = head_specs(rows)
    wide = jax.ShapeDtypeStruct((rows, HEADS * DH), BF16)
    return pl.pallas_call(
        back_kernel,
        grid_spec=pltpu.PrefetchScalarGridSpec(
            num_scalar_prefetch=1,
            grid=(HEADS // PAIR,),
            in_specs=[by_head, by_head, code_spec, spread_spec, by_head, by_head, stat, stat],
            out_specs=[by_head, by_head],
            scratch_shapes=[pltpu.VMEM((PAIR, rows, 2 * DH), BF16)] * 2 + [pltpu.VMEM((PAIR, rows, DH), F32)] * 3,
        ),
        out_shape=(wide, wide),
        compiler_params=pltpu.CompilerParams(vmem_limit_bytes=57 << 20),
        name="attend_back",
        cost_estimate=pl.CostEstimate(
            flops=HEADS * 20 * 6 * 2 * TILE * TILE * DH, bytes_accessed=rows * HEADS * DH * 12, transcendentals=HEADS * 20 * TILE * TILE
        ),
    )(low, shared, values, code, spread, combined, above, lse, lone)


def digits(devices):
    side = 2
    while 8 * side * side < devices:
        side += 1
    assert 8 * side * side == devices, devices
    return 4, side, 2


def neighbours(devices):
    outer, side, core = digits(devices)
    me = lax.axis_index("fsdp")
    c = lax.rem(me, core)
    q = lax.rem(lax.div(me, core), side)
    p = lax.rem(lax.div(me, core * side), side)
    o = lax.div(me, core * side * side)

    def at(o_, p_, q_, c_):
        return ((o_ * side + p_) * side + q_) * core + c_

    core_peer = at(o, p, q, 1 - c)
    q_peers = [(k, at(o, p, k, c)) for k in (lax.rem(q + d, side) for d in range(1, side))]
    p_peers = [(k, at(o, k, q, c)) for k in (lax.rem(p + d, side) for d in range(1, side))]
    o_peers = [(k, at(k, p, q, c)) for k in (lax.rem(o + d, outer) for d in range(1, outer))]
    return (o, p, q, c), core_peer, q_peers, p_peers, o_peers


def peers_of(where):
    return [where[1]] + [device for group in where[2:] for _, device in group]


def greet(peers):
    barrier = pltpu.get_barrier_semaphore()
    for peer in peers:
        pl.semaphore_signal(barrier, inc=1, device_id=(peer,), device_id_type=MESH)
    pl.semaphore_wait(barrier, len(peers))


def remote(src, dst, sems, slot, device):
    return pltpu.make_async_remote_copy(
        src_ref=src, dst_ref=dst, send_sem=sems.at[(0,) + slot], recv_sem=sems.at[(1,) + slot],
        device_id=(device,), device_id_type=MESH,
    )


class Scatter:
    def __init__(self, devices, where, slot, boxes, sems, other, mine, load=None):
        self.outer, self.side, _ = digits(devices)
        (self.o, self.p, self.q, self.c), self.core_peer, self.q_peers, self.p_peers, self.o_peers = where
        self.slot = slot
        self.box_c, box_a0, box_a1, self.box_b, self.box_o = boxes
        self.box_a = (box_a0, box_a1)
        self.sem_c, self.sem_a, self.sem_b, self.sem_o = sems
        self.other, self.mine, self.load = other, mine, load
        half = self.box_o.shape[-1] // 2
        self.columns = (pl.ds(0, half), pl.ds(half, half))

    def core(self):
        return remote(self.other(), self.box_c, self.sem_c, (self.slot,), self.core_peer)

    def first(self, h, d):
        k, device = (self.q_peers, self.p_peers)[h][d]
        spot = (slice(None), slice(None), k) if h == 0 else (slice(None), k, slice(None))
        return remote(self.mine(spot, self.columns[h]), self.box_a[h].at[d], self.sem_a, (self.slot, h, d), device)

    def second(self, h, d):
        k, device = (self.p_peers, self.q_peers)[h][d]
        return remote(
            self.box_a[h].at[0, :, k], self.box_b.at[d, :, :, self.columns[h]], self.sem_b, (self.slot, h, d), device
        )

    def third(self, d):
        k, device = self.o_peers[d]
        return remote(self.box_b.at[0, k], self.box_o.at[d], self.sem_o, (self.slot, d), device)

    def begin(self):
        self.core().start()
        if self.load is not None:
            self.load().start()

    def stage_core(self):
        if self.load is not None:
            self.load().wait()
        self.core().wait_recv()
        side = self.side

        def add(i, carry):
            spot = (lax.div(i, side * side), lax.rem(lax.div(i, side), side), lax.rem(i, side))
            ref = self.mine(spot, slice(None))
            ref[...] = ref[...] + self.box_c[spot]
            return carry

        lax.fori_loop(0, self.outer * side * side, add, 0)
        for h in range(2):
            for d in range(side - 1):
                self.first(h, d).start()

    def stage_first(self):
        side = self.side
        for h in range(2):
            box = self.box_a[h]
            for d in range(side - 1):
                self.first(h, d).wait_recv()

            def add(i, carry):
                a, b = lax.div(i, side), lax.rem(i, side)
                total = self.mine((a, b, self.q) if h == 0 else (a, self.p, b), self.columns[h])[...]
                for d in range(side - 1):
                    total = total + box[d, a, b]
                box[0, a, b] = total
                return carry

            lax.fori_loop(0, self.outer * side, add, 0)
            for d in range(side - 1):
                self.second(h, d).start()

    def stage_second(self):
        box = self.box_b
        for h in range(2):
            k = self.p if h == 0 else self.q
            for d in range(self.side - 1):
                self.second(h, d).wait_recv()

            def add(a, carry):
                total = self.box_a[h][0, a, k]
                for d in range(self.side - 1):
                    total = total + box[d, a, :, self.columns[h]]
                box[0, a, :, self.columns[h]] = total
                return carry

            lax.fori_loop(0, self.outer, add, 0)
        for d in range(self.outer - 1):
            self.third(d).start()

    def stage_third(self):
        total = self.box_b[0, self.o].astype(F32)
        for d in range(self.outer - 1):
            self.third(d).wait_recv()
            total = total + self.box_o[d].astype(F32)
        return total

    def sent_first(self):
        self.core().wait_send()
        for h in range(2):
            for d in range(self.side - 1):
                self.first(h, d).wait_send()

    def sent_last(self):
        for h in range(2):
            for d in range(self.side - 1):
                self.second(h, d).wait_send()
        for d in range(self.outer - 1):
            self.third(d).wait_send()


def boxes_for(devices, rows, width):
    outer, side, _ = digits(devices)
    half = width // 2
    return [
        pltpu.VMEM((outer, side, side, rows, width), BF16),
        pltpu.VMEM((side - 1, outer, side, rows, half), BF16),
        pltpu.VMEM((side - 1, outer, side, rows, half), BF16),
        pltpu.VMEM((side - 1, outer, rows, width), BF16),
        pltpu.VMEM((outer - 1, rows, width), BF16),
    ]


def sems_for(devices, count):
    outer, side, _ = digits(devices)
    dma = pltpu.SemaphoreType.DMA
    return [dma((2, count)), dma((2, count, 2, side - 1)), dma((2, count, 2, side - 1)), dma((2, count, outer - 1))]


def mixing_kernel(
    devices, second_ref, above_ref, expand_ref, reduce_ref, bias_e_ref, bias_r_ref,
    out_ref, back_ref, grad_r_ref, grad_b_ref, grad_e_ref, above_b_ref, act_s, pre_s, grad_s, *rest,
):
    step = pl.program_id(0)
    rows, width = second_ref.shape
    strip = act_s.shape[1]
    per = width // strip
    slices = (len(rest) - 4) // 5
    sems = rest[5 * slices :]
    where = neighbours(devices)
    (o, p, q, c), core_peer, q_peers, p_peers, o_peers = where
    part = grad_s.shape[-2]

    def mover(k):
        def other():
            return grad_s.at[k % 2, :, :, :, 1 - c]

        def mine(spot, cols):
            return grad_s.at[(k % 2,) + tuple(spot) + (c, slice(None), cols)]

        return Scatter(devices, where, k, rest[5 * k : 5 * k + 5], sems, other, mine)

    movers = [mover(k) for k in range(slices)]
    w_e = expand_ref[...].reshape(width, strip)
    w_r = reduce_ref[...].reshape(strip, width)

    @pl.when(step == 0)
    def _():
        greet(peers_of(where))
        out_ref[...] = jnp.broadcast_to(bias_r_ref[...], out_ref.shape)
        back_ref[...] = jnp.zeros(back_ref.shape, F32)
        above_b_ref[...] = jnp.sum(above_ref[...].astype(F32), axis=0, keepdims=True)

    def close(k):
        grad_e_ref[k * part : (k + 1) * part, :] = movers[k].stage_third()

    final = slices * per - 1
    timed, late = [], []
    for k in range(slices):
        begun = 2 * ((k + 1) * per - 1) + 1
        for after, action in zip(
            AFTER, (movers[k].stage_core, movers[k].stage_first, movers[k].stage_second, functools.partial(close, k))
        ):
            if begun + after > 2 * final + 1:
                late.append((begun + after, -k, action))
            else:
                timed.append((begun + after, action))

    def stages(point):
        for when, action in timed:
            if when % 2 == point:
                pl.when(step == when // 2)(action)

    pre = dot(second_ref[...], w_e) + bias_e_ref[...]
    square = pre * pre
    curve = jnp.tanh(CURVE * pre * (1.0 + 0.044715 * square))
    hinge = 0.5 * (1.0 + curve)
    act_s[...] = (pre * hinge).astype(BF16)
    slope = hinge + 0.5 * pre * (1.0 - curve * curve) * (CURVE * (1.0 + 3 * 0.044715 * square))
    d_pre = (dot(above_ref[...], w_r, NT) * slope).astype(BF16)
    pre_s[...] = d_pre
    grad_b_ref[...] = jnp.sum(d_pre.astype(F32), axis=0, keepdims=True)
    stages(0)
    out_ref[...] += dot(act_s[...], w_r)
    back_ref[...] += dot(d_pre, w_e, NT)
    grad_r_ref[...] = dot(act_s[...], above_ref[...], TN).astype(BF16).reshape(grad_r_ref.shape)
    grad_e = dot(second_ref[...], pre_s[...], TN).astype(BF16)
    for k in range(slices):
        for j in range(per):
            @pl.when(step == k * per + j)
            def _():
                if j == 0 and k >= 2:
                    movers[k - 2].sent_first()
                grad_s[k % 2, :, :, :, :, :, j * strip : (j + 1) * strip] = grad_e.reshape(grad_s.shape[1:-1] + (strip,))
                if j == per - 1:
                    movers[k].begin()

    stages(1)

    @pl.when(step == final)
    def _():
        for *_, action in sorted(late, key=lambda entry: entry[:2]):
            action()
        for k in range(max(0, slices - 2), slices):
            movers[k].sent_first()
        for k in range(slices):
            movers[k].sent_last()


def mixing(devices, second, above, gathered, bias_e, bias_r, part):
    rows, width = second.shape
    hidden = bias_e.shape[1]
    many = hidden // devices
    sides = hidden // width
    strip = STRIP
    per = width // strip
    outer, side, core = digits(devices)
    fixed = pl.BlockSpec((rows, width), lambda i: (0, 0), pipeline_mode=pl.Buffered(1))
    whole = pl.BlockSpec(memory_space=pltpu.VMEM)
    scratch = [pltpu.VMEM((rows, strip), BF16)] * 2 + [pltpu.VMEM((2, outer, side, side, core, part, width), BF16)]
    for k in range(sides):
        scratch += boxes_for(devices, part, width)
    return pl.pallas_call(
        functools.partial(mixing_kernel, devices),
        grid=(hidden // strip,),
        in_specs=[
            fixed, fixed,
            pl.BlockSpec((devices, part, strip), lambda i: (0, many // part + 1 + i // per, i % per)),
            pl.BlockSpec((strip // many, many, width), lambda i: (i, 0, 0)),
            pl.BlockSpec((1, strip), lambda i: (0, i)),
            pl.BlockSpec((1, width), lambda i: (0, 0)),
        ],
        out_specs=[
            fixed,
            fixed,
            pl.BlockSpec((strip // many, many, width), lambda i: (i, 0, 0)),
            pl.BlockSpec((1, strip), lambda i: (0, i)),
            pl.BlockSpec((sides * part, width), lambda i: (0, 0)),
            pl.BlockSpec((1, width), lambda i: (0, 0)),
        ],
        out_shape=[
            jax.ShapeDtypeStruct((rows, width), F32),
            jax.ShapeDtypeStruct((rows, width), F32),
            jax.ShapeDtypeStruct((devices, many, width), BF16),
            jax.ShapeDtypeStruct((1, hidden), F32),
            jax.ShapeDtypeStruct((sides * part, width), F32),
            jax.ShapeDtypeStruct((1, width), F32),
        ],
        scratch_shapes=scratch + sems_for(devices, sides),
        compiler_params=pltpu.CompilerParams(collective_id=3, has_side_effects=True, vmem_limit_bytes=57 << 20),
        name="mixing",
    )(second, above, gathered, gathered, bias_e, bias_r)


def join_kernel(
    devices, window_ref, first_ref, final_ref, one_ref, above_ref, live_ref, w_ref, bias_ref, gain_ref, shift_ref,
    combined_ref, out_ref, second_ref, reduce_ref, side_in, part_s, halo_sem,
):
    slots, width = one_ref.shape
    half = slots // 2
    tile = 256
    me = lax.axis_index("fsdp")
    last = devices - 1
    left, right = lax.rem(me + last, devices), lax.rem(me + 1, devices)
    greet([left, right])

    def to_left():
        return remote(window_ref.at[:half], side_in.at[1], halo_sem, (0,), left)

    def to_right():
        return remote(window_ref.at[half + slots :], side_in.at[0], halo_sem, (1,), right)

    @pl.when(me > 0)
    def _():
        to_left().start()

    @pl.when(me < last)
    def _():
        to_right().start()

    @pl.when(me == 0)
    def _():
        side_in[0] = jnp.zeros((half, width), BF16)

    @pl.when(me == last)
    def _():
        side_in[1] = jnp.zeros((half, width), BF16)

    w_o = w_ref[...].reshape(width, width)

    owns = (first_ref, final_ref)

    def before(side, i, carry):
        here = pl.ds(pl.multiple_of(i * tile, tile), tile)
        at = pl.ds(pl.multiple_of(side * half + i * tile, tile), tile)
        part_s[at, :] = dot(owns[side][here, :], w_o)
        reduce_ref[at, :] = (live_ref[at, :] * above_ref[at, :].astype(F32)).astype(BF16)
        return carry

    for side in range(2):
        lax.fori_loop(0, half // tile, functools.partial(before, side), 0)

    def after(side, i, carry):
        here = pl.ds(pl.multiple_of(i * tile, tile), tile)
        at = pl.ds(pl.multiple_of(side * half + i * tile, tile), tile)
        other = side_in[side, here, :]
        combined_ref[at, :] = owns[side][here, :] + other
        attended = part_s[at, :] + dot(other, w_o) + bias_ref[...]
        out = one_ref[at, :].astype(F32) + live_ref[at, :] * attended
        out_ref[at, :] = out
        second_ref[at, :] = layer_norm(out, gain_ref[...], shift_ref[...]).astype(BF16)
        return carry

    @pl.when(me > 0)
    def _():
        to_right().wait_recv()

    lax.fori_loop(0, half // tile, functools.partial(after, 0), 0)

    @pl.when(me < last)
    def _():
        to_left().wait_recv()

    lax.fori_loop(0, half // tile, functools.partial(after, 1), 0)

    @pl.when(me > 0)
    def _():
        to_left().wait_send()

    @pl.when(me < last)
    def _():
        to_right().wait_send()


def join(devices, window, one, above, live, gathered, bias, gain, shift, part, sides):
    slots, width = one.shape
    dma = pltpu.SemaphoreType.DMA
    rows = pl.BlockSpec((slots, width), lambda i: (0, 0))
    thin = pl.BlockSpec((1, width), lambda i: (0, 0))
    low = jax.ShapeDtypeStruct((slots, width), BF16)
    return pl.pallas_call(
        functools.partial(join_kernel, devices),
        grid=(1,),
        in_specs=[
            pl.BlockSpec(memory_space=pl.ANY),
            pl.BlockSpec((slots // 2, width), lambda i: (1, 0)), pl.BlockSpec((slots // 2, width), lambda i: (2, 0)), rows, rows, pl.BlockSpec((slots, 1), lambda i: (0, 0)),
            pl.BlockSpec((devices, part, width), lambda i: (0, sides, 0)), thin, thin, thin,
        ],
        out_specs=[rows] * 4,
        out_shape=[low, jax.ShapeDtypeStruct((slots, width), F32), low, low],
        scratch_shapes=[pltpu.VMEM((2, slots // 2, width), BF16), pltpu.VMEM((slots, width), F32), dma((2, 2))],
        compiler_params=pltpu.CompilerParams(collective_id=6, has_side_effects=True, vmem_limit_bytes=57 << 20),
        name="join",
    )(window, window, window, one, above, live, gathered, bias, gain, shift)


def turn_kernel(
    devices, out_one_ref, d_second_ref, mixed_ref, two_ref, above_ref, combined_ref, live_ref, gain_ref, w_o_ref,
    bias_r_ref, bias_e_ref,
    wide_ref, grad_one_out, one_out, res_two_out, grad_o_out, small_ref,
    mixed_s, two_s, combined_s, one_s, res_two_s, grad_o_s, attend_s, halo_sem, load_sem, store_sem,
):
    slots, width = two_ref.shape
    half = slots // 2
    tile = 256
    part = grad_o_out.shape[1]
    w_o = w_o_ref[...].reshape(width, width)
    me = lax.axis_index("fsdp")
    last = devices - 1
    left, right = lax.rem(me + last, devices), lax.rem(me + 1, devices)
    loads = [
        pltpu.make_async_copy(source, target, load_sem.at[k])
        for k, (source, target) in enumerate(((mixed_ref, mixed_s), (two_ref, two_s), (combined_ref, combined_s)))
    ]
    stores = [
        pltpu.make_async_copy(source, target, store_sem.at[k])
        for k, (source, target) in enumerate(
            ((attend_s, grad_one_out), (one_s, one_out), (res_two_s, res_two_out), (grad_o_s, grad_o_out))
        )
    ]
    for load in loads:
        load.start()
    greet([left, right])

    def to_left():
        return remote(wide_ref.at[half : 2 * half], wide_ref.at[half + slots :], halo_sem, (0,), left)

    def to_right():
        return remote(wide_ref.at[2 * half : 3 * half], wide_ref.at[:half], halo_sem, (1,), right)

    small_ref[...] = jnp.zeros(small_ref.shape, F32)
    gain = gain_ref[...]

    def norm_tile(i, carry):
        at = pl.ds(pl.multiple_of(i * tile, tile), tile)
        live = live_ref[at, :]
        values = out_one_ref[at, :]
        above = d_second_ref[at, :]
        center = values - jnp.mean(values, axis=1, keepdims=True)
        scale = lax.rsqrt(jnp.mean(center * center, axis=1, keepdims=True) + EPS_NORM)
        center = center * scale
        small_ref[2:3, :] += jnp.sum(above * center, axis=0, keepdims=True)
        small_ref[3:4, :] += jnp.sum(above, axis=0, keepdims=True)
        above = above * gain
        mean = jnp.mean(above, axis=1, keepdims=True)
        along = jnp.mean(above * center, axis=1, keepdims=True)
        total = live * (above_ref[at, :].astype(F32) + scale * (above - mean - center * along))
        low = total.astype(BF16)
        attend_s[at, :] = low
        small_ref[4:5, :] += jnp.sum(low.astype(F32), axis=0, keepdims=True)
        wide_ref[pl.ds(pl.multiple_of(half + i * tile, tile), tile), :] = dot(low, w_o, NT).astype(BF16)
        return carry

    lax.fori_loop(0, half // tile, norm_tile, 0)

    @pl.when(me > 0)
    def _():
        to_left().start()

    lax.fori_loop(half // tile, slots // tile, norm_tile, 0)

    @pl.when(me < last)
    def _():
        to_right().start()

    stores[0].start()
    for load in loads:
        load.wait()

    def finish_tile(i, carry):
        at = pl.ds(pl.multiple_of(i * tile, tile), tile)
        live = live_ref[at, :]
        one_s[at, :] = (live * out_one_ref[at, :]).astype(BF16)
        res_two_s[at, :] = (live * (two_s[at, :].astype(F32) + mixed_s[at, :])).astype(BF16)
        return carry

    lax.fori_loop(0, slots // tile, finish_tile, 0)
    stores[1].start()
    stores[2].start()

    def weights(i, carry):
        cols = pl.ds(pl.multiple_of(i * tile, tile), tile)
        many = tile // part
        grad_o_s[pl.ds(pl.multiple_of(i * many, many), many)] = (
            dot(combined_s[:, cols], attend_s[...], TN).astype(BF16).reshape(many, part, width)
        )
        return carry

    lax.fori_loop(0, width // tile, weights, 0)
    stores[3].start()
    small_ref[5:6, :] = bias_r_ref[...]
    for k in range(bias_e_ref.shape[1] // width):
        small_ref[6 + k : 7 + k, :] = bias_e_ref[:, k * width : (k + 1) * width]

    @pl.when(me > 0)
    def _():
        to_right().wait_recv()
        to_left().wait_send()

    @pl.when(me == 0)
    def _():
        wide_ref[:half] = jnp.zeros((half, width), BF16)

    @pl.when(me < last)
    def _():
        to_left().wait_recv()
        to_right().wait_send()

    @pl.when(me == last)
    def _():
        wide_ref[half + slots :] = jnp.zeros((half, width), BF16)

    for store in stores:
        store.wait()


def turn(devices, out_one, d_second, mixed, two, above, combined, live, gain, gathered, bias_r, bias_e, sides):
    slots, width = two.shape
    part = width // devices
    vmem = pl.BlockSpec(memory_space=pltpu.VMEM)
    anywhere = pl.BlockSpec(memory_space=pl.ANY)
    dma = pltpu.SemaphoreType.DMA
    low = pltpu.VMEM((slots, width), BF16)
    rows_low = jax.ShapeDtypeStruct((slots, width), BF16)
    return pl.pallas_call(
        functools.partial(turn_kernel, devices),
        grid=(1,),
        in_specs=[vmem, vmem, anywhere, anywhere, vmem, anywhere, vmem, vmem]
        + [pl.BlockSpec((devices, part, width), lambda i: (0, sides, 0)), vmem, vmem],
        out_specs=(vmem,) + (anywhere,) * 4 + (vmem,),
        out_shape=(
            jax.ShapeDtypeStruct((2 * slots, width), BF16), rows_low, rows_low, rows_low,
            jax.ShapeDtypeStruct((devices, part, width), BF16),
            jax.ShapeDtypeStruct((16, width), F32),
        ),
        scratch_shapes=[
            pltpu.VMEM((slots, width), F32), low, low, low, low, pltpu.VMEM((devices, part, width), BF16), low,
            dma((2, 2)), dma((3,)), dma((4,)),
        ],
        compiler_params=pltpu.CompilerParams(collective_id=5, has_side_effects=True, vmem_limit_bytes=57 << 20),
        name="turn",
    )(out_one, d_second, mixed, two, above, combined, live, gain, gathered, bias_r, bias_e)


def tail_kernel(
    devices, grad_r_ref, grad_o_ref, d_shared_ref, d_value_ref, normed_in, head_ref, own_in, end_ref, above_in, live_ref,
    gain_ref, w_s_ref, w_v_ref, small_ref,
    back_ref, out_s_ref, out_v_ref, out_o_ref, out_r_ref, thin_ref, long_ref,
    normed_ref, own_ref, above_ref, late_sem, side_s, side_in, vector_s, vector_in, grad_s, load_sem, halo_sem, vector_sem, *rest,
):
    window, width = normed_ref.shape
    slots = own_ref.shape[0]
    half = slots // 2
    part = out_s_ref.shape[0]
    many = out_r_ref.shape[0]
    tile = 256
    where = neighbours(devices)
    (o, p, q, c), core_peer, q_peers, p_peers, o_peers = where
    me = lax.axis_index("fsdp")
    outer, side, core = digits(devices)
    owns, rest = rest[:3], rest[3:]
    sems = rest[-4:]

    def distant(source, row, rows, k):
        at = pl.ds(row, rows)

        def other():
            return source.at[:, :, :, 1 - c, at, :]

        def mine(spot, cols):
            return owns[k].at[tuple(spot) + (slice(None), cols)]

        def load():
            return pltpu.make_async_copy(source.at[:, :, :, c, at, :], owns[k], load_sem.at[k])

        return Scatter(devices, where, k, rest[5 * k : 5 * k + 5], sems, other, mine, load)

    def near(j, k):
        def other():
            return grad_s.at[j, :, :, :, 1 - c]

        def mine(spot, cols):
            return grad_s.at[(j,) + tuple(spot) + (c, slice(None), cols)]

        return Scatter(devices, where, k, rest[5 * k : 5 * k + 5], sems, other, mine)

    movers = [
        distant(grad_r_ref, 0, many // 2, 0), distant(grad_r_ref, many // 2, many // 2, 1), distant(grad_o_ref, 0, part, 2),
        near(0, 3), near(1, 4),
    ]
    last = devices - 1
    left, right = lax.rem(me + last, devices), lax.rem(me + 1, devices)
    late = [
        pltpu.make_async_copy(source, target, late_sem.at[k])
        for k, (source, target) in enumerate(((normed_in, normed_ref), (own_in, own_ref), (above_in, above_ref)))
    ]
    for load in late:
        load.start()
    greet(peers_of(where) + [left, right])
    for k in range(3):
        movers[k].begin()

    def to_left():
        return remote(side_s.at[0], side_in.at[1], halo_sem, (0,), left)

    def to_right():
        return remote(side_s.at[1], side_in.at[0], halo_sem, (1,), right)

    vector_s[...] = small_ref[...]
    gain = gain_ref[...]

    def norm_tile(ref, row, at):
        values = ref[pl.ds(row, tile), :].astype(F32)
        above = dot(d_shared_ref[at, :], w_s_ref[...], NT) + dot(d_value_ref[at, :], w_v_ref[...], NT)
        center = values - jnp.mean(values, axis=1, keepdims=True)
        scale = lax.rsqrt(jnp.mean(center * center, axis=1, keepdims=True) + EPS_NORM)
        center = center * scale
        vector_s[0:1, :] += jnp.sum(above * center, axis=0, keepdims=True)
        vector_s[1:2, :] += jnp.sum(above, axis=0, keepdims=True)
        above = above * gain
        mean = jnp.mean(above, axis=1, keepdims=True)
        along = jnp.mean(above * center, axis=1, keepdims=True)
        return scale * (above - mean - center * along)

    def side_tiles(i, carry):
        row = pl.multiple_of(i * tile, tile)
        side_s[0, pl.ds(row, tile), :] = norm_tile(head_ref, row, pl.ds(row, tile)).astype(BF16)
        at = pl.ds(pl.multiple_of(half + slots + i * tile, tile), tile)
        side_s[1, pl.ds(row, tile), :] = norm_tile(end_ref, row, at).astype(BF16)
        return carry

    lax.fori_loop(0, half // tile, side_tiles, 0)

    @pl.when(me > 0)
    def _():
        to_left().start()

    @pl.when(me < last)
    def _():
        to_right().start()

    movers[0].stage_core()

    def weights(j, ref):
        wide = tile // part

        def strip(i, carry):
            cols = pl.ds(pl.multiple_of(i * tile, tile), tile)
            block = dot(normed_ref[:, cols], ref[...], TN).astype(BF16).reshape(wide // core, core, part, width)
            for k in range(wide // core):
                index = i * (wide // core) + k
                spot = (lax.div(index, side * side), lax.rem(lax.div(index, side), side), lax.rem(index, side))
                grad_s[(j,) + spot] = block[k]
            return carry

        lax.fori_loop(0, width // tile, strip, 0)

    for load in late:
        load.wait()
    weights(0, d_shared_ref)
    movers[3].begin()
    movers[1].stage_core()
    movers[0].stage_first()
    weights(1, d_value_ref)
    movers[4].begin()
    movers[2].stage_core()
    movers[1].stage_first()
    movers[0].stage_second()

    def own_tiles(i, carry):
        row = pl.multiple_of(i * tile, tile)
        at = pl.ds(pl.multiple_of(half + i * tile, tile), tile)
        here = pl.ds(row, tile)
        total = above_ref[here, :].astype(F32) + norm_tile(own_ref, row, at)
        back_ref[here, :] = (live_ref[here, :] * total).astype(BF16)
        return carry

    lax.fori_loop(0, slots // tile, own_tiles, 0)

    def vector_copies(stage):
        group = ([(0, core_peer)], q_peers, p_peers, o_peers)[stage]
        base = (0, 1, side, 2 * side - 1)[stage]
        return [
            remote(vector_s if stage == 0 else vector_in.at[base - 1], vector_in.at[base + d], vector_sem, (base + d,), device)
            for d, (_, device) in enumerate(group)
        ]

    def vector_stage(stage):
        base = (0, 1, side, 2 * side - 1)[stage]
        copies = vector_copies(stage)
        total = vector_s[...] if stage == 0 else vector_in[base - 1]
        for d, copy in enumerate(copies):
            copy.wait_recv()
            total = total + vector_in[base + d]
        vector_in[base + len(copies) - 1] = total

    for copy in vector_copies(0):
        copy.start()
    movers[3].stage_core()
    movers[2].stage_first()
    movers[1].stage_second()
    out_r_ref[: many // 2, :] = movers[0].stage_third()
    vector_stage(0)
    for copy in vector_copies(1):
        copy.start()
    movers[4].stage_core()
    movers[3].stage_first()
    movers[2].stage_second()
    out_r_ref[many // 2 :, :] = movers[1].stage_third()
    vector_stage(1)
    for copy in vector_copies(2):
        copy.start()
    movers[4].stage_first()
    movers[3].stage_second()
    out_o_ref[...] = movers[2].stage_third()
    vector_stage(2)
    for copy in vector_copies(3):
        copy.start()

    @pl.when(me > 0)
    def _():
        to_right().wait_recv()

    @pl.when(me == 0)
    def _():
        side_in[0] = jnp.zeros((half, width), BF16)

    @pl.when(me < last)
    def _():
        to_left().wait_recv()

    @pl.when(me == last)
    def _():
        side_in[1] = jnp.zeros((half, width), BF16)

    for k in range(2):
        at = slice(k * half, (k + 1) * half)
        back_ref[at, :] = (back_ref[at, :].astype(F32) + side_in[k].astype(F32)).astype(BF16)
    movers[4].stage_second()
    out_s_ref[...] = movers[3].stage_third()
    vector_stage(3)
    out_v_ref[...] = movers[4].stage_third()
    vectors = 2 * side + outer - 3
    total = vector_in[vectors]
    thin_ref[...] = pltpu.roll(total, lax.rem(width - me * part, width), 1)[:, :DH]
    each = long_ref.shape[1]
    long_rows = [total[6 + k : 7 + k, :] for k in range(devices * each // width)]
    mine = lax.div(me * each, width)
    chosen = long_rows[0]
    for k in range(1, len(long_rows)):
        chosen = jnp.where(mine == k, long_rows[k], chosen)
    long_ref[...] = pltpu.roll(chosen, lax.rem(width - lax.rem(me * each, width), width), 1)[:, :each]
    for stage in range(4):
        for copy in vector_copies(stage):
            copy.wait_send()

    @pl.when(me > 0)
    def _():
        to_left().wait_send()

    @pl.when(me < last)
    def _():
        to_right().wait_send()

    for mover in movers:
        mover.sent_first()
        mover.sent_last()


def tail(devices, grad_r, grad_o, d_shared, d_values, normed, head, own, end, above, live, gain, w_s, w_v, small):
    window, width = normed.shape
    slots = own.shape[0]
    outer, side, core = digits(devices)
    part, many = grad_o.shape[1], grad_r.shape[1]
    each = many
    vmem = pl.BlockSpec(memory_space=pltpu.VMEM)
    anywhere = pl.BlockSpec(memory_space=pl.ANY)
    dma = pltpu.SemaphoreType.DMA
    sizes = [many // 2, many // 2, part, part, part]
    scratch = [
        pltpu.VMEM((window, width), BF16), pltpu.VMEM((slots, width), BF16), pltpu.VMEM((slots, width), BF16), dma((3,)),
        pltpu.VMEM((2, slots // 2, width), BF16), pltpu.VMEM((2, slots // 2, width), BF16),
        pltpu.VMEM((16, width), F32), pltpu.VMEM((2 * side + outer - 2, 16, width), F32),
        pltpu.VMEM((2, outer, side, side, core, part, width), BF16),
        dma((3,)), dma((2, 2)), dma((2, 2 * side + outer - 2)),
    ]
    scratch += [pltpu.VMEM((outer, side, side, rows, width), BF16) for rows in sizes[:3]]
    for rows in sizes:
        scratch += boxes_for(devices, rows, width)
    shape = (outer, side, side, core)
    return pl.pallas_call(
        functools.partial(tail_kernel, devices),
        in_specs=[anywhere, anywhere, vmem, vmem, anywhere, vmem, anywhere, vmem, anywhere] + [vmem] * 5,
        out_specs=(vmem,) * 7,
        out_shape=(
            jax.ShapeDtypeStruct((slots, width), BF16),
            jax.ShapeDtypeStruct((part, width), F32),
            jax.ShapeDtypeStruct((part, width), F32),
            jax.ShapeDtypeStruct((part, width), F32),
            jax.ShapeDtypeStruct((many, width), F32),
            jax.ShapeDtypeStruct((16, DH), F32),
            jax.ShapeDtypeStruct((1, each), F32),
        ),
        scratch_shapes=scratch + sems_for(devices, len(sizes)),
        compiler_params=pltpu.CompilerParams(collective_id=4, has_side_effects=True, vmem_limit_bytes=57 << 20),
        name="tail",
    )(
        grad_r.reshape(shape + grad_r.shape[1:]), grad_o.reshape(shape + grad_o.shape[1:]),
        d_shared, d_values, normed, head, own, end, above, live, gain, w_s, w_v, small,
    )


def find_ranks(length_ref, target_ref, bucket_ref, packed_ref, info_ref, before_s):
    devices = length_ref.shape[0]
    lists, slots = bucket_ref.shape
    me = lax.axis_index("fsdp")
    base = me * slots
    window = 2 * slots

    def look(s, carry):
        start, mine, found, one, two = carry
        size = length_ref[s]
        target = target_ref[s]
        middle = start + lax.shift_right_logical(size, 1)
        inside = (middle >= base) & (middle < base + slots)
        offset = start - base + slots // 2
        entry = (offset, offset + size, target)
        first, second = inside & (found == 0), inside & (found == 1)
        one = tuple(jnp.where(first, new, old) for new, old in zip(entry, one))
        two = tuple(jnp.where(second, new, old) for new, old in zip(entry, two))
        return start + size, jnp.where(target == me, size, mine), found + inside.astype(jnp.int32), one, two

    zero = jnp.int32(0)
    nothing = (jnp.int32(window), jnp.int32(window), zero)
    total, mine, found, one, two = lax.fori_loop(0, devices, look, (zero, zero, zero, nothing, nothing))
    for k, value in enumerate((one[0], one[1], two[0], two[1], one[2], two[2], total, found)):
        info_ref[k] = value

    def fill(i, carry):
        at = pl.ds(pl.multiple_of(i * DH, DH), DH)
        first = lax.broadcasted_iota(jnp.int32, (DH, slots), 0) + i * DH
        second = lax.broadcasted_iota(jnp.int32, (DH, slots), 1)
        before_s[at, :] = jnp.where(first < second, 1.0, 0.0).astype(BF16)
        return carry

    lax.fori_loop(0, slots // DH, fill, 0)
    left = lax.broadcasted_iota(jnp.int32, (DH, DH), 0)
    right = lax.broadcasted_iota(jnp.int32, (DH, DH), 1)
    smaller = jnp.where((left // BUCKETS == right // BUCKETS) & (right < left), 1.0, 0.0).astype(BF16)
    many = DH // BUCKETS
    bucket = lax.broadcasted_iota(jnp.int32, (many, BUCKETS, slots), 1)
    live = lax.broadcasted_iota(jnp.int32, (many, BUCKETS, slots), 2) < mine
    ranks = []
    for g in range(lists // many):
        here = (jnp.broadcast_to(bucket_ref[g * many : (g + 1) * many, :][:, None, :], bucket.shape) == bucket) & live
        one_hot = jnp.where(here, 1.0, 0.0)
        flat = one_hot.reshape(DH, slots).astype(BF16)
        offset = jnp.sum(dot(smaller, flat), axis=1, keepdims=True)
        place = (dot(flat, before_s[...]) + offset).reshape(many, BUCKETS, slots)
        ranks.append(jnp.sum(one_hot * place, axis=1))
    rank = jnp.concatenate(ranks, axis=0)
    live = lax.broadcasted_iota(jnp.int32, (lists, slots), 1) < mine
    packed_ref[:lists, :] = jnp.where(live, jnp.floor(rank * (1.0 / GROUP)), FREE).astype(BF16)


def project_kernel(
    info_ref, head_ref, own_ref, tail_ref, gain_ref, shift_ref, w_s_ref, w_v_ref, one_ref, two_ref,
    normed_ref, shared_ref, value_ref, code_ref,
):
    i = pl.program_id(0)
    tile = own_ref.shape[0]
    steps = pl.num_programs(0)

    def go(ref):
        normed = layer_norm(ref[...].astype(F32), gain_ref[...], shift_ref[...]).astype(BF16)
        normed_ref[...] = normed
        shared_ref[...] = dot(normed, w_s_ref[...]).astype(BF16)
        value_ref[...] = dot(normed, w_v_ref[...]).astype(BF16)

    @pl.when(i < steps // 4)
    def _():
        go(head_ref)

    @pl.when((i >= steps // 4) & (i < steps - steps // 4))
    def _():
        go(own_ref)

    @pl.when(i >= steps - steps // 4)
    def _():
        go(tail_ref)

    @pl.when(i == 0)
    def _():
        lists, window = code_ref.shape
        lane = lax.broadcasted_iota(jnp.int32, (lists, window), 1)
        code = jnp.full((lists, window), FREE, F32)
        for k, ref in enumerate((one_ref, two_ref)):
            begin, end = info_ref[2 * k], info_ref[2 * k + 1]
            rows = ref[0].astype(F32)
            moved = pltpu.roll(jnp.concatenate([rows, rows], axis=1), lax.rem(begin, window), 1)
            code = jnp.where((lane >= begin) & (lane < end), moved + 32.0 * k, code)
        code_ref[...] = code.astype(BF16)


def project(info, head, own, tail, gain, shift, w_s, w_v, blocks):
    slots, width = own.shape
    window = 2 * slots
    lists = ROUNDS * HEADS
    tile = 256
    steps = window // tile
    quarter = steps // 4
    rows = pl.BlockSpec((tile, width), lambda i, info: (i, 0))
    vector = pl.BlockSpec((1, width), lambda i, info: (0, 0))
    matrix = pl.BlockSpec((width, width), lambda i, info: (0, 0), pipeline_mode=pl.Buffered(1))
    wide = jax.ShapeDtypeStruct((window, width), BF16)
    return pl.pallas_call(
        project_kernel,
        grid_spec=pltpu.PrefetchScalarGridSpec(
            num_scalar_prefetch=1,
            grid=(steps,),
            in_specs=[
                pl.BlockSpec((tile, width), lambda i, info: (jnp.minimum(i, quarter - 1), 0)),
                pl.BlockSpec((tile, width), lambda i, info: (jnp.clip(i - quarter, 0, 2 * quarter - 1), 0)),
                pl.BlockSpec((tile, width), lambda i, info: (jnp.clip(i - 3 * quarter, 0, quarter - 1), 0)),
                vector, vector, matrix, matrix,
                pl.BlockSpec((1, lists, slots), lambda i, info: (info[4], 0, 0)),
                pl.BlockSpec((1, lists, slots), lambda i, info: (info[5], 0, 0)),
            ],
            out_specs=[rows, rows, rows, pl.BlockSpec((lists, window), lambda i, info: (0, 0))],
        ),
        out_shape=[wide, wide, wide, jax.ShapeDtypeStruct((lists, window), BF16)],
        compiler_params=pltpu.CompilerParams(vmem_limit_bytes=57 << 20),
        name="project",
    )(info, head, own, tail, gain, shift, w_s, w_v, blocks, blocks)


def gather_kernel(devices, arrays, length_ref, target_ref, bucket_ref, vector_ref, rows_ref, *refs):
    sources, outs, (info_ref, head_ref, end_ref) = refs[: arrays - 1], refs[arrays - 1 : 2 * arrays - 1], refs[2 * arrays - 1 : 2 * arrays + 2]
    packed_s, before_s, own_sem, sem_o, sem_a, sem_b, sem_c, halo_sem, edge_sem = refs[2 * arrays + 2 :]
    sources = sources + (packed_s,)
    outer, side, core = digits(devices)
    (o, p, q, c), core_peer, q_peers, p_peers, o_peers = neighbours(devices)
    me = lax.axis_index("fsdp")
    last_device = devices - 1
    left, right = lax.rem(me + last_device, devices), lax.rem(me + 1, devices)
    greet([core_peer] + [d for _, d in q_peers] + [d for _, d in p_peers] + [d for _, d in o_peers] + [left, right])
    half = sources[0].shape[-1] // 2
    border = head_ref.shape[0]

    def to_left():
        return remote(rows_ref.at[:border], end_ref, halo_sem, (0,), left)

    def to_right():
        return remote(rows_ref.at[border:], head_ref, halo_sem, (1,), right)

    def blank(ref):
        return pltpu.make_async_copy(before_s.at[:border], ref, edge_sem.at[0])

    columns = (pl.ds(0, half), pl.ds(half, half))

    locals_, begun, first, second, last = [], {}, {}, {}, {}
    for s in range(arrays):
        if s == arrays - 1:
            find_ranks(length_ref, target_ref, bucket_ref, packed_s, info_ref, before_s)
            packed_s[bucket_ref.shape[0] :, :] = vector_ref[...]
        locals_.append(pltpu.make_async_copy(sources[s], outs[s].at[o, p, q, c], own_sem.at[s]))
        locals_[s].start()
        for d, (k, device) in enumerate(o_peers):
            begun[s, d] = remote(sources[s], outs[s].at[o, p, q, c], sem_o, (s, d), device)
            begun[s, d].start()

    @pl.when(me > 0)
    def _():
        to_left().start()

    @pl.when(me < last_device)
    def _():
        to_right().start()

    before_s[:border, :] = jnp.zeros((border, before_s.shape[1]), BF16)

    @pl.when(me == 0)
    def _():
        blank(head_ref).start()

    @pl.when(me == last_device)
    def _():
        blank(end_ref).start()

    def stage_a(s):
        locals_[s].wait()
        for d in range(outer - 1):
            begun[s, d].wait_recv()
        for h, peers in enumerate((q_peers, p_peers)):
            piece = outs[s].at[:, p, q, c, :, columns[h]]
            for d, (k, device) in enumerate(peers):
                first[s, h, d] = remote(piece, piece, sem_a, (s, h, d), device)
                first[s, h, d].start()

    def stage_b(s):
        for h, peers in enumerate((p_peers, q_peers)):
            for d in range(side - 1):
                first[s, h, d].wait_recv()
            piece = outs[s].at[:, p, :, c, :, columns[h]] if h == 0 else outs[s].at[:, :, q, c, :, columns[h]]
            for d, (k, device) in enumerate(peers):
                second[s, h, d] = remote(piece, piece, sem_b, (s, h, d), device)
                second[s, h, d].start()

    def stage_c(s):
        for h in range(2):
            for d in range(side - 1):
                second[s, h, d].wait_recv()
        piece = outs[s].at[:, :, :, c]
        last[s] = remote(piece, piece, sem_c, (s,), core_peer)
        last[s].start()

    for t in range(arrays + 2):
        if t < arrays:
            stage_a(t)
        if 0 <= t - 1 < arrays:
            stage_b(t - 1)
        if 0 <= t - 2 < arrays:
            stage_c(t - 2)
    for s in range(arrays):
        last[s].wait_recv()

    @pl.when(me > 0)
    def _():
        to_right().wait_recv()
        to_left().wait_send()

    @pl.when(me == 0)
    def _():
        blank(head_ref).wait()

    @pl.when(me < last_device)
    def _():
        to_left().wait_recv()
        to_right().wait_send()

    @pl.when(me == last_device)
    def _():
        blank(end_ref).wait()

    for group in (begun, first, second, last):
        for copy in group.values():
            copy.wait_send()


def gather(devices, lengths, destination, buckets, vectors, rows, arrays):
    outer, side, core = digits(devices)
    lists, slots = buckets.shape
    packed = jax.ShapeDtypeStruct((lists + vectors.shape[0], slots), BF16)
    shapes = [jax.ShapeDtypeStruct(array.shape, array.dtype) for array in arrays] + [packed]
    count = len(shapes)
    dma = pltpu.SemaphoreType.DMA
    anywhere = pl.BlockSpec(memory_space=pl.ANY)
    hbm = pl.BlockSpec(memory_space=pltpu.HBM)
    smem = pl.BlockSpec(memory_space=pltpu.SMEM)
    vmem = pl.BlockSpec(memory_space=pltpu.VMEM)
    outs = pl.pallas_call(
        functools.partial(gather_kernel, devices, count),
        out_shape=tuple(jax.ShapeDtypeStruct((outer, side, side, core) + shape.shape, shape.dtype) for shape in shapes)
        + (jax.ShapeDtypeStruct((8,), jnp.int32),)
        + (jax.ShapeDtypeStruct((slots // 2, rows.shape[1]), BF16),) * 2,
        in_specs=[smem, smem, vmem, vmem] + [anywhere] * count,
        out_specs=(hbm,) * count + (smem, hbm, hbm),
        scratch_shapes=[
            pltpu.VMEM(packed.shape, BF16), pltpu.VMEM((slots, slots), BF16),
            dma((count,)), dma((2, count, outer - 1)), dma((2, count, 2, side - 1)), dma((2, count, 2, side - 1)), dma((2, count)),
            dma((2, 2)), dma((1,)),
        ],
        compiler_params=pltpu.CompilerParams(collective_id=2, has_side_effects=True, vmem_limit_bytes=57 << 20),
        name="gather",
    )(lengths, destination, buckets, vectors, rows, *arrays)
    return [out.reshape((devices,) + shape.shape) for out, shape in zip(outs, shapes)] + list(outs[count:])


def body(
    input_one, input_two, upstream_one, upstream_two, lengths, destination, buckets,
    w_shared, w_value, w_output, w_expand, w_reduce,
    gain_attend, shift_attend, gain_mixing, shift_mixing, bias_output, bias_expand, bias_reduce,
):
    devices = lax.axis_size("fsdp")
    me = lax.axis_index("fsdp")
    slots, width = input_one.shape
    half = slots // 2
    window = 2 * slots
    part = w_shared.shape[0]
    hidden = w_expand.shape[1]
    sides = hidden // width
    base = me * slots
    lists = ROUNDS * HEADS
    spot = jnp.arange(width, dtype=jnp.int32)
    short = jnp.stack([gain_attend, shift_attend, gain_mixing, shift_mixing, bias_output, bias_reduce])
    short = jnp.where(spot // part == me, jnp.tile(short, (1, devices)), 0.0)
    many = hidden // devices
    long = jnp.tile(bias_expand, width // many)[None]
    long = jnp.where(spot[None] // many + (width // many) * jnp.arange(sides, dtype=jnp.int32)[:, None] == me, long, 0.0)
    vectors = jnp.concatenate([short, long], axis=0)
    high = lax.reduce_precision(vectors, 8, 7)
    count = vectors.shape[0]
    packed = jnp.concatenate(
        [high.astype(BF16), (vectors - high).astype(BF16), jnp.zeros((24 - 2 * count, width), BF16)], axis=0
    )
    second_gather = lax.all_gather(
        jnp.concatenate(
            [w_reduce, w_output] + [w_expand[:, k * width : (k + 1) * width] for k in range(sides)], axis=0
        ),
        "fsdp", axis=0, tiled=False,
    )
    full_shared, full_value, packed, info, two_head, two_tail = gather(
        devices, lengths, destination, buckets[0], packed, input_two, [w_shared, w_value]
    )
    full_shared, full_value = full_shared.reshape(width, width), full_value.reshape(width, width)
    vectors = jnp.sum(packed[:, lists : lists + 2 * count].astype(F32), axis=0)
    vectors = vectors[:count] + vectors[count:]
    gain_a, shift_a, gain_m, shift_m, bias_o, bias_r = (vectors[k : k + 1] for k in range(6))
    bias_e = vectors[6:].reshape(1, hidden)
    lane = jnp.arange(HEADS * DH, dtype=jnp.int32)
    row = jnp.arange(lists, dtype=jnp.int32)[:, None]
    spread = (row == ((lane % 64) // 16) * HEADS + lane // DH).astype(BF16)

    live = ((base + jnp.arange(slots, dtype=jnp.int32)) < info[6]).astype(F32)[:, None]
    normed, shared, values, code = project(
        info, two_head, input_two, two_tail, gain_a, shift_a, full_shared, full_value, packed
    )
    combined_window, lse, lone = attend(info, shared, values, code, spread)
    combined, out_one, second, d_reduce = join(
        devices, combined_window, input_one, upstream_two, live, second_gather, bias_o, gain_m, shift_m, part, sides
    )
    mixed, d_second, grad_reduce, grad_bias_expand, grad_expand, grad_bias_reduce = mixing(
        devices, second, d_reduce, second_gather, bias_e, bias_r, part
    )
    d_combined, grad_one, result_one, result_two, grad_output, small = turn(
        devices, out_one, d_second, mixed, input_two, upstream_one, combined, live, gain_m, second_gather, grad_bias_reduce, grad_bias_expand,
        sides,
    )
    d_shared, d_values = attend_back(
        info, shared, values, code, spread, combined_window, d_combined, lse, lone
    )
    grad_two, grad_shared, grad_value, grad_output, grad_reduce, thin, long = tail(
        devices, grad_reduce, grad_output, d_shared, d_values, normed,
        two_head, input_two, two_tail, upstream_two, live, gain_a, full_shared, full_value, small,
    )
    return (
        result_one,
        result_two,
        grad_one,
        grad_two,
        grad_shared,
        grad_value,
        grad_output,
        jnp.concatenate([grad_expand[k * part : (k + 1) * part] for k in range(sides)], axis=1),
        grad_reduce,
        thin[0, :part],
        thin[1, :part],
        thin[2, :part],
        thin[3, :part],
        thin[4, :part],
        long.reshape(-1),
        thin[5, :part],
    )


def solution(mesh):
    rows, flat, whole = P("fsdp", None), P("fsdp"), P()
    return jax.shard_map(
        body,
        mesh=mesh,
        in_specs=(rows,) * 4 + (whole, whole, P("fsdp", None, None)) + (rows,) * 5 + (flat,) * 7,
        out_specs=(rows,) * 9 + (flat,) * 7,
        check_vma=False,
    )
```

```python
import functools
import math

import jax
import jax.numpy as jnp
from jax import lax
from jax.experimental import pallas as pl
from jax.experimental.pallas import tpu as pltpu
from jax.sharding import PartitionSpec as P

HEADS = 8
DH = 128
GROUP = 64
ROUNDS = 4
BUCKETS = 32
EPS_NORM = 1e-05
EPS_UNIT = 1e-06
LOG2E = math.log2(math.e)
SELF2 = -100000.0 * LOG2E
NEG = -1e30
SCALE = 1.0 / math.sqrt(DH)
TILE = 512
HALF = TILE // 2
KEYS = 256
MANY = TILE // KEYS
STEP = 128.0
SHIFT = 1.5 * 2.0**30
TAME = 3000.0
PAIR = 4
FREE = 99.0
STRIP = 512
AFTER = (2, 4, 6, 8)
CURVE = math.sqrt(2.0 / math.pi)
MESH = pl.DeviceIdType.MESH

NT = (((1,), (1,)), ((), ()))
NN = (((1,), (0,)), ((), ()))
TN = (((0,), (0,)), ((), ()))
F32 = jnp.float32
BF16 = jnp.bfloat16


def dot(a, b, dims=NN):
    return lax.dot_general(a, b, dims, preferred_element_type=F32)


def layer_norm(values, gain, shift):
    center = values - jnp.mean(values, axis=-1, keepdims=True)
    spread = jnp.mean(center * center, axis=-1, keepdims=True)
    return center * lax.rsqrt(spread + EPS_NORM) * gain + shift


def prepare(q, code_ref, spread, ask_s, key_s, h, at):
    lane = lax.broadcasted_iota(jnp.int32, (TILE, DH), 1)
    target = ((lane // 64) * 32 + lane % 16).astype(F32)
    wide = q.astype(F32)
    square = jnp.sum(wide * wide, axis=1, keepdims=True)
    code = dot(code_ref[:, at], spread, TN)
    here = code == target
    ask_s[h, at, :DH] = q
    ask_s[h, at, DH:] = jnp.where(here, STEP, 0.0).astype(BF16)
    key_s[h, at, :DH] = (wide * (lax.rsqrt(square + EPS_UNIT) * (SCALE * LOG2E))).astype(BF16)
    key_s[h, at, DH:] = jnp.where(here | (code + 1.0 == target), 1.0, 0.0).astype(BF16)
    return jnp.max(square)


def lowest(info_ref, i):
    start, stop = i * TILE, (i + 1) * TILE
    one = (info_ref[0] < stop) & (info_ref[1] > start)
    two = (info_ref[2] < stop) & (info_ref[3] > start)
    begin = jnp.where(one, info_ref[0], jnp.where(two, info_ref[2], stop))
    return lax.div(begin, KEYS)


def tile_rows(i):
    return pl.ds(pl.multiple_of(i * TILE, TILE), TILE)


def halves(i):
    start = i * TILE
    return [((0, pl.multiple_of(start, HALF), pl.multiple_of(start, HALF)), HALF),
            ((HALF, pl.multiple_of(start + HALF, HALF), pl.multiple_of(start, HALF)), TILE)]


def part_of(both):
    count = (both + SHIFT) - SHIFT
    return count, both - count


def apart(left, right):
    return dot(left[:, DH:], right[:, DH:], NT), dot(left[:, :DH], right[:, :DH], NT)


def attend_kernel(low_ref, q_ref, v_ref, code_ref, spread_ref, comb_ref, lse_ref, lone_ref, ask_s, key_s, more_s, acc_s, top_s):
    rows = q_ref.shape[0]
    tiles = rows // TILE
    heads = [slice(h * DH, (h + 1) * DH) for h in range(PAIR)]

    def ready(i, largest):
        def fill():
            most = jnp.float32(0.0)
            at = tile_rows(i)
            for h, cols in enumerate(heads):
                most = jnp.maximum(most, prepare(q_ref[at, cols], code_ref, spread_ref[:, cols], ask_s, key_s, h, at))
                more_s[h, at, :DH] = v_ref[at, cols]
                more_s[h, at, DH:] = jnp.ones((TILE, DH), BF16)
            return most

        return jnp.maximum(largest, lax.cond(lowest(low_ref, i) <= (i + 1) * MANY - 1, fill, lambda: jnp.float32(0.0)))

    largest = lax.fori_loop(0, tiles, ready, jnp.float32(0.0))
    tame = largest * (SCALE * LOG2E) ** 2 < TAME
    ask_at = lax.broadcasted_iota(jnp.int32, (TILE, TILE), 0)
    key_at = lax.broadcasted_iota(jnp.int32, (TILE, TILE), 1)

    def finish(h, cols, at, top):
        total = acc_s[h, :, DH:]
        some = total > 0.0
        safe = jnp.where(some, total, 1.0)
        inverse = jnp.where(some, 1.0 / safe, 0.0)
        comb_ref[at, cols] = (acc_s[h, :, :DH] * inverse).astype(BF16)
        lse_ref[h, :, at] = (jnp.log2(safe) + top).T[:1]

    def rows_of(i, carry):
        at = tile_rows(i)
        low = lowest(low_ref, i)

        @pl.when((low < (i + 1) * MANY) & tame)
        def _():
            for h in range(PAIR):
                acc_s[h] = jnp.zeros((TILE, 2 * DH), F32)

            def step(j, carry):
                keys = pl.ds(pl.multiple_of(j * KEYS, KEYS), KEYS)
                for h in range(PAIR):
                    count, score = part_of(dot(ask_s[h, at, :], key_s[h, keys, :], NT))
                    acc_s[h] += dot((count * jnp.exp2(score)).astype(BF16), more_s[h, keys, :])
                return carry

            lax.fori_loop(low, i * MANY, step, 0)
            for h, cols in enumerate(heads):
                for asks, span in halves(i):
                    here = pl.ds(asks[0], HALF)
                    there = pl.ds(asks[1], HALF)
                    keys = pl.ds(asks[2], span)
                    key_at = lax.broadcasted_iota(jnp.int32, (HALF, span), 1)
                    ask_at = lax.broadcasted_iota(jnp.int32, (HALF, span), 0) + (span - HALF)
                    count, score = part_of(dot(ask_s[h, there, :], key_s[h, keys, :], NT))
                    prob = jnp.where(key_at < ask_at, count * jnp.exp2(score), 0.0).astype(BF16)
                    acc_s[h, here, :] += dot(prob, more_s[h, keys, :])
                    active = jnp.max(jnp.where(key_at == ask_at, count, 0.0), axis=1, keepdims=True) > 0.0
                    lone = jnp.where(active & (acc_s[h, here, DH:] == 0.0), 1.0, 0.0)
                    acc_s[h, here, :DH] += lone * v_ref[there, cols].astype(F32)
                    acc_s[h, here, DH:] += lone
                    lone_ref[h, :, there] = lone.T[:1]
                finish(h, cols, at, 0.0)

        @pl.when((low < (i + 1) * MANY) & jnp.logical_not(tame))
        def _():
            for h, cols in enumerate(heads):
                count, score = apart(ask_s[h, at, :], key_s[h, at, :])
                score = jnp.where(key_at == ask_at, SELF2, score)
                score = jnp.where((key_at <= ask_at) & (count > 0.5), score, NEG)
                top = jnp.max(score, axis=1, keepdims=True)
                prob = count * jnp.exp2(score - top)
                acc_s[h] = dot(prob.astype(BF16), more_s[h, at, :])
                top_s[h] = jnp.broadcast_to(top, (TILE, DH))

                def step(j, carry):
                    keys = pl.ds(pl.multiple_of(j * KEYS, KEYS), KEYS)
                    count, score = apart(ask_s[h, at, :], key_s[h, keys, :])
                    score = jnp.where(count > 0.5, score, NEG)
                    top = top_s[h]
                    newer = jnp.maximum(top, jnp.max(score, axis=1, keepdims=True))
                    fade = jnp.exp2(top - newer)
                    prob = count * jnp.exp2(score - newer[:, :1])
                    acc_s[h] = acc_s[h] * jnp.concatenate([fade, fade], axis=1) + dot(prob.astype(BF16), more_s[h, keys, :])
                    top_s[h] = newer
                    return carry

                lax.fori_loop(low, i * MANY, step, 0)
                total = acc_s[h, :, DH:]
                own = STEP * ROUNDS * jnp.exp2(SELF2 - jnp.maximum(top_s[h], SELF2))
                lone_ref[h, :, at] = jnp.where(total > 0.0, own / jnp.where(total > 0.0, total, 1.0), 0.0).T[:1]
                finish(h, cols, at, top_s[h])

        @pl.when(low >= (i + 1) * MANY)
        def _():
            comb_ref[at, :] = jnp.zeros((TILE, PAIR * DH), BF16)
            for h in range(PAIR):
                lse_ref[h, :, at] = jnp.zeros((1, TILE), F32)
                lone_ref[h, :, at] = jnp.zeros((1, TILE), F32)

        return carry

    lax.fori_loop(0, tiles, rows_of, 0)


def back_kernel(
    low_ref, q_ref, v_ref, code_ref, spread_ref, comb_ref, above_ref, lse_ref, lone_ref, *rest,
):
    count = (len(rest) - 9) // 2
    sources, (dq_ref, dv_ref, *targets) = rest[:count], rest[count : 2 * count + 2]
    ask_s, key_s, dunit_s, dvalue_s, dask_s, pass_s, sem = rest[2 * count + 2 :]
    rows = q_ref.shape[0]
    tail_step = pl.num_programs(0) - 1

    def copy_in(k):
        return pltpu.make_async_copy(sources[k], pass_s.at[k], sem.at[k])

    def copy_out(k):
        return pltpu.make_async_copy(pass_s.at[k], targets[k], sem.at[count + k])

    @pl.when(pl.program_id(0) == 0)
    def _():
        for k in range(count):
            copy_in(k).start()

    @pl.when(pl.program_id(0) == tail_step)
    def _():
        for k in range(count):
            copy_in(k).wait()
            copy_out(k).start()

    tiles = rows // TILE
    heads = [slice(h * DH, (h + 1) * DH) for h in range(PAIR)]

    def ready(i, largest):
        def fill():
            most = jnp.float32(0.0)
            at = tile_rows(i)
            for h, cols in enumerate(heads):
                most = jnp.maximum(most, prepare(q_ref[at, cols], code_ref, spread_ref[:, cols], ask_s, key_s, h, at))
                for total in (dunit_s, dvalue_s, dask_s):
                    total[h, at, :] = jnp.zeros((TILE, DH), F32)
            return most

        return jnp.maximum(largest, lax.cond(lowest(low_ref, i) <= (i + 1) * MANY - 1, fill, lambda: jnp.float32(0.0)))

    largest = lax.fori_loop(0, tiles, ready, jnp.float32(0.0))
    tame = largest * (SCALE * LOG2E) ** 2 < TAME

    def pass_over(i, low, split):
        at = tile_rows(i)
        deltas = []
        for h, cols in enumerate(heads):
            mixed = above_ref[at, cols].astype(F32) * comb_ref[at, cols].astype(F32)
            deltas.append(jnp.sum(mixed.T, axis=0, keepdims=True))

        def step(j, carry):
            keys = pl.ds(pl.multiple_of(j * KEYS, KEYS), KEYS)
            for h, cols in enumerate(heads):
                q, above, unit = q_ref[at, cols], above_ref[at, cols], key_s[h, keys, :DH]
                count, score = split(key_s[h, keys, :], ask_s[h, at, :])
                d_prob = dot(v_ref[keys, cols], above, NT)
                prob = count * jnp.exp2(score - lse_ref[h, :, at])
                d_score = (prob * (d_prob - carry[h])).astype(BF16)
                dvalue_s[h, keys, :] += dot(prob.astype(BF16), above)
                dunit_s[h, keys, :] += dot(d_score, q)
                dask_s[h, at, :] += dot(d_score, unit, TN)
            return carry

        deltas = lax.fori_loop(low, i * MANY, step, tuple(deltas))
        for h, cols in enumerate(heads):
            for asks, span in halves(i):
                there = pl.ds(asks[1], HALF)
                keys = pl.ds(asks[2], span)
                key_at = lax.broadcasted_iota(jnp.int32, (span, HALF), 0)
                ask_at = lax.broadcasted_iota(jnp.int32, (span, HALF), 1) + (span - HALF)
                q, above, unit = q_ref[there, cols], above_ref[there, cols], key_s[h, keys, :DH]
                count, score = split(key_s[h, keys, :], ask_s[h, there, :])
                d_prob = dot(v_ref[keys, cols], above, NT)
                prob = count * jnp.exp2(score - lse_ref[h, :, there])
                prob = jnp.where(key_at < ask_at, prob, 0.0)
                d_score = (prob * (d_prob - deltas[h][:, asks[0] : asks[0] + HALF])).astype(BF16)
                prob = jnp.where(key_at == ask_at, lone_ref[h, :, there], prob).astype(BF16)
                dvalue_s[h, keys, :] += dot(prob, above)
                dunit_s[h, keys, :] += dot(d_score, q)
                dask_s[h, there, :] += dot(d_score, unit, TN)

    def together(left, right):
        return part_of(dot(left, right, NT))

    def guarded(left, right):
        count, score = apart(left, right)
        return count, jnp.where(count > 0.5, score, NEG)

    def rows_of(i, carry):
        low = lowest(low_ref, i)

        @pl.when((low < (i + 1) * MANY) & tame)
        def _():
            pass_over(i, low, together)

        @pl.when((low < (i + 1) * MANY) & jnp.logical_not(tame))
        def _():
            pass_over(i, low, guarded)

        return carry

    lax.fori_loop(0, tiles, rows_of, 0)

    def close(i, carry):
        at = tile_rows(i)

        @pl.when(lowest(low_ref, i) <= (i + 1) * MANY - 1)
        def _():
            for h, cols in enumerate(heads):
                q = q_ref[at, cols].astype(F32)
                norm = lax.rsqrt(jnp.sum(q * q, axis=1, keepdims=True) + EPS_UNIT)
                d_unit = dunit_s[h, at, :] * SCALE
                along = jnp.sum(q * d_unit, axis=1, keepdims=True)
                d_q = dask_s[h, at, :] * (1.0 / LOG2E) + d_unit * norm - q * (norm * norm * norm * along)
                dq_ref[at, cols] = d_q.astype(BF16)
                dv_ref[at, cols] = dvalue_s[h, at, :].astype(BF16)

        @pl.when(lowest(low_ref, i) > (i + 1) * MANY - 1)
        def _():
            dq_ref[at, :] = jnp.zeros((TILE, PAIR * DH), BF16)
            dv_ref[at, :] = jnp.zeros((TILE, PAIR * DH), BF16)

        return carry

    lax.fori_loop(0, tiles, close, 0)

    @pl.when(pl.program_id(0) == tail_step)
    def _():
        for k in range(count):
            copy_out(k).wait()


def head_specs(rows):
    by_head = pl.BlockSpec((rows, PAIR * DH), lambda h, low: (0, h))
    code = pl.BlockSpec((ROUNDS * HEADS, rows), lambda h, low: (0, 0))
    spread = pl.BlockSpec((ROUNDS * HEADS, PAIR * DH), lambda h, low: (0, h))
    stat = pl.BlockSpec((PAIR, 1, rows), lambda h, low: (h, 0, 0))
    return by_head, code, spread, stat


def attend(low, shared, values, code, spread):
    rows = shared.shape[0]
    by_head, code_spec, spread_spec, stat = head_specs(rows)
    wide = jax.ShapeDtypeStruct((rows, HEADS * DH), BF16)
    thin = jax.ShapeDtypeStruct((HEADS, 1, rows), F32)
    return pl.pallas_call(
        attend_kernel,
        grid_spec=pltpu.PrefetchScalarGridSpec(
            num_scalar_prefetch=1,
            grid=(HEADS // PAIR,),
            in_specs=[by_head, by_head, code_spec, spread_spec],
            out_specs=[by_head, stat, stat],
            scratch_shapes=[pltpu.VMEM((PAIR, rows, 2 * DH), BF16)] * 3
            + [pltpu.VMEM((PAIR, TILE, 2 * DH), F32), pltpu.VMEM((PAIR, TILE, DH), F32)],
        ),
        out_shape=(wide, thin, thin),
        compiler_params=pltpu.CompilerParams(vmem_limit_bytes=57 << 20),
        name="attend",
        cost_estimate=pl.CostEstimate(
            flops=HEADS * 20 * 3 * 2 * TILE * TILE * DH, bytes_accessed=rows * HEADS * DH * 6, transcendentals=HEADS * 20 * TILE * TILE
        ),
    )(low, shared, values, code, spread)


def attend_back(low, shared, values, code, spread, combined, above, lse, lone, sources):
    rows = shared.shape[0]
    by_head, code_spec, spread_spec, stat = head_specs(rows)
    wide = jax.ShapeDtypeStruct((rows, HEADS * DH), BF16)
    return pl.pallas_call(
        back_kernel,
        grid_spec=pltpu.PrefetchScalarGridSpec(
            num_scalar_prefetch=1,
            grid=(HEADS // PAIR,),
            in_specs=[by_head, by_head, code_spec, spread_spec, by_head, by_head, stat, stat]
            + [pl.BlockSpec(memory_space=pl.ANY)] * len(sources),
            out_specs=[by_head, by_head] + [pl.BlockSpec(memory_space=pl.ANY)] * len(sources),
            scratch_shapes=[pltpu.VMEM((PAIR, rows, 2 * DH), BF16)] * 2 + [pltpu.VMEM((PAIR, rows, DH), F32)] * 3
            + [pltpu.VMEM((len(sources),) + sources[0].shape, BF16), pltpu.SemaphoreType.DMA((2 * len(sources),))],
        ),
        out_shape=(wide, wide) + tuple(jax.ShapeDtypeStruct(source.shape, BF16) for source in sources),
        compiler_params=pltpu.CompilerParams(vmem_limit_bytes=57 << 20),
        name="attend_back",
        cost_estimate=pl.CostEstimate(
            flops=HEADS * 20 * 6 * 2 * TILE * TILE * DH, bytes_accessed=rows * HEADS * DH * 12, transcendentals=HEADS * 20 * TILE * TILE
        ),
    )(low, shared, values, code, spread, combined, above, lse, lone, *sources)


def digits(devices):
    side = 2
    while 8 * side * side < devices:
        side += 1
    assert 8 * side * side == devices, devices
    return 4, side, 2


def neighbours(devices):
    outer, side, core = digits(devices)
    me = lax.axis_index("fsdp")
    c = lax.rem(me, core)
    q = lax.rem(lax.div(me, core), side)
    p = lax.rem(lax.div(me, core * side), side)
    o = lax.div(me, core * side * side)

    def at(o_, p_, q_, c_):
        return ((o_ * side + p_) * side + q_) * core + c_

    core_peer = at(o, p, q, 1 - c)
    q_peers = [(k, at(o, p, k, c)) for k in (lax.rem(q + d, side) for d in range(1, side))]
    p_peers = [(k, at(o, k, q, c)) for k in (lax.rem(p + d, side) for d in range(1, side))]
    o_peers = [(k, at(k, p, q, c)) for k in (lax.rem(o + d, outer) for d in range(1, outer))]
    return (o, p, q, c), core_peer, q_peers, p_peers, o_peers


def peers_of(where):
    return [where[1]] + [device for group in where[2:] for _, device in group]


def greet(peers):
    barrier = pltpu.get_barrier_semaphore()
    for peer in peers:
        pl.semaphore_signal(barrier, inc=1, device_id=(peer,), device_id_type=MESH)
    pl.semaphore_wait(barrier, len(peers))


def remote(src, dst, sems, slot, device):
    return pltpu.make_async_remote_copy(
        src_ref=src, dst_ref=dst, send_sem=sems.at[(0,) + slot], recv_sem=sems.at[(1,) + slot],
        device_id=(device,), device_id_type=MESH,
    )


class Scatter:
    def __init__(self, devices, where, slot, boxes, sems, other, mine, load=None):
        self.outer, self.side, _ = digits(devices)
        (self.o, self.p, self.q, self.c), self.core_peer, self.q_peers, self.p_peers, self.o_peers = where
        self.slot = slot
        self.box_c, box_a0, box_a1, self.box_b, self.box_o = boxes
        self.box_a = (box_a0, box_a1)
        self.sem_c, self.sem_a, self.sem_b, self.sem_o = sems
        self.other, self.mine, self.load = other, mine, load
        half = self.box_o.shape[-1] // 2
        self.columns = (pl.ds(0, half), pl.ds(half, half))

    def core(self):
        return remote(self.other(), self.box_c, self.sem_c, (self.slot,), self.core_peer)

    def first(self, h, d):
        k, device = (self.q_peers, self.p_peers)[h][d]
        spot = (slice(None), slice(None), k) if h == 0 else (slice(None), k, slice(None))
        return remote(self.mine(spot, self.columns[h]), self.box_a[h].at[d], self.sem_a, (self.slot, h, d), device)

    def second(self, h, d):
        k, device = (self.p_peers, self.q_peers)[h][d]
        return remote(
            self.box_a[h].at[0, :, k], self.box_b.at[d, :, :, self.columns[h]], self.sem_b, (self.slot, h, d), device
        )

    def third(self, d):
        k, device = self.o_peers[d]
        return remote(self.box_b.at[0, k], self.box_o.at[d], self.sem_o, (self.slot, d), device)

    def begin(self):
        self.core().start()
        if self.load is not None:
            self.load().start()

    def stage_core(self):
        if self.load is not None:
            self.load().wait()
        self.core().wait_recv()
        side = self.side

        def add(i, carry):
            spot = (lax.div(i, side * side), lax.rem(lax.div(i, side), side), lax.rem(i, side))
            ref = self.mine(spot, slice(None))
            ref[...] = ref[...] + self.box_c[spot]
            return carry

        lax.fori_loop(0, self.outer * side * side, add, 0)
        for h in range(2):
            for d in range(side - 1):
                self.first(h, d).start()

    def stage_first(self):
        side = self.side
        for h in range(2):
            box = self.box_a[h]
            for d in range(side - 1):
                self.first(h, d).wait_recv()

            def add(i, carry):
                a, b = lax.div(i, side), lax.rem(i, side)
                total = self.mine((a, b, self.q) if h == 0 else (a, self.p, b), self.columns[h])[...]
                for d in range(side - 1):
                    total = total + box[d, a, b]
                box[0, a, b] = total
                return carry

            lax.fori_loop(0, self.outer * side, add, 0)
            for d in range(side - 1):
                self.second(h, d).start()

    def stage_second(self):
        box = self.box_b
        for h in range(2):
            k = self.p if h == 0 else self.q
            for d in range(self.side - 1):
                self.second(h, d).wait_recv()

            def add(a, carry):
                total = self.box_a[h][0, a, k]
                for d in range(self.side - 1):
                    total = total + box[d, a, :, self.columns[h]]
                box[0, a, :, self.columns[h]] = total
                return carry

            lax.fori_loop(0, self.outer, add, 0)
        for d in range(self.outer - 1):
            self.third(d).start()

    def stage_third(self):
        total = self.box_b[0, self.o].astype(F32)
        for d in range(self.outer - 1):
            self.third(d).wait_recv()
            total = total + self.box_o[d].astype(F32)
        return total

    def sent_first(self):
        self.core().wait_send()
        for h in range(2):
            for d in range(self.side - 1):
                self.first(h, d).wait_send()

    def sent_last(self):
        for h in range(2):
            for d in range(self.side - 1):
                self.second(h, d).wait_send()
        for d in range(self.outer - 1):
            self.third(d).wait_send()


def boxes_for(devices, rows, width):
    outer, side, _ = digits(devices)
    half = width // 2
    return [
        pltpu.VMEM((outer, side, side, rows, width), BF16),
        pltpu.VMEM((side - 1, outer, side, rows, half), BF16),
        pltpu.VMEM((side - 1, outer, side, rows, half), BF16),
        pltpu.VMEM((side - 1, outer, rows, width), BF16),
        pltpu.VMEM((outer - 1, rows, width), BF16),
    ]


def sems_for(devices, count):
    outer, side, _ = digits(devices)
    dma = pltpu.SemaphoreType.DMA
    return [dma((2, count)), dma((2, count, 2, side - 1)), dma((2, count, 2, side - 1)), dma((2, count, outer - 1))]


def mixing_kernel(
    devices, second_ref, above_ref, expand_ref, reduce_ref, bias_e_ref, bias_r_ref,
    out_ref, back_ref, grad_r_ref, grad_b_ref, grad_e_ref, above_b_ref, act_s, pre_s, grad_s, *rest,
):
    step = pl.program_id(0)
    rows, width = second_ref.shape
    strip = act_s.shape[1]
    per = width // strip
    slices = (len(rest) - 4) // 5
    sems = rest[5 * slices :]
    where = neighbours(devices)
    (o, p, q, c), core_peer, q_peers, p_peers, o_peers = where
    part = grad_s.shape[-2]

    def mover(k):
        def other():
            return grad_s.at[k % 2, :, :, :, 1 - c]

        def mine(spot, cols):
            return grad_s.at[(k % 2,) + tuple(spot) + (c, slice(None), cols)]

        return Scatter(devices, where, k, rest[5 * k : 5 * k + 5], sems, other, mine)

    movers = [mover(k) for k in range(slices)]
    w_e = expand_ref[...].reshape(width, strip)
    w_r = reduce_ref[...].reshape(strip, width)

    @pl.when(step == 0)
    def _():
        greet(peers_of(where))
        out_ref[...] = jnp.broadcast_to(bias_r_ref[...], out_ref.shape)
        back_ref[...] = jnp.zeros(back_ref.shape, F32)
        above_b_ref[...] = jnp.sum(above_ref[...].astype(F32), axis=0, keepdims=True)

    def close(k):
        grad_e_ref[k * part : (k + 1) * part, :] = movers[k].stage_third()

    final = slices * per - 1
    timed, late = [], []
    for k in range(slices):
        begun = 2 * ((k + 1) * per - 1) + 1
        for after, action in zip(
            AFTER, (movers[k].stage_core, movers[k].stage_first, movers[k].stage_second, functools.partial(close, k))
        ):
            if begun + after > 2 * final + 1:
                late.append((begun + after, -k, action))
            else:
                timed.append((begun + after, action))

    def stages(point):
        for when, action in timed:
            if when % 2 == point:
                pl.when(step == when // 2)(action)

    pre = dot(second_ref[...], w_e) + bias_e_ref[...]
    square = pre * pre
    curve = jnp.tanh(CURVE * pre * (1.0 + 0.044715 * square))
    hinge = 0.5 * (1.0 + curve)
    act_s[...] = (pre * hinge).astype(BF16)
    slope = hinge + 0.5 * pre * (1.0 - curve * curve) * (CURVE * (1.0 + 3 * 0.044715 * square))
    d_pre = (dot(above_ref[...], w_r, NT) * slope).astype(BF16)
    pre_s[...] = d_pre
    grad_b_ref[...] = jnp.sum(d_pre.astype(F32), axis=0, keepdims=True)
    stages(0)
    out_ref[...] += dot(act_s[...], w_r)
    back_ref[...] += dot(d_pre, w_e, NT)
    grad_r_ref[...] = dot(act_s[...], above_ref[...], TN).astype(BF16).reshape(grad_r_ref.shape)
    grad_e = dot(second_ref[...], pre_s[...], TN).astype(BF16)
    for k in range(slices):
        for j in range(per):
            @pl.when(step == k * per + j)
            def _():
                if j == 0 and k >= 2:
                    movers[k - 2].sent_first()
                grad_s[k % 2, :, :, :, :, :, j * strip : (j + 1) * strip] = grad_e.reshape(grad_s.shape[1:-1] + (strip,))
                if j == per - 1:
                    movers[k].begin()

    stages(1)

    @pl.when(step == final)
    def _():
        for *_, action in sorted(late, key=lambda entry: entry[:2]):
            action()
        for k in range(max(0, slices - 2), slices):
            movers[k].sent_first()
        for k in range(slices):
            movers[k].sent_last()


def mixing(devices, second, above, gathered, bias_e, bias_r, part):
    rows, width = second.shape
    hidden = bias_e.shape[1]
    many = hidden // devices
    sides = hidden // width
    strip = STRIP
    per = width // strip
    outer, side, core = digits(devices)
    fixed = pl.BlockSpec((rows, width), lambda i: (0, 0), pipeline_mode=pl.Buffered(1))
    whole = pl.BlockSpec(memory_space=pltpu.VMEM)
    scratch = [pltpu.VMEM((rows, strip), BF16)] * 2 + [pltpu.VMEM((2, outer, side, side, core, part, width), BF16)]
    for k in range(sides):
        scratch += boxes_for(devices, part, width)
    return pl.pallas_call(
        functools.partial(mixing_kernel, devices),
        grid=(hidden // strip,),
        in_specs=[
            fixed, fixed,
            pl.BlockSpec((devices, part, strip), lambda i: (0, many // part + 1 + i // per, i % per)),
            pl.BlockSpec((strip // many, many, width), lambda i: (i, 0, 0)),
            pl.BlockSpec((1, strip), lambda i: (0, i)),
            pl.BlockSpec((1, width), lambda i: (0, 0)),
        ],
        out_specs=[
            fixed,
            fixed,
            pl.BlockSpec((strip // many, many, width), lambda i: (i, 0, 0)),
            pl.BlockSpec((1, strip), lambda i: (0, i)),
            pl.BlockSpec((sides * part, width), lambda i: (0, 0)),
            pl.BlockSpec((1, width), lambda i: (0, 0)),
        ],
        out_shape=[
            jax.ShapeDtypeStruct((rows, width), F32),
            jax.ShapeDtypeStruct((rows, width), F32),
            jax.ShapeDtypeStruct((devices, many, width), BF16),
            jax.ShapeDtypeStruct((1, hidden), F32),
            jax.ShapeDtypeStruct((sides * part, width), F32),
            jax.ShapeDtypeStruct((1, width), F32),
        ],
        scratch_shapes=scratch + sems_for(devices, sides),
        compiler_params=pltpu.CompilerParams(collective_id=3, has_side_effects=True, vmem_limit_bytes=57 << 20),
        name="mixing",
    )(second, above, gathered, gathered, bias_e, bias_r)


def join_kernel(
    devices, window_ref, first_ref, final_ref, one_ref, above_ref, live_ref, w_ref, bias_ref, gain_ref, shift_ref,
    combined_ref, out_ref, second_ref, reduce_ref, side_in, part_s, halo_sem,
):
    slots, width = one_ref.shape
    half = slots // 2
    tile = 256
    me = lax.axis_index("fsdp")
    last = devices - 1
    left, right = lax.rem(me + last, devices), lax.rem(me + 1, devices)
    greet([left, right])

    def to_left():
        return remote(window_ref.at[:half], side_in.at[1], halo_sem, (0,), left)

    def to_right():
        return remote(window_ref.at[half + slots :], side_in.at[0], halo_sem, (1,), right)

    @pl.when(me > 0)
    def _():
        to_left().start()

    @pl.when(me < last)
    def _():
        to_right().start()

    @pl.when(me == 0)
    def _():
        side_in[0] = jnp.zeros((half, width), BF16)

    @pl.when(me == last)
    def _():
        side_in[1] = jnp.zeros((half, width), BF16)

    w_o = w_ref[...].reshape(width, width)

    owns = (first_ref, final_ref)

    def before(side, i, carry):
        here = pl.ds(pl.multiple_of(i * tile, tile), tile)
        at = pl.ds(pl.multiple_of(side * half + i * tile, tile), tile)
        part_s[at, :] = dot(owns[side][here, :], w_o)
        reduce_ref[at, :] = (live_ref[at, :] * above_ref[at, :].astype(F32)).astype(BF16)
        return carry

    for side in range(2):
        lax.fori_loop(0, half // tile, functools.partial(before, side), 0)

    def after(side, i, carry):
        here = pl.ds(pl.multiple_of(i * tile, tile), tile)
        at = pl.ds(pl.multiple_of(side * half + i * tile, tile), tile)
        other = side_in[side, here, :]
        combined_ref[at, :] = owns[side][here, :] + other
        attended = part_s[at, :] + dot(other, w_o) + bias_ref[...]
        out = one_ref[at, :].astype(F32) + live_ref[at, :] * attended
        out_ref[at, :] = out
        second_ref[at, :] = layer_norm(out, gain_ref[...], shift_ref[...]).astype(BF16)
        return carry

    @pl.when(me > 0)
    def _():
        to_right().wait_recv()

    lax.fori_loop(0, half // tile, functools.partial(after, 0), 0)

    @pl.when(me < last)
    def _():
        to_left().wait_recv()

    lax.fori_loop(0, half // tile, functools.partial(after, 1), 0)

    @pl.when(me > 0)
    def _():
        to_left().wait_send()

    @pl.when(me < last)
    def _():
        to_right().wait_send()


def join(devices, window, one, above, live, gathered, bias, gain, shift, part, sides):
    slots, width = one.shape
    dma = pltpu.SemaphoreType.DMA
    rows = pl.BlockSpec((slots, width), lambda i: (0, 0))
    thin = pl.BlockSpec((1, width), lambda i: (0, 0))
    low = jax.ShapeDtypeStruct((slots, width), BF16)
    return pl.pallas_call(
        functools.partial(join_kernel, devices),
        grid=(1,),
        in_specs=[
            pl.BlockSpec(memory_space=pl.ANY),
            pl.BlockSpec((slots // 2, width), lambda i: (1, 0)), pl.BlockSpec((slots // 2, width), lambda i: (2, 0)), rows, rows, pl.BlockSpec((slots, 1), lambda i: (0, 0)),
            pl.BlockSpec((devices, part, width), lambda i: (0, sides, 0)), thin, thin, thin,
        ],
        out_specs=[rows] * 4,
        out_shape=[low, jax.ShapeDtypeStruct((slots, width), F32), low, low],
        scratch_shapes=[pltpu.VMEM((2, slots // 2, width), BF16), pltpu.VMEM((slots, width), F32), dma((2, 2))],
        compiler_params=pltpu.CompilerParams(collective_id=6, has_side_effects=True, vmem_limit_bytes=57 << 20),
        name="join",
    )(window, window, window, one, above, live, gathered, bias, gain, shift)


def turn_kernel(
    devices, out_one_ref, d_second_ref, mixed_ref, two_ref, above_ref, combined_ref, live_ref, gain_ref, w_o_ref,
    bias_r_ref, bias_e_ref,
    wide_ref, grad_one_out, one_out, res_two_out, grad_o_out, small_ref,
    mixed_s, two_s, combined_s, one_s, res_two_s, grad_o_s, attend_s, halo_sem, load_sem, store_sem,
):
    slots, width = two_ref.shape
    half = slots // 2
    tile = 256
    part = grad_o_out.shape[1]
    w_o = w_o_ref[...].reshape(width, width)
    me = lax.axis_index("fsdp")
    last = devices - 1
    left, right = lax.rem(me + last, devices), lax.rem(me + 1, devices)
    loads = [
        pltpu.make_async_copy(source, target, load_sem.at[k])
        for k, (source, target) in enumerate(((mixed_ref, mixed_s), (two_ref, two_s), (combined_ref, combined_s)))
    ]
    stores = [
        pltpu.make_async_copy(source, target, store_sem.at[k])
        for k, (source, target) in enumerate(
            ((attend_s, grad_one_out), (one_s, one_out), (res_two_s, res_two_out), (grad_o_s, grad_o_out))
        )
    ]
    for load in loads:
        load.start()
    greet([left, right])

    def to_left():
        return remote(wide_ref.at[half : 2 * half], wide_ref.at[half + slots :], halo_sem, (0,), left)

    def to_right():
        return remote(wide_ref.at[2 * half : 3 * half], wide_ref.at[:half], halo_sem, (1,), right)

    small_ref[...] = jnp.zeros(small_ref.shape, F32)
    gain = gain_ref[...]

    def norm_tile(i, carry):
        at = pl.ds(pl.multiple_of(i * tile, tile), tile)
        live = live_ref[at, :]
        values = out_one_ref[at, :]
        above = d_second_ref[at, :]
        center = values - jnp.mean(values, axis=1, keepdims=True)
        scale = lax.rsqrt(jnp.mean(center * center, axis=1, keepdims=True) + EPS_NORM)
        center = center * scale
        small_ref[2:3, :] += jnp.sum(above * center, axis=0, keepdims=True)
        small_ref[3:4, :] += jnp.sum(above, axis=0, keepdims=True)
        above = above * gain
        mean = jnp.mean(above, axis=1, keepdims=True)
        along = jnp.mean(above * center, axis=1, keepdims=True)
        total = live * (above_ref[at, :].astype(F32) + scale * (above - mean - center * along))
        low = total.astype(BF16)
        attend_s[at, :] = low
        small_ref[4:5, :] += jnp.sum(low.astype(F32), axis=0, keepdims=True)
        wide_ref[pl.ds(pl.multiple_of(half + i * tile, tile), tile), :] = dot(low, w_o, NT).astype(BF16)
        return carry

    lax.fori_loop(0, half // tile, norm_tile, 0)

    @pl.when(me > 0)
    def _():
        to_left().start()

    lax.fori_loop(half // tile, slots // tile, norm_tile, 0)

    @pl.when(me < last)
    def _():
        to_right().start()

    stores[0].start()
    for load in loads:
        load.wait()

    def finish_tile(i, carry):
        at = pl.ds(pl.multiple_of(i * tile, tile), tile)
        live = live_ref[at, :]
        one_s[at, :] = (live * out_one_ref[at, :]).astype(BF16)
        res_two_s[at, :] = (live * (two_s[at, :].astype(F32) + mixed_s[at, :])).astype(BF16)
        return carry

    lax.fori_loop(0, slots // tile, finish_tile, 0)
    stores[1].start()
    stores[2].start()

    def weights(i, carry):
        cols = pl.ds(pl.multiple_of(i * tile, tile), tile)
        many = tile // part
        grad_o_s[pl.ds(pl.multiple_of(i * many, many), many)] = (
            dot(combined_s[:, cols], attend_s[...], TN).astype(BF16).reshape(many, part, width)
        )
        return carry

    lax.fori_loop(0, width // tile, weights, 0)
    stores[3].start()
    small_ref[5:6, :] = bias_r_ref[...]
    for k in range(bias_e_ref.shape[1] // width):
        small_ref[6 + k : 7 + k, :] = bias_e_ref[:, k * width : (k + 1) * width]

    @pl.when(me > 0)
    def _():
        to_right().wait_recv()
        to_left().wait_send()

    @pl.when(me == 0)
    def _():
        wide_ref[:half] = jnp.zeros((half, width), BF16)

    @pl.when(me < last)
    def _():
        to_left().wait_recv()
        to_right().wait_send()

    @pl.when(me == last)
    def _():
        wide_ref[half + slots :] = jnp.zeros((half, width), BF16)

    for store in stores:
        store.wait()


def turn(devices, out_one, d_second, mixed, two, above, combined, live, gain, gathered, bias_r, bias_e, sides):
    slots, width = two.shape
    part = width // devices
    vmem = pl.BlockSpec(memory_space=pltpu.VMEM)
    anywhere = pl.BlockSpec(memory_space=pl.ANY)
    dma = pltpu.SemaphoreType.DMA
    low = pltpu.VMEM((slots, width), BF16)
    rows_low = jax.ShapeDtypeStruct((slots, width), BF16)
    return pl.pallas_call(
        functools.partial(turn_kernel, devices),
        grid=(1,),
        in_specs=[vmem, vmem, anywhere, anywhere, vmem, anywhere, vmem, vmem]
        + [pl.BlockSpec((devices, part, width), lambda i: (0, sides, 0)), vmem, vmem],
        out_specs=(vmem,) + (anywhere,) * 4 + (vmem,),
        out_shape=(
            jax.ShapeDtypeStruct((2 * slots, width), BF16), rows_low, rows_low, rows_low,
            jax.ShapeDtypeStruct((devices, part, width), BF16),
            jax.ShapeDtypeStruct((16, width), F32),
        ),
        scratch_shapes=[
            pltpu.VMEM((slots, width), F32), low, low, low, low, pltpu.VMEM((devices, part, width), BF16), low,
            dma((2, 2)), dma((3,)), dma((4,)),
        ],
        compiler_params=pltpu.CompilerParams(collective_id=5, has_side_effects=True, vmem_limit_bytes=57 << 20),
        name="turn",
    )(out_one, d_second, mixed, two, above, combined, live, gain, gathered, bias_r, bias_e)


def tail_kernel(
    devices, grad_r_ref, grad_o_ref, d_shared_ref, d_value_ref, normed_in, head_ref, own_in, end_ref, above_in, live_ref,
    gain_ref, w_s_ref, w_v_ref, small_ref,
    back_ref, out_s_ref, out_v_ref, out_o_ref, out_r_ref, thin_ref, long_ref,
    normed_ref, own_ref, above_ref, late_sem, side_s, side_in, vector_s, vector_in, grad_s, load_sem, halo_sem, vector_sem, *rest,
):
    window, width = normed_ref.shape
    slots = own_ref.shape[0]
    half = slots // 2
    part = out_s_ref.shape[0]
    many = out_r_ref.shape[0]
    tile = 256
    where = neighbours(devices)
    (o, p, q, c), core_peer, q_peers, p_peers, o_peers = where
    me = lax.axis_index("fsdp")
    outer, side, core = digits(devices)
    owns, rest = rest[:3], rest[3:]
    sems = rest[-4:]

    def distant(source, row, rows, k):
        at = pl.ds(row, rows)

        def other():
            return source.at[:, :, :, 1 - c, at, :]

        def mine(spot, cols):
            return owns[k].at[tuple(spot) + (slice(None), cols)]

        def load():
            return pltpu.make_async_copy(source.at[:, :, :, c, at, :], owns[k], load_sem.at[k])

        return Scatter(devices, where, k, rest[5 * k : 5 * k + 5], sems, other, mine, load)

    def near(j, k):
        def other():
            return grad_s.at[j, :, :, :, 1 - c]

        def mine(spot, cols):
            return grad_s.at[(j,) + tuple(spot) + (c, slice(None), cols)]

        return Scatter(devices, where, k, rest[5 * k : 5 * k + 5], sems, other, mine)

    movers = [
        distant(grad_r_ref, 0, many // 2, 0), distant(grad_r_ref, many // 2, many // 2, 1), distant(grad_o_ref, 0, part, 2),
        near(0, 3), near(1, 4),
    ]
    last = devices - 1
    left, right = lax.rem(me + last, devices), lax.rem(me + 1, devices)
    late = [
        pltpu.make_async_copy(source, target, late_sem.at[k])
        for k, (source, target) in enumerate(((normed_in, normed_ref), (own_in, own_ref), (above_in, above_ref)))
    ]
    for load in late:
        load.start()
    greet(peers_of(where) + [left, right])
    for k in range(3):
        movers[k].begin()

    def to_left():
        return remote(side_s.at[0], side_in.at[1], halo_sem, (0,), left)

    def to_right():
        return remote(side_s.at[1], side_in.at[0], halo_sem, (1,), right)

    vector_s[...] = small_ref[...]
    gain = gain_ref[...]

    def norm_tile(ref, row, at):
        values = ref[pl.ds(row, tile), :].astype(F32)
        above = dot(d_shared_ref[at, :], w_s_ref[...], NT) + dot(d_value_ref[at, :], w_v_ref[...], NT)
        center = values - jnp.mean(values, axis=1, keepdims=True)
        scale = lax.rsqrt(jnp.mean(center * center, axis=1, keepdims=True) + EPS_NORM)
        center = center * scale
        vector_s[0:1, :] += jnp.sum(above * center, axis=0, keepdims=True)
        vector_s[1:2, :] += jnp.sum(above, axis=0, keepdims=True)
        above = above * gain
        mean = jnp.mean(above, axis=1, keepdims=True)
        along = jnp.mean(above * center, axis=1, keepdims=True)
        return scale * (above - mean - center * along)

    def side_tiles(i, carry):
        row = pl.multiple_of(i * tile, tile)
        side_s[0, pl.ds(row, tile), :] = norm_tile(head_ref, row, pl.ds(row, tile)).astype(BF16)
        at = pl.ds(pl.multiple_of(half + slots + i * tile, tile), tile)
        side_s[1, pl.ds(row, tile), :] = norm_tile(end_ref, row, at).astype(BF16)
        return carry

    movers[0].stage_core()
    lax.fori_loop(0, half // tile, side_tiles, 0)

    @pl.when(me > 0)
    def _():
        to_left().start()

    @pl.when(me < last)
    def _():
        to_right().start()

    movers[1].stage_core()
    movers[0].stage_first()

    def weights(j, ref):
        wide = tile // part

        def strip(i, carry):
            cols = pl.ds(pl.multiple_of(i * tile, tile), tile)
            block = dot(normed_ref[:, cols], ref[...], TN).astype(BF16).reshape(wide // core, core, part, width)
            for k in range(wide // core):
                index = i * (wide // core) + k
                spot = (lax.div(index, side * side), lax.rem(lax.div(index, side), side), lax.rem(index, side))
                grad_s[(j,) + spot] = block[k]
            return carry

        lax.fori_loop(0, width // tile, strip, 0)

    for load in late:
        load.wait()
    weights(0, d_shared_ref)
    movers[3].begin()
    movers[2].stage_core()
    movers[1].stage_first()
    movers[0].stage_second()
    weights(1, d_value_ref)
    movers[4].begin()
    movers[3].stage_core()
    movers[2].stage_first()
    movers[1].stage_second()

    def own_tiles(i, carry):
        row = pl.multiple_of(i * tile, tile)
        at = pl.ds(pl.multiple_of(half + i * tile, tile), tile)
        here = pl.ds(row, tile)
        total = above_ref[here, :].astype(F32) + norm_tile(own_ref, row, at)
        back_ref[here, :] = (live_ref[here, :] * total).astype(BF16)
        return carry

    lax.fori_loop(0, slots // tile, own_tiles, 0)

    def vector_copies(stage):
        group = ([(0, core_peer)], q_peers, p_peers, o_peers)[stage]
        base = (0, 1, side, 2 * side - 1)[stage]
        return [
            remote(vector_s if stage == 0 else vector_in.at[base - 1], vector_in.at[base + d], vector_sem, (base + d,), device)
            for d, (_, device) in enumerate(group)
        ]

    def vector_stage(stage):
        base = (0, 1, side, 2 * side - 1)[stage]
        copies = vector_copies(stage)
        total = vector_s[...] if stage == 0 else vector_in[base - 1]
        for d, copy in enumerate(copies):
            copy.wait_recv()
            total = total + vector_in[base + d]
        vector_in[base + len(copies) - 1] = total

    for copy in vector_copies(0):
        copy.start()
    movers[4].stage_core()
    movers[3].stage_first()
    movers[2].stage_second()
    out_r_ref[: many // 2, :] = movers[0].stage_third()
    vector_stage(0)
    for copy in vector_copies(1):
        copy.start()
    movers[4].stage_first()
    movers[3].stage_second()
    out_r_ref[many // 2 :, :] = movers[1].stage_third()
    vector_stage(1)
    for copy in vector_copies(2):
        copy.start()
    movers[4].stage_second()
    out_o_ref[...] = movers[2].stage_third()
    vector_stage(2)
    for copy in vector_copies(3):
        copy.start()

    @pl.when(me > 0)
    def _():
        to_right().wait_recv()

    @pl.when(me == 0)
    def _():
        side_in[0] = jnp.zeros((half, width), BF16)

    @pl.when(me < last)
    def _():
        to_left().wait_recv()

    @pl.when(me == last)
    def _():
        side_in[1] = jnp.zeros((half, width), BF16)

    for k in range(2):
        at = slice(k * half, (k + 1) * half)
        back_ref[at, :] = (back_ref[at, :].astype(F32) + side_in[k].astype(F32)).astype(BF16)
    out_s_ref[...] = movers[3].stage_third()
    vector_stage(3)
    out_v_ref[...] = movers[4].stage_third()
    vectors = 2 * side + outer - 3
    total = vector_in[vectors]
    thin_ref[...] = pltpu.roll(total, lax.rem(width - me * part, width), 1)[:, :DH]
    each = long_ref.shape[1]
    long_rows = [total[6 + k : 7 + k, :] for k in range(devices * each // width)]
    mine = lax.div(me * each, width)
    chosen = long_rows[0]
    for k in range(1, len(long_rows)):
        chosen = jnp.where(mine == k, long_rows[k], chosen)
    long_ref[...] = pltpu.roll(chosen, lax.rem(width - lax.rem(me * each, width), width), 1)[:, :each]
    for stage in range(4):
        for copy in vector_copies(stage):
            copy.wait_send()

    @pl.when(me > 0)
    def _():
        to_left().wait_send()

    @pl.when(me < last)
    def _():
        to_right().wait_send()

    for mover in movers:
        mover.sent_first()
        mover.sent_last()


def tail(devices, grad_r, grad_o, d_shared, d_values, normed, head, own, end, above, live, gain, w_s, w_v, small):
    window, width = normed.shape
    slots = own.shape[0]
    outer, side, core = digits(devices)
    part, many = grad_o.shape[1], grad_r.shape[1]
    each = many
    vmem = pl.BlockSpec(memory_space=pltpu.VMEM)
    anywhere = pl.BlockSpec(memory_space=pl.ANY)
    dma = pltpu.SemaphoreType.DMA
    sizes = [many // 2, many // 2, part, part, part]
    scratch = [
        pltpu.VMEM((window, width), BF16), pltpu.VMEM((slots, width), BF16), pltpu.VMEM((slots, width), BF16), dma((3,)),
        pltpu.VMEM((2, slots // 2, width), BF16), pltpu.VMEM((2, slots // 2, width), BF16),
        pltpu.VMEM((16, width), F32), pltpu.VMEM((2 * side + outer - 2, 16, width), F32),
        pltpu.VMEM((2, outer, side, side, core, part, width), BF16),
        dma((3,)), dma((2, 2)), dma((2, 2 * side + outer - 2)),
    ]
    scratch += [pltpu.VMEM((outer, side, side, rows, width), BF16) for rows in sizes[:3]]
    for rows in sizes:
        scratch += boxes_for(devices, rows, width)
    shape = (outer, side, side, core)
    return pl.pallas_call(
        functools.partial(tail_kernel, devices),
        in_specs=[anywhere, anywhere, vmem, vmem, anywhere, vmem, anywhere, vmem, anywhere] + [vmem] * 5,
        out_specs=(vmem,) * 7,
        out_shape=(
            jax.ShapeDtypeStruct((slots, width), BF16),
            jax.ShapeDtypeStruct((part, width), F32),
            jax.ShapeDtypeStruct((part, width), F32),
            jax.ShapeDtypeStruct((part, width), F32),
            jax.ShapeDtypeStruct((many, width), F32),
            jax.ShapeDtypeStruct((16, DH), F32),
            jax.ShapeDtypeStruct((1, each), F32),
        ),
        scratch_shapes=scratch + sems_for(devices, len(sizes)),
        compiler_params=pltpu.CompilerParams(collective_id=4, has_side_effects=True, vmem_limit_bytes=57 << 20),
        name="tail",
    )(
        grad_r.reshape(shape + grad_r.shape[1:]), grad_o.reshape(shape + grad_o.shape[1:]),
        d_shared, d_values, normed, head, own, end, above, live, gain, w_s, w_v, small,
    )


def find_ranks(length_ref, target_ref, bucket_ref, packed_ref, info_ref, before_s):
    devices = length_ref.shape[0]
    lists, slots = bucket_ref.shape
    me = lax.axis_index("fsdp")
    base = me * slots
    window = 2 * slots

    def look(s, carry):
        start, mine, found, one, two = carry
        size = length_ref[s]
        target = target_ref[s]
        middle = start + lax.shift_right_logical(size, 1)
        inside = (middle >= base) & (middle < base + slots)
        offset = start - base + slots // 2
        entry = (offset, offset + size, target)
        first, second = inside & (found == 0), inside & (found == 1)
        one = tuple(jnp.where(first, new, old) for new, old in zip(entry, one))
        two = tuple(jnp.where(second, new, old) for new, old in zip(entry, two))
        return start + size, jnp.where(target == me, size, mine), found + inside.astype(jnp.int32), one, two

    zero = jnp.int32(0)
    nothing = (jnp.int32(window), jnp.int32(window), zero)
    total, mine, found, one, two = lax.fori_loop(0, devices, look, (zero, zero, zero, nothing, nothing))
    for k, value in enumerate((one[0], one[1], two[0], two[1], one[2], two[2], total, found)):
        info_ref[k] = value

    def fill(i, carry):
        at = pl.ds(pl.multiple_of(i * DH, DH), DH)
        first = lax.broadcasted_iota(jnp.int32, (DH, slots), 0) + i * DH
        second = lax.broadcasted_iota(jnp.int32, (DH, slots), 1)
        before_s[at, :] = jnp.where(first < second, 1.0, 0.0).astype(BF16)
        return carry

    lax.fori_loop(0, slots // DH, fill, 0)
    left = lax.broadcasted_iota(jnp.int32, (DH, DH), 0)
    right = lax.broadcasted_iota(jnp.int32, (DH, DH), 1)
    smaller = jnp.where((left // BUCKETS == right // BUCKETS) & (right < left), 1.0, 0.0).astype(BF16)
    many = DH // BUCKETS
    bucket = lax.broadcasted_iota(jnp.int32, (many, BUCKETS, slots), 1)
    live = lax.broadcasted_iota(jnp.int32, (many, BUCKETS, slots), 2) < mine
    ranks = []
    for g in range(lists // many):
        here = (jnp.broadcast_to(bucket_ref[g * many : (g + 1) * many, :][:, None, :], bucket.shape) == bucket) & live
        one_hot = jnp.where(here, 1.0, 0.0)
        flat = one_hot.reshape(DH, slots).astype(BF16)
        offset = jnp.sum(dot(smaller, flat), axis=1, keepdims=True)
        place = (dot(flat, before_s[...]) + offset).reshape(many, BUCKETS, slots)
        ranks.append(jnp.sum(one_hot * place, axis=1))
    rank = jnp.concatenate(ranks, axis=0)
    live = lax.broadcasted_iota(jnp.int32, (lists, slots), 1) < mine
    packed_ref[:lists, :] = jnp.where(live, jnp.floor(rank * (1.0 / GROUP)), FREE).astype(BF16)


def project_kernel(
    info_ref, head_ref, own_ref, tail_ref, gain_ref, shift_ref, w_s_ref, w_v_ref, one_ref, two_ref,
    normed_ref, shared_ref, value_ref, code_ref,
):
    i = pl.program_id(0)
    tile = own_ref.shape[0]
    steps = pl.num_programs(0)

    def go(ref):
        normed = layer_norm(ref[...].astype(F32), gain_ref[...], shift_ref[...]).astype(BF16)
        normed_ref[...] = normed
        shared_ref[...] = dot(normed, w_s_ref[...]).astype(BF16)
        value_ref[...] = dot(normed, w_v_ref[...]).astype(BF16)

    @pl.when(i < steps // 4)
    def _():
        go(head_ref)

    @pl.when((i >= steps // 4) & (i < steps - steps // 4))
    def _():
        go(own_ref)

    @pl.when(i >= steps - steps // 4)
    def _():
        go(tail_ref)

    @pl.when(i == 0)
    def _():
        lists, window = code_ref.shape
        lane = lax.broadcasted_iota(jnp.int32, (lists, window), 1)
        code = jnp.full((lists, window), FREE, F32)
        for k, ref in enumerate((one_ref, two_ref)):
            begin, end = info_ref[2 * k], info_ref[2 * k + 1]
            rows = ref[0].astype(F32)
            moved = pltpu.roll(jnp.concatenate([rows, rows], axis=1), lax.rem(begin, window), 1)
            code = jnp.where((lane >= begin) & (lane < end), moved + 32.0 * k, code)
        code_ref[...] = code.astype(BF16)


def project(info, head, own, tail, gain, shift, w_s, w_v, blocks):
    slots, width = own.shape
    window = 2 * slots
    lists = ROUNDS * HEADS
    tile = 256
    steps = window // tile
    quarter = steps // 4
    rows = pl.BlockSpec((tile, width), lambda i, info: (i, 0))
    vector = pl.BlockSpec((1, width), lambda i, info: (0, 0))
    matrix = pl.BlockSpec((width, width), lambda i, info: (0, 0), pipeline_mode=pl.Buffered(1))
    wide = jax.ShapeDtypeStruct((window, width), BF16)
    return pl.pallas_call(
        project_kernel,
        grid_spec=pltpu.PrefetchScalarGridSpec(
            num_scalar_prefetch=1,
            grid=(steps,),
            in_specs=[
                pl.BlockSpec((tile, width), lambda i, info: (jnp.minimum(i, quarter - 1), 0)),
                pl.BlockSpec((tile, width), lambda i, info: (jnp.clip(i - quarter, 0, 2 * quarter - 1), 0)),
                pl.BlockSpec((tile, width), lambda i, info: (jnp.clip(i - 3 * quarter, 0, quarter - 1), 0)),
                vector, vector, matrix, matrix,
                pl.BlockSpec((1, lists, slots), lambda i, info: (info[4], 0, 0)),
                pl.BlockSpec((1, lists, slots), lambda i, info: (info[5], 0, 0)),
            ],
            out_specs=[rows, rows, rows, pl.BlockSpec((lists, window), lambda i, info: (0, 0))],
        ),
        out_shape=[wide, wide, wide, jax.ShapeDtypeStruct((lists, window), BF16)],
        compiler_params=pltpu.CompilerParams(vmem_limit_bytes=57 << 20),
        name="project",
    )(info, head, own, tail, gain, shift, w_s, w_v, blocks, blocks)


def gather_kernel(devices, arrays, length_ref, target_ref, bucket_ref, vector_ref, rows_ref, *refs):
    sources, outs, (info_ref, head_ref, end_ref) = refs[: arrays - 1], refs[arrays - 1 : 2 * arrays - 1], refs[2 * arrays - 1 : 2 * arrays + 2]
    packed_s, before_s, own_sem, sem_o, sem_a, sem_b, sem_c, halo_sem, edge_sem = refs[2 * arrays + 2 :]
    sources = sources + (packed_s,)
    outer, side, core = digits(devices)
    (o, p, q, c), core_peer, q_peers, p_peers, o_peers = neighbours(devices)
    me = lax.axis_index("fsdp")
    last_device = devices - 1
    left, right = lax.rem(me + last_device, devices), lax.rem(me + 1, devices)
    greet([core_peer] + [d for _, d in q_peers] + [d for _, d in p_peers] + [d for _, d in o_peers] + [left, right])
    half = sources[0].shape[-1] // 2
    border = head_ref.shape[0]

    def to_left():
        return remote(rows_ref.at[:border], end_ref, halo_sem, (0,), left)

    def to_right():
        return remote(rows_ref.at[border:], head_ref, halo_sem, (1,), right)

    def blank(ref):
        return pltpu.make_async_copy(before_s.at[:border], ref, edge_sem.at[0])

    columns = (pl.ds(0, half), pl.ds(half, half))

    locals_, begun, first, second, last = [], {}, {}, {}, {}
    for s in range(arrays):
        if s == arrays - 1:
            find_ranks(length_ref, target_ref, bucket_ref, packed_s, info_ref, before_s)
            packed_s[bucket_ref.shape[0] :, :] = vector_ref[...]
        locals_.append(pltpu.make_async_copy(sources[s], outs[s].at[o, p, q, c], own_sem.at[s]))
        locals_[s].start()
        for d, (k, device) in enumerate(o_peers):
            begun[s, d] = remote(sources[s], outs[s].at[o, p, q, c], sem_o, (s, d), device)
            begun[s, d].start()

    @pl.when(me > 0)
    def _():
        to_left().start()

    @pl.when(me < last_device)
    def _():
        to_right().start()

    before_s[:border, :] = jnp.zeros((border, before_s.shape[1]), BF16)

    @pl.when(me == 0)
    def _():
        blank(head_ref).start()

    @pl.when(me == last_device)
    def _():
        blank(end_ref).start()

    def stage_a(s):
        locals_[s].wait()
        for d in range(outer - 1):
            begun[s, d].wait_recv()
        for h, peers in enumerate((q_peers, p_peers)):
            piece = outs[s].at[:, p, q, c, :, columns[h]]
            for d, (k, device) in enumerate(peers):
                first[s, h, d] = remote(piece, piece, sem_a, (s, h, d), device)
                first[s, h, d].start()

    def stage_b(s):
        for h, peers in enumerate((p_peers, q_peers)):
            for d in range(side - 1):
                first[s, h, d].wait_recv()
            piece = outs[s].at[:, p, :, c, :, columns[h]] if h == 0 else outs[s].at[:, :, q, c, :, columns[h]]
            for d, (k, device) in enumerate(peers):
                second[s, h, d] = remote(piece, piece, sem_b, (s, h, d), device)
                second[s, h, d].start()

    def stage_c(s):
        for h in range(2):
            for d in range(side - 1):
                second[s, h, d].wait_recv()
        piece = outs[s].at[:, :, :, c]
        last[s] = remote(piece, piece, sem_c, (s,), core_peer)
        last[s].start()

    for t in range(arrays + 2):
        if t < arrays:
            stage_a(t)
        if 0 <= t - 1 < arrays:
            stage_b(t - 1)
        if 0 <= t - 2 < arrays:
            stage_c(t - 2)
    for s in range(arrays):
        last[s].wait_recv()

    @pl.when(me > 0)
    def _():
        to_right().wait_recv()
        to_left().wait_send()

    @pl.when(me == 0)
    def _():
        blank(head_ref).wait()

    @pl.when(me < last_device)
    def _():
        to_left().wait_recv()
        to_right().wait_send()

    @pl.when(me == last_device)
    def _():
        blank(end_ref).wait()

    for group in (begun, first, second, last):
        for copy in group.values():
            copy.wait_send()


def gather(devices, lengths, destination, buckets, vectors, rows, arrays):
    outer, side, core = digits(devices)
    lists, slots = buckets.shape
    packed = jax.ShapeDtypeStruct((lists + vectors.shape[0], slots), BF16)
    shapes = [jax.ShapeDtypeStruct(array.shape, array.dtype) for array in arrays] + [packed]
    count = len(shapes)
    dma = pltpu.SemaphoreType.DMA
    anywhere = pl.BlockSpec(memory_space=pl.ANY)
    hbm = pl.BlockSpec(memory_space=pltpu.HBM)
    smem = pl.BlockSpec(memory_space=pltpu.SMEM)
    vmem = pl.BlockSpec(memory_space=pltpu.VMEM)
    outs = pl.pallas_call(
        functools.partial(gather_kernel, devices, count),
        out_shape=tuple(jax.ShapeDtypeStruct((outer, side, side, core) + shape.shape, shape.dtype) for shape in shapes)
        + (jax.ShapeDtypeStruct((8,), jnp.int32),)
        + (jax.ShapeDtypeStruct((slots // 2, rows.shape[1]), BF16),) * 2,
        in_specs=[smem, smem, vmem, vmem] + [anywhere] * count,
        out_specs=(hbm,) * count + (smem, hbm, hbm),
        scratch_shapes=[
            pltpu.VMEM(packed.shape, BF16), pltpu.VMEM((slots, slots), BF16),
            dma((count,)), dma((2, count, outer - 1)), dma((2, count, 2, side - 1)), dma((2, count, 2, side - 1)), dma((2, count)),
            dma((2, 2)), dma((1,)),
        ],
        compiler_params=pltpu.CompilerParams(collective_id=2, has_side_effects=True, vmem_limit_bytes=57 << 20),
        name="gather",
    )(lengths, destination, buckets, vectors, rows, *arrays)
    return [out.reshape((devices,) + shape.shape) for out, shape in zip(outs, shapes)] + list(outs[count:])


def body(
    input_one, input_two, upstream_one, upstream_two, lengths, destination, buckets,
    w_shared, w_value, w_output, w_expand, w_reduce,
    gain_attend, shift_attend, gain_mixing, shift_mixing, bias_output, bias_expand, bias_reduce,
):
    devices = lax.axis_size("fsdp")
    me = lax.axis_index("fsdp")
    slots, width = input_one.shape
    half = slots // 2
    window = 2 * slots
    part = w_shared.shape[0]
    hidden = w_expand.shape[1]
    sides = hidden // width
    base = me * slots
    lists = ROUNDS * HEADS
    spot = jnp.arange(width, dtype=jnp.int32)
    short = jnp.stack([gain_attend, shift_attend, gain_mixing, shift_mixing, bias_output, bias_reduce])
    short = jnp.where(spot // part == me, jnp.tile(short, (1, devices)), 0.0)
    many = hidden // devices
    long = jnp.tile(bias_expand, width // many)[None]
    long = jnp.where(spot[None] // many + (width // many) * jnp.arange(sides, dtype=jnp.int32)[:, None] == me, long, 0.0)
    vectors = jnp.concatenate([short, long], axis=0)
    high = lax.reduce_precision(vectors, 8, 7)
    count = vectors.shape[0]
    packed = jnp.concatenate(
        [high.astype(BF16), (vectors - high).astype(BF16), jnp.zeros((24 - 2 * count, width), BF16)], axis=0
    )
    second_gather = lax.all_gather(
        jnp.concatenate(
            [w_reduce, w_output] + [w_expand[:, k * width : (k + 1) * width] for k in range(sides)], axis=0
        ),
        "fsdp", axis=0, tiled=False,
    )
    full_shared, full_value, packed, info, two_head, two_tail = gather(
        devices, lengths, destination, buckets[0], packed, input_two, [w_shared, w_value]
    )
    full_shared, full_value = full_shared.reshape(width, width), full_value.reshape(width, width)
    vectors = jnp.sum(packed[:, lists : lists + 2 * count].astype(F32), axis=0)
    vectors = vectors[:count] + vectors[count:]
    gain_a, shift_a, gain_m, shift_m, bias_o, bias_r = (vectors[k : k + 1] for k in range(6))
    bias_e = vectors[6:].reshape(1, hidden)
    lane = jnp.arange(HEADS * DH, dtype=jnp.int32)
    row = jnp.arange(lists, dtype=jnp.int32)[:, None]
    spread = (row == ((lane % 64) // 16) * HEADS + lane // DH).astype(BF16)

    live = ((base + jnp.arange(slots, dtype=jnp.int32)) < info[6]).astype(F32)[:, None]
    normed, shared, values, code = project(
        info, two_head, input_two, two_tail, gain_a, shift_a, full_shared, full_value, packed
    )
    combined_window, lse, lone = attend(info, shared, values, code, spread)
    combined, out_one, second, d_reduce = join(
        devices, combined_window, input_one, upstream_two, live, second_gather, bias_o, gain_m, shift_m, part, sides
    )
    mixed, d_second, grad_reduce, grad_bias_expand, grad_expand, grad_bias_reduce = mixing(
        devices, second, d_reduce, second_gather, bias_e, bias_r, part
    )
    d_combined, grad_one, result_one, result_two, grad_output, small = turn(
        devices, out_one, d_second, mixed, input_two, upstream_one, combined, live, gain_m, second_gather, grad_bias_reduce, grad_bias_expand,
        sides,
    )
    d_shared, d_values, grad_one, result_one, result_two = attend_back(
        info, shared, values, code, spread, combined_window, d_combined, lse, lone, (grad_one, result_one, result_two)
    )
    grad_two, grad_shared, grad_value, grad_output, grad_reduce, thin, long = tail(
        devices, grad_reduce, grad_output, d_shared, d_values, normed,
        two_head, input_two, two_tail, upstream_two, live, gain_a, full_shared, full_value, small,
    )
    return (
        result_one,
        result_two,
        grad_one,
        grad_two,
        grad_shared,
        grad_value,
        grad_output,
        jnp.concatenate([grad_expand[k * part : (k + 1) * part] for k in range(sides)], axis=1),
        grad_reduce,
        thin[0, :part],
        thin[1, :part],
        thin[2, :part],
        thin[3, :part],
        thin[4, :part],
        long.reshape(-1),
        thin[5, :part],
    )


def solution(mesh):
    rows, flat, whole = P("fsdp", None), P("fsdp"), P()
    return jax.shard_map(
        body,
        mesh=mesh,
        in_specs=(rows,) * 4 + (whole, whole, P("fsdp", None, None)) + (rows,) * 5 + (flat,) * 7,
        out_specs=(rows,) * 9 + (flat,) * 7,
        check_vma=False,
    )
```

```python
import functools
import math

import jax
import jax.numpy as jnp
from jax import lax
from jax.experimental import pallas as pl
from jax.experimental.pallas import tpu as pltpu
from jax.sharding import PartitionSpec as P

HEADS = 8
DH = 128
GROUP = 64
ROUNDS = 4
BUCKETS = 32
EPS_NORM = 1e-05
EPS_UNIT = 1e-06
LOG2E = math.log2(math.e)
SELF2 = -100000.0 * LOG2E
NEG = -1e30
SCALE = 1.0 / math.sqrt(DH)
TILE = 512
HALF = TILE // 2
KEYS = 256
MANY = TILE // KEYS
STEP = 128.0
SHIFT = 1.5 * 2.0**30
TAME = 3000.0
PAIR = 4
FREE = 99.0
STRIP = 512
AFTER = (2, 4, 6, 8)
CURVE = math.sqrt(2.0 / math.pi)
MESH = pl.DeviceIdType.MESH

NT = (((1,), (1,)), ((), ()))
NN = (((1,), (0,)), ((), ()))
TN = (((0,), (0,)), ((), ()))
F32 = jnp.float32
BF16 = jnp.bfloat16


def dot(a, b, dims=NN):
    return lax.dot_general(a, b, dims, preferred_element_type=F32)


def layer_norm(values, gain, shift):
    center = values - jnp.mean(values, axis=-1, keepdims=True)
    spread = jnp.mean(center * center, axis=-1, keepdims=True)
    return center * lax.rsqrt(spread + EPS_NORM) * gain + shift


def prepare(q, code_ref, spread, ask_s, key_s, h, at):
    lane = lax.broadcasted_iota(jnp.int32, (TILE, DH), 1)
    target = ((lane // 64) * 32 + lane % 16).astype(F32)
    wide = q.astype(F32)
    square = jnp.sum(wide * wide, axis=1, keepdims=True)
    code = dot(code_ref[:, at], spread, TN)
    here = code == target
    ask_s[h, at, :DH] = q
    ask_s[h, at, DH:] = jnp.where(here, STEP, 0.0).astype(BF16)
    key_s[h, at, :DH] = (wide * (lax.rsqrt(square + EPS_UNIT) * (SCALE * LOG2E))).astype(BF16)
    key_s[h, at, DH:] = jnp.where(here | (code + 1.0 == target), 1.0, 0.0).astype(BF16)
    return jnp.max(square)


def lowest(info_ref, i):
    start, stop = i * TILE, (i + 1) * TILE
    one = (info_ref[0] < stop) & (info_ref[1] > start)
    two = (info_ref[2] < stop) & (info_ref[3] > start)
    begin = jnp.where(one, info_ref[0], jnp.where(two, info_ref[2], stop))
    return lax.div(begin, KEYS)


def tile_rows(i):
    return pl.ds(pl.multiple_of(i * TILE, TILE), TILE)


def halves(i):
    start = i * TILE
    return [((0, pl.multiple_of(start, HALF), pl.multiple_of(start, HALF)), HALF),
            ((HALF, pl.multiple_of(start + HALF, HALF), pl.multiple_of(start, HALF)), TILE)]


def part_of(both):
    count = (both + SHIFT) - SHIFT
    return count, both - count


def apart(left, right):
    return dot(left[:, DH:], right[:, DH:], NT), dot(left[:, :DH], right[:, :DH], NT)


def attend_kernel(low_ref, q_ref, v_ref, code_ref, spread_ref, comb_ref, lse_ref, lone_ref, ask_s, key_s, more_s, acc_s, top_s):
    rows = q_ref.shape[0]
    tiles = rows // TILE
    heads = [slice(h * DH, (h + 1) * DH) for h in range(PAIR)]

    def ready(i, largest):
        def fill():
            most = jnp.float32(0.0)
            at = tile_rows(i)
            for h, cols in enumerate(heads):
                most = jnp.maximum(most, prepare(q_ref[at, cols], code_ref, spread_ref[:, cols], ask_s, key_s, h, at))
                more_s[h, at, :DH] = v_ref[at, cols]
                more_s[h, at, DH:] = jnp.ones((TILE, DH), BF16)
            return most

        return jnp.maximum(largest, lax.cond(lowest(low_ref, i) <= (i + 1) * MANY - 1, fill, lambda: jnp.float32(0.0)))

    largest = lax.fori_loop(0, tiles, ready, jnp.float32(0.0))
    tame = largest * (SCALE * LOG2E) ** 2 < TAME
    ask_at = lax.broadcasted_iota(jnp.int32, (TILE, TILE), 0)
    key_at = lax.broadcasted_iota(jnp.int32, (TILE, TILE), 1)

    def finish(h, cols, at, top):
        total = acc_s[h, :, DH:]
        some = total > 0.0
        safe = jnp.where(some, total, 1.0)
        inverse = jnp.where(some, 1.0 / safe, 0.0)
        comb_ref[at, cols] = (acc_s[h, :, :DH] * inverse).astype(BF16)
        lse_ref[h, :, at] = (jnp.log2(safe) + top).T[:1]

    def rows_of(i, carry):
        at = tile_rows(i)
        low = lowest(low_ref, i)

        @pl.when((low < (i + 1) * MANY) & tame)
        def _():
            for h in range(PAIR):
                acc_s[h] = jnp.zeros((TILE, 2 * DH), F32)

            def step(j, carry):
                keys = pl.ds(pl.multiple_of(j * KEYS, KEYS), KEYS)
                for h in range(PAIR):
                    count, score = part_of(dot(ask_s[h, at, :], key_s[h, keys, :], NT))
                    acc_s[h] += dot((count * jnp.exp2(score)).astype(BF16), more_s[h, keys, :])
                return carry

            lax.fori_loop(low, i * MANY, step, 0)
            for h, cols in enumerate(heads):
                for asks, span in halves(i):
                    here = pl.ds(asks[0], HALF)
                    there = pl.ds(asks[1], HALF)
                    keys = pl.ds(asks[2], span)
                    key_at = lax.broadcasted_iota(jnp.int32, (HALF, span), 1)
                    ask_at = lax.broadcasted_iota(jnp.int32, (HALF, span), 0) + (span - HALF)
                    count, score = part_of(dot(ask_s[h, there, :], key_s[h, keys, :], NT))
                    prob = jnp.where(key_at < ask_at, count * jnp.exp2(score), 0.0).astype(BF16)
                    acc_s[h, here, :] += dot(prob, more_s[h, keys, :])
                    active = jnp.max(jnp.where(key_at == ask_at, count, 0.0), axis=1, keepdims=True) > 0.0
                    lone = jnp.where(active & (acc_s[h, here, DH:] == 0.0), 1.0, 0.0)
                    acc_s[h, here, :DH] += lone * v_ref[there, cols].astype(F32)
                    acc_s[h, here, DH:] += lone
                    lone_ref[h, :, there] = lone.T[:1]
                finish(h, cols, at, 0.0)

        @pl.when((low < (i + 1) * MANY) & jnp.logical_not(tame))
        def _():
            for h, cols in enumerate(heads):
                count, score = apart(ask_s[h, at, :], key_s[h, at, :])
                score = jnp.where(key_at == ask_at, SELF2, score)
                score = jnp.where((key_at <= ask_at) & (count > 0.5), score, NEG)
                top = jnp.max(score, axis=1, keepdims=True)
                prob = count * jnp.exp2(score - top)
                acc_s[h] = dot(prob.astype(BF16), more_s[h, at, :])
                top_s[h] = jnp.broadcast_to(top, (TILE, DH))

                def step(j, carry):
                    keys = pl.ds(pl.multiple_of(j * KEYS, KEYS), KEYS)
                    count, score = apart(ask_s[h, at, :], key_s[h, keys, :])
                    score = jnp.where(count > 0.5, score, NEG)
                    top = top_s[h]
                    newer = jnp.maximum(top, jnp.max(score, axis=1, keepdims=True))
                    fade = jnp.exp2(top - newer)
                    prob = count * jnp.exp2(score - newer[:, :1])
                    acc_s[h] = acc_s[h] * jnp.concatenate([fade, fade], axis=1) + dot(prob.astype(BF16), more_s[h, keys, :])
                    top_s[h] = newer
                    return carry

                lax.fori_loop(low, i * MANY, step, 0)
                total = acc_s[h, :, DH:]
                own = STEP * ROUNDS * jnp.exp2(SELF2 - jnp.maximum(top_s[h], SELF2))
                lone_ref[h, :, at] = jnp.where(total > 0.0, own / jnp.where(total > 0.0, total, 1.0), 0.0).T[:1]
                finish(h, cols, at, top_s[h])

        @pl.when(low >= (i + 1) * MANY)
        def _():
            comb_ref[at, :] = jnp.zeros((TILE, PAIR * DH), BF16)
            for h in range(PAIR):
                lse_ref[h, :, at] = jnp.zeros((1, TILE), F32)
                lone_ref[h, :, at] = jnp.zeros((1, TILE), F32)

        return carry

    lax.fori_loop(0, tiles, rows_of, 0)


def back_kernel(
    low_ref, q_ref, v_ref, code_ref, spread_ref, comb_ref, above_ref, lse_ref, lone_ref, *rest,
):
    count = (len(rest) - 9) // 2
    sources, (dq_ref, dv_ref, *targets) = rest[:count], rest[count : 2 * count + 2]
    ask_s, key_s, dunit_s, dvalue_s, dask_s, pass_s, sem = rest[2 * count + 2 :]
    rows = q_ref.shape[0]
    tail_step = pl.num_programs(0) - 1

    def copy_in(k):
        return pltpu.make_async_copy(sources[k], pass_s.at[k], sem.at[k])

    def copy_out(k):
        return pltpu.make_async_copy(pass_s.at[k], targets[k], sem.at[count + k])

    @pl.when(pl.program_id(0) == 0)
    def _():
        for k in range(count):
            copy_in(k).start()

    @pl.when(pl.program_id(0) == tail_step)
    def _():
        for k in range(count):
            copy_in(k).wait()
            copy_out(k).start()

    tiles = rows // TILE
    heads = [slice(h * DH, (h + 1) * DH) for h in range(PAIR)]

    def ready(i, largest):
        def fill():
            most = jnp.float32(0.0)
            at = tile_rows(i)
            for h, cols in enumerate(heads):
                most = jnp.maximum(most, prepare(q_ref[at, cols], code_ref, spread_ref[:, cols], ask_s, key_s, h, at))
                for total in (dunit_s, dvalue_s, dask_s):
                    total[h, at, :] = jnp.zeros((TILE, DH), F32)
            return most

        return jnp.maximum(largest, lax.cond(lowest(low_ref, i) <= (i + 1) * MANY - 1, fill, lambda: jnp.float32(0.0)))

    largest = lax.fori_loop(0, tiles, ready, jnp.float32(0.0))
    tame = largest * (SCALE * LOG2E) ** 2 < TAME

    def pass_over(i, low, split):
        at = tile_rows(i)
        deltas = []
        for h, cols in enumerate(heads):
            mixed = above_ref[at, cols].astype(F32) * comb_ref[at, cols].astype(F32)
            deltas.append(jnp.sum(mixed.T, axis=0, keepdims=True))

        def step(j, carry):
            keys = pl.ds(pl.multiple_of(j * KEYS, KEYS), KEYS)
            for h, cols in enumerate(heads):
                q, above, unit = q_ref[at, cols], above_ref[at, cols], key_s[h, keys, :DH]
                count, score = split(key_s[h, keys, :], ask_s[h, at, :])
                d_prob = dot(v_ref[keys, cols], above, NT)
                prob = count * jnp.exp2(score - lse_ref[h, :, at])
                d_score = (prob * (d_prob - carry[h])).astype(BF16)
                dvalue_s[h, keys, :] += dot(prob.astype(BF16), above)
                dunit_s[h, keys, :] += dot(d_score, q)
                dask_s[h, at, :] += dot(d_score, unit, TN)
            return carry

        deltas = lax.fori_loop(low, i * MANY, step, tuple(deltas))
        for h, cols in enumerate(heads):
            for asks, span in halves(i):
                there = pl.ds(asks[1], HALF)
                keys = pl.ds(asks[2], span)
                key_at = lax.broadcasted_iota(jnp.int32, (span, HALF), 0)
                ask_at = lax.broadcasted_iota(jnp.int32, (span, HALF), 1) + (span - HALF)
                q, above, unit = q_ref[there, cols], above_ref[there, cols], key_s[h, keys, :DH]
                count, score = split(key_s[h, keys, :], ask_s[h, there, :])
                d_prob = dot(v_ref[keys, cols], above, NT)
                prob = count * jnp.exp2(score - lse_ref[h, :, there])
                prob = jnp.where(key_at < ask_at, prob, 0.0)
                d_score = (prob * (d_prob - deltas[h][:, asks[0] : asks[0] + HALF])).astype(BF16)
                prob = jnp.where(key_at == ask_at, lone_ref[h, :, there], prob).astype(BF16)
                dvalue_s[h, keys, :] += dot(prob, above)
                dunit_s[h, keys, :] += dot(d_score, q)
                dask_s[h, there, :] += dot(d_score, unit, TN)

    def together(left, right):
        return part_of(dot(left, right, NT))

    def guarded(left, right):
        count, score = apart(left, right)
        return count, jnp.where(count > 0.5, score, NEG)

    def rows_of(i, carry):
        low = lowest(low_ref, i)

        @pl.when((low < (i + 1) * MANY) & tame)
        def _():
            pass_over(i, low, together)

        @pl.when((low < (i + 1) * MANY) & jnp.logical_not(tame))
        def _():
            pass_over(i, low, guarded)

        return carry

    lax.fori_loop(0, tiles, rows_of, 0)

    def close(i, carry):
        at = tile_rows(i)

        @pl.when(lowest(low_ref, i) <= (i + 1) * MANY - 1)
        def _():
            for h, cols in enumerate(heads):
                q = q_ref[at, cols].astype(F32)
                norm = lax.rsqrt(jnp.sum(q * q, axis=1, keepdims=True) + EPS_UNIT)
                d_unit = dunit_s[h, at, :] * SCALE
                along = jnp.sum(q * d_unit, axis=1, keepdims=True)
                d_q = dask_s[h, at, :] * (1.0 / LOG2E) + d_unit * norm - q * (norm * norm * norm * along)
                dq_ref[at, cols] = d_q.astype(BF16)
                dv_ref[at, cols] = dvalue_s[h, at, :].astype(BF16)

        @pl.when(lowest(low_ref, i) > (i + 1) * MANY - 1)
        def _():
            dq_ref[at, :] = jnp.zeros((TILE, PAIR * DH), BF16)
            dv_ref[at, :] = jnp.zeros((TILE, PAIR * DH), BF16)

        return carry

    lax.fori_loop(0, tiles, close, 0)

    @pl.when(pl.program_id(0) == tail_step)
    def _():
        for k in range(count):
            copy_out(k).wait()


def head_specs(rows):
    by_head = pl.BlockSpec((rows, PAIR * DH), lambda h, low: (0, h))
    code = pl.BlockSpec((ROUNDS * HEADS, rows), lambda h, low: (0, 0))
    spread = pl.BlockSpec((ROUNDS * HEADS, PAIR * DH), lambda h, low: (0, h))
    stat = pl.BlockSpec((PAIR, 1, rows), lambda h, low: (h, 0, 0))
    return by_head, code, spread, stat


def attend(low, shared, values, code, spread):
    rows = shared.shape[0]
    by_head, code_spec, spread_spec, stat = head_specs(rows)
    wide = jax.ShapeDtypeStruct((rows, HEADS * DH), BF16)
    thin = jax.ShapeDtypeStruct((HEADS, 1, rows), F32)
    return pl.pallas_call(
        attend_kernel,
        grid_spec=pltpu.PrefetchScalarGridSpec(
            num_scalar_prefetch=1,
            grid=(HEADS // PAIR,),
            in_specs=[by_head, by_head, code_spec, spread_spec],
            out_specs=[by_head, stat, stat],
            scratch_shapes=[pltpu.VMEM((PAIR, rows, 2 * DH), BF16)] * 3
            + [pltpu.VMEM((PAIR, TILE, 2 * DH), F32), pltpu.VMEM((PAIR, TILE, DH), F32)],
        ),
        out_shape=(wide, thin, thin),
        compiler_params=pltpu.CompilerParams(vmem_limit_bytes=57 << 20),
        name="attend",
        cost_estimate=pl.CostEstimate(
            flops=HEADS * 20 * 3 * 2 * TILE * TILE * DH, bytes_accessed=rows * HEADS * DH * 6, transcendentals=HEADS * 20 * TILE * TILE
        ),
    )(low, shared, values, code, spread)


def attend_back(low, shared, values, code, spread, combined, above, lse, lone, sources):
    rows = shared.shape[0]
    by_head, code_spec, spread_spec, stat = head_specs(rows)
    wide = jax.ShapeDtypeStruct((rows, HEADS * DH), BF16)
    return pl.pallas_call(
        back_kernel,
        grid_spec=pltpu.PrefetchScalarGridSpec(
            num_scalar_prefetch=1,
            grid=(HEADS // PAIR,),
            in_specs=[by_head, by_head, code_spec, spread_spec, by_head, by_head, stat, stat]
            + [pl.BlockSpec(memory_space=pl.ANY)] * len(sources),
            out_specs=[by_head, by_head] + [pl.BlockSpec(memory_space=pl.ANY)] * len(sources),
            scratch_shapes=[pltpu.VMEM((PAIR, rows, 2 * DH), BF16)] * 2 + [pltpu.VMEM((PAIR, rows, DH), F32)] * 3
            + [pltpu.VMEM((len(sources),) + sources[0].shape, BF16), pltpu.SemaphoreType.DMA((2 * len(sources),))],
        ),
        out_shape=(wide, wide) + tuple(jax.ShapeDtypeStruct(source.shape, BF16) for source in sources),
        compiler_params=pltpu.CompilerParams(vmem_limit_bytes=57 << 20),
        name="attend_back",
        cost_estimate=pl.CostEstimate(
            flops=HEADS * 20 * 6 * 2 * TILE * TILE * DH, bytes_accessed=rows * HEADS * DH * 12, transcendentals=HEADS * 20 * TILE * TILE
        ),
    )(low, shared, values, code, spread, combined, above, lse, lone, *sources)


def digits(devices):
    side = 2
    while 8 * side * side < devices:
        side += 1
    assert 8 * side * side == devices, devices
    return 4, side, 2


def neighbours(devices):
    outer, side, core = digits(devices)
    me = lax.axis_index("fsdp")
    c = lax.rem(me, core)
    q = lax.rem(lax.div(me, core), side)
    p = lax.rem(lax.div(me, core * side), side)
    o = lax.div(me, core * side * side)

    def at(o_, p_, q_, c_):
        return ((o_ * side + p_) * side + q_) * core + c_

    core_peer = at(o, p, q, 1 - c)
    q_peers = [(k, at(o, p, k, c)) for k in (lax.rem(q + d, side) for d in range(1, side))]
    p_peers = [(k, at(o, k, q, c)) for k in (lax.rem(p + d, side) for d in range(1, side))]
    o_peers = [(k, at(k, p, q, c)) for k in (lax.rem(o + d, outer) for d in range(1, outer))]
    return (o, p, q, c), core_peer, q_peers, p_peers, o_peers


def peers_of(where):
    return [where[1]] + [device for group in where[2:] for _, device in group]


def greet(peers):
    barrier = pltpu.get_barrier_semaphore()
    for peer in peers:
        pl.semaphore_signal(barrier, inc=1, device_id=(peer,), device_id_type=MESH)
    pl.semaphore_wait(barrier, len(peers))


def remote(src, dst, sems, slot, device):
    return pltpu.make_async_remote_copy(
        src_ref=src, dst_ref=dst, send_sem=sems.at[(0,) + slot], recv_sem=sems.at[(1,) + slot],
        device_id=(device,), device_id_type=MESH,
    )


class Scatter:
    def __init__(self, devices, where, slot, boxes, sems, other, mine, load=None):
        self.outer, self.side, _ = digits(devices)
        (self.o, self.p, self.q, self.c), self.core_peer, self.q_peers, self.p_peers, self.o_peers = where
        self.slot = slot
        self.box_c, box_a0, box_a1, self.box_b, self.box_o = boxes
        self.box_a = (box_a0, box_a1)
        self.sem_c, self.sem_a, self.sem_b, self.sem_o = sems
        self.other, self.mine, self.load = other, mine, load
        half = self.box_o.shape[-1] // 2
        self.columns = (pl.ds(0, half), pl.ds(half, half))

    def core(self):
        return remote(self.other(), self.box_c, self.sem_c, (self.slot,), self.core_peer)

    def first(self, h, d):
        k, device = (self.q_peers, self.p_peers)[h][d]
        spot = (slice(None), slice(None), k) if h == 0 else (slice(None), k, slice(None))
        return remote(self.mine(spot, self.columns[h]), self.box_a[h].at[d], self.sem_a, (self.slot, h, d), device)

    def second(self, h, d):
        k, device = (self.p_peers, self.q_peers)[h][d]
        return remote(
            self.box_a[h].at[0, :, k], self.box_b.at[d, :, :, self.columns[h]], self.sem_b, (self.slot, h, d), device
        )

    def third(self, d):
        k, device = self.o_peers[d]
        return remote(self.box_b.at[0, k], self.box_o.at[d], self.sem_o, (self.slot, d), device)

    def begin(self):
        self.core().start()
        if self.load is not None:
            self.load().start()

    def stage_core(self):
        if self.load is not None:
            self.load().wait()
        self.core().wait_recv()
        side = self.side

        def add(i, carry):
            spot = (lax.div(i, side * side), lax.rem(lax.div(i, side), side), lax.rem(i, side))
            ref = self.mine(spot, slice(None))
            ref[...] = ref[...] + self.box_c[spot]
            return carry

        lax.fori_loop(0, self.outer * side * side, add, 0)
        for h in range(2):
            for d in range(side - 1):
                self.first(h, d).start()

    def stage_first(self):
        side = self.side
        for h in range(2):
            box = self.box_a[h]
            for d in range(side - 1):
                self.first(h, d).wait_recv()

            def add(i, carry):
                a, b = lax.div(i, side), lax.rem(i, side)
                total = self.mine((a, b, self.q) if h == 0 else (a, self.p, b), self.columns[h])[...]
                for d in range(side - 1):
                    total = total + box[d, a, b]
                box[0, a, b] = total
                return carry

            lax.fori_loop(0, self.outer * side, add, 0)
            for d in range(side - 1):
                self.second(h, d).start()

    def stage_second(self):
        box = self.box_b
        for h in range(2):
            k = self.p if h == 0 else self.q
            for d in range(self.side - 1):
                self.second(h, d).wait_recv()

            def add(a, carry):
                total = self.box_a[h][0, a, k]
                for d in range(self.side - 1):
                    total = total + box[d, a, :, self.columns[h]]
                box[0, a, :, self.columns[h]] = total
                return carry

            lax.fori_loop(0, self.outer, add, 0)
        for d in range(self.outer - 1):
            self.third(d).start()

    def stage_third(self):
        total = self.box_b[0, self.o].astype(F32)
        for d in range(self.outer - 1):
            self.third(d).wait_recv()
            total = total + self.box_o[d].astype(F32)
        return total

    def sent_first(self):
        self.core().wait_send()
        for h in range(2):
            for d in range(self.side - 1):
                self.first(h, d).wait_send()

    def sent_last(self):
        for h in range(2):
            for d in range(self.side - 1):
                self.second(h, d).wait_send()
        for d in range(self.outer - 1):
            self.third(d).wait_send()


def boxes_for(devices, rows, width):
    outer, side, _ = digits(devices)
    half = width // 2
    return [
        pltpu.VMEM((outer, side, side, rows, width), BF16),
        pltpu.VMEM((side - 1, outer, side, rows, half), BF16),
        pltpu.VMEM((side - 1, outer, side, rows, half), BF16),
        pltpu.VMEM((side - 1, outer, rows, width), BF16),
        pltpu.VMEM((outer - 1, rows, width), BF16),
    ]


def sems_for(devices, count):
    outer, side, _ = digits(devices)
    dma = pltpu.SemaphoreType.DMA
    return [dma((2, count)), dma((2, count, 2, side - 1)), dma((2, count, 2, side - 1)), dma((2, count, outer - 1))]


def mixing_kernel(
    devices, second_ref, above_ref, expand_ref, reduce_ref, bias_e_ref, bias_r_ref,
    out_ref, back_ref, grad_r_ref, grad_b_ref, grad_e_ref, above_b_ref, act_s, pre_s, grad_s, *rest,
):
    step = pl.program_id(0)
    rows, width = second_ref.shape
    strip = act_s.shape[1]
    per = width // strip
    slices = (len(rest) - 4) // 5
    sems = rest[5 * slices :]
    where = neighbours(devices)
    (o, p, q, c), core_peer, q_peers, p_peers, o_peers = where
    part = grad_s.shape[-2]

    def mover(k):
        def other():
            return grad_s.at[k % 2, :, :, :, 1 - c]

        def mine(spot, cols):
            return grad_s.at[(k % 2,) + tuple(spot) + (c, slice(None), cols)]

        return Scatter(devices, where, k, rest[5 * k : 5 * k + 5], sems, other, mine)

    movers = [mover(k) for k in range(slices)]
    w_e = expand_ref[...].reshape(width, strip)
    w_r = reduce_ref[...].reshape(strip, width)

    @pl.when(step == 0)
    def _():
        greet(peers_of(where))
        out_ref[...] = jnp.broadcast_to(bias_r_ref[...], out_ref.shape)
        back_ref[...] = jnp.zeros(back_ref.shape, F32)
        above_b_ref[...] = jnp.sum(above_ref[...].astype(F32), axis=0, keepdims=True)

    def close(k):
        grad_e_ref[k * part : (k + 1) * part, :] = movers[k].stage_third()

    final = slices * per - 1
    timed, late = [], []
    for k in range(slices):
        begun = 2 * ((k + 1) * per - 1) + 1
        for after, action in zip(
            AFTER, (movers[k].stage_core, movers[k].stage_first, movers[k].stage_second, functools.partial(close, k))
        ):
            if begun + after > 2 * final + 1:
                late.append((begun + after, -k, action))
            else:
                timed.append((begun + after, action))

    def stages(point):
        for when, action in timed:
            if when % 2 == point:
                pl.when(step == when // 2)(action)

    pre = dot(second_ref[...], w_e) + bias_e_ref[...]
    square = pre * pre
    curve = jnp.tanh(CURVE * pre * (1.0 + 0.044715 * square))
    hinge = 0.5 * (1.0 + curve)
    act_s[...] = (pre * hinge).astype(BF16)
    slope = hinge + 0.5 * pre * (1.0 - curve * curve) * (CURVE * (1.0 + 3 * 0.044715 * square))
    d_pre = (dot(above_ref[...], w_r, NT) * slope).astype(BF16)
    pre_s[...] = d_pre
    grad_b_ref[...] = jnp.sum(d_pre.astype(F32), axis=0, keepdims=True)
    stages(0)
    out_ref[...] += dot(act_s[...], w_r)
    back_ref[...] += dot(d_pre, w_e, NT)
    grad_r_ref[...] = dot(act_s[...], above_ref[...], TN).astype(BF16).reshape(grad_r_ref.shape)
    grad_e = dot(second_ref[...], pre_s[...], TN).astype(BF16)
    for k in range(slices):
        for j in range(per):
            @pl.when(step == k * per + j)
            def _():
                if j == 0 and k >= 2:
                    movers[k - 2].sent_first()
                grad_s[k % 2, :, :, :, :, :, j * strip : (j + 1) * strip] = grad_e.reshape(grad_s.shape[1:-1] + (strip,))
                if j == per - 1:
                    movers[k].begin()

    stages(1)

    @pl.when(step == final)
    def _():
        for *_, action in sorted(late, key=lambda entry: entry[:2]):
            action()
        for k in range(max(0, slices - 2), slices):
            movers[k].sent_first()
        for k in range(slices):
            movers[k].sent_last()


def mixing(devices, second, above, gathered, bias_e, bias_r, part):
    rows, width = second.shape
    hidden = bias_e.shape[1]
    many = hidden // devices
    sides = hidden // width
    strip = STRIP
    per = width // strip
    outer, side, core = digits(devices)
    fixed = pl.BlockSpec((rows, width), lambda i: (0, 0), pipeline_mode=pl.Buffered(1))
    whole = pl.BlockSpec(memory_space=pltpu.VMEM)
    scratch = [pltpu.VMEM((rows, strip), BF16)] * 2 + [pltpu.VMEM((2, outer, side, side, core, part, width), BF16)]
    for k in range(sides):
        scratch += boxes_for(devices, part, width)
    return pl.pallas_call(
        functools.partial(mixing_kernel, devices),
        grid=(hidden // strip,),
        in_specs=[
            fixed, fixed,
            pl.BlockSpec((devices, part, strip), lambda i: (0, many // part + 1 + i // per, i % per)),
            pl.BlockSpec((strip // many, many, width), lambda i: (i, 0, 0)),
            pl.BlockSpec((1, strip), lambda i: (0, i)),
            pl.BlockSpec((1, width), lambda i: (0, 0)),
        ],
        out_specs=[
            fixed,
            fixed,
            pl.BlockSpec((strip // many, many, width), lambda i: (i, 0, 0)),
            pl.BlockSpec((1, strip), lambda i: (0, i)),
            pl.BlockSpec((sides * part, width), lambda i: (0, 0)),
            pl.BlockSpec((1, width), lambda i: (0, 0)),
        ],
        out_shape=[
            jax.ShapeDtypeStruct((rows, width), F32),
            jax.ShapeDtypeStruct((rows, width), F32),
            jax.ShapeDtypeStruct((devices, many, width), BF16),
            jax.ShapeDtypeStruct((1, hidden), F32),
            jax.ShapeDtypeStruct((sides * part, width), F32),
            jax.ShapeDtypeStruct((1, width), F32),
        ],
        scratch_shapes=scratch + sems_for(devices, sides),
        compiler_params=pltpu.CompilerParams(collective_id=3, has_side_effects=True, vmem_limit_bytes=57 << 20),
        name="mixing",
    )(second, above, gathered, gathered, bias_e, bias_r)


def join_kernel(
    devices, window_ref, first_ref, final_ref, one_ref, above_ref, live_ref, w_ref, bias_ref, gain_ref, shift_ref,
    combined_ref, out_ref, second_ref, reduce_ref, side_in, part_s, halo_sem,
):
    slots, width = one_ref.shape
    half = slots // 2
    tile = 256
    me = lax.axis_index("fsdp")
    last = devices - 1
    left, right = lax.rem(me + last, devices), lax.rem(me + 1, devices)
    greet([left, right])

    def to_left():
        return remote(window_ref.at[:half], side_in.at[1], halo_sem, (0,), left)

    def to_right():
        return remote(window_ref.at[half + slots :], side_in.at[0], halo_sem, (1,), right)

    @pl.when(me > 0)
    def _():
        to_left().start()

    @pl.when(me < last)
    def _():
        to_right().start()

    @pl.when(me == 0)
    def _():
        side_in[0] = jnp.zeros((half, width), BF16)

    @pl.when(me == last)
    def _():
        side_in[1] = jnp.zeros((half, width), BF16)

    w_o = w_ref[...].reshape(width, width)

    owns = (first_ref, final_ref)

    def before(side, i, carry):
        here = pl.ds(pl.multiple_of(i * tile, tile), tile)
        at = pl.ds(pl.multiple_of(side * half + i * tile, tile), tile)
        part_s[at, :] = dot(owns[side][here, :], w_o)
        reduce_ref[at, :] = (live_ref[at, :] * above_ref[at, :].astype(F32)).astype(BF16)
        return carry

    for side in range(2):
        lax.fori_loop(0, half // tile, functools.partial(before, side), 0)

    def after(side, i, carry):
        here = pl.ds(pl.multiple_of(i * tile, tile), tile)
        at = pl.ds(pl.multiple_of(side * half + i * tile, tile), tile)
        other = side_in[side, here, :]
        combined_ref[at, :] = owns[side][here, :] + other
        attended = part_s[at, :] + dot(other, w_o) + bias_ref[...]
        out = one_ref[at, :].astype(F32) + live_ref[at, :] * attended
        out_ref[at, :] = out
        second_ref[at, :] = layer_norm(out, gain_ref[...], shift_ref[...]).astype(BF16)
        return carry

    @pl.when(me > 0)
    def _():
        to_right().wait_recv()

    lax.fori_loop(0, half // tile, functools.partial(after, 0), 0)

    @pl.when(me < last)
    def _():
        to_left().wait_recv()

    lax.fori_loop(0, half // tile, functools.partial(after, 1), 0)

    @pl.when(me > 0)
    def _():
        to_left().wait_send()

    @pl.when(me < last)
    def _():
        to_right().wait_send()


def join(devices, window, one, above, live, gathered, bias, gain, shift, part, sides):
    slots, width = one.shape
    dma = pltpu.SemaphoreType.DMA
    rows = pl.BlockSpec((slots, width), lambda i: (0, 0))
    thin = pl.BlockSpec((1, width), lambda i: (0, 0))
    low = jax.ShapeDtypeStruct((slots, width), BF16)
    return pl.pallas_call(
        functools.partial(join_kernel, devices),
        grid=(1,),
        in_specs=[
            pl.BlockSpec(memory_space=pl.ANY),
            pl.BlockSpec((slots // 2, width), lambda i: (1, 0)), pl.BlockSpec((slots // 2, width), lambda i: (2, 0)), rows, rows, pl.BlockSpec((slots, 1), lambda i: (0, 0)),
            pl.BlockSpec((devices, part, width), lambda i: (0, sides, 0)), thin, thin, thin,
        ],
        out_specs=[rows] * 4,
        out_shape=[low, jax.ShapeDtypeStruct((slots, width), F32), low, low],
        scratch_shapes=[pltpu.VMEM((2, slots // 2, width), BF16), pltpu.VMEM((slots, width), F32), dma((2, 2))],
        compiler_params=pltpu.CompilerParams(collective_id=6, has_side_effects=True, vmem_limit_bytes=57 << 20),
        name="join",
    )(window, window, window, one, above, live, gathered, bias, gain, shift)


def turn_kernel(
    devices, out_one_ref, d_second_ref, mixed_ref, two_ref, above_ref, combined_ref, live_ref, gain_ref, w_o_ref,
    bias_r_ref, bias_e_ref,
    wide_ref, grad_one_out, one_out, res_two_out, grad_o_out, small_ref,
    mixed_s, two_s, combined_s, one_s, res_two_s, grad_o_s, attend_s, halo_sem, load_sem, store_sem,
):
    slots, width = two_ref.shape
    half = slots // 2
    tile = 256
    part = grad_o_out.shape[1]
    w_o = w_o_ref[...].reshape(width, width)
    me = lax.axis_index("fsdp")
    last = devices - 1
    left, right = lax.rem(me + last, devices), lax.rem(me + 1, devices)
    loads = [
        pltpu.make_async_copy(source, target, load_sem.at[k])
        for k, (source, target) in enumerate(((mixed_ref, mixed_s), (two_ref, two_s), (combined_ref, combined_s)))
    ]
    stores = [
        pltpu.make_async_copy(source, target, store_sem.at[k])
        for k, (source, target) in enumerate(
            ((attend_s, grad_one_out), (one_s, one_out), (res_two_s, res_two_out), (grad_o_s, grad_o_out))
        )
    ]
    for load in loads:
        load.start()
    greet([left, right])

    def to_left():
        return remote(wide_ref.at[half : 2 * half], wide_ref.at[half + slots :], halo_sem, (0,), left)

    def to_right():
        return remote(wide_ref.at[2 * half : 3 * half], wide_ref.at[:half], halo_sem, (1,), right)

    small_ref[...] = jnp.zeros(small_ref.shape, F32)
    gain = gain_ref[...]

    def norm_tile(i, carry):
        at = pl.ds(pl.multiple_of(i * tile, tile), tile)
        live = live_ref[at, :]
        values = out_one_ref[at, :]
        above = d_second_ref[at, :]
        center = values - jnp.mean(values, axis=1, keepdims=True)
        scale = lax.rsqrt(jnp.mean(center * center, axis=1, keepdims=True) + EPS_NORM)
        center = center * scale
        small_ref[2:3, :] += jnp.sum(above * center, axis=0, keepdims=True)
        small_ref[3:4, :] += jnp.sum(above, axis=0, keepdims=True)
        above = above * gain
        mean = jnp.mean(above, axis=1, keepdims=True)
        along = jnp.mean(above * center, axis=1, keepdims=True)
        total = live * (above_ref[at, :].astype(F32) + scale * (above - mean - center * along))
        low = total.astype(BF16)
        attend_s[at, :] = low
        small_ref[4:5, :] += jnp.sum(low.astype(F32), axis=0, keepdims=True)
        wide_ref[pl.ds(pl.multiple_of(half + i * tile, tile), tile), :] = dot(low, w_o, NT).astype(BF16)
        return carry

    lax.fori_loop(0, half // tile, norm_tile, 0)

    @pl.when(me > 0)
    def _():
        to_left().start()

    lax.fori_loop(half // tile, slots // tile, norm_tile, 0)

    @pl.when(me < last)
    def _():
        to_right().start()

    stores[0].start()
    for load in loads:
        load.wait()

    def finish_tile(i, carry):
        at = pl.ds(pl.multiple_of(i * tile, tile), tile)
        live = live_ref[at, :]
        one_s[at, :] = (live * out_one_ref[at, :]).astype(BF16)
        res_two_s[at, :] = (live * (two_s[at, :].astype(F32) + mixed_s[at, :])).astype(BF16)
        return carry

    lax.fori_loop(0, slots // tile, finish_tile, 0)
    stores[1].start()
    stores[2].start()

    def weights(i, carry):
        cols = pl.ds(pl.multiple_of(i * tile, tile), tile)
        many = tile // part
        grad_o_s[pl.ds(pl.multiple_of(i * many, many), many)] = (
            dot(combined_s[:, cols], attend_s[...], TN).astype(BF16).reshape(many, part, width)
        )
        return carry

    lax.fori_loop(0, width // tile, weights, 0)
    stores[3].start()
    small_ref[5:6, :] = bias_r_ref[...]
    for k in range(bias_e_ref.shape[1] // width):
        small_ref[6 + k : 7 + k, :] = bias_e_ref[:, k * width : (k + 1) * width]

    @pl.when(me > 0)
    def _():
        to_right().wait_recv()
        to_left().wait_send()

    @pl.when(me == 0)
    def _():
        wide_ref[:half] = jnp.zeros((half, width), BF16)

    @pl.when(me < last)
    def _():
        to_left().wait_recv()
        to_right().wait_send()

    @pl.when(me == last)
    def _():
        wide_ref[half + slots :] = jnp.zeros((half, width), BF16)

    for store in stores:
        store.wait()


def turn(devices, out_one, d_second, mixed, two, above, combined, live, gain, gathered, bias_r, bias_e, sides):
    slots, width = two.shape
    part = width // devices
    vmem = pl.BlockSpec(memory_space=pltpu.VMEM)
    anywhere = pl.BlockSpec(memory_space=pl.ANY)
    dma = pltpu.SemaphoreType.DMA
    low = pltpu.VMEM((slots, width), BF16)
    rows_low = jax.ShapeDtypeStruct((slots, width), BF16)
    return pl.pallas_call(
        functools.partial(turn_kernel, devices),
        grid=(1,),
        in_specs=[vmem, vmem, anywhere, anywhere, vmem, anywhere, vmem, vmem]
        + [pl.BlockSpec((devices, part, width), lambda i: (0, sides, 0)), vmem, vmem],
        out_specs=(vmem,) + (anywhere,) * 4 + (vmem,),
        out_shape=(
            jax.ShapeDtypeStruct((2 * slots, width), BF16), rows_low, rows_low, rows_low,
            jax.ShapeDtypeStruct((devices, part, width), BF16),
            jax.ShapeDtypeStruct((16, width), F32),
        ),
        scratch_shapes=[
            pltpu.VMEM((slots, width), F32), low, low, low, low, pltpu.VMEM((devices, part, width), BF16), low,
            dma((2, 2)), dma((3,)), dma((4,)),
        ],
        compiler_params=pltpu.CompilerParams(collective_id=5, has_side_effects=True, vmem_limit_bytes=57 << 20),
        name="turn",
    )(out_one, d_second, mixed, two, above, combined, live, gain, gathered, bias_r, bias_e)


def tail_kernel(
    devices, grad_r_ref, grad_o_ref, d_shared_ref, d_value_ref, normed_in, head_ref, own_in, end_ref, above_in, live_ref,
    gain_ref, w_s_ref, w_v_ref, small_ref,
    back_ref, out_s_ref, out_v_ref, out_o_ref, out_r_ref, thin_ref, long_ref,
    normed_ref, own_ref, above_ref, late_sem, side_s, side_in, vector_s, vector_in, grad_s, load_sem, halo_sem, vector_sem, *rest,
):
    window, width = normed_ref.shape
    slots = own_ref.shape[0]
    half = slots // 2
    part = out_s_ref.shape[0]
    many = out_r_ref.shape[0]
    tile = 256
    where = neighbours(devices)
    (o, p, q, c), core_peer, q_peers, p_peers, o_peers = where
    me = lax.axis_index("fsdp")
    outer, side, core = digits(devices)
    owns, rest = rest[:5], rest[5:]
    sems = rest[-4:]

    def distant(source, row, rows, k):
        at = pl.ds(row, rows)

        def other():
            return source.at[:, :, :, 1 - c, at, :]

        def mine(spot, cols):
            return owns[k].at[tuple(spot) + (slice(None), cols)]

        def load():
            return pltpu.make_async_copy(source.at[:, :, :, c, at, :], owns[k], load_sem.at[k])

        return Scatter(devices, where, k, rest[5 * k : 5 * k + 5], sems, other, mine, load)

    def near(j, k):
        def other():
            return grad_s.at[j, :, :, :, 1 - c]

        def mine(spot, cols):
            return grad_s.at[(j,) + tuple(spot) + (c, slice(None), cols)]

        return Scatter(devices, where, k, rest[5 * k : 5 * k + 5], sems, other, mine)

    quarter = many // 4
    movers = [distant(grad_r_ref, k * quarter, quarter, k) for k in range(4)]
    movers += [distant(grad_o_ref, 0, part, 4), near(0, 5), near(1, 6)]

    def third(k):
        total = movers[k].stage_third()
        if k < 4:
            out_r_ref[k * quarter : (k + 1) * quarter, :] = total
        else:
            (out_o_ref, out_s_ref, out_v_ref)[k - 4][...] = total

    def tick(t):
        if t < 7:
            movers[t].stage_core()
        if 0 <= t - 1 < 7:
            movers[t - 1].stage_first()
        if 0 <= t - 2 < 7:
            movers[t - 2].stage_second()
        if 0 <= t - 3 < 7:
            third(t - 3)

    last = devices - 1
    left, right = lax.rem(me + last, devices), lax.rem(me + 1, devices)
    late = [
        pltpu.make_async_copy(source, target, late_sem.at[k])
        for k, (source, target) in enumerate(((normed_in, normed_ref), (own_in, own_ref), (above_in, above_ref)))
    ]
    for load in late:
        load.start()
    greet(peers_of(where) + [left, right])
    for k in range(5):
        movers[k].begin()

    def to_left():
        return remote(side_s.at[0], side_in.at[1], halo_sem, (0,), left)

    def to_right():
        return remote(side_s.at[1], side_in.at[0], halo_sem, (1,), right)

    vector_s[...] = small_ref[...]
    gain = gain_ref[...]

    def norm_tile(ref, row, at):
        values = ref[pl.ds(row, tile), :].astype(F32)
        above = dot(d_shared_ref[at, :], w_s_ref[...], NT) + dot(d_value_ref[at, :], w_v_ref[...], NT)
        center = values - jnp.mean(values, axis=1, keepdims=True)
        scale = lax.rsqrt(jnp.mean(center * center, axis=1, keepdims=True) + EPS_NORM)
        center = center * scale
        vector_s[0:1, :] += jnp.sum(above * center, axis=0, keepdims=True)
        vector_s[1:2, :] += jnp.sum(above, axis=0, keepdims=True)
        above = above * gain
        mean = jnp.mean(above, axis=1, keepdims=True)
        along = jnp.mean(above * center, axis=1, keepdims=True)
        return scale * (above - mean - center * along)

    def side_tiles(i, carry):
        row = pl.multiple_of(i * tile, tile)
        side_s[0, pl.ds(row, tile), :] = norm_tile(head_ref, row, pl.ds(row, tile)).astype(BF16)
        at = pl.ds(pl.multiple_of(half + slots + i * tile, tile), tile)
        side_s[1, pl.ds(row, tile), :] = norm_tile(end_ref, row, at).astype(BF16)
        return carry

    tick(0)
    lax.fori_loop(0, half // tile, side_tiles, 0)

    @pl.when(me > 0)
    def _():
        to_left().start()

    @pl.when(me < last)
    def _():
        to_right().start()

    tick(1)
    tick(2)

    def weights(j, ref):
        wide = tile // part

        def strip(i, carry):
            cols = pl.ds(pl.multiple_of(i * tile, tile), tile)
            block = dot(normed_ref[:, cols], ref[...], TN).astype(BF16).reshape(wide // core, core, part, width)
            for k in range(wide // core):
                index = i * (wide // core) + k
                spot = (lax.div(index, side * side), lax.rem(lax.div(index, side), side), lax.rem(index, side))
                grad_s[(j,) + spot] = block[k]
            return carry

        lax.fori_loop(0, width // tile, strip, 0)

    for load in late:
        load.wait()
    weights(0, d_shared_ref)
    movers[5].begin()
    tick(3)
    tick(4)
    weights(1, d_value_ref)
    movers[6].begin()
    tick(5)

    def own_tiles(i, carry):
        row = pl.multiple_of(i * tile, tile)
        at = pl.ds(pl.multiple_of(half + i * tile, tile), tile)
        here = pl.ds(row, tile)
        total = above_ref[here, :].astype(F32) + norm_tile(own_ref, row, at)
        back_ref[here, :] = (live_ref[here, :] * total).astype(BF16)
        return carry

    lax.fori_loop(0, slots // tile, own_tiles, 0)

    def vector_copies(stage):
        group = ([(0, core_peer)], q_peers, p_peers, o_peers)[stage]
        base = (0, 1, side, 2 * side - 1)[stage]
        return [
            remote(vector_s if stage == 0 else vector_in.at[base - 1], vector_in.at[base + d], vector_sem, (base + d,), device)
            for d, (_, device) in enumerate(group)
        ]

    def vector_stage(stage):
        base = (0, 1, side, 2 * side - 1)[stage]
        copies = vector_copies(stage)
        total = vector_s[...] if stage == 0 else vector_in[base - 1]
        for d, copy in enumerate(copies):
            copy.wait_recv()
            total = total + vector_in[base + d]
        vector_in[base + len(copies) - 1] = total

    for copy in vector_copies(0):
        copy.start()
    for stage in range(3):
        tick(6 + stage)
        vector_stage(stage)
        for copy in vector_copies(stage + 1):
            copy.start()

    @pl.when(me > 0)
    def _():
        to_right().wait_recv()

    @pl.when(me == 0)
    def _():
        side_in[0] = jnp.zeros((half, width), BF16)

    @pl.when(me < last)
    def _():
        to_left().wait_recv()

    @pl.when(me == last)
    def _():
        side_in[1] = jnp.zeros((half, width), BF16)

    for k in range(2):
        at = slice(k * half, (k + 1) * half)
        back_ref[at, :] = (back_ref[at, :].astype(F32) + side_in[k].astype(F32)).astype(BF16)
    vector_stage(3)
    tick(9)
    vectors = 2 * side + outer - 3
    total = vector_in[vectors]
    thin_ref[...] = pltpu.roll(total, lax.rem(width - me * part, width), 1)[:, :DH]
    each = long_ref.shape[1]
    long_rows = [total[6 + k : 7 + k, :] for k in range(devices * each // width)]
    mine = lax.div(me * each, width)
    chosen = long_rows[0]
    for k in range(1, len(long_rows)):
        chosen = jnp.where(mine == k, long_rows[k], chosen)
    long_ref[...] = pltpu.roll(chosen, lax.rem(width - lax.rem(me * each, width), width), 1)[:, :each]
    for stage in range(4):
        for copy in vector_copies(stage):
            copy.wait_send()

    @pl.when(me > 0)
    def _():
        to_left().wait_send()

    @pl.when(me < last)
    def _():
        to_right().wait_send()

    for mover in movers:
        mover.sent_first()
        mover.sent_last()


def tail(devices, grad_r, grad_o, d_shared, d_values, normed, head, own, end, above, live, gain, w_s, w_v, small):
    window, width = normed.shape
    slots = own.shape[0]
    outer, side, core = digits(devices)
    part, many = grad_o.shape[1], grad_r.shape[1]
    each = many
    vmem = pl.BlockSpec(memory_space=pltpu.VMEM)
    anywhere = pl.BlockSpec(memory_space=pl.ANY)
    dma = pltpu.SemaphoreType.DMA
    sizes = [many // 4] * 4 + [part] * 3
    scratch = [
        pltpu.VMEM((window, width), BF16), pltpu.VMEM((slots, width), BF16), pltpu.VMEM((slots, width), BF16), dma((3,)),
        pltpu.VMEM((2, slots // 2, width), BF16), pltpu.VMEM((2, slots // 2, width), BF16),
        pltpu.VMEM((16, width), F32), pltpu.VMEM((2 * side + outer - 2, 16, width), F32),
        pltpu.VMEM((2, outer, side, side, core, part, width), BF16),
        dma((5,)), dma((2, 2)), dma((2, 2 * side + outer - 2)),
    ]
    scratch += [pltpu.VMEM((outer, side, side, rows, width), BF16) for rows in sizes[:5]]
    for rows in sizes:
        scratch += boxes_for(devices, rows, width)
    shape = (outer, side, side, core)
    return pl.pallas_call(
        functools.partial(tail_kernel, devices),
        in_specs=[anywhere, anywhere, vmem, vmem, anywhere, vmem, anywhere, vmem, anywhere] + [vmem] * 5,
        out_specs=(vmem,) * 7,
        out_shape=(
            jax.ShapeDtypeStruct((slots, width), BF16),
            jax.ShapeDtypeStruct((part, width), F32),
            jax.ShapeDtypeStruct((part, width), F32),
            jax.ShapeDtypeStruct((part, width), F32),
            jax.ShapeDtypeStruct((many, width), F32),
            jax.ShapeDtypeStruct((16, DH), F32),
            jax.ShapeDtypeStruct((1, each), F32),
        ),
        scratch_shapes=scratch + sems_for(devices, len(sizes)),
        compiler_params=pltpu.CompilerParams(collective_id=4, has_side_effects=True, vmem_limit_bytes=57 << 20),
        name="tail",
    )(
        grad_r.reshape(shape + grad_r.shape[1:]), grad_o.reshape(shape + grad_o.shape[1:]),
        d_shared, d_values, normed, head, own, end, above, live, gain, w_s, w_v, small,
    )


def find_ranks(length_ref, target_ref, bucket_ref, packed_ref, info_ref, before_s):
    devices = length_ref.shape[0]
    lists, slots = bucket_ref.shape
    me = lax.axis_index("fsdp")
    base = me * slots
    window = 2 * slots

    def look(s, carry):
        start, mine, found, one, two = carry
        size = length_ref[s]
        target = target_ref[s]
        middle = start + lax.shift_right_logical(size, 1)
        inside = (middle >= base) & (middle < base + slots)
        offset = start - base + slots // 2
        entry = (offset, offset + size, target)
        first, second = inside & (found == 0), inside & (found == 1)
        one = tuple(jnp.where(first, new, old) for new, old in zip(entry, one))
        two = tuple(jnp.where(second, new, old) for new, old in zip(entry, two))
        return start + size, jnp.where(target == me, size, mine), found + inside.astype(jnp.int32), one, two

    zero = jnp.int32(0)
    nothing = (jnp.int32(window), jnp.int32(window), zero)
    total, mine, found, one, two = lax.fori_loop(0, devices, look, (zero, zero, zero, nothing, nothing))
    for k, value in enumerate((one[0], one[1], two[0], two[1], one[2], two[2], total, found)):
        info_ref[k] = value

    def fill(i, carry):
        at = pl.ds(pl.multiple_of(i * DH, DH), DH)
        first = lax.broadcasted_iota(jnp.int32, (DH, slots), 0) + i * DH
        second = lax.broadcasted_iota(jnp.int32, (DH, slots), 1)
        before_s[at, :] = jnp.where(first < second, 1.0, 0.0).astype(BF16)
        return carry

    lax.fori_loop(0, slots // DH, fill, 0)
    left = lax.broadcasted_iota(jnp.int32, (DH, DH), 0)
    right = lax.broadcasted_iota(jnp.int32, (DH, DH), 1)
    smaller = jnp.where((left // BUCKETS == right // BUCKETS) & (right < left), 1.0, 0.0).astype(BF16)
    many = DH // BUCKETS
    bucket = lax.broadcasted_iota(jnp.int32, (many, BUCKETS, slots), 1)
    live = lax.broadcasted_iota(jnp.int32, (many, BUCKETS, slots), 2) < mine
    ranks = []
    for g in range(lists // many):
        here = (jnp.broadcast_to(bucket_ref[g * many : (g + 1) * many, :][:, None, :], bucket.shape) == bucket) & live
        one_hot = jnp.where(here, 1.0, 0.0)
        flat = one_hot.reshape(DH, slots).astype(BF16)
        offset = jnp.sum(dot(smaller, flat), axis=1, keepdims=True)
        place = (dot(flat, before_s[...]) + offset).reshape(many, BUCKETS, slots)
        ranks.append(jnp.sum(one_hot * place, axis=1))
    rank = jnp.concatenate(ranks, axis=0)
    live = lax.broadcasted_iota(jnp.int32, (lists, slots), 1) < mine
    packed_ref[:lists, :] = jnp.where(live, jnp.floor(rank * (1.0 / GROUP)), FREE).astype(BF16)


def project_kernel(
    info_ref, head_ref, own_ref, tail_ref, gain_ref, shift_ref, w_s_ref, w_v_ref, one_ref, two_ref,
    normed_ref, shared_ref, value_ref, code_ref,
):
    i = pl.program_id(0)
    tile = own_ref.shape[0]
    steps = pl.num_programs(0)

    def go(ref):
        normed = layer_norm(ref[...].astype(F32), gain_ref[...], shift_ref[...]).astype(BF16)
        normed_ref[...] = normed
        shared_ref[...] = dot(normed, w_s_ref[...]).astype(BF16)
        value_ref[...] = dot(normed, w_v_ref[...]).astype(BF16)

    @pl.when(i < steps // 4)
    def _():
        go(head_ref)

    @pl.when((i >= steps // 4) & (i < steps - steps // 4))
    def _():
        go(own_ref)

    @pl.when(i >= steps - steps // 4)
    def _():
        go(tail_ref)

    @pl.when(i == 0)
    def _():
        lists, window = code_ref.shape
        lane = lax.broadcasted_iota(jnp.int32, (lists, window), 1)
        code = jnp.full((lists, window), FREE, F32)
        for k, ref in enumerate((one_ref, two_ref)):
            begin, end = info_ref[2 * k], info_ref[2 * k + 1]
            rows = ref[0].astype(F32)
            moved = pltpu.roll(jnp.concatenate([rows, rows], axis=1), lax.rem(begin, window), 1)
            code = jnp.where((lane >= begin) & (lane < end), moved + 32.0 * k, code)
        code_ref[...] = code.astype(BF16)


def project(info, head, own, tail, gain, shift, w_s, w_v, blocks):
    slots, width = own.shape
    window = 2 * slots
    lists = ROUNDS * HEADS
    tile = 512
    steps = window // tile
    quarter = steps // 4
    rows = pl.BlockSpec((tile, width), lambda i, info: (i, 0))
    vector = pl.BlockSpec((1, width), lambda i, info: (0, 0))
    matrix = pl.BlockSpec((width, width), lambda i, info: (0, 0), pipeline_mode=pl.Buffered(1))
    wide = jax.ShapeDtypeStruct((window, width), BF16)
    return pl.pallas_call(
        project_kernel,
        grid_spec=pltpu.PrefetchScalarGridSpec(
            num_scalar_prefetch=1,
            grid=(steps,),
            in_specs=[
                pl.BlockSpec((tile, width), lambda i, info: (jnp.minimum(i, quarter - 1), 0)),
                pl.BlockSpec((tile, width), lambda i, info: (jnp.clip(i - quarter, 0, 2 * quarter - 1), 0)),
                pl.BlockSpec((tile, width), lambda i, info: (jnp.clip(i - 3 * quarter, 0, quarter - 1), 0)),
                vector, vector, matrix, matrix,
                pl.BlockSpec((1, lists, slots), lambda i, info: (info[4], 0, 0)),
                pl.BlockSpec((1, lists, slots), lambda i, info: (info[5], 0, 0)),
            ],
            out_specs=[rows, rows, rows, pl.BlockSpec((lists, window), lambda i, info: (0, 0))],
        ),
        out_shape=[wide, wide, wide, jax.ShapeDtypeStruct((lists, window), BF16)],
        compiler_params=pltpu.CompilerParams(vmem_limit_bytes=57 << 20),
        name="project",
    )(info, head, own, tail, gain, shift, w_s, w_v, blocks, blocks)


def gather_kernel(devices, arrays, length_ref, target_ref, bucket_ref, vector_ref, rows_ref, *refs):
    sources, outs, (info_ref, head_ref, end_ref) = refs[: arrays - 1], refs[arrays - 1 : 2 * arrays - 1], refs[2 * arrays - 1 : 2 * arrays + 2]
    packed_s, before_s, own_sem, sem_o, sem_a, sem_b, sem_c, halo_sem, edge_sem = refs[2 * arrays + 2 :]
    sources = sources + (packed_s,)
    outer, side, core = digits(devices)
    (o, p, q, c), core_peer, q_peers, p_peers, o_peers = neighbours(devices)
    me = lax.axis_index("fsdp")
    last_device = devices - 1
    left, right = lax.rem(me + last_device, devices), lax.rem(me + 1, devices)
    greet([core_peer] + [d for _, d in q_peers] + [d for _, d in p_peers] + [d for _, d in o_peers] + [left, right])
    half = sources[0].shape[-1] // 2
    border = head_ref.shape[0]

    def to_left():
        return remote(rows_ref.at[:border], end_ref, halo_sem, (0,), left)

    def to_right():
        return remote(rows_ref.at[border:], head_ref, halo_sem, (1,), right)

    def blank(ref):
        return pltpu.make_async_copy(before_s.at[:border], ref, edge_sem.at[0])

    columns = (pl.ds(0, half), pl.ds(half, half))

    locals_, begun, first, second, last = [], {}, {}, {}, {}
    for s in range(arrays):
        if s == arrays - 1:
            find_ranks(length_ref, target_ref, bucket_ref, packed_s, info_ref, before_s)
            packed_s[bucket_ref.shape[0] :, :] = vector_ref[...]
        locals_.append(pltpu.make_async_copy(sources[s], outs[s].at[o, p, q, c], own_sem.at[s]))
        locals_[s].start()
        for d, (k, device) in enumerate(o_peers):
            begun[s, d] = remote(sources[s], outs[s].at[o, p, q, c], sem_o, (s, d), device)
            begun[s, d].start()

    @pl.when(me > 0)
    def _():
        to_left().start()

    @pl.when(me < last_device)
    def _():
        to_right().start()

    before_s[:border, :] = jnp.zeros((border, before_s.shape[1]), BF16)

    @pl.when(me == 0)
    def _():
        blank(head_ref).start()

    @pl.when(me == last_device)
    def _():
        blank(end_ref).start()

    def stage_a(s):
        locals_[s].wait()
        for d in range(outer - 1):
            begun[s, d].wait_recv()
        for h, peers in enumerate((q_peers, p_peers)):
            piece = outs[s].at[:, p, q, c, :, columns[h]]
            for d, (k, device) in enumerate(peers):
                first[s, h, d] = remote(piece, piece, sem_a, (s, h, d), device)
                first[s, h, d].start()

    def stage_b(s):
        for h, peers in enumerate((p_peers, q_peers)):
            for d in range(side - 1):
                first[s, h, d].wait_recv()
            piece = outs[s].at[:, p, :, c, :, columns[h]] if h == 0 else outs[s].at[:, :, q, c, :, columns[h]]
            for d, (k, device) in enumerate(peers):
                second[s, h, d] = remote(piece, piece, sem_b, (s, h, d), device)
                second[s, h, d].start()

    def stage_c(s):
        for h in range(2):
            for d in range(side - 1):
                second[s, h, d].wait_recv()
        piece = outs[s].at[:, :, :, c]
        last[s] = remote(piece, piece, sem_c, (s,), core_peer)
        last[s].start()

    for t in range(arrays + 2):
        if t < arrays:
            stage_a(t)
        if 0 <= t - 1 < arrays:
            stage_b(t - 1)
        if 0 <= t - 2 < arrays:
            stage_c(t - 2)
    for s in range(arrays):
        last[s].wait_recv()

    @pl.when(me > 0)
    def _():
        to_right().wait_recv()
        to_left().wait_send()

    @pl.when(me == 0)
    def _():
        blank(head_ref).wait()

    @pl.when(me < last_device)
    def _():
        to_left().wait_recv()
        to_right().wait_send()

    @pl.when(me == last_device)
    def _():
        blank(end_ref).wait()

    for group in (begun, first, second, last):
        for copy in group.values():
            copy.wait_send()


def gather(devices, lengths, destination, buckets, vectors, rows, arrays):
    outer, side, core = digits(devices)
    lists, slots = buckets.shape
    packed = jax.ShapeDtypeStruct((lists + vectors.shape[0], slots), BF16)
    shapes = [jax.ShapeDtypeStruct(array.shape, array.dtype) for array in arrays] + [packed]
    count = len(shapes)
    dma = pltpu.SemaphoreType.DMA
    anywhere = pl.BlockSpec(memory_space=pl.ANY)
    hbm = pl.BlockSpec(memory_space=pltpu.HBM)
    smem = pl.BlockSpec(memory_space=pltpu.SMEM)
    vmem = pl.BlockSpec(memory_space=pltpu.VMEM)
    outs = pl.pallas_call(
        functools.partial(gather_kernel, devices, count),
        out_shape=tuple(jax.ShapeDtypeStruct((outer, side, side, core) + shape.shape, shape.dtype) for shape in shapes)
        + (jax.ShapeDtypeStruct((8,), jnp.int32),)
        + (jax.ShapeDtypeStruct((slots // 2, rows.shape[1]), BF16),) * 2,
        in_specs=[smem, smem, vmem, vmem] + [anywhere] * count,
        out_specs=(hbm,) * count + (smem, hbm, hbm),
        scratch_shapes=[
            pltpu.VMEM(packed.shape, BF16), pltpu.VMEM((slots, slots), BF16),
            dma((count,)), dma((2, count, outer - 1)), dma((2, count, 2, side - 1)), dma((2, count, 2, side - 1)), dma((2, count)),
            dma((2, 2)), dma((1,)),
        ],
        compiler_params=pltpu.CompilerParams(collective_id=2, has_side_effects=True, vmem_limit_bytes=57 << 20),
        name="gather",
    )(lengths, destination, buckets, vectors, rows, *arrays)
    return [out.reshape((devices,) + shape.shape) for out, shape in zip(outs, shapes)] + list(outs[count:])


def body(
    input_one, input_two, upstream_one, upstream_two, lengths, destination, buckets,
    w_shared, w_value, w_output, w_expand, w_reduce,
    gain_attend, shift_attend, gain_mixing, shift_mixing, bias_output, bias_expand, bias_reduce,
):
    devices = lax.axis_size("fsdp")
    me = lax.axis_index("fsdp")
    slots, width = input_one.shape
    half = slots // 2
    window = 2 * slots
    part = w_shared.shape[0]
    hidden = w_expand.shape[1]
    sides = hidden // width
    base = me * slots
    lists = ROUNDS * HEADS
    spot = jnp.arange(width, dtype=jnp.int32)
    short = jnp.stack([gain_attend, shift_attend, gain_mixing, shift_mixing, bias_output, bias_reduce])
    short = jnp.where(spot // part == me, jnp.tile(short, (1, devices)), 0.0)
    many = hidden // devices
    long = jnp.tile(bias_expand, width // many)[None]
    long = jnp.where(spot[None] // many + (width // many) * jnp.arange(sides, dtype=jnp.int32)[:, None] == me, long, 0.0)
    vectors = jnp.concatenate([short, long], axis=0)
    high = lax.reduce_precision(vectors, 8, 7)
    count = vectors.shape[0]
    packed = jnp.concatenate(
        [high.astype(BF16), (vectors - high).astype(BF16), jnp.zeros((24 - 2 * count, width), BF16)], axis=0
    )
    second_gather = lax.all_gather(
        jnp.concatenate(
            [w_reduce, w_output] + [w_expand[:, k * width : (k + 1) * width] for k in range(sides)], axis=0
        ),
        "fsdp", axis=0, tiled=False,
    )
    full_shared, full_value, packed, info, two_head, two_tail = gather(
        devices, lengths, destination, buckets[0], packed, input_two, [w_shared, w_value]
    )
    full_shared, full_value = full_shared.reshape(width, width), full_value.reshape(width, width)
    vectors = jnp.sum(packed[:, lists : lists + 2 * count].astype(F32), axis=0)
    vectors = vectors[:count] + vectors[count:]
    gain_a, shift_a, gain_m, shift_m, bias_o, bias_r = (vectors[k : k + 1] for k in range(6))
    bias_e = vectors[6:].reshape(1, hidden)
    lane = jnp.arange(HEADS * DH, dtype=jnp.int32)
    row = jnp.arange(lists, dtype=jnp.int32)[:, None]
    spread = (row == ((lane % 64) // 16) * HEADS + lane // DH).astype(BF16)

    live = ((base + jnp.arange(slots, dtype=jnp.int32)) < info[6]).astype(F32)[:, None]
    normed, shared, values, code = project(
        info, two_head, input_two, two_tail, gain_a, shift_a, full_shared, full_value, packed
    )
    combined_window, lse, lone = attend(info, shared, values, code, spread)
    combined, out_one, second, d_reduce = join(
        devices, combined_window, input_one, upstream_two, live, second_gather, bias_o, gain_m, shift_m, part, sides
    )
    mixed, d_second, grad_reduce, grad_bias_expand, grad_expand, grad_bias_reduce = mixing(
        devices, second, d_reduce, second_gather, bias_e, bias_r, part
    )
    d_combined, grad_one, result_one, result_two, grad_output, small = turn(
        devices, out_one, d_second, mixed, input_two, upstream_one, combined, live, gain_m, second_gather, grad_bias_reduce, grad_bias_expand,
        sides,
    )
    d_shared, d_values, grad_one, result_one, result_two = attend_back(
        info, shared, values, code, spread, combined_window, d_combined, lse, lone, (grad_one, result_one, result_two)
    )
    grad_two, grad_shared, grad_value, grad_output, grad_reduce, thin, long = tail(
        devices, grad_reduce, grad_output, d_shared, d_values, normed,
        two_head, input_two, two_tail, upstream_two, live, gain_a, full_shared, full_value, small,
    )
    return (
        result_one,
        result_two,
        grad_one,
        grad_two,
        grad_shared,
        grad_value,
        grad_output,
        jnp.concatenate([grad_expand[k * part : (k + 1) * part] for k in range(sides)], axis=1),
        grad_reduce,
        thin[0, :part],
        thin[1, :part],
        thin[2, :part],
        thin[3, :part],
        thin[4, :part],
        long.reshape(-1),
        thin[5, :part],
    )


def solution(mesh):
    rows, flat, whole = P("fsdp", None), P("fsdp"), P()
    return jax.shard_map(
        body,
        mesh=mesh,
        in_specs=(rows,) * 4 + (whole, whole, P("fsdp", None, None)) + (rows,) * 5 + (flat,) * 7,
        out_specs=(rows,) * 9 + (flat,) * 7,
        check_vma=False,
    )
```
